32 devices in a mesh: dp: 8 (over z, y), mp: 4 (over x, core).
Axes of the slice: x: 2, y: 2, z: 4, core: 2. Of those that a mesh axis runs over, the one named last changes fastest.
Arguments:
- tokens: bfloat16 [8, 2048, 768], P('dp', 'mp'), may hold values from -6 to 6
- picture_ids: int32 [8, 2048], P('dp'), may hold values from -1 to 10, as said below
- w_qkv: bfloat16 [768, 3, 768], P('dp', None, 'mp'), may hold values from -0.21875 to 0.21875
- w_out: bfloat16 [768, 768], P('dp', 'mp'), may hold values from -3.5 to 3.5
- w_up: bfloat16 [768, 3072], P('dp', 'mp'), may hold values from -0.21875 to 0.21875
- w_down: bfloat16 [768, 3072], P('dp', 'mp'), may hold values from -0.109375 to 0.109375
- ln1_gain: float32 [768], P(('dp', 'mp')), may hold values from 0.5 to 1.5
- ln1_bias: float32 [768], P(('dp', 'mp')), may hold values from -3 to 3
- q_gain: float32 [768], P(('dp', 'mp')), may hold values from 0.5 to 2
- k_gain: float32 [768], P(('dp', 'mp')), may hold values from 0.5 to 2
- out_bias: float32 [768], P(('dp', 'mp')), may hold values from -3 to 3
- ln2_gain: float32 [768], P(('dp', 'mp')), may hold values from 0.5 to 1.5
- ln2_bias: float32 [768], P(('dp', 'mp')), may hold values from -3 to 3
- up_bias: float32 [3072], P(('dp', 'mp')), may hold values from -3 to 3
- down_bias: float32 [768], P(('dp', 'mp')), may hold values from -3 to 3
- cotangent: bfloat16 [8, 2048, 768], P('dp', 'mp'), may hold values from -6 to 6
Outputs:
- output: bfloat16 [8, 2048, 768], P('dp', 'mp')
- tokens_grad: bfloat16 [8, 2048, 768], P('dp', 'mp')
- w_qkv_grad: float32 [768, 3, 768], P('dp', None, 'mp')
- w_out_grad: float32 [768, 768], P('dp', 'mp')
- w_up_grad: float32 [768, 3072], P('dp', 'mp')
- w_down_grad: float32 [768, 3072], P('dp', 'mp')
- ln1_gain_grad: float32 [768], P(('dp', 'mp'))
- ln1_bias_grad: float32 [768], P(('dp', 'mp'))
- q_gain_grad: float32 [768], P(('dp', 'mp'))
- k_gain_grad: float32 [768], P(('dp', 'mp'))
- out_bias_grad: float32 [768], P(('dp', 'mp'))
- ln2_gain_grad: float32 [768], P(('dp', 'mp'))
- ln2_bias_grad: float32 [768], P(('dp', 'mp'))
- up_bias_grad: float32 [3072], P(('dp', 'mp'))
- down_bias_grad: float32 [768], P(('dp', 'mp'))
The draws below stay inside these ranges and needn't reach their ends.
Inputs may be any that keep to these rules, and one draw needn't show every extreme that they name: `picture_ids`: in each row the positions form consecutive pictures numbered 0, 1, 2, ... from the start, each of 100 to 1024 positions, and one of the first two pictures has exactly 1024; the positions after the last whole picture are padding, marked -1. Some row holds the largest number of pictures that fits.
All inputs are finite; a program needn't handle non-finite values.
Results may differ from the reference program's by a relative error of at most 0.019.
Values may be sent and summed in bfloat16 or wider, within the bound.
A program may use at most 128 MiB of HBM per device.

```python
import math
import jax
import jax.numpy as jnp
from jax import lax

D = 768
HEADS = 12
HEAD_DIM = 64
FF = 3072
ROW = 2048
QBLOCK = 512
PIC_MIN = 100
PIC_MAX = 1024
HHD = 768
ROWS = 8


def draw_picture_ids(key, part):
    slots = ROW // PIC_MIN + 1

    def one_row(row_key, row_number):
        size_key, place_key = jax.random.split(row_key)
        picture_sizes = jax.random.randint(size_key, (slots,), PIC_MIN, PIC_MAX + 1)
        widest = jax.random.randint(place_key, (), 0, 2)
        widest = jnp.where(row_number == 0, 0, widest)
        slot_index = jnp.arange(slots, dtype=jnp.int32)
        picture_sizes = jnp.where(row_number == 0, PIC_MIN, picture_sizes)
        picture_sizes = jnp.where(slot_index == widest, PIC_MAX, picture_sizes).astype(jnp.int32)
        endings = jnp.cumsum(picture_sizes)
        places = jnp.arange(ROW, dtype=jnp.int32)
        labels = jnp.sum((endings[None, :] <= places[:, None]).astype(jnp.int32), axis=1)
        fitted = jnp.sum((endings <= ROW).astype(jnp.int32))
        return jnp.where(labels < fitted, labels, -1).astype(jnp.int32)
    return jax.vmap(one_row)(jax.random.split(key, ROWS), jnp.arange(ROWS, dtype=jnp.int32))


def strengthened(drawn, own_key, source, target, parts, factor):
    owner, partner = [(jnp.arange(drawn.shape[position]) // (drawn.shape[position] // parts)).reshape([-1 if axis == position else 1 for axis in range(drawn.ndim)]) for position in (source, target)]
    chosen = jax.random.permutation(own_key, parts)[partner]
    strong = (owner == chosen) | (owner == (partner + parts // 2) % parts)
    return jnp.where(strong, factor * drawn, drawn)


def level_of(own_key, dims, cuts, least, largest):
    gain, own = 1.0, jax.random.fold_in(own_key, 6)
    for dim, blocks in cuts:
        draws = jnp.exp(jax.random.uniform(jax.random.fold_in(own, dim), (blocks,), jnp.float32, least / len(cuts), largest / len(cuts)))
        gain = gain * jnp.repeat(draws, dims[dim] // blocks).reshape([-1 if axis == dim else 1 for axis in range(len(dims))])
    return gain


def noise(own_key, dims, deviation, bound, shards=(), held_as=jnp.bfloat16):
    level = level_of(own_key, dims, shards, -0.22, 0.18) if shards else 1.0
    values = jax.random.normal(own_key, dims, jnp.float32) * deviation * level
    return jnp.minimum(jnp.maximum(values, -bound), bound).astype(held_as)


def gaussian_with(rng, shape, width, limit, cuts, heavy, held_as=jnp.bfloat16):
    drawn = width * jax.random.normal(rng, shape, jnp.float32)
    if cuts:
        drawn = drawn * level_of(rng, shape, cuts, -0.22, 0.18)
    return jnp.clip(strengthened(drawn, jax.random.fold_in(rng, 3), *heavy), -limit, limit).astype(held_as)


def setup_inputs(seed: int = 0) -> dict:
    key_of = jax.random.split(jax.random.key(seed), 17)
    tokens = gaussian_with(key_of[0], (ROWS, ROW, D), 1.0, 6.0, ((0, 8), (1, 4)), (0, 2, 8, 2.0))
    picture_ids = draw_picture_ids(jax.random.fold_in(key_of[16], 71), 0)
    w_qkv = noise(key_of[2], (D, 3, HHD), D ** -0.5, 0.21875, ((0, 8), (2, 4)))
    w_out = noise(key_of[3], (D, HHD), (HHD * 4 // PIC_MAX) ** -0.5, 3.5, ((0, 8), (1, 4)))
    w_up = noise(key_of[4], (D, FF), D ** -0.5, 0.21875, ((0, 8), (1, 4)))
    w_down = noise(key_of[5], (D, FF), FF ** -0.5, 0.109375, ((0, 8), (1, 4)))
    ln1_gain = jnp.clip(0.5 + 1.0 * jax.random.uniform(key_of[6], (D,), jnp.float32) ** level_of(key_of[6], (D,), ((0, 32),), -0.2, 0.2), 0.5, 1.5)
    ln1_bias = noise(key_of[7], (D,), 0.5, 3.0, ((0, 32),), jnp.float32)
    q_gain = jnp.clip(jnp.exp(math.log(2.0) - 1.3862944 * jax.random.uniform(key_of[8], (HHD,), jnp.float32) ** level_of(key_of[8], (HHD,), ((0, 32),), -0.2, 0.2)), 0.5, 2.0)
    k_gain = jnp.clip(jnp.exp(math.log(2.0) - 1.3862944 * jax.random.uniform(key_of[9], (HHD,), jnp.float32) ** level_of(key_of[9], (HHD,), ((0, 32),), -0.2, 0.2)), 0.5, 2.0)
    out_bias = noise(key_of[10], (D,), 0.5, 3.0, ((0, 32),), jnp.float32)
    ln2_gain = jnp.clip(0.5 + 1.0 * jax.random.uniform(key_of[11], (D,), jnp.float32) ** level_of(key_of[11], (D,), ((0, 32),), -0.2, 0.2), 0.5, 1.5)
    ln2_bias = noise(key_of[12], (D,), 0.5, 3.0, ((0, 32),), jnp.float32)
    up_bias = noise(key_of[13], (FF,), 0.5, 3.0, ((0, 32),), jnp.float32)
    down_bias = noise(key_of[14], (D,), 0.5, 3.0, ((0, 32),), jnp.float32)
    cotangent = gaussian_with(key_of[15], (ROWS, ROW, D), 1.0, 6.0, ((0, 8), (1, 4)), (0, 2, 8, 2.0))
    return {"tokens": tokens, "picture_ids": picture_ids, "w_qkv": w_qkv, "w_out": w_out, "w_up": w_up, "w_down": w_down, "ln1_gain": ln1_gain, "ln1_bias": ln1_bias, "q_gain": q_gain, "k_gain": k_gain, "out_bias": out_bias, "ln2_gain": ln2_gain, "ln2_bias": ln2_bias, "up_bias": up_bias, "down_bias": down_bias, "cotangent": cotangent}


@jax.custom_vjp
def low(v):
    return lax.optimization_barrier(v.astype(jnp.bfloat16)).astype(jnp.float32)

@jax.custom_vjp
def low_back(v):
    return v

def low_keep(v):
    return (low(v), None)

def low_pass(kept, grad):
    return (grad,)

def back_keep(v):
    return (v, None)

def back_low(kept, grad):
    return (low(grad),)
low.defvjp(low_keep, low_pass)
low_back.defvjp(back_keep, back_low)
EPSILON = 1e-06
HIGHEST = lax.Precision.HIGHEST

def layer_norm(values, scaling, shifts):
    centre = lax.optimization_barrier(jnp.mean(values, axis=-1, keepdims=True))
    centred = values - centre
    spread = lax.optimization_barrier(jnp.mean(centred * centred, axis=-1, keepdims=True))
    return centred * lax.rsqrt(spread + EPSILON) * scaling + shifts

def head_norm(values, scaling):
    centre = lax.optimization_barrier(jnp.mean(values, axis=-1, keepdims=True))
    centred = values - centre
    spread = lax.optimization_barrier(jnp.mean(centred * centred, axis=-1, keepdims=True))
    return centred * lax.rsqrt(spread + EPSILON) * scaling

def permitted(label_rows, label_cols, place_rows, place_cols):
    same_pic = (label_rows[:, None] == label_cols[None, :]) & (label_rows[:, None] >= 0)
    return same_pic | (place_rows[:, None] == place_cols[None, :])

def attend(query_rows, key_rows, value_rows, labels):
    length = query_rows.shape[0]
    places = jnp.arange(length, dtype=jnp.int32)
    scaling = HEAD_DIM ** (-0.5)

    def one_block(inputs):
        query_block, label_block, place_block = inputs
        scores = low_back(scaling * jnp.einsum('qhd,khd->hqk', query_block, key_rows, precision=HIGHEST))
        allowed = permitted(label_block, labels, place_block, places)
        scores = jnp.where(allowed[None], scores, -1e+30)
        chances = low(jax.nn.softmax(scores, axis=-1))
        return jnp.einsum('hqk,khd->qhd', chances, value_rows, precision=HIGHEST)
    blocks = length // QBLOCK
    result = lax.map(jax.checkpoint(one_block), (query_rows.reshape(blocks, QBLOCK, HEADS, HEAD_DIM), labels.reshape(blocks, QBLOCK), places.reshape(blocks, QBLOCK)))
    return result.reshape(length, HEADS * HEAD_DIM)

def block_forward(row_tokens, labels, w_qkv, w_out, w_up, w_down, ln1_gain, ln1_bias, q_gain, k_gain, out_bias, ln2_gain, ln2_bias, up_bias, down_bias):
    length = row_tokens.shape[0]
    normed = low(layer_norm(row_tokens, ln1_gain, ln1_bias))
    projected = low_back(jnp.einsum('td,dce->tce', normed, w_qkv, precision=HIGHEST))
    query_raw = projected[:, 0].reshape(length, HEADS, HEAD_DIM)
    key_raw = projected[:, 1].reshape(length, HEADS, HEAD_DIM)
    value_raw = projected[:, 2].reshape(length, HEADS, HEAD_DIM)
    query_low = low(head_norm(query_raw, q_gain.reshape(HEADS, HEAD_DIM)))
    key_low = low(head_norm(key_raw, k_gain.reshape(HEADS, HEAD_DIM)))
    value_low = low(value_raw)
    attended = low_back(low(attend(query_low, key_low, value_low, labels)))
    branch = low_back(jnp.einsum('te,de->td', attended, w_out, precision=HIGHEST))
    middle = row_tokens + branch + out_bias
    normed_two = low(layer_norm(middle, ln2_gain, ln2_bias))
    up_pre = low_back(jnp.einsum('td,df->tf', normed_two, w_up, precision=HIGHEST) + up_bias)
    activated = low(jax.nn.gelu(up_pre, approximate=False))
    mlp_out = low_back(jnp.einsum('tf,df->td', activated, w_down, precision=HIGHEST))
    return middle + mlp_out + down_bias

def reference(tokens, picture_ids, w_qkv, w_out, w_up, w_down, ln1_gain, ln1_bias, q_gain, k_gain, out_bias, ln2_gain, ln2_bias, up_bias, down_bias, cotangent):
    floats = [item.astype(jnp.float32) for item in (tokens, w_qkv, w_out, w_up, w_down, ln1_gain, ln1_bias, q_gain, k_gain, out_bias, ln2_gain, ln2_bias, up_bias, down_bias)]

    def whole_layer(inputs_f32, *params):

        def one_row(carried, row_inputs):
            row_tokens, labels = row_inputs
            return (carried, jax.checkpoint(block_forward)(row_tokens, labels, *params))
        _, result = lax.scan(one_row, jnp.float32(0.0), (inputs_f32, picture_ids))
        return result
    result, pullback = jax.vjp(whole_layer, *floats)
    gradients = pullback(cotangent.astype(jnp.float32))
    return (result.astype(jnp.bfloat16), gradients[0].astype(jnp.bfloat16), gradients[1], gradients[2], gradients[3], gradients[4], gradients[5], gradients[6], gradients[7], gradients[8], gradients[9], gradients[10], gradients[11], gradients[12], gradients[13])
```

```python
import functools

import jax
import jax.numpy as jnp
from jax import lax
from jax.experimental import pallas as pl
from jax.experimental.pallas import tpu as pltpu
from jax.sharding import PartitionSpec as P

F32 = jnp.float32
BF = jnp.bfloat16
HEAD = 64
EPS = 1e-06
TB = 256
BIG = 32768.0
LOG2E = 1.4426950408889634
MESH = pl.DeviceIdType.MESH
ANY = pl.BlockSpec(memory_space=pl.ANY)
VM = pl.BlockSpec(memory_space=pltpu.VMEM)
SM = pl.BlockSpec(memory_space=pltpu.SMEM)
VLIM = 60 * 1024 * 1024


def nn(a, b):
    return lax.dot_general(a, b, (((1,), (0,)), ((), ())), preferred_element_type=F32)


def nt(a, b):
    return lax.dot_general(a, b, (((1,), (1,)), ((), ())), preferred_element_type=F32)


def tn(a, b):
    return lax.dot_general(a, b, (((0,), (0,)), ((), ())), preferred_element_type=F32)


def sds(shape, dtype):
    return jax.ShapeDtypeStruct(shape, dtype)


def params(**kw):
    return pltpu.CompilerParams(vmem_limit_bytes=VLIM, **kw)


def cost(flops, nbytes, trans=0):
    return pl.CostEstimate(flops=int(flops), bytes_accessed=int(nbytes), transcendentals=int(trans))


def rcopy(src, dst, ssem, rsem, peer):
    return pltpu.make_async_remote_copy(
        src_ref=src,
        dst_ref=dst,
        send_sem=ssem,
        recv_sem=rsem,
        device_id=peer,
        device_id_type=MESH,
    )


def greet(peers):
    bar = pltpu.get_barrier_semaphore()
    for p in peers:
        pl.semaphore_signal(bar, inc=1, device_id=p, device_id_type=MESH)
    pl.semaphore_wait(bar, len(peers))


def gather_kernel(
    nz, nc, tok, w, vec, tok_all, w_all, vec_all, loc, zs, zr, ys, yr, xs, xr, cs, cr, tx, rx, tc, rc
):
    dp, mp = lax.axis_index("dp"), lax.axis_index("mp")
    z, y, x, c = dp // 2, dp % 2, mp // 2, mp % 2
    xm, cm, dm = (1 - x) * 2 + c, x * 2 + 1 - c, (1 - x) * 2 + 1 - c
    ypeer, xpeer, cpeer = (z * 2 + 1 - y, mp), (dp, xm), (dp, cm)
    zpeers = [(((z + k) % nz) * 2 + y, mp) for k in range(1, nz)]
    greet(zpeers + [ypeer, xpeer, cpeer])
    rows = tok.shape[0] // nc
    xt = []
    for i in range(nc):
        part = pl.ds(i * rows, rows)
        cp = rcopy(tok.at[part], tok_all.at[mp, part], tx.at[i], rx.at[i], xpeer)
        cp.start()
        xt.append(cp)
    zc = []
    for k in range(1, nz):
        for kind, (src, dst) in enumerate(((vec, vec_all.at[mp, dp]), (w, w_all.at[dp]))):
            cp = rcopy(src, dst, zs.at[kind, k], zr.at[kind, k], zpeers[k - 1])
            cp.start()
            zc.append(cp)
    yc = []
    for kind, (src, dst) in enumerate(((vec, vec_all.at[mp, dp]), (w, w_all.at[dp]))):
        cp = rcopy(src, dst, ys.at[kind, 0], yr.at[kind, 0], ypeer)
        cp.start()
        yc.append(cp)
    own_tok = rcopy(tok, tok_all.at[mp], tc.at[nc], rc.at[nc], cpeer)
    own_tok.start()
    locs = [
        pltpu.make_async_copy(tok, tok_all.at[mp], loc.at[0]),
        pltpu.make_async_copy(w, w_all.at[dp], loc.at[1]),
        pltpu.make_async_copy(vec, vec_all.at[mp, dp], loc.at[2]),
    ]
    for cp in locs:
        cp.start()
    for k in range(1, nz):
        src_dp = ((z + nz - k) % nz) * 2 + y
        for kind in range(2):
            zc[(k - 1) * 2 + kind].wait_recv()
            ref = (vec_all.at[mp, src_dp], w_all.at[src_dp])[kind]
            cp = rcopy(ref, ref, ys.at[kind, k], yr.at[kind, k], ypeer)
            cp.start()
            yc.append(cp)
    ct = []

    def forward(i):
        part = pl.ds(i * rows, rows)
        xt[i].wait_recv()
        cp = rcopy(tok_all.at[xm, part], tok_all.at[xm, part], tc.at[i], rc.at[i], cpeer)
        cp.start()
        ct.append(cp)

    forward(0)
    for cp in locs:
        cp.wait()
    for k in range(nz):
        yc[k * 2].wait_recv()
    vx = rcopy(vec_all.at[mp], vec_all.at[mp], xs, xr, xpeer)
    vx.start()
    vc0 = rcopy(vec_all.at[mp], vec_all.at[mp], cs.at[0], cr.at[0], cpeer)
    vc0.start()
    if nc > 1:
        forward(1)
    vx.wait_recv()
    vc1 = rcopy(vec_all.at[xm], vec_all.at[xm], cs.at[1], cr.at[1], cpeer)
    vc1.start()
    for i in range(2, nc):
        forward(i)
    for k in range(nz):
        yc[k * 2 + 1].wait_recv()
    for cp in ct:
        cp.wait_recv()
    own_tok.wait()
    vc0.wait()
    vc1.wait()
    vx.wait_send()
    for cp in zc + yc + xt + ct:
        cp.wait_send()


def gather_all(tok, w, vec, ndp, nmp):
    nz, nc = ndp // 2, 4
    dma = pltpu.SemaphoreType.DMA
    return pl.pallas_call(
        functools.partial(gather_kernel, nz, nc),
        out_shape=(
            sds((nmp,) + tok.shape, BF),
            sds((ndp,) + w.shape, BF),
            sds((nmp, ndp) + vec.shape, F32),
        ),
        in_specs=[ANY] * 3,
        out_specs=(ANY,) * 3,
        scratch_shapes=[
            dma((3,)),
            dma((2, nz)),
            dma((2, nz)),
            dma((2, nz)),
            dma((2, nz)),
            dma,
            dma,
            dma((2,)),
            dma((2,)),
            dma((nc,)),
            dma((nc,)),
            dma((nc + 1,)),
            dma((nc + 1,)),
        ],
        compiler_params=pltpu.CompilerParams(collective_id=0, has_side_effects=True),
        name="gather_start",
    )(tok, w, vec)


def swap_kernel(forward, nmp, src, dst, loc, ss, rs):
    dp, mp = lax.axis_index("dp"), lax.axis_index("mp")
    own = dst.shape[2] if forward else src.shape[2]
    peers = [(mp + k) % nmp for k in range(1, nmp)]
    greet([(dp, m) for m in peers])

    def ends(m):
        if forward:
            return src.at[:, pl.ds(pl.multiple_of(m * own, own), own)], dst.at[mp]
        return src.at[m], dst.at[:, pl.ds(pl.multiple_of(mp * own, own), own)]

    cps = []
    for k, m in enumerate(peers):
        s, d = ends(m)
        cp = rcopy(s, d, ss.at[k], rs.at[k], (dp, m))
        cp.start()
        cps.append(cp)
    s, d = ends(mp)
    lc = pltpu.make_async_copy(s, d, loc)
    lc.start()
    lc.wait()
    for cp in cps:
        cp.wait()


def swap(src, forward, nmp, cid):
    dma = pltpu.SemaphoreType.DMA
    if forward:
        shape = (nmp, src.shape[0], src.shape[1] // nmp)
    else:
        shape = (src.shape[1], src.shape[2] * nmp)
    return pl.pallas_call(
        functools.partial(swap_kernel, forward, nmp),
        out_shape=sds(shape, BF),
        in_specs=[ANY],
        out_specs=ANY,
        scratch_shapes=[dma, dma((nmp - 1,)), dma((nmp - 1,))],
        compiler_params=pltpu.CompilerParams(collective_id=cid, has_side_effects=True),
        name="swap_fwd" if forward else "swap_bwd",
    )(src)


def vector_kernel(ndp, nmp, src, out, got, ss, rs):
    dp, mp = lax.axis_index("dp"), lax.axis_index("mp")
    me, n = dp * nmp + mp, ndp * nmp
    peers = [(me + k) % n for k in range(1, n)]
    greet([(p // nmp, p % nmp) for p in peers])
    cps = []
    for k, p in enumerate(peers):
        cp = rcopy(src.at[p], got.at[k], ss.at[k], rs.at[k], (p // nmp, p % nmp))
        cp.start()
        cps.append(cp)
    total = src[me]
    for k, cp in enumerate(cps):
        cp.wait_recv()
        total = total + got[k]
    out[...] = total
    for cp in cps:
        cp.wait_send()


def vector_sums(parts, ndp, nmp):
    n = ndp * nmp
    dma = pltpu.SemaphoreType.DMA
    return pl.pallas_call(
        functools.partial(vector_kernel, ndp, nmp),
        out_shape=sds(parts.shape[1:], F32),
        in_specs=[VM],
        out_specs=VM,
        scratch_shapes=[pltpu.VMEM((n - 1,) + parts.shape[1:], F32), dma((n - 1,)), dma((n - 1,))],
        compiler_params=pltpu.CompilerParams(collective_id=3, has_side_effects=True),
        name="vector_sums",
    )(parts)


def norm_rows(v):
    centre = jnp.mean(v, axis=-1, keepdims=True)
    v = v - centre
    r = lax.rsqrt(jnp.mean(v * v, axis=-1, keepdims=True) + EPS)
    return v * r, r


def norm_cols(v):
    centre = jnp.mean(v, axis=0, keepdims=True)
    v = v - centre
    r = lax.rsqrt(jnp.mean(v * v, axis=0, keepdims=True) + EPS)
    return v * r, r


def qkv_kernel(heads, tok, w, gain, shift, gains, normed, raw, low, wt):
    @pl.when(pl.program_id(0) == 0)
    def _():
        wt[...] = w[...].T

    cols = heads * HEAD
    hat, _ = norm_rows(tok[0].astype(F32))
    n = (hat * gain[...] + shift[...]).astype(BF)
    normed[...] = n
    proj = nt(wt[0 : 3 * cols, :], n)
    raw[...] = proj[0 : 2 * cols]
    for h in range(2 * heads):
        part = slice(h * HEAD, (h + 1) * HEAD)
        hat, _ = norm_cols(proj[part])
        low[part, :] = (hat * gains[part, :]).astype(BF)
    low[2 * cols :, :] = proj[2 * cols :].astype(BF)


def project(tok_all, w, gain, shift, gains, heads):
    nb, rows, d = tok_all.shape
    cols = heads * HEAD
    t = nb * rows
    full = lambda shape: pl.BlockSpec(shape, lambda i: (0,) * len(shape))
    return pl.pallas_call(
        functools.partial(qkv_kernel, heads),
        grid=(nb,),
        out_shape=(
            sds((t, d), BF),
            sds((2 * cols, t), F32),
            sds((3 * cols, t), BF),
            sds((w.shape[1], w.shape[0]), BF),
        ),
        in_specs=[
            pl.BlockSpec((1, rows, d), lambda i: (i, 0, 0)),
            full(w.shape),
            full((1, d)),
            full((1, d)),
            full((2 * cols, 1)),
        ],
        out_specs=(
            pl.BlockSpec((rows, d), lambda i: (i, 0)),
            pl.BlockSpec((2 * cols, rows), lambda i: (0, i)),
            pl.BlockSpec((3 * cols, rows), lambda i: (0, i)),
            full((w.shape[1], w.shape[0])),
        ),
        compiler_params=params(),
        cost_estimate=cost(2 * t * d * 3 * cols, 12 * 2**20),
        name="project_qkv",
    )(tok_all, w, gain, shift, gains)


def masks(ids):
    t = ids.shape[1]
    r = lax.broadcasted_iota(jnp.int32, (2 * HEAD, t), 0)
    pad = ids < 0
    mq = jnp.where(r == ids, 1.0, 0.0)
    mq = jnp.where((r == 31) & pad, 1.0, mq)
    mk = jnp.where((r < 31) & (r != ids), -BIG, 0.0)
    mk = jnp.where(r == 31, -BIG, mk)
    mk = jnp.where((r >= 32) & (r < 35), 1.0, mk)
    return mq, mk


def three(v):
    a = v.astype(BF).astype(F32)
    b = (v - a).astype(BF).astype(F32)
    return a, b, v - a - b


def split_query(q):
    s = q.astype(F32) * (LOG2E * HEAD**-0.5)
    hi = s.astype(BF)
    return hi, (s - hi.astype(F32)).astype(BF)


def attend_kernel(heads, nblk, span, low, ids, out, lse, qa, ka, va, acc):
    cols = heads * HEAD
    t = ids.shape[1]
    mq, mk = masks(ids[...])
    mq, mkt = mq.astype(BF), mk.T.astype(BF)
    one = jnp.where(lax.broadcasted_iota(jnp.int32, (16, t), 0) == 0, 1.0, 0.0).astype(BF)
    for h in range(heads):
        hi, lo = split_query(low[h * HEAD : (h + 1) * HEAD, :])
        qa[h, 0:HEAD, :] = hi
        qa[h, HEAD : 2 * HEAD, :] = lo
        qa[h, 2 * HEAD :, :] = mq
        k = low[cols + h * HEAD : cols + (h + 1) * HEAD, :].astype(F32)
        ka[h, :, 0 : 2 * HEAD] = jnp.concatenate([k, k], axis=0).T.astype(BF)
        ka[h, :, 2 * HEAD :] = mkt
        va[h, 0:HEAD, :] = low[2 * cols + h * HEAD : 2 * cols + (h + 1) * HEAD, :]
        va[h, HEAD:, :] = one
    acc[...] = jnp.zeros_like(acc)

    def row(i, _):
        qi = pl.ds(pl.multiple_of(i * TB, TB), TB)

        def col(j, _):
            kj = pl.ds(pl.multiple_of(j * TB, TB), TB)
            for h in range(heads):
                s = nn(ka[h, kj, :], qa[h, :, qi])
                acc[h, :, qi] += nn(va[h, :, kj], jnp.exp2(s).astype(BF))
            return 0

        return lax.fori_loop(span[i], span[nblk + i], col, 0)

    lax.fori_loop(0, nblk, row, 0)
    pad = ids[...] < 0
    lse[...] = jnp.zeros_like(lse)
    for h in range(heads):
        total = jnp.where(pad, 1.0, acc[h, HEAD : HEAD + 1, :])
        value = low[2 * cols + h * HEAD : 2 * cols + (h + 1) * HEAD, :].astype(F32)
        o = jnp.where(pad, value, acc[h, 0:HEAD, :] / total)
        out[h * HEAD : (h + 1) * HEAD, :] = o.astype(BF)
        lse[h : h + 1, :] = jnp.log2(total)


def attend(span, low, ids, heads):
    cols, t = heads * HEAD, low.shape[1]
    return pl.pallas_call(
        functools.partial(attend_kernel, heads, t // TB),
        out_shape=(sds((cols, t), BF), sds((8, t), F32)),
        in_specs=[SM, VM, VM],
        out_specs=(VM, VM),
        scratch_shapes=[
            pltpu.VMEM((heads, 4 * HEAD, t), BF),
            pltpu.VMEM((heads, t, 4 * HEAD), BF),
            pltpu.VMEM((heads, HEAD + 16, t), BF),
            pltpu.VMEM((heads, HEAD + 16, t), F32),
        ],
        compiler_params=params(),
        cost_estimate=cost(12e9, 4 * 2**20),
        name="attend",
    )(span, low, ids)


def head_back(raw, gain, grad):
    hat, r = norm_cols(raw)
    e = grad * gain
    m1 = jnp.mean(e, axis=0, keepdims=True)
    m2 = jnp.mean(e * hat, axis=0, keepdims=True)
    return (e - m1 - hat * m2) * r, jnp.sum(grad * hat, axis=1, keepdims=True)


def attend_back_kernel(
    heads, nblk, span, low, raw, att, lse, dout, ids, gains, gproj, ggain, qa, ka, va, da, dq, dk, dv
):
    cols = heads * HEAD
    t = ids.shape[1]
    mq, mk = masks(ids[...])
    mkt = mk.T.astype(BF)
    r = lax.broadcasted_iota(jnp.int32, (2 * HEAD, t), 0)
    r64 = lax.broadcasted_iota(jnp.int32, (HEAD, t), 0)
    one = jnp.where(r64 < 3, 1.0, 0.0)
    for h in range(heads):
        hs = slice(h * HEAD, (h + 1) * HEAD)
        hi, lo = split_query(low[hs, :])
        qa[h, 0:HEAD, :] = hi
        qa[h, HEAD : 2 * HEAD, :] = lo
        a, b, c = three(-lse[h : h + 1, :])
        m = jnp.where(r == 32, a, jnp.where(r == 33, b, jnp.where(r == 34, c, mq)))
        qa[h, 2 * HEAD :, :] = m.astype(BF)
        k = low[cols + h * HEAD : cols + (h + 1) * HEAD, :].astype(F32)
        ka[h, :, 0 : 2 * HEAD] = jnp.concatenate([k, k], axis=0).T.astype(BF)
        ka[h, :, 2 * HEAD :] = mkt
        v = low[2 * cols + h * HEAD : 2 * cols + (h + 1) * HEAD, :].astype(F32)
        va[h, :, :] = jnp.concatenate([v, one], axis=0).T.astype(BF)
        do = dout[hs, :]
        delta = jnp.sum(do.astype(F32) * att[hs, :].astype(F32), axis=0, keepdims=True)
        a, b, c = three(-delta)
        da[h, 0:HEAD, :] = do
        da[h, HEAD:, :] = jnp.where(
            r64 == 0, a, jnp.where(r64 == 1, b, jnp.where(r64 == 2, c, 0.0))
        ).astype(BF)
    dq[...] = jnp.zeros_like(dq)
    dk[...] = jnp.zeros_like(dk)
    dv[...] = jnp.zeros_like(dv)

    def row(i, _):
        qi = pl.ds(pl.multiple_of(i * TB, TB), TB)

        def col(j, _):
            kj = pl.ds(pl.multiple_of(j * TB, TB), TB)
            for h in range(heads):
                hs = pl.ds(h * HEAD, HEAD)
                p = jnp.exp2(nn(ka[h, kj, :], qa[h, :, qi]))
                ds = (p * nn(va[h, kj, :], da[h, :, qi])).astype(BF)
                dv[hs, kj] += nt(dout[hs, qi], p.astype(BF))
                dk[hs, kj] += nt(low[hs, qi], ds)
                dq[hs, qi] += nn(low[pl.ds(cols + h * HEAD, HEAD), kj], ds)
            return 0

        return lax.fori_loop(span[i], span[nblk + i], col, 0)

    lax.fori_loop(0, nblk, row, 0)
    pad = ids[...] < 0
    scale = HEAD**-0.5
    for h in range(heads):
        hs = slice(h * HEAD, (h + 1) * HEAD)
        for part, grad in ((0, dq), (1, dk)):
            ps = slice(part * cols + h * HEAD, part * cols + (h + 1) * HEAD)
            g, gg = head_back(raw[ps, :], gains[ps, :], grad[hs, :] * scale)
            gproj[ps, :] = g.astype(BF)
            ggain[ps, :] = gg
        g = dv[hs, :] + jnp.where(pad, dout[hs, :].astype(F32), 0.0)
        gproj[2 * cols + h * HEAD : 2 * cols + (h + 1) * HEAD, :] = g.astype(BF)


def attend_back(span, low, raw, att, lse, dout, ids, gains, heads):
    cols, t = heads * HEAD, low.shape[1]
    return pl.pallas_call(
        functools.partial(attend_back_kernel, heads, t // TB),
        out_shape=(sds((3 * cols, t), BF), sds((2 * cols, 1), F32)),
        in_specs=[SM] + [VM] * 7,
        out_specs=(VM, VM),
        scratch_shapes=[
            pltpu.VMEM((heads, 4 * HEAD, t), BF),
            pltpu.VMEM((heads, t, 4 * HEAD), BF),
            pltpu.VMEM((heads, t, 2 * HEAD), BF),
            pltpu.VMEM((heads, 2 * HEAD, t), BF),
            pltpu.VMEM((cols, t), F32),
            pltpu.VMEM((cols, t), F32),
            pltpu.VMEM((cols, t), F32),
        ],
        compiler_params=params(),
        cost_estimate=cost(30e9, 12 * 2**20),
        name="attend_back",
    )(span, low, raw, att, lse, dout, ids, gains)


def place_out(pieces, dest):
    mp = lax.axis_index("mp")
    x, c = mp // 2, mp % 2
    order = (mp, (1 - x) * 2 + c, x * 2 + 1 - c, (1 - x) * 2 + 1 - c)
    rows = pieces[0].shape[0]
    for piece, m in zip(pieces, order):
        dest[pl.ds(pl.multiple_of(m * rows, rows), rows), :] = piece[...]


def middle_kernel(att, w0, w1, w2, w3, tok, bias, gain, shift, mid, low, wo):
    place_out((w0, w1, w2, w3), wo)
    m = tok[...].astype(F32) + tn(att[...], wo[...]) + bias[...]
    mid[...] = m
    hat, _ = norm_rows(m)
    low[...] = (hat * gain[...] + shift[...]).astype(BF)


def middle_part(att, wos, tok, bias, gain, shift):
    rows, d = tok.shape
    return pl.pallas_call(
        middle_kernel,
        out_shape=(sds((rows, d), F32), sds((rows, d), BF)),
        in_specs=[VM] * 9,
        out_specs=(VM, VM),
        scratch_shapes=[pltpu.VMEM((d, d), BF)],
        compiler_params=params(),
        cost_estimate=cost(2 * rows * d * d, 6 * 2**20),
        name="middle",
    )(att, *wos, tok, bias, gain, shift)


def middle_back_kernel(
    nmp, g0, g1, mid, cot, att, w0, w1, w2, w3, gain, gmid, gatt, gwo, sums, wo
):
    place_out((w0, w1, w2, w3), wo)
    gy = cot[...].astype(F32)
    g = g0[...] + g1[...].astype(F32)
    hat, r = norm_rows(mid[...])
    e = g * gain[...]
    m1 = jnp.mean(e, axis=-1, keepdims=True)
    m2 = jnp.mean(e * hat, axis=-1, keepdims=True)
    gm = gy + (e - m1 - hat * m2) * r
    gmid[...] = gm
    low = gm.astype(BF)
    rows = att.shape[0] // nmp
    ga = nt(wo[...], low).astype(BF)
    for m in range(nmp):
        gatt[m] = ga[m * rows : (m + 1) * rows]
    gw = nt(gm.T.astype(BF), att[...]).astype(BF)
    mp = lax.axis_index("mp")
    for m in range(nmp):
        gwo[m] = gw[:, m * rows : (m + 1) * rows]
    sums[...] = jnp.zeros_like(sums)
    for k, v in enumerate((gm, g * hat, g, gy)):
        sums[k : k + 1, :] = jnp.sum(v, axis=0, keepdims=True)


def middle_back(g0, g1, mid, cot, att, wos, gain, nmp):
    rows, d = mid.shape
    return pl.pallas_call(
        functools.partial(middle_back_kernel, nmp),
        out_shape=(
            sds((rows, d), F32),
            sds((nmp, d // nmp, rows), BF),
            sds((nmp, d, d // nmp), BF),
            sds((8, d), F32),
        ),
        in_specs=[VM] * 10,
        out_specs=(VM,) * 4,
        scratch_shapes=[pltpu.VMEM((d, d), BF)],
        compiler_params=params(),
        cost_estimate=cost(4 * rows * d * d, 10 * 2**20),
        name="middle_back",
    )(g0, g1, mid, cot, att, *wos, gain)


def feed_kernel(npiece, nz, *refs):
    n0, n1, c0, c1, bias = refs[:5]
    pieces = refs[5 : 5 + npiece]
    out_own, out_send, g_own, g_send, dwu, dwd, gbias = refs[5 + npiece : 12 + npiece]
    wu, wd, n2, gy, n2t, gyt, acts, gps, oacc, gacc, sem = refs[12 + npiece :]
    dp, mp = lax.axis_index("dp"), lax.axis_index("mp")
    z, y, x, c = dp // 2, dp % 2, mp // 2, mp % 2
    copies = []
    half = npiece // 2
    for a, piece in enumerate(pieces):
        dest = (wu, wd)[a // half]
        rel = a % half
        count, rows = piece.shape[0], piece.shape[1]
        for k in range(count):
            if half == 2:
                at, colidx = 0, rel
            else:
                zz = (z + nz - k) % nz
                at = (zz * 2 + (y if rel % 2 == 0 else 1 - y)) * rows
                at, colidx = pl.multiple_of(at, rows), rel // 2
            cp = pltpu.make_async_copy(piece.at[k], dest.at[colidx, pl.ds(at, rows), :], sem.at[a, k])
            cp.start()
            copies.append(cp)
    hr = n0.shape[0]
    for i, (n, g) in enumerate(((n0, c0), (n1, c1))):
        part = slice(i * hr, (i + 1) * hr)
        n2[part, :] = n[...]
        gy[part, :] = g[...]
        n2t[:, part] = n[...].T
        gyt[:, part] = g[...].T
    oacc[...] = jnp.zeros_like(oacc)
    gacc[...] = jnp.zeros_like(gacc)
    for cp in copies:
        cp.wait()
    rows, d = n2.shape
    cw = acts.shape[1]
    per = wu.shape[2] // cw
    ones = jnp.ones((16, rows), BF)

    def chunk(i, _):
        col, off = i // per, pl.multiple_of((i % per) * cw, cw)
        cs = pl.ds(off, cw)
        m = jnp.where(col == 0, mp, (1 - x) * 2 + c)
        b = bias[pl.ds(m, 1), cs]
        for rb in range(rows // 256):
            rs = slice(rb * 256, (rb + 1) * 256)
            u = nn(n2[rs, :], wu[col, :, cs]) + b
            ga = nn(gy[rs, :], wd[col, :, cs])
            cdf = 0.5 + 0.5 * lax.erf(u * 0.7071067811865476)
            act = (u * cdf).astype(BF)
            gp = (ga * (cdf + u * (jnp.exp(-0.5 * u * u) * 0.3989422804014327))).astype(BF)
            acts[rs, :] = act
            gps[rs, :] = gp
            oacc[rs, :] += nt(act, wd[col, :, cs])
            gacc[rs, :] += nt(gp, wu[col, :, cs])
        dwd[col, :, cs] = nn(gyt[...], acts[...]).astype(BF)
        dwu[col, :, cs] = nn(n2t[...], gps[...]).astype(BF)
        gbias[col, :, cs] = nn(ones, gps[...])[0:8]
        return 0

    lax.fori_loop(0, 2 * per, chunk, 0)
    out_own[...] = oacc[0:hr]
    out_send[...] = oacc[hr:].astype(BF)
    g_own[...] = gacc[0:hr]
    g_send[...] = gacc[hr:].astype(BF)


def feed(n0, n1, c0, c1, bias, ups, downs, nz):
    hr, d = n0.shape
    rows, cw = 2 * hr, 256
    unit = ups[0].shape[2]
    pieces = list(ups) + list(downs)
    kmax = max(p.shape[0] for p in pieces)
    vm = pltpu.VMEM
    return pl.pallas_call(
        functools.partial(feed_kernel, len(pieces), nz),
        out_shape=(
            sds((hr, d), F32),
            sds((hr, d), BF),
            sds((hr, d), F32),
            sds((hr, d), BF),
            sds((2, d, unit), BF),
            sds((2, d, unit), BF),
            sds((2, 8, unit), F32),
        ),
        in_specs=[VM] * 5 + [ANY] * len(pieces),
        out_specs=(VM,) * 7,
        scratch_shapes=[
            vm((2, d, unit), BF),
            vm((2, d, unit), BF),
            vm((rows, d), BF),
            vm((rows, d), BF),
            vm((d, rows), BF),
            vm((d, rows), BF),
            vm((rows, cw), BF),
            vm((rows, cw), BF),
            vm((rows, d), F32),
            vm((rows, d), F32),
            pltpu.SemaphoreType.DMA((len(pieces), kmax)),
        ],
        compiler_params=params(),
        cost_estimate=cost(12 * rows * d * 2 * unit, 22 * 2**20),
        name="feed_forward",
    )(n0, n1, c0, c1, bias, *pieces)


def project_back_kernel(order, gproj, normed, tok, wt, gn, gw, sums, acc):
    @pl.when(pl.program_id(0) == 0)
    def _():
        acc[...] = jnp.zeros_like(acc)
        sums[...] = jnp.zeros_like(sums)

    acc[...] += nn(gproj[...], normed[...])
    g = tn(gproj[...], wt[...])
    gn[0] = g.astype(BF)
    hat, _ = norm_rows(tok[0].astype(F32))
    sums[0:1, :] += jnp.sum(g * hat, axis=0, keepdims=True)
    sums[1:2, :] += jnp.sum(g, axis=0, keepdims=True)

    @pl.when(pl.program_id(0) == pl.num_programs(0) - 1)
    def _():
        gw[...] = acc[...].T.astype(BF)


def project_back(order, gproj, normed, tok_all, wt):
    nb, rows, d = tok_all.shape
    n = gproj.shape[0]
    t = nb * rows
    return pl.pallas_call(
        project_back_kernel,
        grid_spec=pltpu.PrefetchScalarGridSpec(
            num_scalar_prefetch=1,
            grid=(nb,),
            in_specs=[
                pl.BlockSpec((n, rows), lambda i, o: (0, o[i])),
                pl.BlockSpec((rows, d), lambda i, o: (o[i], 0)),
                pl.BlockSpec((1, rows, d), lambda i, o: (o[i], 0, 0)),
                pl.BlockSpec((n, d), lambda i, o: (0, 0)),
            ],
            out_specs=(
                pl.BlockSpec((1, rows, d), lambda i, o: (i, 0, 0)),
                pl.BlockSpec((d, n), lambda i, o: (0, 0)),
                pl.BlockSpec((8, d), lambda i, o: (0, 0)),
            ),
            scratch_shapes=[pltpu.VMEM((n, d), F32)],
        ),
        out_shape=(sds((nb, rows, d), BF), sds((d, n), BF), sds((8, d), F32)),
        compiler_params=params(),
        cost_estimate=cost(4 * t * d * n, 14 * 2**20),
        name="project_back",
    )(order, gproj, normed, tok_all, wt)


def tokens_back(gn, tok, gain, gmid):
    hat, r = norm_rows(tok.astype(F32))
    e = gn * gain
    m1 = jnp.mean(e, axis=-1, keepdims=True)
    m2 = jnp.mean(e * hat, axis=-1, keepdims=True)
    return (gmid + (e - m1 - hat * m2) * r).astype(BF)


def spans(ids):
    b = ids.reshape(-1, TB)
    low = jnp.min(jnp.where(b < 0, 1000, b), axis=1)
    high = jnp.max(b, axis=1)
    n = b.shape[0]
    k = jnp.arange(n)
    lo = jnp.sum((high[None, :] < low[:, None]) & (k[None, :] <= k[:, None]), axis=1)
    hi = jnp.sum(low[None, :] <= high[:, None], axis=1)
    return jnp.concatenate([lo, hi]).astype(jnp.int32)


def solution(mesh):
    ndp, nmp = mesh.shape["dp"], mesh.shape["mp"]
    ndev, nz = ndp * nmp, ndp // 2

    def permute(v, kind, k=0):
        pairs = []
        for d in range(ndp):
            for m in range(nmp):
                z, y, x, c = d // 2, d % 2, m // 2, m % 2
                if kind == "core":
                    c = 1 - c
                if kind == "x":
                    x = 1 - x
                if kind == "y":
                    y = 1 - y
                if kind == "z":
                    z = (z + k) % nz
                pairs.append((d * nmp + m, (z * 2 + y) * nmp + x * 2 + c))
        return lax.ppermute(v, ("dp", "mp"), pairs)

    def columns(w, first, second):
        if w.shape[0] % 16:
            own = lax.all_gather(w, "dp", axis=0, tiled=True)[None]
            return [own, permute(own, "x")]
        s = jnp.stack([w] + [permute(w, "z", k) for k in range(1, nz)])
        got = {(0, 0): s}
        one = permute(s, first)
        two = permute(s, second)
        both = permute(one, second)
        got[(0, 1)] = one if first == "y" else two
        got[(1, 0)] = two if first == "y" else one
        got[(1, 1)] = both
        return [got[(0, 0)], got[(0, 1)], got[(1, 0)], got[(1, 1)]]

    def body(
        tokens,
        picture_ids,
        w_qkv,
        w_out,
        w_up,
        w_down,
        ln1_gain,
        ln1_bias,
        q_gain,
        k_gain,
        out_bias,
        ln2_gain,
        ln2_bias,
        up_bias,
        down_bias,
        cotangent,
    ):
        rows, d = tokens.shape[1], tokens.shape[2]
        drow = w_qkv.shape[0]
        cols = w_qkv.shape[2]
        heads = cols // HEAD
        unit = w_up.shape[1]
        dp, mp = lax.axis_index("dp"), lax.axis_index("mp")
        z, y, x, c = dp // 2, dp % 2, mp // 2, mp % 2
        tok, cot = tokens[0], cotangent[0]

        vs = [ln1_gain, ln1_bias, q_gain, k_gain, out_bias, ln2_gain, ln2_bias, down_bias, up_bias]
        small = vs[0].shape[0]
        flat = jnp.concatenate(vs)
        used = flat.shape[0]
        vec = jnp.pad(flat, (0, 1024 - used)).reshape(8, 128)
        wcat = jnp.concatenate([w_qkv.reshape(drow, 3 * cols), w_out], axis=1)
        tok_all, w_all, vec_all = gather_all(tok, wcat, vec, ndp, nmp)
        vec_all = vec_all.reshape(nmp, ndp, 1024).transpose(1, 0, 2).reshape(ndev, 1024)
        gain1, shift1, qg, kg, obias, gain2, shift2, dbias = [
            vec_all[:, i * small : (i + 1) * small].reshape(1, d) for i in range(8)
        ]
        ubias = vec_all[:, 8 * small : used].reshape(nmp, unit)
        gains = jnp.concatenate(
            [
                lax.dynamic_slice_in_dim(qg[0], mp * cols, cols),
                lax.dynamic_slice_in_dim(kg[0], mp * cols, cols),
            ]
        ).reshape(2 * cols, 1)

        ups = columns(w_up, "y", "x")
        downs = columns(w_down, "x", "y")
        cot_other = permute(cot, "core")

        normed, raw, low, wt = project(
            tok_all, w_all.reshape(d, 3 * cols + w_out.shape[1]), gain1, shift1, gains, heads
        )
        wo0 = wt[3 * cols :]
        wo1 = permute(wo0, "x")
        wo2, wo3 = permute(wo0, "core"), permute(wo1, "core")
        wos = (wo0, wo1, wo2, wo3)
        ids = picture_ids
        span = spans(ids[0])
        att, lse = attend(span, low, ids, heads)
        att_own = swap(att, True, nmp, 1).reshape(d, rows)
        mid, n2 = middle_part(att_own, wos, tok, obias, gain2, shift2)
        n2_other = permute(n2, "core")
        o_own, o_send, g_own, g_send, dwu, dwd, gbias = feed(
            n2, n2_other, cot, cot_other, ubias, ups, downs, nz
        )
        g_got = permute(g_send, "core")
        gmid, gatt, gwo, sums2 = middle_back(g_own, g_got, mid, cot, att_own, wos, gain2, nmp)
        o_got = permute(o_send, "core")
        result = (mid + o_own + o_got.astype(F32) + dbias).astype(BF)
        dout = swap(gatt, False, nmp, 2)
        gproj, ggain = attend_back(span, low, raw, att, lse, dout, ids, gains, heads)
        order = jnp.stack([mp, x * 2 + 1 - c, (1 - x) * 2 + c, (1 - x) * 2 + 1 - c]).astype(jnp.int32)
        gn, gwq, sums1 = project_back(order, gproj, normed, tok_all, wt[: 3 * cols])
        got = permute(gn[1::2], "core")
        mine = gn[0::2].astype(F32) + got.astype(F32)
        far = permute(mine[1].astype(BF), "x")
        gnormed = mine[0] + far.astype(F32)
        grad_tokens = tokens_back(gnormed, tok, gain1, gmid)

        def pick(v, i):
            return lax.dynamic_index_in_dim(v, i, 0, keepdims=False)

        def along(v, kind):
            i = {"x": None, "y": y}[kind]
            if i is None:
                keep, send = v[0], v[1]
            else:
                keep, send = pick(v, i), pick(v, 1 - i)
            return (keep.astype(F32) + permute(send, kind).astype(F32)).astype(BF)

        def along_z(v):
            total = pick(v, z).astype(F32)
            for k in range(1, nz):
                total = total + permute(pick(v, (z + k) % nz), "z", k).astype(F32)
            return total

        def over_dp(v):
            if drow % 16:
                return lax.psum_scatter(v.astype(F32), "dp", scatter_dimension=0, tiled=True)
            v = v.reshape(nz, 2, drow, v.shape[-1]).transpose(1, 0, 2, 3)
            return along_z(along(v, "y"))

        def reduce_columns(v, y_first):
            if drow % 16 or not y_first:
                return over_dp(along(v, "x"))
            v = v.reshape(2, nz, 2, drow, unit).transpose(2, 0, 1, 3, 4)
            return along_z(along(along(v, "y"), "x"))

        grad_up = reduce_columns(dwu, False)
        grad_down = reduce_columns(dwd, True)
        mine_o = jnp.stack([pick(gwo, mp), pick(gwo, (1 - x) * 2 + c)])
        send_o = jnp.stack([pick(gwo, x * 2 + 1 - c), pick(gwo, (1 - x) * 2 + 1 - c)])
        go = (mine_o.astype(F32) + permute(send_o, "core").astype(F32)).astype(BF)
        go = along(go, "x")
        grad_att = over_dp(jnp.concatenate([gwq, go], axis=1))

        def spread(v, at, size):
            return lax.dynamic_update_slice_in_dim(jnp.zeros((size,), F32), v, at, 0)

        gq = spread(ggain[:cols, 0], mp * cols, d)
        gk = spread(ggain[cols:, 0], mp * cols, d)
        gb = spread(gbias[0, 0], mp * unit, nmp * unit)
        gb = gb + spread(gbias[1, 0], ((1 - x) * 2 + c) * unit, nmp * unit)
        eight = jnp.stack([sums1[0], sums1[1], gq, gk, sums2[0], sums2[1], sums2[2], sums2[3]])
        parts = jnp.concatenate(
            [
                eight.reshape(8, ndev, small).transpose(1, 0, 2).reshape(ndev, 8 * small),
                gb.reshape(ndev, used - 8 * small),
            ],
            axis=1,
        )
        parts = jnp.pad(parts, ((0, 0), (0, 1024 - used))).reshape(ndev, 8, 128)
        tot = vector_sums(parts, ndp, nmp).reshape(1024)
        vgrads = [tot[i * small : (i + 1) * small] for i in range(8)] + [tot[8 * small : used]]

        return (
            result[None],
            grad_tokens[None],
            grad_att[:, : 3 * cols].reshape(drow, 3, cols),
            grad_att[:, 3 * cols :],
            grad_up,
            grad_down,
            vgrads[0],
            vgrads[1],
            vgrads[2],
            vgrads[3],
            vgrads[4],
            vgrads[5],
            vgrads[6],
            vgrads[8],
            vgrads[7],
        )

    vec_spec = P(("dp", "mp"))
    return jax.shard_map(
        body,
        mesh=mesh,
        in_specs=(
            P("dp", "mp", None),
            P("dp", None),
            P("dp", None, "mp"),
            P("dp", "mp"),
            P("dp", "mp"),
            P("dp", "mp"),
        )
        + (vec_spec,) * 9
        + (P("dp", "mp", None),),
        out_specs=(
            P("dp", "mp", None),
            P("dp", "mp", None),
            P("dp", None, "mp"),
            P("dp", "mp"),
            P("dp", "mp"),
            P("dp", "mp"),
        )
        + (vec_spec,) * 9,
        check_vma=False,
    )
```

```python
import functools

import jax
import jax.numpy as jnp
from jax import lax
from jax.experimental import pallas as pl
from jax.experimental.pallas import tpu as pltpu
from jax.sharding import PartitionSpec as P

F32 = jnp.float32
BF = jnp.bfloat16
HEAD = 64
EPS = 1e-06
TB = 512
BIG = 32768.0
LOG2E = 1.4426950408889634
MESH = pl.DeviceIdType.MESH
ANY = pl.BlockSpec(memory_space=pl.ANY)
VM = pl.BlockSpec(memory_space=pltpu.VMEM)
SM = pl.BlockSpec(memory_space=pltpu.SMEM)
VLIM = 60 * 1024 * 1024


def nn(a, b):
    return lax.dot_general(a, b, (((1,), (0,)), ((), ())), preferred_element_type=F32)


def nt(a, b):
    return lax.dot_general(a, b, (((1,), (1,)), ((), ())), preferred_element_type=F32)


def tn(a, b):
    return lax.dot_general(a, b, (((0,), (0,)), ((), ())), preferred_element_type=F32)


def sds(shape, dtype):
    return jax.ShapeDtypeStruct(shape, dtype)


def params(**kw):
    return pltpu.CompilerParams(vmem_limit_bytes=VLIM, **kw)


def cost(flops, nbytes, trans=0):
    return pl.CostEstimate(flops=int(flops), bytes_accessed=int(nbytes), transcendentals=int(trans))


def rcopy(src, dst, ssem, rsem, peer):
    return pltpu.make_async_remote_copy(
        src_ref=src,
        dst_ref=dst,
        send_sem=ssem,
        recv_sem=rsem,
        device_id=peer,
        device_id_type=MESH,
    )


def greet(peers):
    bar = pltpu.get_barrier_semaphore()
    for p in peers:
        pl.semaphore_signal(bar, inc=1, device_id=p, device_id_type=MESH)
    pl.semaphore_wait(bar, len(peers))


def gather_kernel(
    nz, nc, tok, w, vec, tok_all, w_all, vec_all, loc, zs, zr, ys, yr, xs, xr, cs, cr, tx, rx, tc, rc
):
    dp, mp = lax.axis_index("dp"), lax.axis_index("mp")
    z, y, x, c = dp // 2, dp % 2, mp // 2, mp % 2
    xm, cm, dm = (1 - x) * 2 + c, x * 2 + 1 - c, (1 - x) * 2 + 1 - c
    ypeer, xpeer, cpeer = (z * 2 + 1 - y, mp), (dp, xm), (dp, cm)
    zpeers = [(((z + k) % nz) * 2 + y, mp) for k in range(1, nz)]
    greet(zpeers + [ypeer, xpeer, cpeer])
    rows = tok.shape[0] // nc
    xt = []
    for i in range(nc):
        part = pl.ds(i * rows, rows)
        cp = rcopy(tok.at[part], tok_all.at[mp, part], tx.at[i], rx.at[i], xpeer)
        cp.start()
        xt.append(cp)
    zc = []
    for k in range(1, nz):
        for kind, (src, dst) in enumerate(((vec, vec_all.at[mp, dp]), (w, w_all.at[dp]))):
            cp = rcopy(src, dst, zs.at[kind, k], zr.at[kind, k], zpeers[k - 1])
            cp.start()
            zc.append(cp)
    yc = []
    for kind, (src, dst) in enumerate(((vec, vec_all.at[mp, dp]), (w, w_all.at[dp]))):
        cp = rcopy(src, dst, ys.at[kind, 0], yr.at[kind, 0], ypeer)
        cp.start()
        yc.append(cp)
    own_tok = rcopy(tok, tok_all.at[mp], tc.at[nc], rc.at[nc], cpeer)
    own_tok.start()
    locs = [
        pltpu.make_async_copy(tok, tok_all.at[mp], loc.at[0]),
        pltpu.make_async_copy(w, w_all.at[dp], loc.at[1]),
        pltpu.make_async_copy(vec, vec_all.at[mp, dp], loc.at[2]),
    ]
    for cp in locs:
        cp.start()
    for k in range(1, nz):
        src_dp = ((z + nz - k) % nz) * 2 + y
        for kind in range(2):
            zc[(k - 1) * 2 + kind].wait_recv()
            ref = (vec_all.at[mp, src_dp], w_all.at[src_dp])[kind]
            cp = rcopy(ref, ref, ys.at[kind, k], yr.at[kind, k], ypeer)
            cp.start()
            yc.append(cp)
    ct = []

    def forward(i):
        part = pl.ds(i * rows, rows)
        xt[i].wait_recv()
        cp = rcopy(tok_all.at[xm, part], tok_all.at[xm, part], tc.at[i], rc.at[i], cpeer)
        cp.start()
        ct.append(cp)

    forward(0)
    for cp in locs:
        cp.wait()
    for k in range(nz):
        yc[k * 2].wait_recv()
    vx = rcopy(vec_all.at[mp], vec_all.at[mp], xs, xr, xpeer)
    vx.start()
    vc0 = rcopy(vec_all.at[mp], vec_all.at[mp], cs.at[0], cr.at[0], cpeer)
    vc0.start()
    if nc > 1:
        forward(1)
    vx.wait_recv()
    vc1 = rcopy(vec_all.at[xm], vec_all.at[xm], cs.at[1], cr.at[1], cpeer)
    vc1.start()
    for i in range(2, nc):
        forward(i)
    for k in range(nz):
        yc[k * 2 + 1].wait_recv()
    for cp in ct:
        cp.wait_recv()
    own_tok.wait()
    vc0.wait()
    vc1.wait()
    vx.wait_send()
    for cp in zc + yc + xt + ct:
        cp.wait_send()


def gather_all(tok, w, vec, ndp, nmp):
    nz, nc = ndp // 2, 4
    dma = pltpu.SemaphoreType.DMA
    return pl.pallas_call(
        functools.partial(gather_kernel, nz, nc),
        out_shape=(
            sds((nmp,) + tok.shape, BF),
            sds((ndp,) + w.shape, BF),
            sds((nmp, ndp) + vec.shape, F32),
        ),
        in_specs=[ANY] * 3,
        out_specs=(ANY,) * 3,
        scratch_shapes=[
            dma((3,)),
            dma((2, nz)),
            dma((2, nz)),
            dma((2, nz)),
            dma((2, nz)),
            dma,
            dma,
            dma((2,)),
            dma((2,)),
            dma((nc,)),
            dma((nc,)),
            dma((nc + 1,)),
            dma((nc + 1,)),
        ],
        compiler_params=pltpu.CompilerParams(collective_id=0, has_side_effects=True),
        name="gather_start",
    )(tok, w, vec)


def swap_kernel(forward, nmp, src, dst, loc, ss, rs):
    dp, mp = lax.axis_index("dp"), lax.axis_index("mp")
    own = dst.shape[2] if forward else src.shape[2]
    peers = [(mp + k) % nmp for k in range(1, nmp)]
    greet([(dp, m) for m in peers])

    def ends(m):
        if forward:
            return src.at[:, pl.ds(pl.multiple_of(m * own, own), own)], dst.at[mp]
        return src.at[m], dst.at[:, pl.ds(pl.multiple_of(mp * own, own), own)]

    cps = []
    for k, m in enumerate(peers):
        s, d = ends(m)
        cp = rcopy(s, d, ss.at[k], rs.at[k], (dp, m))
        cp.start()
        cps.append(cp)
    s, d = ends(mp)
    lc = pltpu.make_async_copy(s, d, loc)
    lc.start()
    lc.wait()
    for cp in cps:
        cp.wait()


def swap(src, forward, nmp, cid):
    dma = pltpu.SemaphoreType.DMA
    if forward:
        shape = (nmp, src.shape[0], src.shape[1] // nmp)
    else:
        shape = (src.shape[1], src.shape[2] * nmp)
    return pl.pallas_call(
        functools.partial(swap_kernel, forward, nmp),
        out_shape=sds(shape, BF),
        in_specs=[ANY],
        out_specs=ANY,
        scratch_shapes=[dma, dma((nmp - 1,)), dma((nmp - 1,))],
        compiler_params=pltpu.CompilerParams(collective_id=cid, has_side_effects=True),
        name="swap_fwd" if forward else "swap_bwd",
    )(src)


def vector_kernel(ndp, nmp, src, out, got, ss, rs):
    dp, mp = lax.axis_index("dp"), lax.axis_index("mp")
    me, n = dp * nmp + mp, ndp * nmp
    peers = [(me + k) % n for k in range(1, n)]
    greet([(p // nmp, p % nmp) for p in peers])
    cps = []
    for k, p in enumerate(peers):
        cp = rcopy(src.at[p], got.at[k], ss.at[k], rs.at[k], (p // nmp, p % nmp))
        cp.start()
        cps.append(cp)
    total = src[me]
    for k, cp in enumerate(cps):
        cp.wait_recv()
        total = total + got[k]
    out[...] = total
    for cp in cps:
        cp.wait_send()


def vector_sums(parts, ndp, nmp):
    n = ndp * nmp
    dma = pltpu.SemaphoreType.DMA
    return pl.pallas_call(
        functools.partial(vector_kernel, ndp, nmp),
        out_shape=sds(parts.shape[1:], F32),
        in_specs=[VM],
        out_specs=VM,
        scratch_shapes=[pltpu.VMEM((n - 1,) + parts.shape[1:], F32), dma((n - 1,)), dma((n - 1,))],
        compiler_params=pltpu.CompilerParams(collective_id=3, has_side_effects=True),
        name="vector_sums",
    )(parts)


def norm_rows(v):
    centre = jnp.mean(v, axis=-1, keepdims=True)
    v = v - centre
    r = lax.rsqrt(jnp.mean(v * v, axis=-1, keepdims=True) + EPS)
    return v * r, r


def norm_cols(v):
    centre = jnp.mean(v, axis=0, keepdims=True)
    v = v - centre
    r = lax.rsqrt(jnp.mean(v * v, axis=0, keepdims=True) + EPS)
    return v * r, r


def qkv_kernel(heads, tok, w, gain, shift, gains, normed, raw, low, wt):
    @pl.when(pl.program_id(0) == 0)
    def _():
        wt[...] = w[...].T

    cols = heads * HEAD
    hat, _ = norm_rows(tok[0].astype(F32))
    n = (hat * gain[...] + shift[...]).astype(BF)
    normed[...] = n
    proj = nt(wt[0 : 3 * cols, :], n)
    raw[...] = proj[0 : 2 * cols]
    for h in range(2 * heads):
        part = slice(h * HEAD, (h + 1) * HEAD)
        hat, _ = norm_cols(proj[part])
        low[part, :] = (hat * gains[part, :]).astype(BF)
    low[2 * cols :, :] = proj[2 * cols :].astype(BF)


def project(tok_all, w, gain, shift, gains, heads):
    nb, rows, d = tok_all.shape
    cols = heads * HEAD
    t = nb * rows
    full = lambda shape: pl.BlockSpec(shape, lambda i: (0,) * len(shape))
    return pl.pallas_call(
        functools.partial(qkv_kernel, heads),
        grid=(nb,),
        out_shape=(
            sds((t, d), BF),
            sds((2 * cols, t), F32),
            sds((3 * cols, t), BF),
            sds((w.shape[1], w.shape[0]), BF),
        ),
        in_specs=[
            pl.BlockSpec((1, rows, d), lambda i: (i, 0, 0)),
            full(w.shape),
            full((1, d)),
            full((1, d)),
            full((2 * cols, 1)),
        ],
        out_specs=(
            pl.BlockSpec((rows, d), lambda i: (i, 0)),
            pl.BlockSpec((2 * cols, rows), lambda i: (0, i)),
            pl.BlockSpec((3 * cols, rows), lambda i: (0, i)),
            full((w.shape[1], w.shape[0])),
        ),
        compiler_params=params(),
        cost_estimate=cost(2 * t * d * 3 * cols, 12 * 2**20),
        name="project_qkv",
    )(tok_all, w, gain, shift, gains)


def masks(ids):
    t = ids.shape[1]
    r = lax.broadcasted_iota(jnp.int32, (HEAD, t), 0)
    pad = ids < 0
    mq = jnp.where((r == ids) | ((r == 31) & pad), 1.0, 0.0)
    mk = jnp.where((r <= 31) & (r != ids), -BIG, 0.0)
    mk = jnp.where((r >= 32) & (r < 35), 1.0, mk)
    return r, mq, mk


def three(v):
    a = v.astype(BF).astype(F32)
    b = (v - a).astype(BF).astype(F32)
    return a, b, v - a - b


SCALE = HEAD**-0.5


def attend_kernel(heads, nblk, span, low, ids, out, lse, qa, ka, va, acc):
    cols = heads * HEAD
    t = ids.shape[1]
    _, mq, mk = masks(ids[...])
    mq, mk = mq.astype(BF), mk.astype(BF)
    one = jnp.where(lax.broadcasted_iota(jnp.int32, (16, t), 0) == 0, 1.0, 0.0).astype(BF)
    for h in range(heads):
        qa[h, 0:HEAD, :] = low[h * HEAD : (h + 1) * HEAD, :]
        qa[h, HEAD:, :] = mq
        k = low[cols + h * HEAD : cols + (h + 1) * HEAD, :]
        ka[h, :, :] = jnp.concatenate([k, mk], axis=0).T
        va[h, 0:HEAD, :] = low[2 * cols + h * HEAD : 2 * cols + (h + 1) * HEAD, :]
        va[h, HEAD:, :] = one
    acc[...] = jnp.zeros_like(acc)

    def row(i, _):
        qi = pl.ds(pl.multiple_of(i * TB, TB), TB)

        def col(j, _):
            kj = pl.ds(pl.multiple_of(j * TB, TB), TB)
            s = [nn(ka[h, kj, :], qa[h, :, qi]) for h in range(heads)]
            p = [jnp.exp2(v * (SCALE * LOG2E)).astype(BF) for v in s]
            for h in range(heads):
                acc[h, :, qi] += nn(va[h, :, kj], p[h])
            return 0

        return lax.fori_loop(span[i], span[nblk + i], col, 0)

    lax.fori_loop(0, nblk, row, 0)
    pad = ids[...] < 0
    lse[...] = jnp.zeros_like(lse)
    for h in range(heads):
        total = jnp.where(pad, 1.0, acc[h, HEAD : HEAD + 1, :])
        value = low[2 * cols + h * HEAD : 2 * cols + (h + 1) * HEAD, :].astype(F32)
        o = jnp.where(pad, value, acc[h, 0:HEAD, :] * (1.0 / total))
        out[h * HEAD : (h + 1) * HEAD, :] = o.astype(BF)
        lse[h : h + 1, :] = jnp.log(total)


def attend(span, low, ids, heads):
    cols, t = heads * HEAD, low.shape[1]
    return pl.pallas_call(
        functools.partial(attend_kernel, heads, t // TB),
        out_shape=(sds((cols, t), BF), sds((8, t), F32)),
        in_specs=[SM, VM, VM],
        out_specs=(VM, VM),
        scratch_shapes=[
            pltpu.VMEM((heads, 2 * HEAD, t), BF),
            pltpu.VMEM((heads, t, 2 * HEAD), BF),
            pltpu.VMEM((heads, HEAD + 16, t), BF),
            pltpu.VMEM((heads, HEAD + 16, t), F32),
        ],
        compiler_params=params(),
        cost_estimate=cost(12e9, 4 * 2**20),
        name="attend",
    )(span, low, ids)


def head_back(raw, gain, grad):
    hat, r = norm_cols(raw)
    e = grad * gain
    m1 = jnp.mean(e, axis=0, keepdims=True)
    m2 = jnp.mean(e * hat, axis=0, keepdims=True)
    return (e - m1 - hat * m2) * r, jnp.sum(grad * hat, axis=1, keepdims=True)


def attend_back_kernel(
    heads, nblk, span, low, raw, att, lse, dout, ids, gains, gproj, ggain, qa, ka, va, da, dq, dk, dv
):
    cols = heads * HEAD
    t = ids.shape[1]
    r, mq, mk = masks(ids[...])
    mk = mk.astype(BF)
    one = jnp.where(r < 3, 1.0, 0.0).astype(BF)
    for h in range(heads):
        hs = slice(h * HEAD, (h + 1) * HEAD)
        qa[h, 0:HEAD, :] = low[hs, :]
        a, b, c = three(lse[h : h + 1, :] * (-1.0 / SCALE))
        m = jnp.where(r == 32, a, jnp.where(r == 33, b, jnp.where(r == 34, c, mq)))
        qa[h, HEAD:, :] = m.astype(BF)
        k = low[cols + h * HEAD : cols + (h + 1) * HEAD, :]
        ka[h, :, :] = jnp.concatenate([k, mk], axis=0).T
        v = low[2 * cols + h * HEAD : 2 * cols + (h + 1) * HEAD, :]
        va[h, :, :] = jnp.concatenate([v, one], axis=0).T
        do = dout[hs, :]
        delta = jnp.sum(do.astype(F32) * att[hs, :].astype(F32), axis=0, keepdims=True)
        a, b, c = three(-delta)
        da[h, 0:HEAD, :] = do
        da[h, HEAD:, :] = jnp.where(
            r == 0, a, jnp.where(r == 1, b, jnp.where(r == 2, c, 0.0))
        ).astype(BF)
    dq[...] = jnp.zeros_like(dq)
    dk[...] = jnp.zeros_like(dk)
    dv[...] = jnp.zeros_like(dv)

    def row(i, _):
        qi = pl.ds(pl.multiple_of(i * TB, TB), TB)

        def col(j, _):
            kj = pl.ds(pl.multiple_of(j * TB, TB), TB)
            s = [nn(ka[h, kj, :], qa[h, :, qi]) for h in range(heads)]
            d = [nn(va[h, kj, :], da[h, :, qi]) for h in range(heads)]
            p = [jnp.exp2(v * (SCALE * LOG2E)) for v in s]
            ds = [(p[h] * d[h]).astype(BF) for h in range(heads)]
            for h in range(heads):
                hs = pl.ds(h * HEAD, HEAD)
                dv[hs, kj] += nt(dout[hs, qi], p[h].astype(BF))
                dk[hs, kj] += nt(low[hs, qi], ds[h])
                dq[hs, qi] += nn(low[pl.ds(cols + h * HEAD, HEAD), kj], ds[h])
            return 0

        return lax.fori_loop(span[i], span[nblk + i], col, 0)

    lax.fori_loop(0, nblk, row, 0)
    pad = ids[...] < 0
    for h in range(heads):
        hs = slice(h * HEAD, (h + 1) * HEAD)
        for part, grad in ((0, dq), (1, dk)):
            ps = slice(part * cols + h * HEAD, part * cols + (h + 1) * HEAD)
            g, gg = head_back(raw[ps, :], gains[ps, :], grad[hs, :] * SCALE)
            gproj[ps, :] = g.astype(BF)
            ggain[ps, :] = gg
        g = dv[hs, :] + jnp.where(pad, dout[hs, :].astype(F32), 0.0)
        gproj[2 * cols + h * HEAD : 2 * cols + (h + 1) * HEAD, :] = g.astype(BF)


def attend_back(span, low, raw, att, lse, dout, ids, gains, heads):
    cols, t = heads * HEAD, low.shape[1]
    return pl.pallas_call(
        functools.partial(attend_back_kernel, heads, t // TB),
        out_shape=(sds((3 * cols, t), BF), sds((2 * cols, 1), F32)),
        in_specs=[SM] + [VM] * 7,
        out_specs=(VM, VM),
        scratch_shapes=[
            pltpu.VMEM((heads, 2 * HEAD, t), BF),
            pltpu.VMEM((heads, t, 2 * HEAD), BF),
            pltpu.VMEM((heads, t, 2 * HEAD), BF),
            pltpu.VMEM((heads, 2 * HEAD, t), BF),
            pltpu.VMEM((cols, t), F32),
            pltpu.VMEM((cols, t), F32),
            pltpu.VMEM((cols, t), F32),
        ],
        compiler_params=params(),
        cost_estimate=cost(30e9, 12 * 2**20),
        name="attend_back",
    )(span, low, raw, att, lse, dout, ids, gains)


def place_out(pieces, dest):
    mp = lax.axis_index("mp")
    x, c = mp // 2, mp % 2
    order = (mp, (1 - x) * 2 + c, x * 2 + 1 - c, (1 - x) * 2 + 1 - c)
    rows = pieces[0].shape[0]
    for piece, m in zip(pieces, order):
        dest[pl.ds(pl.multiple_of(m * rows, rows), rows), :] = piece[...]


def middle_kernel(att, w0, w1, w2, w3, tok, bias, gain, shift, mid, low, wo):
    place_out((w0, w1, w2, w3), wo)
    m = tok[...].astype(F32) + tn(att[...], wo[...]) + bias[...]
    mid[...] = m
    hat, _ = norm_rows(m)
    low[...] = (hat * gain[...] + shift[...]).astype(BF)


def middle_part(att, wos, tok, bias, gain, shift):
    rows, d = tok.shape
    return pl.pallas_call(
        middle_kernel,
        out_shape=(sds((rows, d), F32), sds((rows, d), BF)),
        in_specs=[VM] * 9,
        out_specs=(VM, VM),
        scratch_shapes=[pltpu.VMEM((d, d), BF)],
        compiler_params=params(),
        cost_estimate=cost(2 * rows * d * d, 6 * 2**20),
        name="middle",
    )(att, *wos, tok, bias, gain, shift)


def middle_back_kernel(nmp, g0, g1, mid, cot, att, *refs):
    pieces, (gain, gmid, gatt, gwo, sums, wo) = refs[:-6], refs[-6:]
    if len(pieces) > 1:
        place_out(pieces, wo)
    else:
        wo = pieces[0]
    gy = cot[...].astype(F32)
    g = g0[...] + g1[...].astype(F32)
    hat, r = norm_rows(mid[...])
    e = g * gain[...]
    m1 = jnp.mean(e, axis=-1, keepdims=True)
    m2 = jnp.mean(e * hat, axis=-1, keepdims=True)
    gm = gy + (e - m1 - hat * m2) * r
    gmid[...] = gm
    low = gm.astype(BF)
    rows = att.shape[0] // nmp
    ga = nt(wo[...], low).astype(BF)
    for m in range(nmp):
        gatt[m] = ga[m * rows : (m + 1) * rows]
    gw = nt(gm.T.astype(BF), att[...]).astype(BF)
    mp = lax.axis_index("mp")
    for m in range(nmp):
        gwo[m] = gw[:, m * rows : (m + 1) * rows]
    sums[...] = jnp.zeros_like(sums)
    for k, v in enumerate((gm, g * hat, g, gy)):
        sums[k : k + 1, :] = jnp.sum(v, axis=0, keepdims=True)


def middle_back(g0, g1, mid, cot, att, wos, gain, nmp):
    rows, d = mid.shape
    return pl.pallas_call(
        functools.partial(middle_back_kernel, nmp),
        out_shape=(
            sds((rows, d), F32),
            sds((nmp, d // nmp, rows), BF),
            sds((nmp, d, d // nmp), BF),
            sds((8, d), F32),
        ),
        in_specs=[VM] * (6 + len(wos)),
        out_specs=(VM,) * 4,
        scratch_shapes=[pltpu.VMEM((d, d), BF)],
        compiler_params=params(),
        cost_estimate=cost(4 * rows * d * d, 10 * 2**20),
        name="middle_back",
    )(g0, g1, mid, cot, att, *wos, gain)


def feed_kernel(npiece, nz, *refs):
    n0, n1, c0, c1, bias = refs[:5]
    pieces = refs[5 : 5 + npiece]
    out_own, out_send, g_own, g_send, dwu, dwd, gbias = refs[5 + npiece : 12 + npiece]
    wu, wd, n2, gy, n2t, gyt, acts, gps, oacc, gacc, sem = refs[12 + npiece :]
    dp, mp = lax.axis_index("dp"), lax.axis_index("mp")
    z, y, x, c = dp // 2, dp % 2, mp // 2, mp % 2
    copies = []
    half = npiece // 2
    for a, piece in enumerate(pieces):
        dest = (wu, wd)[a // half]
        rel = a % half
        count, rows = piece.shape[0], piece.shape[1]
        for k in range(count):
            if half <= 2:
                at, colidx = 0, (k if half == 1 else rel)
            else:
                zz = (z + nz - k) % nz
                at = (zz * 2 + (y if rel % 2 == 0 else 1 - y)) * rows
                at, colidx = pl.multiple_of(at, rows), rel // 2
            cp = pltpu.make_async_copy(piece.at[k], dest.at[colidx, pl.ds(at, rows), :], sem.at[a, k])
            cp.start()
            copies.append(cp)
    hr = n0.shape[0]
    for i, (n, g) in enumerate(((n0, c0), (n1, c1))):
        part = slice(i * hr, (i + 1) * hr)
        n2[part, :] = n[...]
        gy[part, :] = g[...]
        n2t[:, part] = n[...].T
        gyt[:, part] = g[...].T
    oacc[...] = jnp.zeros_like(oacc)
    gacc[...] = jnp.zeros_like(gacc)
    for cp in copies:
        cp.wait()
    rows, d = n2.shape
    cw = acts.shape[1]
    per = wu.shape[2] // cw
    ones = jnp.ones((16, rows), BF)

    def chunk(i, _):
        col, off = i // per, pl.multiple_of((i % per) * cw, cw)
        cs = pl.ds(off, cw)
        m = jnp.where(col == 0, mp, (1 - x) * 2 + c)
        b = bias[pl.ds(m, 1), cs]
        for rb in range(rows // 256):
            rs = slice(rb * 256, (rb + 1) * 256)
            u = nn(n2[rs, :], wu[col, :, cs]) + b
            ga = nn(gy[rs, :], wd[col, :, cs])
            cdf = 0.5 + 0.5 * lax.erf(u * 0.7071067811865476)
            act = (u * cdf).astype(BF)
            gp = (ga * (cdf + u * (jnp.exp(-0.5 * u * u) * 0.3989422804014327))).astype(BF)
            acts[rs, :] = act
            gps[rs, :] = gp
            oacc[rs, :] += nt(act, wd[col, :, cs])
            gacc[rs, :] += nt(gp, wu[col, :, cs])
        dwd[col, :, cs] = nn(gyt[...], acts[...]).astype(BF)
        dwu[col, :, cs] = nn(n2t[...], gps[...]).astype(BF)
        gbias[col, :, cs] = nn(ones, gps[...])[0:8]
        return 0

    lax.fori_loop(0, 2 * per, chunk, 0)
    out_own[...] = oacc[0:hr]
    out_send[...] = oacc[hr:].astype(BF)
    g_own[...] = gacc[0:hr]
    g_send[...] = gacc[hr:].astype(BF)


def feed(n0, n1, c0, c1, bias, ups, downs, nz):
    hr, d = n0.shape
    rows, cw = 2 * hr, 256
    unit = ups[0].shape[2]
    pieces = list(ups) + list(downs)
    kmax = max(p.shape[0] for p in pieces)
    vm = pltpu.VMEM
    return pl.pallas_call(
        functools.partial(feed_kernel, len(pieces), nz),
        out_shape=(
            sds((hr, d), F32),
            sds((hr, d), BF),
            sds((hr, d), F32),
            sds((hr, d), BF),
            sds((2, d, unit), BF),
            sds((2, d, unit), BF),
            sds((2, 8, unit), F32),
        ),
        in_specs=[VM] * 5 + [ANY] * len(pieces),
        out_specs=(VM,) * 7,
        scratch_shapes=[
            vm((2, d, unit), BF),
            vm((2, d, unit), BF),
            vm((rows, d), BF),
            vm((rows, d), BF),
            vm((d, rows), BF),
            vm((d, rows), BF),
            vm((rows, cw), BF),
            vm((rows, cw), BF),
            vm((rows, d), F32),
            vm((rows, d), F32),
            pltpu.SemaphoreType.DMA((len(pieces), kmax)),
        ],
        compiler_params=params(),
        cost_estimate=cost(12 * rows * d * 2 * unit, 22 * 2**20),
        name="feed_forward",
    )(n0, n1, c0, c1, bias, *pieces)


def project_back_kernel(order, gproj, normed, tok, wt, gn, gw, sums, acc):
    @pl.when(pl.program_id(0) == 0)
    def _():
        acc[...] = jnp.zeros_like(acc)
        sums[...] = jnp.zeros_like(sums)

    acc[...] += nn(gproj[...], normed[...])
    g = tn(gproj[...], wt[...])
    gn[0] = g.astype(BF)
    hat, _ = norm_rows(tok[0].astype(F32))
    sums[0:1, :] += jnp.sum(g * hat, axis=0, keepdims=True)
    sums[1:2, :] += jnp.sum(g, axis=0, keepdims=True)

    @pl.when(pl.program_id(0) == pl.num_programs(0) - 1)
    def _():
        gw[...] = acc[...].T.astype(BF)


def project_back(order, gproj, normed, tok_all, wt):
    nb, rows, d = tok_all.shape
    n = gproj.shape[0]
    t = nb * rows
    return pl.pallas_call(
        project_back_kernel,
        grid_spec=pltpu.PrefetchScalarGridSpec(
            num_scalar_prefetch=1,
            grid=(nb,),
            in_specs=[
                pl.BlockSpec((n, rows), lambda i, o: (0, o[i])),
                pl.BlockSpec((rows, d), lambda i, o: (o[i], 0)),
                pl.BlockSpec((1, rows, d), lambda i, o: (o[i], 0, 0)),
                pl.BlockSpec((n, d), lambda i, o: (0, 0)),
            ],
            out_specs=(
                pl.BlockSpec((1, rows, d), lambda i, o: (i, 0, 0)),
                pl.BlockSpec((d, n), lambda i, o: (0, 0)),
                pl.BlockSpec((8, d), lambda i, o: (0, 0)),
            ),
            scratch_shapes=[pltpu.VMEM((n, d), F32)],
        ),
        out_shape=(sds((nb, rows, d), BF), sds((d, n), BF), sds((8, d), F32)),
        compiler_params=params(),
        cost_estimate=cost(4 * t * d * n, 14 * 2**20),
        name="project_back",
    )(order, gproj, normed, tok_all, wt)


def tokens_back(gn, tok, gain, gmid):
    hat, r = norm_rows(tok.astype(F32))
    e = gn * gain
    m1 = jnp.mean(e, axis=-1, keepdims=True)
    m2 = jnp.mean(e * hat, axis=-1, keepdims=True)
    return (gmid + (e - m1 - hat * m2) * r).astype(BF)


class Where:
    def __init__(self, nz):
        dp, mp = lax.axis_index("dp"), lax.axis_index("mp")
        z, y, x, c = dp // 2, dp % 2, mp // 2, mp % 2
        self.dp, self.mp, self.z, self.y, self.x, self.c = dp, mp, z, y, x, c
        self.xm, self.cm, self.dm = (1 - x) * 2 + c, x * 2 + 1 - c, (1 - x) * 2 + 1 - c
        self.ydp = z * 2 + 1 - y
        self.zfrom = [((z + nz - k) % nz) * 2 + y for k in range(nz)]
        self.yfrom = [((z + nz - k) % nz) * 2 + 1 - y for k in range(nz)]
        self.py, self.px, self.pc, self.pd = (self.ydp, mp), (dp, self.xm), (dp, self.cm), (dp, self.dm)
        self.pz = [None] + [(((z + k) % nz) * 2 + y, mp) for k in range(1, nz)]
        self.all = self.pz[1:] + [self.py, self.px, self.pc, self.pd]


class Sender:
    def __init__(self, ss, rs):
        self.ss, self.rs, self.n, self.open = ss, rs, 0, []

    def send(self, src, dst, peer):
        cp = rcopy(src, dst, self.ss.at[self.n], self.rs.at[self.n], peer)
        cp.start()
        self.n += 1
        self.open.append(cp)
        return cp

    def finish(self):
        for cp in self.open:
            cp.wait_send()


def vector_rows(vecv, small, d):
    nmp, ndp, vr, lanes = vecv.shape
    v = vecv[...].reshape(nmp * ndp * vr, lanes)
    parts = [p.astype(BF) for p in three(v)]
    lane = lax.broadcasted_iota(jnp.int32, (lanes, d), 1)
    sub = lax.broadcasted_iota(jnp.int32, (lanes, d), 0)
    s = lax.broadcasted_iota(jnp.int32, (nmp * ndp, vr, d), 0)
    col = lax.broadcasted_iota(jnp.int32, (nmp * ndp, vr, d), 2)
    dev = (s % ndp) * nmp + s // ndp

    def spread(width):
        sel = jnp.where(lane % width == sub, 1.0, 0.0).astype(BF)
        return sum(nn(p, sel) for p in parts).reshape(nmp * ndp, vr, d)

    a = jnp.sum(jnp.where(col // small == dev, spread(small), 0.0), axis=0)
    wide = nmp * small
    b = spread(wide)
    per = nmp * ndp // nmp
    ups = []
    for m in range(nmp):
        keep = (dev // per == m) & (col // wide == dev % per)
        ups.append(jnp.sum(jnp.where(keep, b, 0.0), axis=0)[8:9])
    return a[0:8], jnp.concatenate(ups, axis=0)


def front_kernel(nz, heads, small, *refs):
    tok, wq, wo, wup, wdn, vec, cot, ids = refs[:8]
    normed_o, raw_o, wu_o, wd_o, cotx_o, tok_o = refs[8:14]
    low_o, wt_o, wotv, att_o, lse, own_o, rows_o, gains, mid_o, n2_o, n2x_o = refs[14:25]
    tokv, wqv, wov, vecv, normv, rawv, qa, ka, va, acc, ss, rs, ls = refs[25:]
    w = Where(nz)
    dp, mp = w.dp, w.mp
    cols = heads * HEAD
    t, d = normv.shape
    nmp, rows = tokv.shape[0], tokv.shape[1]
    greet(w.all)
    tx = Sender(ss, rs)
    count, late = [0], []

    def keep(src, dst, wait_late=True):
        cp = pltpu.make_async_copy(src, dst, ls.at[count[0]])
        cp.start()
        count[0] += 1
        if wait_late:
            late.append(cp)
        return cp

    nc = 4
    part = [pl.ds(i * (rows // nc), rows // nc) for i in range(nc)]
    vz = [None] + [tx.send(vec, vecv.at[mp, dp], w.pz[k]) for k in range(1, nz)]
    vy = [tx.send(vec, vecv.at[mp, dp], w.py)]
    xt = [tx.send(tok.at[part[i]], tokv.at[mp, part[i]], w.px) for i in range(nc)]
    qz = [None] + [tx.send(wq, wqv.at[dp], w.pz[k]) for k in range(1, nz)]
    qy = [tx.send(wq, wqv.at[dp], w.py)]
    ctok = tx.send(tok, tokv.at[mp], w.pc)
    dx = tx.send(wdn, wd_o.at[1, dp], w.px)
    cx = tx.send(cot, cotx_o, w.pc)
    first = [
        keep(vec, vecv.at[mp, dp], False),
        keep(tok, tokv.at[mp], False),
        keep(wq, wqv.at[dp], False),
        keep(wo, wov.at[dp], False),
    ]
    keep(wup, wu_o.at[0, dp])
    keep(wdn, wd_o.at[0, dp])
    for k in range(1, nz):
        vz[k].wait_recv()
        ref = vecv.at[mp, w.zfrom[k]]
        vy.append(tx.send(ref, ref, w.py))
    for k in range(nz):
        vy[k].wait_recv()
    for cp in first:
        cp.wait()
    vx = tx.send(vecv.at[mp], vecv.at[mp], w.px)
    vc = tx.send(vecv.at[mp], vecv.at[mp], w.pc)
    for k in range(1, nz):
        qz[k].wait_recv()
        ref = wqv.at[w.zfrom[k]]
        qy.append(tx.send(ref, ref, w.py))
    oz = [None] + [tx.send(wo, wov.at[dp], w.pz[k]) for k in range(1, nz)]
    oy = [tx.send(wo, wov.at[dp], w.py)]
    uz = [None] + [tx.send(wup, wu_o.at[0, dp], w.pz[k]) for k in range(1, nz)]
    dz = [None] + [tx.send(wdn, wd_o.at[0, dp], w.pz[k]) for k in range(1, nz)]
    uy = [tx.send(wup, wu_o.at[0, dp], w.py)]
    vx.wait_recv()
    vd = tx.send(vecv.at[w.xm], vecv.at[w.xm], w.pc)
    ct = []

    def forward(i):
        xt[i].wait_recv()
        ref = tokv.at[w.xm, part[i]]
        ct.append(tx.send(ref, ref, w.pc))

    forward(0)
    forward(1)
    vc.wait_recv()
    vd.wait_recv()
    main, ups = vector_rows(vecv, small, d)
    rows_o[0:8, :] = main
    rows_o[8:12, :] = ups
    rows_o[12:16, :] = jnp.zeros((4, d), F32)
    lane = lax.broadcasted_iota(jnp.int32, (cols, d), 1)
    pick = lane == lax.broadcasted_iota(jnp.int32, (cols, d), 0) + mp * cols
    for i in range(2):
        gains[i * cols : (i + 1) * cols, :] = jnp.sum(
            jnp.where(pick, main[2 + i : 3 + i], 0.0), axis=1, keepdims=True
        )
    for k in range(nz):
        qy[k].wait_recv()
    wt_o[...] = wqv[...].reshape(d, 3 * cols).T
    one = jnp.where(lax.broadcasted_iota(jnp.int32, (16, rows), 0) == 0, 1.0, 0.0).astype(BF)

    def project(m):
        ts = pl.ds(pl.multiple_of(m * rows, rows), rows)
        hat, _ = norm_rows(tokv[m].astype(F32))
        n = (hat * rows_o[0:1, :] + rows_o[1:2, :]).astype(BF)
        normv[ts, :] = n
        proj = nt(wt_o[...], n)
        rawv[:, ts] = proj[0 : 2 * cols]
        _, mq, mk = masks(ids[:, ts])
        mq, mk = mq.astype(BF), mk.astype(BF)
        for h in range(heads):
            qs, ks = h * HEAD, cols + h * HEAD
            hat, _ = norm_cols(proj[qs : qs + HEAD])
            q = (hat * gains[qs : qs + HEAD, :]).astype(BF)
            low_o[qs : qs + HEAD, ts] = q
            qa[h, 0:HEAD, ts] = q
            qa[h, HEAD:, ts] = mq
            hat, _ = norm_cols(proj[ks : ks + HEAD])
            k = (hat * gains[ks : ks + HEAD, :]).astype(BF)
            low_o[ks : ks + HEAD, ts] = k
            ka[h, ts, :] = jnp.concatenate([k, mk], axis=0).T
            v = proj[2 * cols + h * HEAD : 2 * cols + (h + 1) * HEAD].astype(BF)
            low_o[2 * cols + h * HEAD : 2 * cols + (h + 1) * HEAD, ts] = v
            va[h, 0:HEAD, ts] = v
            va[h, HEAD:, ts] = one

    project(mp)
    forward(2)
    ctok.wait_recv()
    project(w.cm)
    forward(3)
    project(w.xm)
    for cp in ct:
        cp.wait_recv()
    project(w.dm)
    keep(normv, normed_o)
    keep(rawv, raw_o)
    keep(tokv, tok_o)
    dx.wait_recv()
    ref = wd_o.at[1, dp]
    ez = [None] + [tx.send(ref, ref, w.pz[k]) for k in range(1, nz)]
    for k in range(1, nz):
        oz[k].wait_recv()
        ref = wov.at[w.zfrom[k]]
        oy.append(tx.send(ref, ref, w.py))
    ux, dy = [tx.send(wup, wu_o.at[1, dp], w.px)], [tx.send(wdn, wd_o.at[0, dp], w.py)]

    def attend_row(i):
        qi = pl.ds(pl.multiple_of(i * rows, rows), rows)
        acc[...] = jnp.zeros_like(acc)

        def tile(j, _):
            kj = pl.ds(pl.multiple_of(j * rows, rows), rows)
            s = [nn(ka[h, kj, :], qa[h, :, qi]) for h in range(heads)]
            p = [jnp.exp2(v * (SCALE * LOG2E)).astype(BF) for v in s]
            for h in range(heads):
                acc[h] += nn(va[h, :, kj], p[h])
            return 0

        lax.fori_loop(jnp.maximum(i - 2, 0), jnp.minimum(i + 3, nmp), tile, 0)
        pad = ids[:, qi] < 0
        lse[:, qi] = jnp.zeros((8, rows), F32)
        for h in range(heads):
            total = jnp.where(pad, 1.0, acc[h, HEAD : HEAD + 1, :])
            value = va[h, 0:HEAD, qi].astype(F32)
            o = jnp.where(pad, value, acc[h, 0:HEAD, :] * (1.0 / total))
            att_o[h * HEAD : (h + 1) * HEAD, qi] = o.astype(BF)
            lse[h : h + 1, qi] = jnp.log(total)
        return att_o.at[:, qi]

    at = [tx.send(attend_row(w.xm), own_o.at[mp], w.px)]
    for k in range(nz):
        oy[k].wait_recv()
    wotv[mp] = wov[...].reshape(d, cols).T
    ox = tx.send(wotv.at[mp], wotv.at[mp], w.px)
    oc = tx.send(wotv.at[mp], wotv.at[mp], w.pc)
    at.append(tx.send(attend_row(w.dm), own_o.at[mp], w.pd))
    for k in range(1, nz):
        uz[k].wait_recv()
        ref = wu_o.at[0, w.zfrom[k]]
        uy.append(tx.send(ref, ref, w.py))
        ux.append(tx.send(ref, wu_o.at[1, w.zfrom[k]], w.px))
    at.append(tx.send(attend_row(w.cm), own_o.at[mp], w.pc))
    for k in range(1, nz):
        dz[k].wait_recv()
        ref = wd_o.at[0, w.zfrom[k]]
        dy.append(tx.send(ref, ref, w.py))
    own = attend_row(mp)
    keep(own, own_o.at[mp], False).wait()
    ox.wait_recv()
    od = tx.send(wotv.at[w.xm], wotv.at[w.xm], w.pc)
    ey = [tx.send(wd_o.at[1, dp], wd_o.at[1, dp], w.py)]
    for k in range(1, nz):
        ez[k].wait_recv()
        ref = wd_o.at[1, w.zfrom[k]]
        ey.append(tx.send(ref, ref, w.py))
    uw = []
    for k in range(nz):
        uy[k].wait_recv()
        ref = wu_o.at[0, w.yfrom[k]]
        uw.append(tx.send(ref, wu_o.at[1, w.yfrom[k]], w.px))
    oc.wait_recv()
    od.wait_recv()
    for cp in at:
        cp.wait_recv()
    m = tokv[mp].astype(F32) + rows_o[4:5, :]
    m = m + tn(own_o[...].reshape(d, rows), wotv[...].reshape(d, d))
    mid_o[...] = m
    hat, _ = norm_rows(m)
    n2_o[...] = (hat * rows_o[5:6, :] + rows_o[6:7, :]).astype(BF)
    nx = tx.send(n2_o, n2x_o, w.pc)
    nx.wait_recv()
    cx.wait_recv()
    for cp in ux + dy + ey + uw:
        cp.wait_recv()
    tx.finish()
    for cp in late:
        cp.wait()


def front(tok, wq, wo, wup, wdn, vec, cot, ids, ndp, nmp, small):
    rows, d = tok.shape
    drow, unit, cols = wup.shape[0], wup.shape[1], wo.shape[1]
    heads, t, nsend, nlocal = cols // HEAD, rows * nmp, 80, 12
    dma, vm = pltpu.SemaphoreType.DMA, pltpu.VMEM
    return pl.pallas_call(
        functools.partial(front_kernel, ndp // 2, heads, small),
        out_shape=(
            sds((t, d), BF),
            sds((2 * cols, t), F32),
            sds((2, ndp, drow, unit), BF),
            sds((2, ndp, drow, unit), BF),
            sds((rows, d), BF),
            sds((nmp, rows, d), BF),
            sds((3 * cols, t), BF),
            sds((3 * cols, d), BF),
            sds((nmp, cols, d), BF),
            sds((cols, t), BF),
            sds((8, t), F32),
            sds((nmp, cols, rows), BF),
            sds((16, d), F32),
            sds((2 * cols, 1), F32),
            sds((rows, d), F32),
            sds((rows, d), BF),
            sds((rows, d), BF),
        ),
        in_specs=[ANY] * 7 + [VM],
        out_specs=(ANY,) * 6 + (VM,) * 11,
        scratch_shapes=[
            vm((nmp, rows, d), BF),
            vm((ndp, drow, 3 * cols), BF),
            vm((ndp, drow, cols), BF),
            vm((nmp, ndp) + vec.shape, F32),
            vm((t, d), BF),
            vm((2 * cols, t), F32),
            vm((heads, 2 * HEAD, t), BF),
            vm((heads, t, 2 * HEAD), BF),
            vm((heads, HEAD + 16, t), BF),
            vm((heads, HEAD + 16, rows), F32),
            dma((nsend,)),
            dma((nsend,)),
            dma((nlocal,)),
        ],
        compiler_params=params(collective_id=4, has_side_effects=True),
        cost_estimate=cost(20e9, 40 * 2**20),
        name="front",
    )(tok, wq, wo, wup, wdn, vec, cot, ids)


def spans(ids):
    b = ids.reshape(-1, TB)
    low = jnp.min(jnp.where(b < 0, 1000, b), axis=1)
    high = jnp.max(b, axis=1)
    n = b.shape[0]
    k = jnp.arange(n)
    lo = jnp.sum((high[None, :] < low[:, None]) & (k[None, :] <= k[:, None]), axis=1)
    hi = jnp.sum(low[None, :] <= high[:, None], axis=1)
    return jnp.concatenate([lo, hi]).astype(jnp.int32)


def solution(mesh):
    ndp, nmp = mesh.shape["dp"], mesh.shape["mp"]
    ndev, nz = ndp * nmp, ndp // 2

    def permute(v, kind, k=0):
        pairs = []
        for d in range(ndp):
            for m in range(nmp):
                z, y, x, c = d // 2, d % 2, m // 2, m % 2
                if kind == "core":
                    c = 1 - c
                if kind == "x":
                    x = 1 - x
                if kind == "y":
                    y = 1 - y
                if kind == "z":
                    z = (z + k) % nz
                pairs.append((d * nmp + m, (z * 2 + y) * nmp + x * 2 + c))
        return lax.ppermute(v, ("dp", "mp"), pairs)

    def columns(w, first, second):
        if w.shape[0] % 16:
            own = lax.all_gather(w, "dp", axis=0, tiled=True)[None]
            return [own, permute(own, "x")]
        s = jnp.stack([w] + [permute(w, "z", k) for k in range(1, nz)])
        got = {(0, 0): s}
        one = permute(s, first)
        two = permute(s, second)
        both = permute(one, second)
        got[(0, 1)] = one if first == "y" else two
        got[(1, 0)] = two if first == "y" else one
        got[(1, 1)] = both
        return [got[(0, 0)], got[(0, 1)], got[(1, 0)], got[(1, 1)]]

    def body(
        tokens,
        picture_ids,
        w_qkv,
        w_out,
        w_up,
        w_down,
        ln1_gain,
        ln1_bias,
        q_gain,
        k_gain,
        out_bias,
        ln2_gain,
        ln2_bias,
        up_bias,
        down_bias,
        cotangent,
    ):
        rows, d = tokens.shape[1], tokens.shape[2]
        drow = w_qkv.shape[0]
        cols = w_qkv.shape[2]
        heads = cols // HEAD
        unit = w_up.shape[1]
        dp, mp = lax.axis_index("dp"), lax.axis_index("mp")
        z, y, x, c = dp // 2, dp % 2, mp // 2, mp % 2
        tok, cot = tokens[0], cotangent[0]
        ids = picture_ids
        span = spans(ids[0])
        whole = drow % 16 == 0 and ndev == 32

        vs = [ln1_gain, ln1_bias, q_gain, k_gain, out_bias, ln2_gain, ln2_bias, down_bias, up_bias]
        small = vs[0].shape[0]
        used = 8 * small + up_bias.shape[0]
        if whole:
            vec = jnp.stack([jnp.pad(v, (0, 128 - v.shape[0])) for v in vs])
            vec = jnp.pad(vec, ((0, 16 - len(vs)), (0, 0)))
            (
                normed,
                raw,
                wu,
                wd,
                cot_other,
                tok_all,
                low,
                wt,
                wot,
                att,
                lse,
                att_own,
                rowv,
                gains,
                mid,
                n2,
                n2_other,
            ) = front(
                tok, w_qkv.reshape(drow, 3 * cols), w_out, w_up, w_down, vec, cot, ids, ndp, nmp, small
            )
            att_own = att_own.reshape(d, rows)
            ups, downs = [wu.reshape(2, d, unit)], [wd.reshape(2, d, unit)]
            wos = (wot.reshape(d, d),)
            ubias = rowv[8:12]
            gain1, gain2, dbias = rowv[0:1], rowv[5:6], rowv[7:8]
        else:
            flat = jnp.concatenate(vs)
            vec = jnp.pad(flat, (0, 1024 - used)).reshape(8, 128)
            wcat = jnp.concatenate([w_qkv.reshape(drow, 3 * cols), w_out], axis=1)
            tok_all, w_all, vec_all = gather_all(tok, wcat, vec, ndp, nmp)
            vec_all = vec_all.reshape(nmp, ndp, 1024).transpose(1, 0, 2).reshape(ndev, 1024)
            gain1, shift1, qg, kg, obias, gain2, shift2, dbias = [
                vec_all[:, i * small : (i + 1) * small].reshape(1, d) for i in range(8)
            ]
            ubias = vec_all[:, 8 * small : used].reshape(nmp, unit)
            gains = jnp.concatenate(
                [
                    lax.dynamic_slice_in_dim(qg[0], mp * cols, cols),
                    lax.dynamic_slice_in_dim(kg[0], mp * cols, cols),
                ]
            ).reshape(2 * cols, 1)

            ups = columns(w_up, "y", "x")
            downs = columns(w_down, "x", "y")
            cot_other = permute(cot, "core")

            normed, raw, low, wt = project(
                tok_all, w_all.reshape(d, 3 * cols + w_out.shape[1]), gain1, shift1, gains, heads
            )
            wo0 = wt[3 * cols :]
            wo1 = permute(wo0, "x")
            wo2, wo3 = permute(wo0, "core"), permute(wo1, "core")
            wos = (wo0, wo1, wo2, wo3)
            att, lse = attend(span, low, ids, heads)
            att_own = swap(att, True, nmp, 1).reshape(d, rows)
            mid, n2 = middle_part(att_own, wos, tok, obias, gain2, shift2)
            n2_other = permute(n2, "core")
        o_own, o_send, g_own, g_send, dwu, dwd, gbias = feed(
            n2, n2_other, cot, cot_other, ubias, ups, downs, nz
        )
        g_got = permute(g_send, "core")
        gmid, gatt, gwo, sums2 = middle_back(g_own, g_got, mid, cot, att_own, wos, gain2, nmp)
        o_got = permute(o_send, "core")
        result = (mid + o_own + o_got.astype(F32) + dbias).astype(BF)
        dout = swap(gatt, False, nmp, 2)
        gproj, ggain = attend_back(span, low, raw, att, lse, dout, ids, gains, heads)
        order = jnp.stack([mp, x * 2 + 1 - c, (1 - x) * 2 + c, (1 - x) * 2 + 1 - c]).astype(jnp.int32)
        gn, gwq, sums1 = project_back(order, gproj, normed, tok_all, wt[: 3 * cols])
        got = permute(gn[1::2], "core")
        mine = gn[0::2].astype(F32) + got.astype(F32)
        far = permute(mine[1].astype(BF), "x")
        gnormed = mine[0] + far.astype(F32)
        grad_tokens = tokens_back(gnormed, tok, gain1, gmid)

        def pick(v, i):
            return lax.dynamic_index_in_dim(v, i, 0, keepdims=False)

        def along(v, kind):
            i = {"x": None, "y": y}[kind]
            if i is None:
                keep, send = v[0], v[1]
            else:
                keep, send = pick(v, i), pick(v, 1 - i)
            return (keep.astype(F32) + permute(send, kind).astype(F32)).astype(BF)

        def along_z(v):
            total = pick(v, z).astype(F32)
            for k in range(1, nz):
                total = total + permute(pick(v, (z + k) % nz), "z", k).astype(F32)
            return total

        def over_dp(v):
            if drow % 16:
                return lax.psum_scatter(v.astype(F32), "dp", scatter_dimension=0, tiled=True)
            v = v.reshape(nz, 2, drow, v.shape[-1]).transpose(1, 0, 2, 3)
            return along_z(along(v, "y"))

        def reduce_columns(v, y_first):
            if drow % 16 or not y_first:
                return over_dp(along(v, "x"))
            v = v.reshape(2, nz, 2, drow, unit).transpose(2, 0, 1, 3, 4)
            return along_z(along(along(v, "y"), "x"))

        grad_up = reduce_columns(dwu, False)
        grad_down = reduce_columns(dwd, True)
        mine_o = jnp.stack([pick(gwo, mp), pick(gwo, (1 - x) * 2 + c)])
        send_o = jnp.stack([pick(gwo, x * 2 + 1 - c), pick(gwo, (1 - x) * 2 + 1 - c)])
        go = (mine_o.astype(F32) + permute(send_o, "core").astype(F32)).astype(BF)
        go = along(go, "x")
        grad_att = over_dp(jnp.concatenate([gwq, go], axis=1))

        def spread(v, at, size):
            return lax.dynamic_update_slice_in_dim(jnp.zeros((size,), F32), v, at, 0)

        gq = spread(ggain[:cols, 0], mp * cols, d)
        gk = spread(ggain[cols:, 0], mp * cols, d)
        gb = spread(gbias[0, 0], mp * unit, nmp * unit)
        gb = gb + spread(gbias[1, 0], ((1 - x) * 2 + c) * unit, nmp * unit)
        eight = jnp.stack([sums1[0], sums1[1], gq, gk, sums2[0], sums2[1], sums2[2], sums2[3]])
        parts = jnp.concatenate(
            [
                eight.reshape(8, ndev, small).transpose(1, 0, 2).reshape(ndev, 8 * small),
                gb.reshape(ndev, used - 8 * small),
            ],
            axis=1,
        )
        parts = jnp.pad(parts, ((0, 0), (0, 1024 - used))).reshape(ndev, 8, 128)
        tot = vector_sums(parts, ndp, nmp).reshape(1024)
        vgrads = [tot[i * small : (i + 1) * small] for i in range(8)] + [tot[8 * small : used]]

        return (
            result[None],
            grad_tokens[None],
            grad_att[:, : 3 * cols].reshape(drow, 3, cols),
            grad_att[:, 3 * cols :],
            grad_up,
            grad_down,
            vgrads[0],
            vgrads[1],
            vgrads[2],
            vgrads[3],
            vgrads[4],
            vgrads[5],
            vgrads[6],
            vgrads[8],
            vgrads[7],
        )

    vec_spec = P(("dp", "mp"))
    return jax.shard_map(
        body,
        mesh=mesh,
        in_specs=(
            P("dp", "mp", None),
            P("dp", None),
            P("dp", None, "mp"),
            P("dp", "mp"),
            P("dp", "mp"),
            P("dp", "mp"),
        )
        + (vec_spec,) * 9
        + (P("dp", "mp", None),),
        out_specs=(
            P("dp", "mp", None),
            P("dp", "mp", None),
            P("dp", None, "mp"),
            P("dp", "mp"),
            P("dp", "mp"),
            P("dp", "mp"),
        )
        + (vec_spec,) * 9,
        check_vma=False,
    )
```

```python
import functools

import jax
import jax.numpy as jnp
from jax import lax
from jax.experimental import pallas as pl
from jax.experimental.pallas import tpu as pltpu
from jax.sharding import PartitionSpec as P

F32 = jnp.float32
BF = jnp.bfloat16
HEAD = 64
EPS = 1e-06
TB = 512
BIG = 32768.0
LOG2E = 1.4426950408889634
MESH = pl.DeviceIdType.MESH
ANY = pl.BlockSpec(memory_space=pl.ANY)
VM = pl.BlockSpec(memory_space=pltpu.VMEM)
SM = pl.BlockSpec(memory_space=pltpu.SMEM)
VLIM = 60 * 1024 * 1024


def nn(a, b):
    return lax.dot_general(a, b, (((1,), (0,)), ((), ())), preferred_element_type=F32)


def nt(a, b):
    return lax.dot_general(a, b, (((1,), (1,)), ((), ())), preferred_element_type=F32)


def tn(a, b):
    return lax.dot_general(a, b, (((0,), (0,)), ((), ())), preferred_element_type=F32)


def sds(shape, dtype):
    return jax.ShapeDtypeStruct(shape, dtype)


def params(**kw):
    return pltpu.CompilerParams(vmem_limit_bytes=VLIM, **kw)


def cost(flops, nbytes, trans=0):
    return pl.CostEstimate(flops=int(flops), bytes_accessed=int(nbytes), transcendentals=int(trans))


def rcopy(src, dst, ssem, rsem, peer):
    return pltpu.make_async_remote_copy(
        src_ref=src,
        dst_ref=dst,
        send_sem=ssem,
        recv_sem=rsem,
        device_id=peer,
        device_id_type=MESH,
    )


def greet(peers):
    bar = pltpu.get_barrier_semaphore()
    for p in peers:
        pl.semaphore_signal(bar, inc=1, device_id=p, device_id_type=MESH)
    pl.semaphore_wait(bar, len(peers))


def gather_kernel(
    nz, nc, tok, w, vec, tok_all, w_all, vec_all, loc, zs, zr, ys, yr, xs, xr, cs, cr, tx, rx, tc, rc
):
    dp, mp = lax.axis_index("dp"), lax.axis_index("mp")
    z, y, x, c = dp // 2, dp % 2, mp // 2, mp % 2
    xm, cm, dm = (1 - x) * 2 + c, x * 2 + 1 - c, (1 - x) * 2 + 1 - c
    ypeer, xpeer, cpeer = (z * 2 + 1 - y, mp), (dp, xm), (dp, cm)
    zpeers = [(((z + k) % nz) * 2 + y, mp) for k in range(1, nz)]
    greet(zpeers + [ypeer, xpeer, cpeer])
    rows = tok.shape[0] // nc
    xt = []
    for i in range(nc):
        part = pl.ds(i * rows, rows)
        cp = rcopy(tok.at[part], tok_all.at[mp, part], tx.at[i], rx.at[i], xpeer)
        cp.start()
        xt.append(cp)
    zc = []
    for k in range(1, nz):
        for kind, (src, dst) in enumerate(((vec, vec_all.at[mp, dp]), (w, w_all.at[dp]))):
            cp = rcopy(src, dst, zs.at[kind, k], zr.at[kind, k], zpeers[k - 1])
            cp.start()
            zc.append(cp)
    yc = []
    for kind, (src, dst) in enumerate(((vec, vec_all.at[mp, dp]), (w, w_all.at[dp]))):
        cp = rcopy(src, dst, ys.at[kind, 0], yr.at[kind, 0], ypeer)
        cp.start()
        yc.append(cp)
    own_tok = rcopy(tok, tok_all.at[mp], tc.at[nc], rc.at[nc], cpeer)
    own_tok.start()
    locs = [
        pltpu.make_async_copy(tok, tok_all.at[mp], loc.at[0]),
        pltpu.make_async_copy(w, w_all.at[dp], loc.at[1]),
        pltpu.make_async_copy(vec, vec_all.at[mp, dp], loc.at[2]),
    ]
    for cp in locs:
        cp.start()
    for k in range(1, nz):
        src_dp = ((z + nz - k) % nz) * 2 + y
        for kind in range(2):
            zc[(k - 1) * 2 + kind].wait_recv()
            ref = (vec_all.at[mp, src_dp], w_all.at[src_dp])[kind]
            cp = rcopy(ref, ref, ys.at[kind, k], yr.at[kind, k], ypeer)
            cp.start()
            yc.append(cp)
    ct = []

    def forward(i):
        part = pl.ds(i * rows, rows)
        xt[i].wait_recv()
        cp = rcopy(tok_all.at[xm, part], tok_all.at[xm, part], tc.at[i], rc.at[i], cpeer)
        cp.start()
        ct.append(cp)

    forward(0)
    for cp in locs:
        cp.wait()
    for k in range(nz):
        yc[k * 2].wait_recv()
    vx = rcopy(vec_all.at[mp], vec_all.at[mp], xs, xr, xpeer)
    vx.start()
    vc0 = rcopy(vec_all.at[mp], vec_all.at[mp], cs.at[0], cr.at[0], cpeer)
    vc0.start()
    if nc > 1:
        forward(1)
    vx.wait_recv()
    vc1 = rcopy(vec_all.at[xm], vec_all.at[xm], cs.at[1], cr.at[1], cpeer)
    vc1.start()
    for i in range(2, nc):
        forward(i)
    for k in range(nz):
        yc[k * 2 + 1].wait_recv()
    for cp in ct:
        cp.wait_recv()
    own_tok.wait()
    vc0.wait()
    vc1.wait()
    vx.wait_send()
    for cp in zc + yc + xt + ct:
        cp.wait_send()


def gather_all(tok, w, vec, ndp, nmp):
    nz, nc = ndp // 2, 4
    dma = pltpu.SemaphoreType.DMA
    return pl.pallas_call(
        functools.partial(gather_kernel, nz, nc),
        out_shape=(
            sds((nmp,) + tok.shape, BF),
            sds((ndp,) + w.shape, BF),
            sds((nmp, ndp) + vec.shape, F32),
        ),
        in_specs=[ANY] * 3,
        out_specs=(ANY,) * 3,
        scratch_shapes=[
            dma((3,)),
            dma((2, nz)),
            dma((2, nz)),
            dma((2, nz)),
            dma((2, nz)),
            dma,
            dma,
            dma((2,)),
            dma((2,)),
            dma((nc,)),
            dma((nc,)),
            dma((nc + 1,)),
            dma((nc + 1,)),
        ],
        compiler_params=pltpu.CompilerParams(collective_id=0, has_side_effects=True),
        name="gather_start",
    )(tok, w, vec)


def swap_kernel(forward, nmp, src, dst, loc, ss, rs):
    dp, mp = lax.axis_index("dp"), lax.axis_index("mp")
    own = dst.shape[2] if forward else src.shape[2]
    peers = [(mp + k) % nmp for k in range(1, nmp)]
    greet([(dp, m) for m in peers])

    def ends(m):
        if forward:
            return src.at[:, pl.ds(pl.multiple_of(m * own, own), own)], dst.at[mp]
        return src.at[m], dst.at[:, pl.ds(pl.multiple_of(mp * own, own), own)]

    cps = []
    for k, m in enumerate(peers):
        s, d = ends(m)
        cp = rcopy(s, d, ss.at[k], rs.at[k], (dp, m))
        cp.start()
        cps.append(cp)
    s, d = ends(mp)
    lc = pltpu.make_async_copy(s, d, loc)
    lc.start()
    lc.wait()
    for cp in cps:
        cp.wait()


def swap(src, forward, nmp, cid):
    dma = pltpu.SemaphoreType.DMA
    if forward:
        shape = (nmp, src.shape[0], src.shape[1] // nmp)
    else:
        shape = (src.shape[1], src.shape[2] * nmp)
    return pl.pallas_call(
        functools.partial(swap_kernel, forward, nmp),
        out_shape=sds(shape, BF),
        in_specs=[ANY],
        out_specs=ANY,
        scratch_shapes=[dma, dma((nmp - 1,)), dma((nmp - 1,))],
        compiler_params=pltpu.CompilerParams(collective_id=cid, has_side_effects=True),
        name="swap_fwd" if forward else "swap_bwd",
    )(src)


def vector_kernel(ndp, nmp, src, out, got, ss, rs):
    dp, mp = lax.axis_index("dp"), lax.axis_index("mp")
    me, n = dp * nmp + mp, ndp * nmp
    peers = [(me + k) % n for k in range(1, n)]
    greet([(p // nmp, p % nmp) for p in peers])
    cps = []
    for k, p in enumerate(peers):
        cp = rcopy(src.at[p], got.at[k], ss.at[k], rs.at[k], (p // nmp, p % nmp))
        cp.start()
        cps.append(cp)
    total = src[me]
    for k, cp in enumerate(cps):
        cp.wait_recv()
        total = total + got[k]
    out[...] = total
    for cp in cps:
        cp.wait_send()


def vector_sums(parts, ndp, nmp):
    n = ndp * nmp
    dma = pltpu.SemaphoreType.DMA
    return pl.pallas_call(
        functools.partial(vector_kernel, ndp, nmp),
        out_shape=sds(parts.shape[1:], F32),
        in_specs=[VM],
        out_specs=VM,
        scratch_shapes=[pltpu.VMEM((n - 1,) + parts.shape[1:], F32), dma((n - 1,)), dma((n - 1,))],
        compiler_params=pltpu.CompilerParams(collective_id=3, has_side_effects=True),
        name="vector_sums",
    )(parts)


def norm_rows(v):
    centre = jnp.mean(v, axis=-1, keepdims=True)
    v = v - centre
    r = lax.rsqrt(jnp.mean(v * v, axis=-1, keepdims=True) + EPS)
    return v * r, r


def norm_cols(v):
    centre = jnp.mean(v, axis=0, keepdims=True)
    v = v - centre
    r = lax.rsqrt(jnp.mean(v * v, axis=0, keepdims=True) + EPS)
    return v * r, r


def qkv_kernel(heads, tok, w, gain, shift, gains, normed, raw, low, wt):
    @pl.when(pl.program_id(0) == 0)
    def _():
        wt[...] = w[...].T

    cols = heads * HEAD
    hat, _ = norm_rows(tok[0].astype(F32))
    n = (hat * gain[...] + shift[...]).astype(BF)
    normed[...] = n
    proj = nt(wt[0 : 3 * cols, :], n)
    raw[...] = proj[0 : 2 * cols]
    for h in range(2 * heads):
        part = slice(h * HEAD, (h + 1) * HEAD)
        hat, _ = norm_cols(proj[part])
        low[part, :] = (hat * gains[part, :]).astype(BF)
    low[2 * cols :, :] = proj[2 * cols :].astype(BF)


def project(tok_all, w, gain, shift, gains, heads):
    nb, rows, d = tok_all.shape
    cols = heads * HEAD
    t = nb * rows
    full = lambda shape: pl.BlockSpec(shape, lambda i: (0,) * len(shape))
    return pl.pallas_call(
        functools.partial(qkv_kernel, heads),
        grid=(nb,),
        out_shape=(
            sds((t, d), BF),
            sds((2 * cols, t), F32),
            sds((3 * cols, t), BF),
            sds((w.shape[1], w.shape[0]), BF),
        ),
        in_specs=[
            pl.BlockSpec((1, rows, d), lambda i: (i, 0, 0)),
            full(w.shape),
            full((1, d)),
            full((1, d)),
            full((2 * cols, 1)),
        ],
        out_specs=(
            pl.BlockSpec((rows, d), lambda i: (i, 0)),
            pl.BlockSpec((2 * cols, rows), lambda i: (0, i)),
            pl.BlockSpec((3 * cols, rows), lambda i: (0, i)),
            full((w.shape[1], w.shape[0])),
        ),
        compiler_params=params(),
        cost_estimate=cost(2 * t * d * 3 * cols, 12 * 2**20),
        name="project_qkv",
    )(tok_all, w, gain, shift, gains)


def masks(ids):
    t = ids.shape[1]
    r = lax.broadcasted_iota(jnp.int32, (HEAD, t), 0)
    pad = ids < 0
    mq = jnp.where((r == ids) | ((r == 31) & pad), 1.0, 0.0)
    mk = jnp.where((r <= 31) & (r != ids), -BIG, 0.0)
    mk = jnp.where((r >= 32) & (r < 35), 1.0, mk)
    return r, mq, mk


def three(v):
    a = v.astype(BF).astype(F32)
    b = (v - a).astype(BF).astype(F32)
    return a, b, v - a - b


SCALE = HEAD**-0.5


def attend_kernel(heads, nblk, span, low, ids, out, lse, qa, ka, va, acc):
    cols = heads * HEAD
    t = ids.shape[1]
    _, mq, mk = masks(ids[...])
    mq, mk = mq.astype(BF), mk.astype(BF)
    one = jnp.where(lax.broadcasted_iota(jnp.int32, (16, t), 0) == 0, 1.0, 0.0).astype(BF)
    for h in range(heads):
        qa[h, 0:HEAD, :] = low[h * HEAD : (h + 1) * HEAD, :]
        qa[h, HEAD:, :] = mq
        k = low[cols + h * HEAD : cols + (h + 1) * HEAD, :]
        ka[h, :, :] = jnp.concatenate([k, mk], axis=0).T
        va[h, 0:HEAD, :] = low[2 * cols + h * HEAD : 2 * cols + (h + 1) * HEAD, :]
        va[h, HEAD:, :] = one
    acc[...] = jnp.zeros_like(acc)

    def row(i, _):
        qi = pl.ds(pl.multiple_of(i * TB, TB), TB)

        def col(j, _):
            kj = pl.ds(pl.multiple_of(j * TB, TB), TB)
            s = [nn(ka[h, kj, :], qa[h, :, qi]) for h in range(heads)]
            p = [jnp.exp2(v * (SCALE * LOG2E)).astype(BF) for v in s]
            for h in range(heads):
                acc[h, :, qi] += nn(va[h, :, kj], p[h])
            return 0

        return lax.fori_loop(span[i], span[nblk + i], col, 0)

    lax.fori_loop(0, nblk, row, 0)
    pad = ids[...] < 0
    lse[...] = jnp.zeros_like(lse)
    for h in range(heads):
        total = jnp.where(pad, 1.0, acc[h, HEAD : HEAD + 1, :])
        value = low[2 * cols + h * HEAD : 2 * cols + (h + 1) * HEAD, :].astype(F32)
        o = jnp.where(pad, value, acc[h, 0:HEAD, :] * (1.0 / total))
        out[h * HEAD : (h + 1) * HEAD, :] = o.astype(BF)
        lse[h : h + 1, :] = jnp.log(total)


def attend(span, low, ids, heads):
    cols, t = heads * HEAD, low.shape[1]
    return pl.pallas_call(
        functools.partial(attend_kernel, heads, t // TB),
        out_shape=(sds((cols, t), BF), sds((8, t), F32)),
        in_specs=[SM, VM, VM],
        out_specs=(VM, VM),
        scratch_shapes=[
            pltpu.VMEM((heads, 2 * HEAD, t), BF),
            pltpu.VMEM((heads, t, 2 * HEAD), BF),
            pltpu.VMEM((heads, HEAD + 16, t), BF),
            pltpu.VMEM((heads, HEAD + 16, t), F32),
        ],
        compiler_params=params(),
        cost_estimate=cost(12e9, 4 * 2**20),
        name="attend",
    )(span, low, ids)


def head_back(raw, gain, grad):
    hat, r = norm_cols(raw)
    e = grad * gain
    m1 = jnp.mean(e, axis=0, keepdims=True)
    m2 = jnp.mean(e * hat, axis=0, keepdims=True)
    return (e - m1 - hat * m2) * r, jnp.sum(grad * hat, axis=1, keepdims=True)


def attend_back_kernel(
    heads, nblk, span, low, raw, att, lse, dout, ids, gains, gproj, ggain, qa, ka, va, da, dq, dk, dv
):
    cols = heads * HEAD
    t = ids.shape[1]
    r, mq, mk = masks(ids[...])
    mk = mk.astype(BF)
    one = jnp.where(r < 3, 1.0, 0.0).astype(BF)
    for h in range(heads):
        hs = slice(h * HEAD, (h + 1) * HEAD)
        qa[h, 0:HEAD, :] = low[hs, :]
        a, b, c = three(lse[h : h + 1, :] * (-1.0 / SCALE))
        m = jnp.where(r == 32, a, jnp.where(r == 33, b, jnp.where(r == 34, c, mq)))
        qa[h, HEAD:, :] = m.astype(BF)
        k = low[cols + h * HEAD : cols + (h + 1) * HEAD, :]
        ka[h, :, :] = jnp.concatenate([k, mk], axis=0).T
        v = low[2 * cols + h * HEAD : 2 * cols + (h + 1) * HEAD, :]
        va[h, :, :] = jnp.concatenate([v, one], axis=0).T
        do = dout[hs, :]
        delta = jnp.sum(do.astype(F32) * att[hs, :].astype(F32), axis=0, keepdims=True)
        a, b, c = three(-delta)
        da[h, 0:HEAD, :] = do
        da[h, HEAD:, :] = jnp.where(
            r == 0, a, jnp.where(r == 1, b, jnp.where(r == 2, c, 0.0))
        ).astype(BF)
    dq[...] = jnp.zeros_like(dq)
    dk[...] = jnp.zeros_like(dk)
    dv[...] = jnp.zeros_like(dv)

    def row(i, _):
        qi = pl.ds(pl.multiple_of(i * TB, TB), TB)

        def col(j, _):
            kj = pl.ds(pl.multiple_of(j * TB, TB), TB)
            s = [nn(ka[h, kj, :], qa[h, :, qi]) for h in range(heads)]
            d = [nn(va[h, kj, :], da[h, :, qi]) for h in range(heads)]
            p = [jnp.exp2(v * (SCALE * LOG2E)) for v in s]
            ds = [(p[h] * d[h]).astype(BF) for h in range(heads)]
            for h in range(heads):
                hs = pl.ds(h * HEAD, HEAD)
                dv[hs, kj] += nt(dout[hs, qi], p[h].astype(BF))
                dk[hs, kj] += nt(low[hs, qi], ds[h])
                dq[hs, qi] += nn(low[pl.ds(cols + h * HEAD, HEAD), kj], ds[h])
            return 0

        return lax.fori_loop(span[i], span[nblk + i], col, 0)

    lax.fori_loop(0, nblk, row, 0)
    pad = ids[...] < 0
    for h in range(heads):
        hs = slice(h * HEAD, (h + 1) * HEAD)
        for part, grad in ((0, dq), (1, dk)):
            ps = slice(part * cols + h * HEAD, part * cols + (h + 1) * HEAD)
            g, gg = head_back(raw[ps, :], gains[ps, :], grad[hs, :] * SCALE)
            gproj[ps, :] = g.astype(BF)
            ggain[ps, :] = gg
        g = dv[hs, :] + jnp.where(pad, dout[hs, :].astype(F32), 0.0)
        gproj[2 * cols + h * HEAD : 2 * cols + (h + 1) * HEAD, :] = g.astype(BF)


def attend_back(span, low, raw, att, lse, dout, ids, gains, heads):
    cols, t = heads * HEAD, low.shape[1]
    return pl.pallas_call(
        functools.partial(attend_back_kernel, heads, t // TB),
        out_shape=(sds((3 * cols, t), BF), sds((2 * cols, 1), F32)),
        in_specs=[SM] + [VM] * 7,
        out_specs=(VM, VM),
        scratch_shapes=[
            pltpu.VMEM((heads, 2 * HEAD, t), BF),
            pltpu.VMEM((heads, t, 2 * HEAD), BF),
            pltpu.VMEM((heads, t, 2 * HEAD), BF),
            pltpu.VMEM((heads, 2 * HEAD, t), BF),
            pltpu.VMEM((cols, t), F32),
            pltpu.VMEM((cols, t), F32),
            pltpu.VMEM((cols, t), F32),
        ],
        compiler_params=params(),
        cost_estimate=cost(30e9, 12 * 2**20),
        name="attend_back",
    )(span, low, raw, att, lse, dout, ids, gains)


def place_out(pieces, dest):
    mp = lax.axis_index("mp")
    x, c = mp // 2, mp % 2
    order = (mp, (1 - x) * 2 + c, x * 2 + 1 - c, (1 - x) * 2 + 1 - c)
    rows = pieces[0].shape[0]
    for piece, m in zip(pieces, order):
        dest[pl.ds(pl.multiple_of(m * rows, rows), rows), :] = piece[...]


def middle_kernel(att, w0, w1, w2, w3, tok, bias, gain, shift, mid, low, wo):
    place_out((w0, w1, w2, w3), wo)
    m = tok[...].astype(F32) + tn(att[...], wo[...]) + bias[...]
    mid[...] = m
    hat, _ = norm_rows(m)
    low[...] = (hat * gain[...] + shift[...]).astype(BF)


def middle_part(att, wos, tok, bias, gain, shift):
    rows, d = tok.shape
    return pl.pallas_call(
        middle_kernel,
        out_shape=(sds((rows, d), F32), sds((rows, d), BF)),
        in_specs=[VM] * 9,
        out_specs=(VM, VM),
        scratch_shapes=[pltpu.VMEM((d, d), BF)],
        compiler_params=params(),
        cost_estimate=cost(2 * rows * d * d, 6 * 2**20),
        name="middle",
    )(att, *wos, tok, bias, gain, shift)


def middle_back_kernel(nmp, g0, g1, mid, cot, att, *refs):
    pieces, (gain, gmid, gatt, gwo, sums, wo) = refs[:-6], refs[-6:]
    if len(pieces) > 1:
        place_out(pieces, wo)
    else:
        wo = pieces[0]
    gy = cot[...].astype(F32)
    g = g0[...] + g1[...].astype(F32)
    hat, r = norm_rows(mid[...])
    e = g * gain[...]
    m1 = jnp.mean(e, axis=-1, keepdims=True)
    m2 = jnp.mean(e * hat, axis=-1, keepdims=True)
    gm = gy + (e - m1 - hat * m2) * r
    gmid[...] = gm
    low = gm.astype(BF)
    rows = att.shape[0] // nmp
    ga = nt(wo[...], low).astype(BF)
    for m in range(nmp):
        gatt[m] = ga[m * rows : (m + 1) * rows]
    gw = nt(gm.T.astype(BF), att[...]).astype(BF)
    mp = lax.axis_index("mp")
    for m in range(nmp):
        gwo[m] = gw[:, m * rows : (m + 1) * rows]
    sums[...] = jnp.zeros_like(sums)
    for k, v in enumerate((gm, g * hat, g, gy)):
        sums[k : k + 1, :] = jnp.sum(v, axis=0, keepdims=True)


def middle_back(g0, g1, mid, cot, att, wos, gain, nmp):
    rows, d = mid.shape
    return pl.pallas_call(
        functools.partial(middle_back_kernel, nmp),
        out_shape=(
            sds((rows, d), F32),
            sds((nmp, d // nmp, rows), BF),
            sds((nmp, d, d // nmp), BF),
            sds((8, d), F32),
        ),
        in_specs=[VM] * (6 + len(wos)),
        out_specs=(VM,) * 4,
        scratch_shapes=[pltpu.VMEM((d, d), BF)],
        compiler_params=params(),
        cost_estimate=cost(4 * rows * d * d, 10 * 2**20),
        name="middle_back",
    )(g0, g1, mid, cot, att, *wos, gain)


def feed_kernel(npiece, nz, *refs):
    n0, n1, c0, c1, bias = refs[:5]
    pieces = refs[5 : 5 + npiece]
    out_own, out_send, g_own, g_send, dwu, dwd, gbias = refs[5 + npiece : 12 + npiece]
    wu, wd, n2, gy, n2t, gyt, acts, gps, oacc, gacc, sem = refs[12 + npiece :]
    dp, mp = lax.axis_index("dp"), lax.axis_index("mp")
    z, y, x, c = dp // 2, dp % 2, mp // 2, mp % 2
    copies = []
    half = npiece // 2
    for a, piece in enumerate(pieces):
        dest = (wu, wd)[a // half]
        rel = a % half
        count, rows = piece.shape[0], piece.shape[1]
        for k in range(count):
            if half <= 2:
                at, colidx = 0, (k if half == 1 else rel)
            else:
                zz = (z + nz - k) % nz
                at = (zz * 2 + (y if rel % 2 == 0 else 1 - y)) * rows
                at, colidx = pl.multiple_of(at, rows), rel // 2
            cp = pltpu.make_async_copy(piece.at[k], dest.at[colidx, pl.ds(at, rows), :], sem.at[a, k])
            cp.start()
            copies.append(cp)
    hr = n0.shape[0]
    for i, (n, g) in enumerate(((n0, c0), (n1, c1))):
        part = slice(i * hr, (i + 1) * hr)
        n2[part, :] = n[...]
        gy[part, :] = g[...]
        n2t[:, part] = n[...].T
        gyt[:, part] = g[...].T
    oacc[...] = jnp.zeros_like(oacc)
    gacc[...] = jnp.zeros_like(gacc)
    for cp in copies:
        cp.wait()
    rows, d = n2.shape
    cw = acts.shape[1]
    per = wu.shape[2] // cw
    ones = jnp.ones((16, rows), BF)

    def chunk(i, _):
        col, off = i // per, pl.multiple_of((i % per) * cw, cw)
        cs = pl.ds(off, cw)
        m = jnp.where(col == 0, mp, (1 - x) * 2 + c)
        b = bias[pl.ds(m, 1), cs]
        for rb in range(rows // 256):
            rs = slice(rb * 256, (rb + 1) * 256)
            u = nn(n2[rs, :], wu[col, :, cs]) + b
            ga = nn(gy[rs, :], wd[col, :, cs])
            cdf = 0.5 + 0.5 * lax.erf(u * 0.7071067811865476)
            act = (u * cdf).astype(BF)
            gp = (ga * (cdf + u * (jnp.exp(-0.5 * u * u) * 0.3989422804014327))).astype(BF)
            acts[rs, :] = act
            gps[rs, :] = gp
            oacc[rs, :] += nt(act, wd[col, :, cs])
            gacc[rs, :] += nt(gp, wu[col, :, cs])
        dwd[col, :, cs] = nn(gyt[...], acts[...]).astype(BF)
        dwu[col, :, cs] = nn(n2t[...], gps[...]).astype(BF)
        gbias[col, :, cs] = nn(ones, gps[...])[0:8]
        return 0

    lax.fori_loop(0, 2 * per, chunk, 0)
    out_own[...] = oacc[0:hr]
    out_send[...] = oacc[hr:].astype(BF)
    g_own[...] = gacc[0:hr]
    g_send[...] = gacc[hr:].astype(BF)


def feed(n0, n1, c0, c1, bias, ups, downs, nz):
    hr, d = n0.shape
    rows, cw = 2 * hr, 256
    unit = ups[0].shape[2]
    pieces = list(ups) + list(downs)
    kmax = max(p.shape[0] for p in pieces)
    vm = pltpu.VMEM
    return pl.pallas_call(
        functools.partial(feed_kernel, len(pieces), nz),
        out_shape=(
            sds((hr, d), F32),
            sds((hr, d), BF),
            sds((hr, d), F32),
            sds((hr, d), BF),
            sds((2, d, unit), BF),
            sds((2, d, unit), BF),
            sds((2, 8, unit), F32),
        ),
        in_specs=[VM] * 5 + [ANY] * len(pieces),
        out_specs=(VM,) * 7,
        scratch_shapes=[
            vm((2, d, unit), BF),
            vm((2, d, unit), BF),
            vm((rows, d), BF),
            vm((rows, d), BF),
            vm((d, rows), BF),
            vm((d, rows), BF),
            vm((rows, cw), BF),
            vm((rows, cw), BF),
            vm((rows, d), F32),
            vm((rows, d), F32),
            pltpu.SemaphoreType.DMA((len(pieces), kmax)),
        ],
        compiler_params=params(),
        cost_estimate=cost(12 * rows * d * 2 * unit, 22 * 2**20),
        name="feed_forward",
    )(n0, n1, c0, c1, bias, *pieces)


def project_back_kernel(order, gproj, normed, tok, wt, gn, gw, sums, acc):
    @pl.when(pl.program_id(0) == 0)
    def _():
        acc[...] = jnp.zeros_like(acc)
        sums[...] = jnp.zeros_like(sums)

    acc[...] += nn(gproj[...], normed[...])
    g = tn(gproj[...], wt[...])
    gn[0] = g.astype(BF)
    hat, _ = norm_rows(tok[0].astype(F32))
    sums[0:1, :] += jnp.sum(g * hat, axis=0, keepdims=True)
    sums[1:2, :] += jnp.sum(g, axis=0, keepdims=True)

    @pl.when(pl.program_id(0) == pl.num_programs(0) - 1)
    def _():
        gw[...] = acc[...].T.astype(BF)


def project_back(order, gproj, normed, tok_all, wt):
    nb, rows, d = tok_all.shape
    n = gproj.shape[0]
    t = nb * rows
    return pl.pallas_call(
        project_back_kernel,
        grid_spec=pltpu.PrefetchScalarGridSpec(
            num_scalar_prefetch=1,
            grid=(nb,),
            in_specs=[
                pl.BlockSpec((n, rows), lambda i, o: (0, o[i])),
                pl.BlockSpec((rows, d), lambda i, o: (o[i], 0)),
                pl.BlockSpec((1, rows, d), lambda i, o: (o[i], 0, 0)),
                pl.BlockSpec((n, d), lambda i, o: (0, 0)),
            ],
            out_specs=(
                pl.BlockSpec((1, rows, d), lambda i, o: (i, 0, 0)),
                pl.BlockSpec((d, n), lambda i, o: (0, 0)),
                pl.BlockSpec((8, d), lambda i, o: (0, 0)),
            ),
            scratch_shapes=[pltpu.VMEM((n, d), F32)],
        ),
        out_shape=(sds((nb, rows, d), BF), sds((d, n), BF), sds((8, d), F32)),
        compiler_params=params(),
        cost_estimate=cost(4 * t * d * n, 14 * 2**20),
        name="project_back",
    )(order, gproj, normed, tok_all, wt)


def tokens_back(gn, tok, gain, gmid):
    hat, r = norm_rows(tok.astype(F32))
    e = gn * gain
    m1 = jnp.mean(e, axis=-1, keepdims=True)
    m2 = jnp.mean(e * hat, axis=-1, keepdims=True)
    return (gmid + (e - m1 - hat * m2) * r).astype(BF)


class Where:
    def __init__(self, nz):
        dp, mp = lax.axis_index("dp"), lax.axis_index("mp")
        z, y, x, c = dp // 2, dp % 2, mp // 2, mp % 2
        self.dp, self.mp, self.z, self.y, self.x, self.c = dp, mp, z, y, x, c
        self.xm, self.cm, self.dm = (1 - x) * 2 + c, x * 2 + 1 - c, (1 - x) * 2 + 1 - c
        self.ydp = z * 2 + 1 - y
        self.zfrom = [((z + nz - k) % nz) * 2 + y for k in range(nz)]
        self.yfrom = [((z + nz - k) % nz) * 2 + 1 - y for k in range(nz)]
        self.py, self.px, self.pc, self.pd = (self.ydp, mp), (dp, self.xm), (dp, self.cm), (dp, self.dm)
        self.pz = [None] + [(((z + k) % nz) * 2 + y, mp) for k in range(1, nz)]
        self.all = self.pz[1:] + [self.py, self.px, self.pc, self.pd]


class Sender:
    def __init__(self, ss, rs):
        self.ss, self.rs, self.n, self.open = ss, rs, 0, []

    def send(self, src, dst, peer):
        cp = rcopy(src, dst, self.ss.at[self.n], self.rs.at[self.n], peer)
        cp.start()
        self.n += 1
        self.open.append(cp)
        return cp

    def sent(self, cp):
        cp.wait_send()
        self.open = [o for o in self.open if o is not cp]

    def finish(self):
        for cp in self.open:
            cp.wait_send()


def vector_rows(vecv, small, d):
    nmp, ndp, vr, lanes = vecv.shape
    v = vecv[...].reshape(nmp * ndp * vr, lanes)
    parts = [p.astype(BF) for p in three(v)]
    lane = lax.broadcasted_iota(jnp.int32, (lanes, d), 1)
    sub = lax.broadcasted_iota(jnp.int32, (lanes, d), 0)
    s = lax.broadcasted_iota(jnp.int32, (nmp * ndp, vr, d), 0)
    col = lax.broadcasted_iota(jnp.int32, (nmp * ndp, vr, d), 2)
    dev = (s % ndp) * nmp + s // ndp

    def spread(width):
        sel = jnp.where(lane % width == sub, 1.0, 0.0).astype(BF)
        return sum(nn(p, sel) for p in parts).reshape(nmp * ndp, vr, d)

    a = jnp.sum(jnp.where(col // small == dev, spread(small), 0.0), axis=0)
    wide = nmp * small
    b = spread(wide)
    per = nmp * ndp // nmp
    ups = []
    for m in range(nmp):
        keep = (dev // per == m) & (col // wide == dev % per)
        ups.append(jnp.sum(jnp.where(keep, b, 0.0), axis=0)[8:9])
    return a[0:8], jnp.concatenate(ups, axis=0)


def front_kernel(nz, heads, small, *refs):
    tok, wq, wo, wup, wdn, vec, cot, ids = refs[:8]
    normed_o, raw_o, wu_o, wd_o, cotx_o, tok_o = refs[8:14]
    low_o, wt_o, wotv, att_o, lse, own_o, rows_o, gains, mid_o, n2_o, n2x_o = refs[14:25]
    tokv, wqv, wov, vecv, normv, rawv, qa, ka, va, acc, ss, rs, ls = refs[25:]
    w = Where(nz)
    dp, mp = w.dp, w.mp
    cols = heads * HEAD
    t, d = normv.shape
    nmp, rows = tokv.shape[0], tokv.shape[1]
    greet(w.all)
    tx = Sender(ss, rs)
    count, late = [0], []

    def keep(src, dst, wait_late=True):
        cp = pltpu.make_async_copy(src, dst, ls.at[count[0]])
        cp.start()
        count[0] += 1
        if wait_late:
            late.append(cp)
        return cp

    nc = 4
    part = [pl.ds(i * (rows // nc), rows // nc) for i in range(nc)]
    vz = [None] + [tx.send(vec, vecv.at[mp, dp], w.pz[k]) for k in range(1, nz)]
    vy = [tx.send(vec, vecv.at[mp, dp], w.py)]
    xt = [tx.send(tok.at[part[i]], tokv.at[mp, part[i]], w.px) for i in range(nc)]
    qz = [None] + [tx.send(wq, wqv.at[dp], w.pz[k]) for k in range(1, nz)]
    qy = [tx.send(wq, wqv.at[dp], w.py)]
    ctok = tx.send(tok, tokv.at[mp], w.pc)
    dx = tx.send(wdn, wd_o.at[1, dp], w.px)
    cx = tx.send(cot, cotx_o, w.pc)
    first = [
        keep(vec, vecv.at[mp, dp], False),
        keep(tok, tokv.at[mp], False),
        keep(wq, wqv.at[dp], False),
        keep(wo, wov.at[dp], False),
    ]
    keep(wup, wu_o.at[0, dp])
    keep(wdn, wd_o.at[0, dp])
    for k in range(1, nz):
        vz[k].wait_recv()
        ref = vecv.at[mp, w.zfrom[k]]
        vy.append(tx.send(ref, ref, w.py))
    for k in range(nz):
        vy[k].wait_recv()
    for cp in first:
        cp.wait()
    vx = tx.send(vecv.at[mp], vecv.at[mp], w.px)
    vc = tx.send(vecv.at[mp], vecv.at[mp], w.pc)
    for k in range(1, nz):
        qz[k].wait_recv()
        ref = wqv.at[w.zfrom[k]]
        qy.append(tx.send(ref, ref, w.py))
    oz = [None] + [tx.send(wo, wov.at[dp], w.pz[k]) for k in range(1, nz)]
    oy = [tx.send(wo, wov.at[dp], w.py)]
    uz = [None] + [tx.send(wup, wu_o.at[0, dp], w.pz[k]) for k in range(1, nz)]
    dz = [None] + [tx.send(wdn, wd_o.at[0, dp], w.pz[k]) for k in range(1, nz)]
    uy = [tx.send(wup, wu_o.at[0, dp], w.py)]
    vx.wait_recv()
    vd = tx.send(vecv.at[w.xm], vecv.at[w.xm], w.pc)
    ct = []

    def forward(i):
        xt[i].wait_recv()
        ref = tokv.at[w.xm, part[i]]
        ct.append(tx.send(ref, ref, w.pc))

    forward(0)
    forward(1)
    vc.wait_recv()
    vd.wait_recv()
    main, ups = vector_rows(vecv, small, d)
    rows_o[0:8, :] = main
    rows_o[8:12, :] = ups
    rows_o[12:16, :] = jnp.zeros((4, d), F32)
    lane = lax.broadcasted_iota(jnp.int32, (cols, d), 1)
    pick = lane == lax.broadcasted_iota(jnp.int32, (cols, d), 0) + mp * cols
    for i in range(2):
        gains[i * cols : (i + 1) * cols, :] = jnp.sum(
            jnp.where(pick, main[2 + i : 3 + i], 0.0), axis=1, keepdims=True
        )
    for k in range(nz):
        qy[k].wait_recv()
    wt_o[...] = wqv[...].reshape(d, 3 * cols).T
    one = jnp.where(lax.broadcasted_iota(jnp.int32, (16, rows), 0) == 0, 1.0, 0.0).astype(BF)

    def project(m):
        ts = pl.ds(pl.multiple_of(m * rows, rows), rows)
        hat, _ = norm_rows(tokv[m].astype(F32))
        n = (hat * rows_o[0:1, :] + rows_o[1:2, :]).astype(BF)
        normv[ts, :] = n
        proj = nt(wt_o[...], n)
        rawv[:, ts] = proj[0 : 2 * cols]
        _, mq, mk = masks(ids[:, ts])
        mq, mk = mq.astype(BF), mk.astype(BF)
        for h in range(heads):
            qs, ks = h * HEAD, cols + h * HEAD
            hat, _ = norm_cols(proj[qs : qs + HEAD])
            q = (hat * gains[qs : qs + HEAD, :]).astype(BF)
            low_o[qs : qs + HEAD, ts] = q
            qa[h, 0:HEAD, ts] = q
            qa[h, HEAD:, ts] = mq
            hat, _ = norm_cols(proj[ks : ks + HEAD])
            k = (hat * gains[ks : ks + HEAD, :]).astype(BF)
            low_o[ks : ks + HEAD, ts] = k
            ka[h, ts, :] = jnp.concatenate([k, mk], axis=0).T
            v = proj[2 * cols + h * HEAD : 2 * cols + (h + 1) * HEAD].astype(BF)
            low_o[2 * cols + h * HEAD : 2 * cols + (h + 1) * HEAD, ts] = v
            va[h, 0:HEAD, ts] = v
            va[h, HEAD:, ts] = one

    project(mp)
    forward(2)
    ctok.wait_recv()
    project(w.cm)
    forward(3)
    project(w.xm)
    for cp in ct:
        cp.wait_recv()
    project(w.dm)
    keep(normv, normed_o)
    keep(rawv, raw_o)
    keep(tokv, tok_o)
    dx.wait_recv()
    ref = wd_o.at[1, dp]
    ez = [None] + [tx.send(ref, ref, w.pz[k]) for k in range(1, nz)]
    for k in range(1, nz):
        oz[k].wait_recv()
        ref = wov.at[w.zfrom[k]]
        oy.append(tx.send(ref, ref, w.py))
    ux, dy = [tx.send(wup, wu_o.at[1, dp], w.px)], [tx.send(wdn, wd_o.at[0, dp], w.py)]

    def attend_row(i):
        qi = pl.ds(pl.multiple_of(i * rows, rows), rows)
        acc[...] = jnp.zeros_like(acc)

        def tile(j, _):
            kj = pl.ds(pl.multiple_of(j * rows, rows), rows)
            s = [nn(ka[h, kj, :], qa[h, :, qi]) for h in range(heads)]
            p = [jnp.exp2(v * (SCALE * LOG2E)).astype(BF) for v in s]
            for h in range(heads):
                acc[h] += nn(va[h, :, kj], p[h])
            return 0

        lax.fori_loop(jnp.maximum(i - 2, 0), jnp.minimum(i + 3, nmp), tile, 0)
        pad = ids[:, qi] < 0
        lse[:, qi] = jnp.zeros((8, rows), F32)
        for h in range(heads):
            total = jnp.where(pad, 1.0, acc[h, HEAD : HEAD + 1, :])
            value = va[h, 0:HEAD, qi].astype(F32)
            o = jnp.where(pad, value, acc[h, 0:HEAD, :] * (1.0 / total))
            att_o[h * HEAD : (h + 1) * HEAD, qi] = o.astype(BF)
            lse[h : h + 1, qi] = jnp.log(total)
        return att_o.at[:, qi]

    at = [tx.send(attend_row(w.xm), own_o.at[mp], w.px)]
    for k in range(nz):
        oy[k].wait_recv()
    wotv[mp] = wov[...].reshape(d, cols).T
    ox = tx.send(wotv.at[mp], wotv.at[mp], w.px)
    oc = tx.send(wotv.at[mp], wotv.at[mp], w.pc)
    at.append(tx.send(attend_row(w.dm), own_o.at[mp], w.pd))
    for k in range(1, nz):
        uz[k].wait_recv()
        ref = wu_o.at[0, w.zfrom[k]]
        uy.append(tx.send(ref, ref, w.py))
        ux.append(tx.send(ref, wu_o.at[1, w.zfrom[k]], w.px))
    at.append(tx.send(attend_row(w.cm), own_o.at[mp], w.pc))
    for k in range(1, nz):
        dz[k].wait_recv()
        ref = wd_o.at[0, w.zfrom[k]]
        dy.append(tx.send(ref, ref, w.py))
    own = attend_row(mp)
    keep(own, own_o.at[mp], False).wait()
    ox.wait_recv()
    od = tx.send(wotv.at[w.xm], wotv.at[w.xm], w.pc)
    ey = [tx.send(wd_o.at[1, dp], wd_o.at[1, dp], w.py)]
    for k in range(1, nz):
        ez[k].wait_recv()
        ref = wd_o.at[1, w.zfrom[k]]
        ey.append(tx.send(ref, ref, w.py))
    uw = []
    for k in range(nz):
        uy[k].wait_recv()
        ref = wu_o.at[0, w.yfrom[k]]
        uw.append(tx.send(ref, wu_o.at[1, w.yfrom[k]], w.px))
    oc.wait_recv()
    od.wait_recv()
    for cp in at:
        cp.wait_recv()
    m = tokv[mp].astype(F32) + rows_o[4:5, :]
    m = m + tn(own_o[...].reshape(d, rows), wotv[...].reshape(d, d))
    mid_o[...] = m
    hat, _ = norm_rows(m)
    n2_o[...] = (hat * rows_o[5:6, :] + rows_o[6:7, :]).astype(BF)
    nx = tx.send(n2_o, n2x_o, w.pc)
    nx.wait_recv()
    cx.wait_recv()
    for cp in ux + dy + ey + uw:
        cp.wait_recv()
    tx.finish()
    for cp in late:
        cp.wait()


def front(tok, wq, wo, wup, wdn, vec, cot, ids, ndp, nmp, small):
    rows, d = tok.shape
    drow, unit, cols = wup.shape[0], wup.shape[1], wo.shape[1]
    heads, t, nsend, nlocal = cols // HEAD, rows * nmp, 80, 12
    dma, vm = pltpu.SemaphoreType.DMA, pltpu.VMEM
    return pl.pallas_call(
        functools.partial(front_kernel, ndp // 2, heads, small),
        out_shape=(
            sds((t, d), BF),
            sds((2 * cols, t), F32),
            sds((2, ndp, drow, unit), BF),
            sds((2, ndp, drow, unit), BF),
            sds((rows, d), BF),
            sds((nmp, rows, d), BF),
            sds((3 * cols, t), BF),
            sds((3 * cols, d), BF),
            sds((nmp, cols, d), BF),
            sds((cols, t), BF),
            sds((8, t), F32),
            sds((nmp, cols, rows), BF),
            sds((16, d), F32),
            sds((2 * cols, 1), F32),
            sds((rows, d), F32),
            sds((rows, d), BF),
            sds((rows, d), BF),
        ),
        in_specs=[ANY] * 7 + [VM],
        out_specs=(ANY,) * 6 + (VM,) * 11,
        scratch_shapes=[
            vm((nmp, rows, d), BF),
            vm((ndp, drow, 3 * cols), BF),
            vm((ndp, drow, cols), BF),
            vm((nmp, ndp) + vec.shape, F32),
            vm((t, d), BF),
            vm((2 * cols, t), F32),
            vm((heads, 2 * HEAD, t), BF),
            vm((heads, t, 2 * HEAD), BF),
            vm((heads, HEAD + 16, t), BF),
            vm((heads, HEAD + 16, rows), F32),
            dma((nsend,)),
            dma((nsend,)),
            dma((nlocal,)),
        ],
        compiler_params=params(collective_id=4, has_side_effects=True),
        cost_estimate=cost(20e9, 40 * 2**20),
        name="front",
    )(tok, wq, wo, wup, wdn, vec, cot, ids)


def three_sum(m, sel):
    return sum(nn(p.astype(BF), sel) for p in three(m))


def pack_vectors(main, gb0, gb1, w, small, vt):
    nmp, nz = vt.shape[0], vt.shape[1]
    n, d = nmp * nz * 2, main.shape[1]
    s = lax.broadcasted_iota(jnp.int32, (n, 8, d), 0)
    v = lax.broadcasted_iota(jnp.int32, (n, 8, d), 1)
    l = lax.broadcasted_iota(jnp.int32, (n, 8, d), 2)
    per = n // nmp
    dev = (s % per) * nmp + s // per
    sub = lax.broadcasted_iota(jnp.int32, (d, 128), 0)
    lane = lax.broadcasted_iota(jnp.int32, (d, 128), 1)
    m = jnp.where(l // small == dev, main[None], 0.0).reshape(n * 8, d)
    sel = jnp.where(sub % small == lane, 1.0, 0.0).astype(BF)
    a = three_sum(m, sel).reshape(n, 8, 128)
    wide = nmp * small
    here = (l // wide == dev % per) & (v == 0)
    m = jnp.where(here & (dev // per == w.mp), gb0[None], 0.0)
    m = m + jnp.where(here & (dev // per == w.xm), gb1[None], 0.0)
    sel = jnp.where(sub % wide == lane, 1.0, 0.0).astype(BF)
    b = three_sum(m.reshape(n * 8, d), sel).reshape(n, 8, 128)
    vt[...] = jnp.concatenate([a, b], axis=1).reshape(vt.shape)


def back_kernel(nz, heads, small, *refs):
    g_own, g_send, o_own, o_send, mid, cot, att_own, wot, wt, low = refs[:10]
    att, raw, normed, tok_all, dwu, dwd, lse, rowv, gains, ids, gbias = refs[10:21]
    res_o, gtok_o, gq_o, go_o, gu_o, gd_o, vec_o = refs[21:28]
    (
        f1, f2, f3, ggot, ogot, cotv, attov, wotv, wtv, lowv, attv, rawv, dwdv,
        rxu, ryu, ru, rzu, ryd, rzd, rd, rxd, gattv, doutv, gwov, rco, go2, rxo, gov, ryo, ro, rzo,
        gprojv, qa, ka, va, da, dk, dv, dqa, tokv, normv, acc, gnv, rgc, rgx, dwqv, ryq, rq, rzq, sumv, ggv, vt, rv1, rv2, rv3, va4, rv4,
        ss, rs, ls,
    ) = refs[28:]
    w = Where(nz)
    dp, mp, z, y = w.dp, w.mp, w.z, w.y
    cols = heads * HEAD
    t = lowv.shape[1]
    rows, d = f1.shape
    nmp = t // rows
    greet(w.all)
    tx = Sender(ss, rs)
    count = [0]
    zto = [(z + k) % nz for k in range(nz)]

    def load(src, dst):
        cp = pltpu.make_async_copy(src, dst, ls.at[count[0]])
        cp.start()
        count[0] += 1
        return cp

    gx = tx.send(g_send, ggot, w.pc)
    l1 = [load(g_own, f1), load(mid, f2), load(cot, cotv), load(wot, wotv)]
    l2 = [load(o_own, f3), load(att_own, attov), load(low, lowv), load(att, attv)]
    ox = tx.send(o_send, ogot, w.pc)
    dy = tx.send(dwd.at[:, :, 1 - y], ryd, w.py)
    ux = [tx.send(dwu.at[1, 0], rxu.at[0], w.px)]
    l3 = [load(wt, wtv), load(raw, rawv)]
    l4 = load(dwd.at[:, :, y], dwdv)

    for cp in l1:
        cp.wait()
    gx.wait_recv()
    gy = cotv[...].astype(F32)
    g = f1[...] + ggot[...].astype(F32)
    hat, r = norm_rows(f2[...])
    e = g * rowv[5:6, :]
    m1 = jnp.mean(e, axis=-1, keepdims=True)
    m2 = jnp.mean(e * hat, axis=-1, keepdims=True)
    gm = gy + (e - m1 - hat * m2) * r
    sumv[...] = jnp.zeros_like(sumv)
    for k, v in enumerate((gm, g * hat, g, gy)):
        sumv[4 + k : 5 + k, :] = jnp.sum(v, axis=0, keepdims=True)
    f1[...] = gm
    gmb = gm.astype(BF)
    gattv[...] = nt(wotv[...], gmb).astype(BF).reshape(nmp, cols, rows)

    def block(m):
        return pl.ds(pl.multiple_of(m * rows, rows), rows)

    ax = tx.send(gattv.at[w.xm], doutv.at[:, block(mp)], w.px)
    ad = tx.send(gattv.at[w.dm], doutv.at[:, block(mp)], w.pd)
    ac = tx.send(gattv.at[w.cm], doutv.at[:, block(mp)], w.pc)
    ux += [tx.send(dwu.at[1, k], rxu.at[k], w.px) for k in range(1, nz)]
    own = load(gattv.at[mp], doutv.at[:, block(mp)])
    for cp in l2:
        cp.wait()
    ox.wait_recv()
    res_o[...] = (f2[...] + f3[...] + ogot[...].astype(F32) + rowv[7:8, :]).astype(BF)
    gw = nt(gm.T.astype(BF), attov[...]).astype(BF)
    for m in range(nmp):
        gwov[m] = gw[:, m * cols : (m + 1) * cols].reshape(gwov.shape[1:])
    oc = [tx.send(gwov.at[w.cm], rco.at[0], w.pc), tx.send(gwov.at[w.dm], rco.at[1], w.pc)]
    for cp in l3:
        cp.wait()
    ggv[...] = jnp.zeros_like(ggv)

    def attention(qa, ka, va, da, dk, dv):
        def build(m, _):
            ts = block(m)
            r, _, mk = masks(ids[:, ts])
            mk = mk.astype(BF)
            one = jnp.where(r < 3, 1.0, 0.0).astype(BF)
            for h in range(heads):
                k = lowv[cols + h * HEAD : cols + (h + 1) * HEAD, ts]
                ka[h, ts, :] = jnp.concatenate([k, mk], axis=0).T
                v = lowv[2 * cols + h * HEAD : 2 * cols + (h + 1) * HEAD, ts]
                va[h, ts, :] = jnp.concatenate([v, one], axis=0).T
            return 0

        lax.fori_loop(0, nmp, build, 0)
        dk[...] = jnp.zeros_like(dk)
        dv[...] = jnp.zeros_like(dv)

        def row(i):
            qi = block(i)
            r, mq, _ = masks(ids[:, qi])
            for h in range(heads):
                hs = slice(h * HEAD, (h + 1) * HEAD)
                qa[h, 0:HEAD, :] = lowv[hs, qi]
                a, b, c = three(lse[h : h + 1, qi] * (-1.0 / SCALE))
                aug = jnp.where(r == 32, a, jnp.where(r == 33, b, jnp.where(r == 34, c, mq)))
                qa[h, HEAD:, :] = aug.astype(BF)
                do = doutv[hs, qi]
                delta = jnp.sum(do.astype(F32) * attv[hs, qi].astype(F32), axis=0, keepdims=True)
                a, b, c = three(-delta)
                da[h, 0:HEAD, :] = do
                da[h, HEAD:, :] = jnp.where(
                    r == 0, a, jnp.where(r == 1, b, jnp.where(r == 2, c, 0.0))
                ).astype(BF)
            dqa[...] = jnp.zeros_like(dqa)

            def tile(j, _):
                kj = block(j)
                s = [nn(ka[h, kj, :], qa[h]) for h in range(heads)]
                e = [nn(va[h, kj, :], da[h]) for h in range(heads)]
                p = [jnp.exp2(v * (SCALE * LOG2E)) for v in s]
                ds = [(p[h] * e[h]).astype(BF) for h in range(heads)]
                for h in range(heads):
                    hs = slice(h * HEAD, (h + 1) * HEAD)
                    dv[hs, kj] += nt(da[h, 0:HEAD, :], p[h].astype(BF))
                    dk[hs, kj] += nt(lowv[hs, qi], ds[h])
                    dqa[hs, :] += nn(lowv[cols + h * HEAD : cols + (h + 1) * HEAD, kj], ds[h])
                return 0

            lax.fori_loop(jnp.maximum(i - 2, 0), jnp.minimum(i + 3, nmp), tile, 0)
            for h in range(heads):
                hs = slice(h * HEAD, (h + 1) * HEAD)
                v, gg = head_back(rawv[hs, qi], gains[hs, :], dqa[hs, :] * SCALE)
                gprojv[hs, qi] = v.astype(BF)
                ggv[hs, :] += gg

        own.wait()
        row(mp)
        for cp in oc:
            cp.wait_recv()
        go2[...] = (gwov[w.xm].astype(F32) + rco[1].astype(F32)).astype(BF)
        oxx = tx.send(go2, rxo, w.px)
        ac.wait_recv()
        row(w.cm)
        l4.wait()
        dy.wait_recv()
        for k in range(2):
            ryd[k] = (ryd[k].astype(F32) + dwdv[k].astype(F32)).astype(BF)
        l9 = [load(dwu.at[0, k], dwdv.at[:, k]) for k in range(nz)]
        dz = [tx.send(ryd.at[:, zto[k]], rzd.at[k - 1], w.pz[k]) for k in range(1, nz)]
        ax.wait_recv()
        row(w.xm)
        for cp in ux:
            cp.wait_recv()
        for cp in l9:
            cp.wait()
        for k in range(nz):
            rxu[k] = (rxu[k].astype(F32) + dwdv[:, k].astype(F32)).astype(BF)
        uy = tx.send(rxu.at[:, 1 - y], ryu, w.py)
        ad.wait_recv()
        row(w.dm)
        oxx.wait_recv()
        gov[...] = (gwov[mp].astype(F32) + rco[0].astype(F32) + rxo[...].astype(F32)).astype(BF)
        oy = tx.send(gov.at[:, 1 - y], ryo, w.py)

        def keys(m, _):
            ts = block(m)
            pad = ids[:, ts] < 0
            for h in range(heads):
                hs = slice(h * HEAD, (h + 1) * HEAD)
                ps = slice(cols + h * HEAD, cols + (h + 1) * HEAD)
                v, gg = head_back(rawv[ps, ts], gains[ps, :], dk[hs, ts] * SCALE)
                gprojv[ps, ts] = v.astype(BF)
                ggv[ps, :] += gg
                v = dv[hs, ts] + jnp.where(pad, doutv[hs, ts].astype(F32), 0.0)
                gprojv[2 * cols + h * HEAD : 2 * cols + (h + 1) * HEAD, ts] = v.astype(BF)
            return 0

        lax.fori_loop(0, nmp, keys, 0)
        return dz, uy, oy

    dz, uy, oy = attention(qa, ka, va, da, dk, dv)

    def projections(tokv, normv, acc):
        acc[...] = jnp.zeros_like(acc)

        def part(m):
            return tn(gprojv[:, block(m)], wtv[...])

        def fetch(n, m):
            return load(normed.at[block(m), :], normv.at[n % 2]), load(tok_all.at[m], tokv.at[n % 2])

        def rest(n, m, g, copies):
            for cp in copies:
                cp.wait()
            acc[...] += nn(gprojv[:, block(m)], normv[n % 2])
            hat, _ = norm_rows(tokv[n % 2].astype(F32))
            sumv[0:1, :] += jnp.sum(g * hat, axis=0, keepdims=True)
            sumv[1:2, :] += jnp.sum(g, axis=0, keepdims=True)

        l5, l6 = fetch(0, w.dm), fetch(1, w.xm)
        g = part(w.dm)
        gnv[0] = g.astype(BF)
        c1 = tx.send(gnv.at[0], rgc.at[1], w.pc)
        f2[...] = part(w.xm)
        c1.wait_recv()
        gnv[1] = (f2[...] + rgc[1].astype(F32)).astype(BF)
        gxx = tx.send(gnv.at[1], rgx, w.px)
        rest(0, w.dm, g, l5)
        l7 = fetch(2, w.cm)
        rest(1, w.xm, f2[...], l6)
        l8 = fetch(3, mp)
        g = part(w.cm)
        tx.sent(c1)
        gnv[0] = g.astype(BF)
        c2 = tx.send(gnv.at[0], rgc.at[0], w.pc)
        rest(2, w.cm, g, l7)
        f2[...] = part(mp)
        rest(3, mp, f2[...], l8)
        dwqv[...] = acc[...].T.astype(BF).reshape(dwqv.shape)
        qy = tx.send(dwqv.at[:, 1 - y], ryq, w.py)
        lane = lax.broadcasted_iota(jnp.int32, (cols, d), 1)
        pick = lane == lax.broadcasted_iota(jnp.int32, (cols, d), 0) + mp * cols
        for i in range(2):
            v = jnp.where(pick, ggv[i * cols : (i + 1) * cols, :], 0.0)
            sumv[2 + i : 3 + i, :] = jnp.sum(v, axis=0, keepdims=True)
        pack_vectors(sumv[...], gbias[0, 0:1, :], gbias[1, 0:1, :], w, small, vt)
        v1 = [tx.send(vt.at[w.cm], rv1.at[0], w.pc), tx.send(vt.at[w.dm], rv1.at[1], w.pc)]
        uy.wait_recv()
        ru[...] = (rxu[:, y].astype(F32) + ryu[...].astype(F32)).astype(BF)
        uz = [tx.send(ru.at[zto[k]], rzu.at[k - 1], w.pz[k]) for k in range(1, nz)]
        for cp in v1:
            cp.wait_recv()
        vt[w.xm] = vt[w.xm] + rv1[1]
        v2 = tx.send(vt.at[w.xm], rv2, w.px)
        oy.wait_recv()
        ro[...] = (gov[:, y].astype(F32) + ryo[...].astype(F32)).astype(BF)
        oz = [tx.send(ro.at[zto[k]], rzo.at[k - 1], w.pz[k]) for k in range(1, nz)]
        for cp in dz:
            cp.wait_recv()
        tot = ryd[:, z].astype(F32)
        for k in range(nz - 1):
            tot = tot + rzd[k].astype(F32)
        rd[...] = tot[1].astype(BF)
        dx = tx.send(rd, rxd, w.px)
        gd_o[...] = tot[0]
        qy.wait_recv()
        rq[...] = (dwqv[:, y].astype(F32) + ryq[...].astype(F32)).astype(BF)
        qz = [tx.send(rq.at[zto[k]], rzq.at[k - 1], w.pz[k]) for k in range(1, nz)]
        v2.wait_recv()
        vt[mp] = vt[mp] + rv1[0] + rv2[...]
        v3 = tx.send(vt.at[mp, :, 1 - y], rv3, w.py)
        c2.wait_recv()
        f2[...] += rgc[0].astype(F32)
        v3.wait_recv()
        va4[...] = vt[mp, :, y] + rv3[...]
        v4 = [tx.send(va4.at[zto[k]], rv4.at[k - 1], w.pz[k]) for k in range(1, nz)]

        def last(copies, own, got, out):
            for cp in copies:
                cp.wait_recv()
            tot = own.astype(F32)
            for k in range(nz - 1):
                tot = tot + got[k].astype(F32)
            out[...] = tot

        last(uz, ru[z], rzu, gu_o)
        last(oz, ro[z], rzo, go_o)
        last(v4, va4[z], rv4, vec_o)
        dx.wait_recv()
        gd_o[...] += rxd[...].astype(F32)
        last(qz, rq[z], rzq, gq_o)
        gxx.wait_recv()
        g = f2[...] + rgx[...].astype(F32)
        hat, r = norm_rows(tokv[1].astype(F32))
        e = g * rowv[0:1, :]
        m1 = jnp.mean(e, axis=-1, keepdims=True)
        m2 = jnp.mean(e * hat, axis=-1, keepdims=True)
        gtok_o[...] = (f1[...] + (e - m1 - hat * m2) * r).astype(BF)

    projections(tokv, normv, acc)
    tx.finish()


def back(hbm, small_in, nz, heads, small):
    g_own, dwu = hbm[0], hbm[14]
    rows, d = g_own.shape
    drow, unit = dwu.shape[3], dwu.shape[4]
    cols = heads * HEAD
    nmp = d // cols
    t = nmp * rows
    v = pltpu.VMEM
    dma = pltpu.SemaphoreType.DMA
    scratch = [
        v((rows, d), F32), v((rows, d), F32), v((rows, d), F32),
        v((rows, d), BF), v((rows, d), BF), v((rows, d), BF), v((d, rows), BF), v((d, d), BF),
        v((3 * cols, d), BF), v((3 * cols, t), BF), v((cols, t), BF), v((2 * cols, t), F32),
        v((2, nz, drow, unit), BF),
        v((nz, 2, drow, unit), BF), v((nz, drow, unit), BF), v((nz, drow, unit), BF), v((nz - 1, drow, unit), BF),
        v((2, nz, drow, unit), BF), v((nz - 1, 2, drow, unit), BF), v((drow, unit), BF), v((drow, unit), BF),
        v((nmp, cols, rows), BF), v((cols, t), BF),
        v((nmp, nz, 2, drow, cols), BF), v((2, nz, 2, drow, cols), BF), v((nz, 2, drow, cols), BF),
        v((nz, 2, drow, cols), BF), v((nz, 2, drow, cols), BF),
        v((nz, drow, cols), BF), v((nz, drow, cols), BF), v((nz - 1, drow, cols), BF),
        v((3 * cols, t), BF),
        v((heads, 2 * HEAD, rows), BF), v((heads, t, 2 * HEAD), BF), v((heads, t, 2 * HEAD), BF),
        v((heads, 2 * HEAD, rows), BF), v((cols, t), F32), v((cols, t), F32), v((cols, rows), F32),
        v((2, rows, d), BF), v((2, rows, d), BF), v((3 * cols, d), F32),
        v((2, rows, d), BF), v((2, rows, d), BF), v((rows, d), BF),
        v((nz, 2, drow, 3 * cols), BF), v((nz, drow, 3 * cols), BF), v((nz, drow, 3 * cols), BF),
        v((nz - 1, drow, 3 * cols), BF),
        v((8, d), F32), v((2 * cols, 1), F32),
        v((nmp, nz, 2, 16, 128), F32), v((2, nz, 2, 16, 128), F32), v((nz, 2, 16, 128), F32),
        v((nz, 16, 128), F32), v((nz, 16, 128), F32), v((nz - 1, 16, 128), F32),
        dma((64,)), dma((64,)), dma((24,)),
    ]
    return pl.pallas_call(
        functools.partial(back_kernel, nz, heads, small),
        out_shape=(
            sds((rows, d), BF),
            sds((rows, d), BF),
            sds((drow, 3 * cols), F32),
            sds((drow, cols), F32),
            sds((drow, unit), F32),
            sds((drow, unit), F32),
            sds((16, 128), F32),
        ),
        in_specs=[ANY] * len(hbm) + [VM] * len(small_in),
        out_specs=(VM,) * 7,
        scratch_shapes=scratch,
        compiler_params=params(collective_id=5, has_side_effects=True),
        cost_estimate=cost(40e9, 60 * 2**20),
        name="back",
    )(*hbm, *small_in)


def spans(ids):
    b = ids.reshape(-1, TB)
    low = jnp.min(jnp.where(b < 0, 1000, b), axis=1)
    high = jnp.max(b, axis=1)
    n = b.shape[0]
    k = jnp.arange(n)
    lo = jnp.sum((high[None, :] < low[:, None]) & (k[None, :] <= k[:, None]), axis=1)
    hi = jnp.sum(low[None, :] <= high[:, None], axis=1)
    return jnp.concatenate([lo, hi]).astype(jnp.int32)


def solution(mesh):
    ndp, nmp = mesh.shape["dp"], mesh.shape["mp"]
    ndev, nz = ndp * nmp, ndp // 2

    def permute(v, kind, k=0):
        pairs = []
        for d in range(ndp):
            for m in range(nmp):
                z, y, x, c = d // 2, d % 2, m // 2, m % 2
                if kind == "core":
                    c = 1 - c
                if kind == "x":
                    x = 1 - x
                if kind == "y":
                    y = 1 - y
                if kind == "z":
                    z = (z + k) % nz
                pairs.append((d * nmp + m, (z * 2 + y) * nmp + x * 2 + c))
        return lax.ppermute(v, ("dp", "mp"), pairs)

    def columns(w, first, second):
        if w.shape[0] % 16:
            own = lax.all_gather(w, "dp", axis=0, tiled=True)[None]
            return [own, permute(own, "x")]
        s = jnp.stack([w] + [permute(w, "z", k) for k in range(1, nz)])
        got = {(0, 0): s}
        one = permute(s, first)
        two = permute(s, second)
        both = permute(one, second)
        got[(0, 1)] = one if first == "y" else two
        got[(1, 0)] = two if first == "y" else one
        got[(1, 1)] = both
        return [got[(0, 0)], got[(0, 1)], got[(1, 0)], got[(1, 1)]]

    def body(
        tokens,
        picture_ids,
        w_qkv,
        w_out,
        w_up,
        w_down,
        ln1_gain,
        ln1_bias,
        q_gain,
        k_gain,
        out_bias,
        ln2_gain,
        ln2_bias,
        up_bias,
        down_bias,
        cotangent,
    ):
        rows, d = tokens.shape[1], tokens.shape[2]
        drow = w_qkv.shape[0]
        cols = w_qkv.shape[2]
        heads = cols // HEAD
        unit = w_up.shape[1]
        dp, mp = lax.axis_index("dp"), lax.axis_index("mp")
        z, y, x, c = dp // 2, dp % 2, mp // 2, mp % 2
        tok, cot = tokens[0], cotangent[0]
        ids = picture_ids
        span = spans(ids[0])
        whole = drow % 16 == 0 and ndev == 32

        vs = [ln1_gain, ln1_bias, q_gain, k_gain, out_bias, ln2_gain, ln2_bias, down_bias, up_bias]
        small = vs[0].shape[0]
        used = 8 * small + up_bias.shape[0]
        if whole:
            vec = jnp.stack([jnp.pad(v, (0, 128 - v.shape[0])) for v in vs])
            vec = jnp.pad(vec, ((0, 16 - len(vs)), (0, 0)))
            (
                normed,
                raw,
                wu,
                wd,
                cot_other,
                tok_all,
                low,
                wt,
                wot,
                att,
                lse,
                att_own,
                rowv,
                gains,
                mid,
                n2,
                n2_other,
            ) = front(
                tok, w_qkv.reshape(drow, 3 * cols), w_out, w_up, w_down, vec, cot, ids, ndp, nmp, small
            )
            att_own = att_own.reshape(d, rows)
            ups, downs = [wu.reshape(2, d, unit)], [wd.reshape(2, d, unit)]
            wos = (wot.reshape(d, d),)
            ubias = rowv[8:12]
            gain1, gain2, dbias = rowv[0:1], rowv[5:6], rowv[7:8]
        else:
            flat = jnp.concatenate(vs)
            vec = jnp.pad(flat, (0, 1024 - used)).reshape(8, 128)
            wcat = jnp.concatenate([w_qkv.reshape(drow, 3 * cols), w_out], axis=1)
            tok_all, w_all, vec_all = gather_all(tok, wcat, vec, ndp, nmp)
            vec_all = vec_all.reshape(nmp, ndp, 1024).transpose(1, 0, 2).reshape(ndev, 1024)
            gain1, shift1, qg, kg, obias, gain2, shift2, dbias = [
                vec_all[:, i * small : (i + 1) * small].reshape(1, d) for i in range(8)
            ]
            ubias = vec_all[:, 8 * small : used].reshape(nmp, unit)
            gains = jnp.concatenate(
                [
                    lax.dynamic_slice_in_dim(qg[0], mp * cols, cols),
                    lax.dynamic_slice_in_dim(kg[0], mp * cols, cols),
                ]
            ).reshape(2 * cols, 1)

            ups = columns(w_up, "y", "x")
            downs = columns(w_down, "x", "y")
            cot_other = permute(cot, "core")

            normed, raw, low, wt = project(
                tok_all, w_all.reshape(d, 3 * cols + w_out.shape[1]), gain1, shift1, gains, heads
            )
            wo0 = wt[3 * cols :]
            wo1 = permute(wo0, "x")
            wo2, wo3 = permute(wo0, "core"), permute(wo1, "core")
            wos = (wo0, wo1, wo2, wo3)
            att, lse = attend(span, low, ids, heads)
            att_own = swap(att, True, nmp, 1).reshape(d, rows)
            mid, n2 = middle_part(att_own, wos, tok, obias, gain2, shift2)
            n2_other = permute(n2, "core")
        o_own, o_send, g_own, g_send, dwu, dwd, gbias = feed(
            n2, n2_other, cot, cot_other, ubias, ups, downs, nz
        )
        if whole:
            shape = (2, nz, 2, drow, unit)
            res, gtok, gqw, gow, gup, gdn, vt = back(
                (g_own, g_send, o_own, o_send, mid, cot, att_own, wos[0], wt, low)
                + (att, raw, normed, tok_all, dwu.reshape(shape), dwd.reshape(shape)),
                (lse, rowv, gains, ids, gbias),
                nz,
                heads,
                small,
            )
            vg = [vt[i, :small] for i in range(8)] + [vt[8, : nmp * small]]
            return (
                res[None],
                gtok[None],
                gqw.reshape(drow, 3, cols),
                gow,
                gup,
                gdn,
                *vg[:7],
                vg[8],
                vg[7],
            )
        g_got = permute(g_send, "core")
        gmid, gatt, gwo, sums2 = middle_back(g_own, g_got, mid, cot, att_own, wos, gain2, nmp)
        o_got = permute(o_send, "core")
        result = (mid + o_own + o_got.astype(F32) + dbias).astype(BF)
        dout = swap(gatt, False, nmp, 2)
        gproj, ggain = attend_back(span, low, raw, att, lse, dout, ids, gains, heads)
        order = jnp.stack([mp, x * 2 + 1 - c, (1 - x) * 2 + c, (1 - x) * 2 + 1 - c]).astype(jnp.int32)
        gn, gwq, sums1 = project_back(order, gproj, normed, tok_all, wt[: 3 * cols])
        got = permute(gn[1::2], "core")
        mine = gn[0::2].astype(F32) + got.astype(F32)
        far = permute(mine[1].astype(BF), "x")
        gnormed = mine[0] + far.astype(F32)
        grad_tokens = tokens_back(gnormed, tok, gain1, gmid)

        def pick(v, i):
            return lax.dynamic_index_in_dim(v, i, 0, keepdims=False)

        def along(v, kind):
            i = {"x": None, "y": y}[kind]
            if i is None:
                keep, send = v[0], v[1]
            else:
                keep, send = pick(v, i), pick(v, 1 - i)
            return (keep.astype(F32) + permute(send, kind).astype(F32)).astype(BF)

        def along_z(v):
            total = pick(v, z).astype(F32)
            for k in range(1, nz):
                total = total + permute(pick(v, (z + k) % nz), "z", k).astype(F32)
            return total

        def over_dp(v):
            if drow % 16:
                return lax.psum_scatter(v.astype(F32), "dp", scatter_dimension=0, tiled=True)
            v = v.reshape(nz, 2, drow, v.shape[-1]).transpose(1, 0, 2, 3)
            return along_z(along(v, "y"))

        def reduce_columns(v, y_first):
            if drow % 16 or not y_first:
                return over_dp(along(v, "x"))
            v = v.reshape(2, nz, 2, drow, unit).transpose(2, 0, 1, 3, 4)
            return along_z(along(along(v, "y"), "x"))

        grad_up = reduce_columns(dwu, False)
        grad_down = reduce_columns(dwd, True)
        mine_o = jnp.stack([pick(gwo, mp), pick(gwo, (1 - x) * 2 + c)])
        send_o = jnp.stack([pick(gwo, x * 2 + 1 - c), pick(gwo, (1 - x) * 2 + 1 - c)])
        go = (mine_o.astype(F32) + permute(send_o, "core").astype(F32)).astype(BF)
        go = along(go, "x")
        grad_att = over_dp(jnp.concatenate([gwq, go], axis=1))

        def spread(v, at, size):
            return lax.dynamic_update_slice_in_dim(jnp.zeros((size,), F32), v, at, 0)

        gq = spread(ggain[:cols, 0], mp * cols, d)
        gk = spread(ggain[cols:, 0], mp * cols, d)
        gb = spread(gbias[0, 0], mp * unit, nmp * unit)
        gb = gb + spread(gbias[1, 0], ((1 - x) * 2 + c) * unit, nmp * unit)
        eight = jnp.stack([sums1[0], sums1[1], gq, gk, sums2[0], sums2[1], sums2[2], sums2[3]])
        parts = jnp.concatenate(
            [
                eight.reshape(8, ndev, small).transpose(1, 0, 2).reshape(ndev, 8 * small),
                gb.reshape(ndev, used - 8 * small),
            ],
            axis=1,
        )
        parts = jnp.pad(parts, ((0, 0), (0, 1024 - used))).reshape(ndev, 8, 128)
        tot = vector_sums(parts, ndp, nmp).reshape(1024)
        vgrads = [tot[i * small : (i + 1) * small] for i in range(8)] + [tot[8 * small : used]]

        return (
            result[None],
            grad_tokens[None],
            grad_att[:, : 3 * cols].reshape(drow, 3, cols),
            grad_att[:, 3 * cols :],
            grad_up,
            grad_down,
            vgrads[0],
            vgrads[1],
            vgrads[2],
            vgrads[3],
            vgrads[4],
            vgrads[5],
            vgrads[6],
            vgrads[8],
            vgrads[7],
        )

    vec_spec = P(("dp", "mp"))
    return jax.shard_map(
        body,
        mesh=mesh,
        in_specs=(
            P("dp", "mp", None),
            P("dp", None),
            P("dp", None, "mp"),
            P("dp", "mp"),
            P("dp", "mp"),
            P("dp", "mp"),
        )
        + (vec_spec,) * 9
        + (P("dp", "mp", None),),
        out_specs=(
            P("dp", "mp", None),
            P("dp", "mp", None),
            P("dp", None, "mp"),
            P("dp", "mp"),
            P("dp", "mp"),
            P("dp", "mp"),
        )
        + (vec_spec,) * 9,
        check_vma=False,
    )
```

```python
import functools

import jax
import jax.numpy as jnp
from jax import lax
from jax.experimental import pallas as pl
from jax.experimental.pallas import tpu as pltpu
from jax.sharding import PartitionSpec as P

F32 = jnp.float32
BF = jnp.bfloat16
HEAD = 64
EPS = 1e-06
TB = 512
BIG = 32768.0
LOG2E = 1.4426950408889634
MESH = pl.DeviceIdType.MESH
ANY = pl.BlockSpec(memory_space=pl.ANY)
VM = pl.BlockSpec(memory_space=pltpu.VMEM)
SM = pl.BlockSpec(memory_space=pltpu.SMEM)
VLIM = 60 * 1024 * 1024


def nn(a, b):
    return lax.dot_general(a, b, (((1,), (0,)), ((), ())), preferred_element_type=F32)


def nt(a, b):
    return lax.dot_general(a, b, (((1,), (1,)), ((), ())), preferred_element_type=F32)


def tn(a, b):
    return lax.dot_general(a, b, (((0,), (0,)), ((), ())), preferred_element_type=F32)


def sds(shape, dtype):
    return jax.ShapeDtypeStruct(shape, dtype)


def params(**kw):
    return pltpu.CompilerParams(vmem_limit_bytes=VLIM, **kw)


def cost(flops, nbytes, trans=0):
    return pl.CostEstimate(flops=int(flops), bytes_accessed=int(nbytes), transcendentals=int(trans))


def rcopy(src, dst, ssem, rsem, peer):
    return pltpu.make_async_remote_copy(
        src_ref=src,
        dst_ref=dst,
        send_sem=ssem,
        recv_sem=rsem,
        device_id=peer,
        device_id_type=MESH,
    )


def greet(peers):
    bar = pltpu.get_barrier_semaphore()
    for p in peers:
        pl.semaphore_signal(bar, inc=1, device_id=p, device_id_type=MESH)
    pl.semaphore_wait(bar, len(peers))


def gather_kernel(
    nz, nc, tok, w, vec, tok_all, w_all, vec_all, loc, zs, zr, ys, yr, xs, xr, cs, cr, tx, rx, tc, rc
):
    dp, mp = lax.axis_index("dp"), lax.axis_index("mp")
    z, y, x, c = dp // 2, dp % 2, mp // 2, mp % 2
    xm, cm, dm = (1 - x) * 2 + c, x * 2 + 1 - c, (1 - x) * 2 + 1 - c
    ypeer, xpeer, cpeer = (z * 2 + 1 - y, mp), (dp, xm), (dp, cm)
    zpeers = [(((z + k) % nz) * 2 + y, mp) for k in range(1, nz)]
    greet(zpeers + [ypeer, xpeer, cpeer])
    rows = tok.shape[0] // nc
    xt = []
    for i in range(nc):
        part = pl.ds(i * rows, rows)
        cp = rcopy(tok.at[part], tok_all.at[mp, part], tx.at[i], rx.at[i], xpeer)
        cp.start()
        xt.append(cp)
    zc = []
    for k in range(1, nz):
        for kind, (src, dst) in enumerate(((vec, vec_all.at[mp, dp]), (w, w_all.at[dp]))):
            cp = rcopy(src, dst, zs.at[kind, k], zr.at[kind, k], zpeers[k - 1])
            cp.start()
            zc.append(cp)
    yc = []
    for kind, (src, dst) in enumerate(((vec, vec_all.at[mp, dp]), (w, w_all.at[dp]))):
        cp = rcopy(src, dst, ys.at[kind, 0], yr.at[kind, 0], ypeer)
        cp.start()
        yc.append(cp)
    own_tok = rcopy(tok, tok_all.at[mp], tc.at[nc], rc.at[nc], cpeer)
    own_tok.start()
    locs = [
        pltpu.make_async_copy(tok, tok_all.at[mp], loc.at[0]),
        pltpu.make_async_copy(w, w_all.at[dp], loc.at[1]),
        pltpu.make_async_copy(vec, vec_all.at[mp, dp], loc.at[2]),
    ]
    for cp in locs:
        cp.start()
    for k in range(1, nz):
        src_dp = ((z + nz - k) % nz) * 2 + y
        for kind in range(2):
            zc[(k - 1) * 2 + kind].wait_recv()
            ref = (vec_all.at[mp, src_dp], w_all.at[src_dp])[kind]
            cp = rcopy(ref, ref, ys.at[kind, k], yr.at[kind, k], ypeer)
            cp.start()
            yc.append(cp)
    ct = []

    def forward(i):
        part = pl.ds(i * rows, rows)
        xt[i].wait_recv()
        cp = rcopy(tok_all.at[xm, part], tok_all.at[xm, part], tc.at[i], rc.at[i], cpeer)
        cp.start()
        ct.append(cp)

    forward(0)
    for cp in locs:
        cp.wait()
    for k in range(nz):
        yc[k * 2].wait_recv()
    vx = rcopy(vec_all.at[mp], vec_all.at[mp], xs, xr, xpeer)
    vx.start()
    vc0 = rcopy(vec_all.at[mp], vec_all.at[mp], cs.at[0], cr.at[0], cpeer)
    vc0.start()
    if nc > 1:
        forward(1)
    vx.wait_recv()
    vc1 = rcopy(vec_all.at[xm], vec_all.at[xm], cs.at[1], cr.at[1], cpeer)
    vc1.start()
    for i in range(2, nc):
        forward(i)
    for k in range(nz):
        yc[k * 2 + 1].wait_recv()
    for cp in ct:
        cp.wait_recv()
    own_tok.wait()
    vc0.wait()
    vc1.wait()
    vx.wait_send()
    for cp in zc + yc + xt + ct:
        cp.wait_send()


def gather_all(tok, w, vec, ndp, nmp):
    nz, nc = ndp // 2, 4
    dma = pltpu.SemaphoreType.DMA
    return pl.pallas_call(
        functools.partial(gather_kernel, nz, nc),
        out_shape=(
            sds((nmp,) + tok.shape, BF),
            sds((ndp,) + w.shape, BF),
            sds((nmp, ndp) + vec.shape, F32),
        ),
        in_specs=[ANY] * 3,
        out_specs=(ANY,) * 3,
        scratch_shapes=[
            dma((3,)),
            dma((2, nz)),
            dma((2, nz)),
            dma((2, nz)),
            dma((2, nz)),
            dma,
            dma,
            dma((2,)),
            dma((2,)),
            dma((nc,)),
            dma((nc,)),
            dma((nc + 1,)),
            dma((nc + 1,)),
        ],
        compiler_params=pltpu.CompilerParams(collective_id=0, has_side_effects=True),
        name="gather_start",
    )(tok, w, vec)


def swap_kernel(forward, nmp, src, dst, loc, ss, rs):
    dp, mp = lax.axis_index("dp"), lax.axis_index("mp")
    own = dst.shape[2] if forward else src.shape[2]
    peers = [(mp + k) % nmp for k in range(1, nmp)]
    greet([(dp, m) for m in peers])

    def ends(m):
        if forward:
            return src.at[:, pl.ds(pl.multiple_of(m * own, own), own)], dst.at[mp]
        return src.at[m], dst.at[:, pl.ds(pl.multiple_of(mp * own, own), own)]

    cps = []
    for k, m in enumerate(peers):
        s, d = ends(m)
        cp = rcopy(s, d, ss.at[k], rs.at[k], (dp, m))
        cp.start()
        cps.append(cp)
    s, d = ends(mp)
    lc = pltpu.make_async_copy(s, d, loc)
    lc.start()
    lc.wait()
    for cp in cps:
        cp.wait()


def swap(src, forward, nmp, cid):
    dma = pltpu.SemaphoreType.DMA
    if forward:
        shape = (nmp, src.shape[0], src.shape[1] // nmp)
    else:
        shape = (src.shape[1], src.shape[2] * nmp)
    return pl.pallas_call(
        functools.partial(swap_kernel, forward, nmp),
        out_shape=sds(shape, BF),
        in_specs=[ANY],
        out_specs=ANY,
        scratch_shapes=[dma, dma((nmp - 1,)), dma((nmp - 1,))],
        compiler_params=pltpu.CompilerParams(collective_id=cid, has_side_effects=True),
        name="swap_fwd" if forward else "swap_bwd",
    )(src)


def vector_kernel(ndp, nmp, src, out, got, ss, rs):
    dp, mp = lax.axis_index("dp"), lax.axis_index("mp")
    me, n = dp * nmp + mp, ndp * nmp
    peers = [(me + k) % n for k in range(1, n)]
    greet([(p // nmp, p % nmp) for p in peers])
    cps = []
    for k, p in enumerate(peers):
        cp = rcopy(src.at[p], got.at[k], ss.at[k], rs.at[k], (p // nmp, p % nmp))
        cp.start()
        cps.append(cp)
    total = src[me]
    for k, cp in enumerate(cps):
        cp.wait_recv()
        total = total + got[k]
    out[...] = total
    for cp in cps:
        cp.wait_send()


def vector_sums(parts, ndp, nmp):
    n = ndp * nmp
    dma = pltpu.SemaphoreType.DMA
    return pl.pallas_call(
        functools.partial(vector_kernel, ndp, nmp),
        out_shape=sds(parts.shape[1:], F32),
        in_specs=[VM],
        out_specs=VM,
        scratch_shapes=[pltpu.VMEM((n - 1,) + parts.shape[1:], F32), dma((n - 1,)), dma((n - 1,))],
        compiler_params=pltpu.CompilerParams(collective_id=3, has_side_effects=True),
        name="vector_sums",
    )(parts)


def norm_rows(v):
    centre = jnp.mean(v, axis=-1, keepdims=True)
    v = v - centre
    r = lax.rsqrt(jnp.mean(v * v, axis=-1, keepdims=True) + EPS)
    return v * r, r


def norm_cols(v):
    centre = jnp.mean(v, axis=0, keepdims=True)
    v = v - centre
    r = lax.rsqrt(jnp.mean(v * v, axis=0, keepdims=True) + EPS)
    return v * r, r


def qkv_kernel(heads, tok, w, gain, shift, gains, normed, raw, low, wt):
    @pl.when(pl.program_id(0) == 0)
    def _():
        wt[...] = w[...].T

    cols = heads * HEAD
    hat, _ = norm_rows(tok[0].astype(F32))
    n = (hat * gain[...] + shift[...]).astype(BF)
    normed[...] = n
    proj = nt(wt[0 : 3 * cols, :], n)
    raw[...] = proj[0 : 2 * cols]
    for h in range(2 * heads):
        part = slice(h * HEAD, (h + 1) * HEAD)
        hat, _ = norm_cols(proj[part])
        low[part, :] = (hat * gains[part, :]).astype(BF)
    low[2 * cols :, :] = proj[2 * cols :].astype(BF)


def project(tok_all, w, gain, shift, gains, heads):
    nb, rows, d = tok_all.shape
    cols = heads * HEAD
    t = nb * rows
    full = lambda shape: pl.BlockSpec(shape, lambda i: (0,) * len(shape))
    return pl.pallas_call(
        functools.partial(qkv_kernel, heads),
        grid=(nb,),
        out_shape=(
            sds((t, d), BF),
            sds((2 * cols, t), F32),
            sds((3 * cols, t), BF),
            sds((w.shape[1], w.shape[0]), BF),
        ),
        in_specs=[
            pl.BlockSpec((1, rows, d), lambda i: (i, 0, 0)),
            full(w.shape),
            full((1, d)),
            full((1, d)),
            full((2 * cols, 1)),
        ],
        out_specs=(
            pl.BlockSpec((rows, d), lambda i: (i, 0)),
            pl.BlockSpec((2 * cols, rows), lambda i: (0, i)),
            pl.BlockSpec((3 * cols, rows), lambda i: (0, i)),
            full((w.shape[1], w.shape[0])),
        ),
        compiler_params=params(),
        cost_estimate=cost(2 * t * d * 3 * cols, 12 * 2**20),
        name="project_qkv",
    )(tok_all, w, gain, shift, gains)


def masks(ids):
    t = ids.shape[1]
    r = lax.broadcasted_iota(jnp.int32, (HEAD, t), 0)
    pad = ids < 0
    mq = jnp.where((r == ids) | ((r == 31) & pad), 1.0, 0.0)
    mk = jnp.where((r <= 31) & (r != ids), -BIG, 0.0)
    mk = jnp.where((r >= 32) & (r < 35), 1.0, mk)
    return r, mq, mk


def three(v):
    a = v.astype(BF).astype(F32)
    b = (v - a).astype(BF).astype(F32)
    return a, b, v - a - b


SCALE = HEAD**-0.5


def attend_kernel(heads, nblk, span, low, ids, out, lse, qa, ka, va, acc):
    cols = heads * HEAD
    t = ids.shape[1]
    _, mq, mk = masks(ids[...])
    mq, mk = mq.astype(BF), mk.astype(BF)
    one = jnp.where(lax.broadcasted_iota(jnp.int32, (16, t), 0) == 0, 1.0, 0.0).astype(BF)
    for h in range(heads):
        qa[h, 0:HEAD, :] = low[h * HEAD : (h + 1) * HEAD, :]
        qa[h, HEAD:, :] = mq
        k = low[cols + h * HEAD : cols + (h + 1) * HEAD, :]
        ka[h, :, :] = jnp.concatenate([k, mk], axis=0).T
        va[h, 0:HEAD, :] = low[2 * cols + h * HEAD : 2 * cols + (h + 1) * HEAD, :]
        va[h, HEAD:, :] = one
    acc[...] = jnp.zeros_like(acc)

    def row(i, _):
        qi = pl.ds(pl.multiple_of(i * TB, TB), TB)

        def col(j, _):
            kj = pl.ds(pl.multiple_of(j * TB, TB), TB)
            s = [nn(ka[h, kj, :], qa[h, :, qi]) for h in range(heads)]
            p = [jnp.exp2(v * (SCALE * LOG2E)).astype(BF) for v in s]
            for h in range(heads):
                acc[h, :, qi] += nn(va[h, :, kj], p[h])
            return 0

        return lax.fori_loop(span[i], span[nblk + i], col, 0)

    lax.fori_loop(0, nblk, row, 0)
    pad = ids[...] < 0
    lse[...] = jnp.zeros_like(lse)
    for h in range(heads):
        total = jnp.where(pad, 1.0, acc[h, HEAD : HEAD + 1, :])
        value = low[2 * cols + h * HEAD : 2 * cols + (h + 1) * HEAD, :].astype(F32)
        o = jnp.where(pad, value, acc[h, 0:HEAD, :] * (1.0 / total))
        out[h * HEAD : (h + 1) * HEAD, :] = o.astype(BF)
        lse[h : h + 1, :] = jnp.log(total)


def attend(span, low, ids, heads):
    cols, t = heads * HEAD, low.shape[1]
    return pl.pallas_call(
        functools.partial(attend_kernel, heads, t // TB),
        out_shape=(sds((cols, t), BF), sds((8, t), F32)),
        in_specs=[SM, VM, VM],
        out_specs=(VM, VM),
        scratch_shapes=[
            pltpu.VMEM((heads, 2 * HEAD, t), BF),
            pltpu.VMEM((heads, t, 2 * HEAD), BF),
            pltpu.VMEM((heads, HEAD + 16, t), BF),
            pltpu.VMEM((heads, HEAD + 16, t), F32),
        ],
        compiler_params=params(),
        cost_estimate=cost(12e9, 4 * 2**20),
        name="attend",
    )(span, low, ids)


def head_back(raw, gain, grad):
    hat, r = norm_cols(raw)
    e = grad * gain
    m1 = jnp.mean(e, axis=0, keepdims=True)
    m2 = jnp.mean(e * hat, axis=0, keepdims=True)
    return (e - m1 - hat * m2) * r, jnp.sum(grad * hat, axis=1, keepdims=True)


def attend_back_kernel(
    heads, nblk, span, low, raw, att, lse, dout, ids, gains, gproj, ggain, qa, ka, va, da, dq, dk, dv
):
    cols = heads * HEAD
    t = ids.shape[1]
    r, mq, mk = masks(ids[...])
    mk = mk.astype(BF)
    one = jnp.where(r < 3, 1.0, 0.0).astype(BF)
    for h in range(heads):
        hs = slice(h * HEAD, (h + 1) * HEAD)
        qa[h, 0:HEAD, :] = low[hs, :]
        a, b, c = three(lse[h : h + 1, :] * (-1.0 / SCALE))
        m = jnp.where(r == 32, a, jnp.where(r == 33, b, jnp.where(r == 34, c, mq)))
        qa[h, HEAD:, :] = m.astype(BF)
        k = low[cols + h * HEAD : cols + (h + 1) * HEAD, :]
        ka[h, :, :] = jnp.concatenate([k, mk], axis=0).T
        v = low[2 * cols + h * HEAD : 2 * cols + (h + 1) * HEAD, :]
        va[h, :, :] = jnp.concatenate([v, one], axis=0).T
        do = dout[hs, :]
        delta = jnp.sum(do.astype(F32) * att[hs, :].astype(F32), axis=0, keepdims=True)
        a, b, c = three(-delta)
        da[h, 0:HEAD, :] = do
        da[h, HEAD:, :] = jnp.where(
            r == 0, a, jnp.where(r == 1, b, jnp.where(r == 2, c, 0.0))
        ).astype(BF)
    dq[...] = jnp.zeros_like(dq)
    dk[...] = jnp.zeros_like(dk)
    dv[...] = jnp.zeros_like(dv)

    def row(i, _):
        qi = pl.ds(pl.multiple_of(i * TB, TB), TB)

        def col(j, _):
            kj = pl.ds(pl.multiple_of(j * TB, TB), TB)
            s = [nn(ka[h, kj, :], qa[h, :, qi]) for h in range(heads)]
            d = [nn(va[h, kj, :], da[h, :, qi]) for h in range(heads)]
            p = [jnp.exp2(v * (SCALE * LOG2E)) for v in s]
            ds = [(p[h] * d[h]).astype(BF) for h in range(heads)]
            for h in range(heads):
                hs = pl.ds(h * HEAD, HEAD)
                dv[hs, kj] += nt(dout[hs, qi], p[h].astype(BF))
                dk[hs, kj] += nt(low[hs, qi], ds[h])
                dq[hs, qi] += nn(low[pl.ds(cols + h * HEAD, HEAD), kj], ds[h])
            return 0

        return lax.fori_loop(span[i], span[nblk + i], col, 0)

    lax.fori_loop(0, nblk, row, 0)
    pad = ids[...] < 0
    for h in range(heads):
        hs = slice(h * HEAD, (h + 1) * HEAD)
        for part, grad in ((0, dq), (1, dk)):
            ps = slice(part * cols + h * HEAD, part * cols + (h + 1) * HEAD)
            g, gg = head_back(raw[ps, :], gains[ps, :], grad[hs, :] * SCALE)
            gproj[ps, :] = g.astype(BF)
            ggain[ps, :] = gg
        g = dv[hs, :] + jnp.where(pad, dout[hs, :].astype(F32), 0.0)
        gproj[2 * cols + h * HEAD : 2 * cols + (h + 1) * HEAD, :] = g.astype(BF)


def attend_back(span, low, raw, att, lse, dout, ids, gains, heads):
    cols, t = heads * HEAD, low.shape[1]
    return pl.pallas_call(
        functools.partial(attend_back_kernel, heads, t // TB),
        out_shape=(sds((3 * cols, t), BF), sds((2 * cols, 1), F32)),
        in_specs=[SM] + [VM] * 7,
        out_specs=(VM, VM),
        scratch_shapes=[
            pltpu.VMEM((heads, 2 * HEAD, t), BF),
            pltpu.VMEM((heads, t, 2 * HEAD), BF),
            pltpu.VMEM((heads, t, 2 * HEAD), BF),
            pltpu.VMEM((heads, 2 * HEAD, t), BF),
            pltpu.VMEM((cols, t), F32),
            pltpu.VMEM((cols, t), F32),
            pltpu.VMEM((cols, t), F32),
        ],
        compiler_params=params(),
        cost_estimate=cost(30e9, 12 * 2**20),
        name="attend_back",
    )(span, low, raw, att, lse, dout, ids, gains)


def place_out(pieces, dest):
    mp = lax.axis_index("mp")
    x, c = mp // 2, mp % 2
    order = (mp, (1 - x) * 2 + c, x * 2 + 1 - c, (1 - x) * 2 + 1 - c)
    rows = pieces[0].shape[0]
    for piece, m in zip(pieces, order):
        dest[pl.ds(pl.multiple_of(m * rows, rows), rows), :] = piece[...]


def middle_kernel(att, w0, w1, w2, w3, tok, bias, gain, shift, mid, low, wo):
    place_out((w0, w1, w2, w3), wo)
    m = tok[...].astype(F32) + tn(att[...], wo[...]) + bias[...]
    mid[...] = m
    hat, _ = norm_rows(m)
    low[...] = (hat * gain[...] + shift[...]).astype(BF)


def middle_part(att, wos, tok, bias, gain, shift):
    rows, d = tok.shape
    return pl.pallas_call(
        middle_kernel,
        out_shape=(sds((rows, d), F32), sds((rows, d), BF)),
        in_specs=[VM] * 9,
        out_specs=(VM, VM),
        scratch_shapes=[pltpu.VMEM((d, d), BF)],
        compiler_params=params(),
        cost_estimate=cost(2 * rows * d * d, 6 * 2**20),
        name="middle",
    )(att, *wos, tok, bias, gain, shift)


def middle_back_kernel(nmp, g0, g1, mid, cot, att, *refs):
    pieces, (gain, gmid, gatt, gwo, sums, wo) = refs[:-6], refs[-6:]
    if len(pieces) > 1:
        place_out(pieces, wo)
    else:
        wo = pieces[0]
    gy = cot[...].astype(F32)
    g = g0[...] + g1[...].astype(F32)
    hat, r = norm_rows(mid[...])
    e = g * gain[...]
    m1 = jnp.mean(e, axis=-1, keepdims=True)
    m2 = jnp.mean(e * hat, axis=-1, keepdims=True)
    gm = gy + (e - m1 - hat * m2) * r
    gmid[...] = gm
    low = gm.astype(BF)
    rows = att.shape[0] // nmp
    ga = nt(wo[...], low).astype(BF)
    for m in range(nmp):
        gatt[m] = ga[m * rows : (m + 1) * rows]
    gw = nt(gm.T.astype(BF), att[...]).astype(BF)
    mp = lax.axis_index("mp")
    for m in range(nmp):
        gwo[m] = gw[:, m * rows : (m + 1) * rows]
    sums[...] = jnp.zeros_like(sums)
    for k, v in enumerate((gm, g * hat, g, gy)):
        sums[k : k + 1, :] = jnp.sum(v, axis=0, keepdims=True)


def middle_back(g0, g1, mid, cot, att, wos, gain, nmp):
    rows, d = mid.shape
    return pl.pallas_call(
        functools.partial(middle_back_kernel, nmp),
        out_shape=(
            sds((rows, d), F32),
            sds((nmp, d // nmp, rows), BF),
            sds((nmp, d, d // nmp), BF),
            sds((8, d), F32),
        ),
        in_specs=[VM] * (6 + len(wos)),
        out_specs=(VM,) * 4,
        scratch_shapes=[pltpu.VMEM((d, d), BF)],
        compiler_params=params(),
        cost_estimate=cost(4 * rows * d * d, 10 * 2**20),
        name="middle_back",
    )(g0, g1, mid, cot, att, *wos, gain)


def feed_kernel(npiece, nz, first, *refs):
    n0, n1, c0, c1, bias = refs[:5]
    pieces = refs[5 : 5 + npiece]
    out_own, out_send, g_own, g_send, dwu, dwd, gbias = refs[5 + npiece : 12 + npiece]
    wu, wd, n2, gy, n2t, gyt, acts, gps, oacc, gacc, sem = refs[12 + npiece :]
    dp, mp = lax.axis_index("dp"), lax.axis_index("mp")
    z, y, x, c = dp // 2, dp % 2, mp // 2, mp % 2
    copies = []
    half = npiece // 2
    for a, piece in enumerate(pieces):
        dest = (wu, wd)[a // half]
        rel = a % half
        count, rows = piece.shape[0], piece.shape[1]
        for k in range(count):
            if half <= 2:
                at, colidx = 0, (k if half == 1 else rel)
            else:
                zz = (z + nz - k) % nz
                at = (zz * 2 + (y if rel % 2 == 0 else 1 - y)) * rows
                at, colidx = pl.multiple_of(at, rows), rel // 2
            cp = pltpu.make_async_copy(piece.at[k], dest.at[colidx, pl.ds(at, rows), :], sem.at[a, k])
            cp.start()
            copies.append(cp)
    hr = n0.shape[0]
    for i, (n, g) in enumerate(((n0, c0), (n1, c1))):
        part = slice(i * hr, (i + 1) * hr)
        n2[part, :] = n[...]
        gy[part, :] = g[...]
        n2t[:, part] = n[...].T
        gyt[:, part] = g[...].T
    oacc[...] = jnp.zeros_like(oacc)
    gacc[...] = jnp.zeros_like(gacc)
    for cp in copies:
        cp.wait()
    rows, d = n2.shape
    cw = acts.shape[1]
    per = wu.shape[2] // cw
    ones = jnp.ones((16, rows), BF)

    def chunk(i, _):
        col, off = i // per, pl.multiple_of((i % per) * cw, cw)
        cs = pl.ds(off, cw)
        m = jnp.where(col == 0, mp, (1 - x) * 2 + c)
        b = bias[pl.ds(first + m, 1), cs]
        for rb in range(rows // 256):
            rs = slice(rb * 256, (rb + 1) * 256)
            u = nn(n2[rs, :], wu[col, :, cs]) + b
            ga = nn(gy[rs, :], wd[col, :, cs])
            cdf = 0.5 + 0.5 * lax.erf(u * 0.7071067811865476)
            act = (u * cdf).astype(BF)
            gp = (ga * (cdf + u * (jnp.exp(-0.5 * u * u) * 0.3989422804014327))).astype(BF)
            acts[rs, :] = act
            gps[rs, :] = gp
            oacc[rs, :] += nt(act, wd[col, :, cs])
            gacc[rs, :] += nt(gp, wu[col, :, cs])
        dwd[col, :, cs] = nn(gyt[...], acts[...]).astype(BF)
        dwu[col, :, cs] = nn(n2t[...], gps[...]).astype(BF)
        gbias[col, :, cs] = nn(ones, gps[...])[0:8]
        return 0

    lax.fori_loop(0, 2 * per, chunk, 0)
    out_own[...] = oacc[0:hr]
    out_send[...] = oacc[hr:].astype(BF)
    g_own[...] = gacc[0:hr]
    g_send[...] = gacc[hr:].astype(BF)


def feed(n0, n1, c0, c1, bias, ups, downs, nz):
    hr, d = n0.shape
    rows, cw = 2 * hr, 256
    unit = ups[0].shape[2]
    pieces = list(ups) + list(downs)
    kmax = max(p.shape[0] for p in pieces)
    vm = pltpu.VMEM
    return pl.pallas_call(
        functools.partial(feed_kernel, len(pieces), nz, bias.shape[0] // 16 * 8),
        out_shape=(
            sds((hr, d), F32),
            sds((hr, d), BF),
            sds((hr, d), F32),
            sds((hr, d), BF),
            sds((2, d, unit), BF),
            sds((2, d, unit), BF),
            sds((2, 8, unit), F32),
        ),
        in_specs=[VM] * 5 + [ANY] * len(pieces),
        out_specs=(VM,) * 7,
        scratch_shapes=[
            vm((2, d, unit), BF),
            vm((2, d, unit), BF),
            vm((rows, d), BF),
            vm((rows, d), BF),
            vm((d, rows), BF),
            vm((d, rows), BF),
            vm((rows, cw), BF),
            vm((rows, cw), BF),
            vm((rows, d), F32),
            vm((rows, d), F32),
            pltpu.SemaphoreType.DMA((len(pieces), kmax)),
        ],
        compiler_params=params(),
        cost_estimate=cost(12 * rows * d * 2 * unit, 22 * 2**20),
        name="feed_forward",
    )(n0, n1, c0, c1, bias, *pieces)


def project_back_kernel(order, gproj, normed, tok, wt, gn, gw, sums, acc):
    @pl.when(pl.program_id(0) == 0)
    def _():
        acc[...] = jnp.zeros_like(acc)
        sums[...] = jnp.zeros_like(sums)

    acc[...] += nn(gproj[...], normed[...])
    g = tn(gproj[...], wt[...])
    gn[0] = g.astype(BF)
    hat, _ = norm_rows(tok[0].astype(F32))
    sums[0:1, :] += jnp.sum(g * hat, axis=0, keepdims=True)
    sums[1:2, :] += jnp.sum(g, axis=0, keepdims=True)

    @pl.when(pl.program_id(0) == pl.num_programs(0) - 1)
    def _():
        gw[...] = acc[...].T.astype(BF)


def project_back(order, gproj, normed, tok_all, wt):
    nb, rows, d = tok_all.shape
    n = gproj.shape[0]
    t = nb * rows
    return pl.pallas_call(
        project_back_kernel,
        grid_spec=pltpu.PrefetchScalarGridSpec(
            num_scalar_prefetch=1,
            grid=(nb,),
            in_specs=[
                pl.BlockSpec((n, rows), lambda i, o: (0, o[i])),
                pl.BlockSpec((rows, d), lambda i, o: (o[i], 0)),
                pl.BlockSpec((1, rows, d), lambda i, o: (o[i], 0, 0)),
                pl.BlockSpec((n, d), lambda i, o: (0, 0)),
            ],
            out_specs=(
                pl.BlockSpec((1, rows, d), lambda i, o: (i, 0, 0)),
                pl.BlockSpec((d, n), lambda i, o: (0, 0)),
                pl.BlockSpec((8, d), lambda i, o: (0, 0)),
            ),
            scratch_shapes=[pltpu.VMEM((n, d), F32)],
        ),
        out_shape=(sds((nb, rows, d), BF), sds((d, n), BF), sds((8, d), F32)),
        compiler_params=params(),
        cost_estimate=cost(4 * t * d * n, 14 * 2**20),
        name="project_back",
    )(order, gproj, normed, tok_all, wt)


def tokens_back(gn, tok, gain, gmid):
    hat, r = norm_rows(tok.astype(F32))
    e = gn * gain
    m1 = jnp.mean(e, axis=-1, keepdims=True)
    m2 = jnp.mean(e * hat, axis=-1, keepdims=True)
    return (gmid + (e - m1 - hat * m2) * r).astype(BF)


class Where:
    def __init__(self, nz):
        dp, mp = lax.axis_index("dp"), lax.axis_index("mp")
        z, y, x, c = dp // 2, dp % 2, mp // 2, mp % 2
        self.dp, self.mp, self.z, self.y, self.x, self.c = dp, mp, z, y, x, c
        self.xm, self.cm, self.dm = (1 - x) * 2 + c, x * 2 + 1 - c, (1 - x) * 2 + 1 - c
        self.ydp = z * 2 + 1 - y
        self.zfrom = [((z + nz - k) % nz) * 2 + y for k in range(nz)]
        self.yfrom = [((z + nz - k) % nz) * 2 + 1 - y for k in range(nz)]
        self.py, self.px, self.pc, self.pd = (self.ydp, mp), (dp, self.xm), (dp, self.cm), (dp, self.dm)
        self.pz = [None] + [(((z + k) % nz) * 2 + y, mp) for k in range(1, nz)]
        self.all = self.pz[1:] + [self.py, self.px, self.pc, self.pd]


class Sender:
    def __init__(self, ss, rs):
        self.ss, self.rs, self.n, self.open = ss, rs, 0, []

    def send(self, src, dst, peer):
        cp = rcopy(src, dst, self.ss.at[self.n], self.rs.at[self.n], peer)
        cp.start()
        self.n += 1
        self.open.append(cp)
        return cp

    def sent(self, cp):
        cp.wait_send()
        self.open = [o for o in self.open if o is not cp]

    def finish(self):
        for cp in self.open:
            cp.wait_send()


def vector_rows(vecv, small, d):
    nmp, ndp, vr, lanes = vecv.shape
    v = vecv[...].reshape(nmp * ndp * vr, lanes)
    parts = [p.astype(BF) for p in three(v)]
    lane = lax.broadcasted_iota(jnp.int32, (lanes, d), 1)
    sub = lax.broadcasted_iota(jnp.int32, (lanes, d), 0)
    s = lax.broadcasted_iota(jnp.int32, (nmp * ndp, vr, d), 0)
    col = lax.broadcasted_iota(jnp.int32, (nmp * ndp, vr, d), 2)
    dev = (s % ndp) * nmp + s // ndp

    def spread(width):
        sel = jnp.where(lane % width == sub, 1.0, 0.0).astype(BF)
        return sum(nn(p, sel) for p in parts).reshape(nmp * ndp, vr, d)

    a = jnp.sum(jnp.where(col // small == dev, spread(small), 0.0), axis=0)
    wide = nmp * small
    b = spread(wide)
    per = nmp * ndp // nmp
    ups = []
    for m in range(nmp):
        keep = (dev // per == m) & (col // wide == dev % per)
        ups.append(jnp.sum(jnp.where(keep, b, 0.0), axis=0)[8:9])
    return a[0:8], jnp.concatenate(ups, axis=0)


def front_kernel(nz, heads, small, *refs):
    tok, wup, wdn, cot = refs[:4]
    wq, wo, ids = refs[4:7]
    vecs = refs[7:16]
    normed_o, raw_o, tok_o, low_h, wt_h, wot_h, att_h, own_h, mid_h = refs[16:25]
    dwu_h, dwd_h, oown_h, gown_h, ogot_h, ggot_h = refs[25:31]
    lse, rows_o, gains, gbias = refs[31:35]
    tokv, wqv, vecv, normv, rawv, low_o, wt_o, wotv, att_o, own_o, mid_o, n2_o = refs[35:47]
    qa, ka, va, acc, wu_o, wd_o, cotv, cotx_o, n2x_o = refs[47:56]
    n2t, gyt, acts, gps, oacc, gacc, dwu, dwd, osend, gsend, ss, rs, ls = refs[56:]
    w = Where(nz)
    dp, mp = w.dp, w.mp
    cols = heads * HEAD
    t, d = normv.shape
    nmp, rows = tokv.shape[0], tokv.shape[1]
    greet(w.all)
    tx = Sender(ss, rs)
    count, late = [0], []

    def keep(src, dst, wait_late=True):
        cp = pltpu.make_async_copy(src, dst, ls.at[count[0]])
        cp.start()
        count[0] += 1
        if wait_late:
            late.append(cp)
        return cp

    nc = 4
    part = [pl.ds(i * (rows // nc), rows // nc) for i in range(nc)]
    xt = [tx.send(tok.at[part[i]], tokv.at[mp, part[i]], w.px) for i in range(nc)]
    vecv[mp, dp] = jnp.zeros(vecv.shape[2:], F32)
    for i, v in enumerate(vecs):
        vecv[mp, dp, i : i + 1, 0 : v.shape[1]] = v[...]
    ref = vecv.at[mp, dp]
    vz = [None] + [tx.send(ref, ref, w.pz[k]) for k in range(1, nz)]
    vy = [tx.send(ref, ref, w.py)]
    for i in range(3):
        wqv[dp, :, i * cols : (i + 1) * cols] = wq[i]
    wqv[dp, :, 3 * cols :] = wo[...]
    ref = wqv.at[dp]
    qz = [None] + [tx.send(ref, ref, w.pz[k]) for k in range(1, nz)]
    qy = [tx.send(ref, ref, w.py)]
    dx = tx.send(wdn, wd_o.at[1, dp], w.px)
    ux = [tx.send(wup, wu_o.at[1, dp], w.px)]
    ctok = tx.send(tok, tokv.at[mp], w.pc)
    cx = tx.send(cot, cotx_o, w.pc)
    own_tok = keep(tok, tokv.at[mp], False)
    own_w = [keep(wup, wu_o.at[0, dp], False), keep(wdn, wd_o.at[0, dp], False)]
    own_cot = keep(cot, cotv, False)
    for k in range(1, nz):
        vz[k].wait_recv()
        ref = vecv.at[mp, w.zfrom[k]]
        vy.append(tx.send(ref, ref, w.py))
    for k in range(nz):
        vy[k].wait_recv()
    vx = tx.send(vecv.at[mp], vecv.at[mp], w.px)
    vc = tx.send(vecv.at[mp], vecv.at[mp], w.pc)
    for k in range(1, nz):
        qz[k].wait_recv()
        ref = wqv.at[w.zfrom[k]]
        qy.append(tx.send(ref, ref, w.py))
    uz = [None] + [tx.send(wup, wu_o.at[0, dp], w.pz[k]) for k in range(1, nz)]
    uy = [tx.send(wup, wu_o.at[0, dp], w.py)]
    dy = [tx.send(wdn, wd_o.at[0, dp], w.py)]
    vx.wait_recv()
    vd = tx.send(vecv.at[w.xm], vecv.at[w.xm], w.pc)
    ct = []

    def forward(i):
        xt[i].wait_recv()
        ref = tokv.at[w.xm, part[i]]
        ct.append(tx.send(ref, ref, w.pc))

    forward(0)
    forward(1)
    vc.wait_recv()
    vd.wait_recv()
    main, ups = vector_rows(vecv, small, d)
    rows_o[0:8, :] = main
    rows_o[8:12, :] = ups
    rows_o[12:16, :] = jnp.zeros((4, d), F32)
    lane = lax.broadcasted_iota(jnp.int32, (cols, d), 1)
    pick = lane == lax.broadcasted_iota(jnp.int32, (cols, d), 0) + mp * cols
    for i in range(2):
        gains[i * cols : (i + 1) * cols, :] = jnp.sum(
            jnp.where(pick, main[2 + i : 3 + i], 0.0), axis=1, keepdims=True
        )
    for k in range(nz):
        qy[k].wait_recv()
    wall = wqv[...].reshape(d, 4 * cols).T
    wt_o[...] = wall[0 : 3 * cols]
    wotv[mp] = wall[3 * cols :]
    keep(wt_o, wt_h)
    one = jnp.where(lax.broadcasted_iota(jnp.int32, (16, rows), 0) == 0, 1.0, 0.0).astype(BF)

    def project(m):
        ts = pl.ds(pl.multiple_of(m * rows, rows), rows)
        hat, _ = norm_rows(tokv[m].astype(F32))
        n = (hat * rows_o[0:1, :] + rows_o[1:2, :]).astype(BF)
        normv[ts, :] = n
        proj = nt(wt_o[...], n)
        rawv[:, ts] = proj[0 : 2 * cols]
        _, mq, mk = masks(ids[:, ts])
        mq, mk = mq.astype(BF), mk.astype(BF)
        for h in range(heads):
            qs, ks = h * HEAD, cols + h * HEAD
            hat, _ = norm_cols(proj[qs : qs + HEAD])
            q = (hat * gains[qs : qs + HEAD, :]).astype(BF)
            low_o[qs : qs + HEAD, ts] = q
            qa[h, 0:HEAD, ts] = q
            qa[h, HEAD:, ts] = mq
            hat, _ = norm_cols(proj[ks : ks + HEAD])
            k = (hat * gains[ks : ks + HEAD, :]).astype(BF)
            low_o[ks : ks + HEAD, ts] = k
            ka[h, ts, :] = jnp.concatenate([k, mk], axis=0).T
            v = proj[2 * cols + h * HEAD : 2 * cols + (h + 1) * HEAD].astype(BF)
            low_o[2 * cols + h * HEAD : 2 * cols + (h + 1) * HEAD, ts] = v
            va[h, 0:HEAD, ts] = v
            va[h, HEAD:, ts] = one

    own_tok.wait()
    project(mp)
    forward(2)
    ctok.wait_recv()
    forward(3)
    project(w.cm)
    ox = tx.send(wotv.at[mp], wotv.at[mp], w.px)
    oc = tx.send(wotv.at[mp], wotv.at[mp], w.pc)
    uy[0].wait_recv()
    uw = [tx.send(wu_o.at[0, w.ydp], wu_o.at[1, w.ydp], w.px)]
    dz = [None] + [tx.send(wdn, wd_o.at[0, dp], w.pz[k]) for k in range(1, nz)]
    project(w.xm)
    for cp in ct:
        cp.wait_recv()
    project(w.dm)
    keep(normv, normed_o)
    keep(rawv, raw_o)
    keep(tokv, tok_o)
    keep(low_o, low_h)
    for k in range(1, nz):
        uz[k].wait_recv()
        ref = wu_o.at[0, w.zfrom[k]]
        uy.append(tx.send(ref, ref, w.py))
        ux.append(tx.send(ref, wu_o.at[1, w.zfrom[k]], w.px))
    dx.wait_recv()
    ref = wd_o.at[1, dp]
    ez = [None] + [tx.send(ref, ref, w.pz[k]) for k in range(1, nz)]
    ey = [tx.send(ref, ref, w.py)]

    def attend_row(i):
        qi = pl.ds(pl.multiple_of(i * rows, rows), rows)
        acc[...] = jnp.zeros_like(acc)

        def tile(j, _):
            kj = pl.ds(pl.multiple_of(j * rows, rows), rows)
            s = [nn(ka[h, kj, :], qa[h, :, qi]) for h in range(heads)]
            p = [jnp.exp2(v * (SCALE * LOG2E)).astype(BF) for v in s]
            for h in range(heads):
                acc[h] += nn(va[h, :, kj], p[h])
            return 0

        lax.fori_loop(jnp.maximum(i - 2, 0), jnp.minimum(i + 3, nmp), tile, 0)
        pad = ids[:, qi] < 0
        lse[:, qi] = jnp.zeros((8, rows), F32)
        for h in range(heads):
            total = jnp.where(pad, 1.0, acc[h, HEAD : HEAD + 1, :])
            value = va[h, 0:HEAD, qi].astype(F32)
            o = jnp.where(pad, value, acc[h, 0:HEAD, :] * (1.0 / total))
            att_o[h * HEAD : (h + 1) * HEAD, qi] = o.astype(BF)
            lse[h : h + 1, qi] = jnp.log(total)
        return att_o.at[:, qi]

    at = [tx.send(attend_row(w.xm), own_o.at[mp], w.px)]
    at.append(tx.send(attend_row(w.dm), own_o.at[mp], w.pd))
    for k in range(1, nz):
        uy[k].wait_recv()
        ref = wu_o.at[0, w.yfrom[k]]
        uw.append(tx.send(ref, wu_o.at[1, w.yfrom[k]], w.px))
    ox.wait_recv()
    od = tx.send(wotv.at[w.xm], wotv.at[w.xm], w.pc)
    at.append(tx.send(attend_row(w.cm), own_o.at[mp], w.pc))
    for k in range(1, nz):
        dz[k].wait_recv()
        ref = wd_o.at[0, w.zfrom[k]]
        dy.append(tx.send(ref, ref, w.py))
    own = keep(attend_row(mp), own_o.at[mp], False)
    keep(att_o, att_h)
    oc.wait_recv()
    od.wait_recv()
    keep(wotv, wot_h)
    own.wait()
    for cp in at:
        cp.wait_recv()
    keep(own_o, own_h)
    m = tokv[mp].astype(F32) + rows_o[4:5, :]
    m = m + tn(own_o[...].reshape(d, rows), wotv[...].reshape(d, d))
    mid_o[...] = m
    keep(mid_o, mid_h)
    hat, _ = norm_rows(m)
    n2_o[...] = (hat * rows_o[5:6, :] + rows_o[6:7, :]).astype(BF)
    nx = tx.send(n2_o, n2x_o, w.pc)
    own_cot.wait()
    cx.wait_recv()
    gyt[:, 0:rows] = cotv[...].T
    gyt[:, rows:] = cotx_o[...].T
    n2t[:, 0:rows] = n2_o[...].T
    for k in range(1, nz):
        ez[k].wait_recv()
        ref = wd_o.at[1, w.zfrom[k]]
        ey.append(tx.send(ref, ref, w.py))
    nx.wait_recv()
    n2t[:, rows:] = n2x_o[...].T
    unit = wu_o.shape[3]
    ones = jnp.ones((16, 2 * rows), BF)
    step = rows // 2

    def column(i, m):
        wu, wd = wu_o[i].reshape(d, unit), wd_o[i].reshape(d, unit)
        b = rows_o[pl.ds(8 + m, 1), :]
        for rb in range(4):
            rs = slice(rb * step, (rb + 1) * step)
            src = slice((rb % 2) * step, (rb % 2 + 1) * step)
            u = nn((n2_o, n2x_o)[rb // 2][src, :], wu) + b
            ga = nn((cotv, cotx_o)[rb // 2][src, :], wd)
            cdf = 0.5 + 0.5 * lax.erf(u * 0.7071067811865476)
            acts[rs, :] = (u * cdf).astype(BF)
            gps[rs, :] = (ga * (cdf + u * (jnp.exp(-0.5 * u * u) * 0.3989422804014327))).astype(BF)
        if i == 0:
            oacc[...] = nt(acts[...], wd)
            gacc[...] = nt(gps[...], wu)
        else:
            gacc[...] += nt(gps[...], wu)
            gsend[...] = gacc[rows:].astype(BF)
            gx = tx.send(gsend, ggot_h, w.pc)
            oacc[...] += nt(acts[...], wd)
            osend[...] = oacc[rows:].astype(BF)
            sent.extend([gx, tx.send(osend, ogot_h, w.pc)])
            keep(gacc.at[0:rows], gown_h)
            keep(oacc.at[0:rows], oown_h)
        dwd[i] = nn(gyt[...], acts[...]).astype(BF)
        keep(dwd.at[i], dwd_h.at[i])
        dwu[i] = nn(n2t[...], gps[...]).astype(BF)
        keep(dwu.at[i], dwu_h.at[i])
        gbias[i] = nn(ones, gps[...])[0:8]

    sent = []
    for cp in own_w:
        cp.wait()
    for cp in dy:
        cp.wait_recv()
    column(0, mp)
    for cp in ux + ey + uw:
        cp.wait_recv()
    column(1, w.xm)
    for cp in sent:
        cp.wait_recv()
    tx.finish()
    for cp in late:
        cp.wait()


def front(tok, wq, wo, wup, wdn, vecs, cot, ids, ndp, nmp):
    rows, d = tok.shape
    drow, unit, cols = wup.shape[0], wup.shape[1], wo.shape[1]
    small = vecs[0].shape[1]
    heads, t, nsend, nlocal = cols // HEAD, rows * nmp, 80, 32
    dma, vm = pltpu.SemaphoreType.DMA, pltpu.VMEM
    return pl.pallas_call(
        functools.partial(front_kernel, ndp // 2, heads, small),
        out_shape=(
            sds((t, d), BF),
            sds((2 * cols, t), F32),
            sds((nmp, rows, d), BF),
            sds((3 * cols, t), BF),
            sds((3 * cols, d), BF),
            sds((nmp, cols, d), BF),
            sds((cols, t), BF),
            sds((nmp, cols, rows), BF),
            sds((rows, d), F32),
            sds((2, d, unit), BF),
            sds((2, d, unit), BF),
            sds((rows, d), F32),
            sds((rows, d), F32),
            sds((rows, d), BF),
            sds((rows, d), BF),
            sds((8, t), F32),
            sds((16, d), F32),
            sds((2 * cols, 1), F32),
            sds((2, 8, unit), F32),
        ),
        in_specs=[ANY] * 4 + [VM] * 12,
        out_specs=(ANY,) * 15 + (VM,) * 4,
        scratch_shapes=[
            vm((nmp, rows, d), BF),
            vm((ndp, drow, 4 * cols), BF),
            vm((nmp, ndp, 16, 128), F32),
            vm((t, d), BF),
            vm((2 * cols, t), F32),
            vm((3 * cols, t), BF),
            vm((3 * cols, d), BF),
            vm((nmp, cols, d), BF),
            vm((cols, t), BF),
            vm((nmp, cols, rows), BF),
            vm((rows, d), F32),
            vm((rows, d), BF),
            vm((heads, 2 * HEAD, t), BF),
            vm((heads, t, 2 * HEAD), BF),
            vm((heads, HEAD + 16, t), BF),
            vm((heads, HEAD + 16, rows), F32),
            vm((2, ndp, drow, unit), BF),
            vm((2, ndp, drow, unit), BF),
            vm((rows, d), BF),
            vm((rows, d), BF),
            vm((rows, d), BF),
            vm((d, 2 * rows), BF),
            vm((d, 2 * rows), BF),
            vm((2 * rows, unit), BF),
            vm((2 * rows, unit), BF),
            vm((2 * rows, d), F32),
            vm((2 * rows, d), F32),
            vm((2, d, unit), BF),
            vm((2, d, unit), BF),
            vm((rows, d), BF),
            vm((rows, d), BF),
            dma((nsend,)),
            dma((nsend,)),
            dma((nlocal,)),
        ],
        compiler_params=params(collective_id=4, has_side_effects=True),
        cost_estimate=cost(40e9, 60 * 2**20),
        name="front",
    )(tok, wup, wdn, cot, wq, wo, ids, *vecs)


def three_sum(m, sel):
    return sum(nn(p.astype(BF), sel) for p in three(m))


def pack_vectors(main, gb0, gb1, w, small, vt):
    nmp, nz = vt.shape[0], vt.shape[1]
    n, d = nmp * nz * 2, main.shape[1]
    s = lax.broadcasted_iota(jnp.int32, (n, 8, d), 0)
    v = lax.broadcasted_iota(jnp.int32, (n, 8, d), 1)
    l = lax.broadcasted_iota(jnp.int32, (n, 8, d), 2)
    per = n // nmp
    dev = (s % per) * nmp + s // per
    sub = lax.broadcasted_iota(jnp.int32, (d, 128), 0)
    lane = lax.broadcasted_iota(jnp.int32, (d, 128), 1)
    m = jnp.where(l // small == dev, main[None], 0.0).reshape(n * 8, d)
    sel = jnp.where(sub % small == lane, 1.0, 0.0).astype(BF)
    a = three_sum(m, sel).reshape(n, 8, 128)
    wide = nmp * small
    here = (l // wide == dev % per) & (v == 0)
    m = jnp.where(here & (dev // per == w.mp), gb0[None], 0.0)
    m = m + jnp.where(here & (dev // per == w.xm), gb1[None], 0.0)
    sel = jnp.where(sub % wide == lane, 1.0, 0.0).astype(BF)
    b = three_sum(m.reshape(n * 8, d), sel).reshape(n, 8, 128)
    vt[...] = jnp.concatenate([a, b], axis=1).reshape(vt.shape)


def back_kernel(nz, heads, small, *refs):
    g_own, g_send, o_own, o_send, mid, cot, att_own, wot, wt, low = refs[:10]
    att, raw, normed, tok_all, dwu, dwd, lse, rowv, gains, ids, gbias = refs[10:21]
    res_o, gtok_o, gq_o, go_o, gu_o, gd_o, vec_o = refs[21:28]
    (
        f1, f2, f3, ggot, ogot, cotv, attov, wotv, wtv, lowv, attv, rawv, dwdv,
        rxu, ryu, ru, rzu, ryd, rzd, rd, rxd, gattv, doutv, gwov, rco, go2, rxo, gov, ryo, ro, rzo,
        gprojv, qa, ka, va, da, dk, dv, dqa, tokv, normv, acc, gnv, rgc, rgx, dwqv, ryq, rq, rzq, sumv, ggv, vt, rv1, rv2, rv3, va4, rv4,
        ss, rs, ls,
    ) = refs[28:]
    w = Where(nz)
    dp, mp, z, y = w.dp, w.mp, w.z, w.y
    cols = heads * HEAD
    t = lowv.shape[1]
    rows, d = f1.shape
    nmp = t // rows
    greet(w.all)
    tx = Sender(ss, rs)
    count = [0]
    zto = [(z + k) % nz for k in range(nz)]

    def load(src, dst):
        cp = pltpu.make_async_copy(src, dst, ls.at[count[0]])
        cp.start()
        count[0] += 1
        return cp

    l1 = [load(g_send, ggot), load(g_own, f1), load(mid, f2), load(cot, cotv), load(wot, wotv)]
    l2 = [load(o_send, ogot), load(o_own, f3), load(att_own, attov), load(low, lowv), load(att, attv)]
    dy = tx.send(dwd.at[:, :, 1 - y], ryd, w.py)
    ux = [tx.send(dwu.at[1, 0], rxu.at[0], w.px)]
    l3 = [load(wt, wtv), load(raw, rawv)]
    l4 = load(dwd.at[:, :, y], dwdv)

    for cp in l1:
        cp.wait()
    gy = cotv[...].astype(F32)
    g = f1[...] + ggot[...].astype(F32)
    hat, r = norm_rows(f2[...])
    e = g * rowv[5:6, :]
    m1 = jnp.mean(e, axis=-1, keepdims=True)
    m2 = jnp.mean(e * hat, axis=-1, keepdims=True)
    gm = gy + (e - m1 - hat * m2) * r
    sumv[...] = jnp.zeros_like(sumv)
    for k, v in enumerate((gm, g * hat, g, gy)):
        sumv[4 + k : 5 + k, :] = jnp.sum(v, axis=0, keepdims=True)
    f1[...] = gm
    gmb = gm.astype(BF)
    gattv[...] = nt(wotv[...], gmb).astype(BF).reshape(nmp, cols, rows)

    def block(m):
        return pl.ds(pl.multiple_of(m * rows, rows), rows)

    ax = tx.send(gattv.at[w.xm], doutv.at[:, block(mp)], w.px)
    ad = tx.send(gattv.at[w.dm], doutv.at[:, block(mp)], w.pd)
    ac = tx.send(gattv.at[w.cm], doutv.at[:, block(mp)], w.pc)
    ux += [tx.send(dwu.at[1, k], rxu.at[k], w.px) for k in range(1, nz)]
    own = load(gattv.at[mp], doutv.at[:, block(mp)])
    for cp in l2:
        cp.wait()
    res_o[...] = (f2[...] + f3[...] + ogot[...].astype(F32) + rowv[7:8, :]).astype(BF)
    gw = nt(gm.T.astype(BF), attov[...]).astype(BF)
    for m in range(nmp):
        gwov[m] = gw[:, m * cols : (m + 1) * cols].reshape(gwov.shape[1:])
    oc = [tx.send(gwov.at[w.cm], rco.at[0], w.pc), tx.send(gwov.at[w.dm], rco.at[1], w.pc)]
    for cp in l3:
        cp.wait()
    ggv[...] = jnp.zeros_like(ggv)

    def attention(qa, ka, va, da, dk, dv):
        def build(m, _):
            ts = block(m)
            r, _, mk = masks(ids[:, ts])
            mk = mk.astype(BF)
            one = jnp.where(r < 3, 1.0, 0.0).astype(BF)
            for h in range(heads):
                k = lowv[cols + h * HEAD : cols + (h + 1) * HEAD, ts]
                ka[h, ts, :] = jnp.concatenate([k, mk], axis=0).T
                v = lowv[2 * cols + h * HEAD : 2 * cols + (h + 1) * HEAD, ts]
                va[h, ts, :] = jnp.concatenate([v, one], axis=0).T
            return 0

        lax.fori_loop(0, nmp, build, 0)
        dk[...] = jnp.zeros_like(dk)
        dv[...] = jnp.zeros_like(dv)

        def row(i):
            qi = block(i)
            r, mq, _ = masks(ids[:, qi])
            for h in range(heads):
                hs = slice(h * HEAD, (h + 1) * HEAD)
                qa[h, 0:HEAD, :] = lowv[hs, qi]
                a, b, c = three(lse[h : h + 1, qi] * (-1.0 / SCALE))
                aug = jnp.where(r == 32, a, jnp.where(r == 33, b, jnp.where(r == 34, c, mq)))
                qa[h, HEAD:, :] = aug.astype(BF)
                do = doutv[hs, qi]
                delta = jnp.sum(do.astype(F32) * attv[hs, qi].astype(F32), axis=0, keepdims=True)
                a, b, c = three(-delta)
                da[h, 0:HEAD, :] = do
                da[h, HEAD:, :] = jnp.where(
                    r == 0, a, jnp.where(r == 1, b, jnp.where(r == 2, c, 0.0))
                ).astype(BF)
            dqa[...] = jnp.zeros_like(dqa)

            def tile(j, _):
                kj = block(j)
                s = [nn(ka[h, kj, :], qa[h]) for h in range(heads)]
                e = [nn(va[h, kj, :], da[h]) for h in range(heads)]
                p = [jnp.exp2(v * (SCALE * LOG2E)) for v in s]
                ds = [(p[h] * e[h]).astype(BF) for h in range(heads)]
                for h in range(heads):
                    hs = slice(h * HEAD, (h + 1) * HEAD)
                    dv[hs, kj] += nt(da[h, 0:HEAD, :], p[h].astype(BF))
                    dk[hs, kj] += nt(lowv[hs, qi], ds[h])
                    dqa[hs, :] += nn(lowv[cols + h * HEAD : cols + (h + 1) * HEAD, kj], ds[h])
                return 0

            lax.fori_loop(jnp.maximum(i - 2, 0), jnp.minimum(i + 3, nmp), tile, 0)
            for h in range(heads):
                hs = slice(h * HEAD, (h + 1) * HEAD)
                v, gg = head_back(rawv[hs, qi], gains[hs, :], dqa[hs, :] * SCALE)
                gprojv[hs, qi] = v.astype(BF)
                ggv[hs, :] += gg

        own.wait()
        row(mp)
        for cp in oc:
            cp.wait_recv()
        go2[...] = (gwov[w.xm].astype(F32) + rco[1].astype(F32)).astype(BF)
        oxx = tx.send(go2, rxo, w.px)
        ac.wait_recv()
        row(w.cm)
        l4.wait()
        dy.wait_recv()
        for k in range(2):
            ryd[k] = (ryd[k].astype(F32) + dwdv[k].astype(F32)).astype(BF)
        l9 = [load(dwu.at[0, k], dwdv.at[:, k]) for k in range(nz)]
        dz = [tx.send(ryd.at[:, zto[k]], rzd.at[k - 1], w.pz[k]) for k in range(1, nz)]
        ax.wait_recv()
        row(w.xm)
        for cp in ux:
            cp.wait_recv()
        for cp in l9:
            cp.wait()
        for k in range(nz):
            rxu[k] = (rxu[k].astype(F32) + dwdv[:, k].astype(F32)).astype(BF)
        uy = tx.send(rxu.at[:, 1 - y], ryu, w.py)
        ad.wait_recv()
        row(w.dm)
        oxx.wait_recv()
        gov[...] = (gwov[mp].astype(F32) + rco[0].astype(F32) + rxo[...].astype(F32)).astype(BF)
        oy = tx.send(gov.at[:, 1 - y], ryo, w.py)

        def keys(m, _):
            ts = block(m)
            pad = ids[:, ts] < 0
            for h in range(heads):
                hs = slice(h * HEAD, (h + 1) * HEAD)
                ps = slice(cols + h * HEAD, cols + (h + 1) * HEAD)
                v, gg = head_back(rawv[ps, ts], gains[ps, :], dk[hs, ts] * SCALE)
                gprojv[ps, ts] = v.astype(BF)
                ggv[ps, :] += gg
                v = dv[hs, ts] + jnp.where(pad, doutv[hs, ts].astype(F32), 0.0)
                gprojv[2 * cols + h * HEAD : 2 * cols + (h + 1) * HEAD, ts] = v.astype(BF)
            return 0

        lax.fori_loop(0, nmp, keys, 0)
        return dz, uy, oy

    dz, uy, oy = attention(qa, ka, va, da, dk, dv)

    def projections(tokv, normv, acc):
        acc[...] = jnp.zeros_like(acc)

        def part(m):
            return tn(gprojv[:, block(m)], wtv[...])

        def fetch(n, m):
            return load(normed.at[block(m), :], normv.at[n % 2]), load(tok_all.at[m], tokv.at[n % 2])

        def rest(n, m, g, copies):
            for cp in copies:
                cp.wait()
            acc[...] += nn(gprojv[:, block(m)], normv[n % 2])
            hat, _ = norm_rows(tokv[n % 2].astype(F32))
            sumv[0:1, :] += jnp.sum(g * hat, axis=0, keepdims=True)
            sumv[1:2, :] += jnp.sum(g, axis=0, keepdims=True)

        l5, l6 = fetch(0, w.dm), fetch(1, w.xm)
        g = part(w.dm)
        gnv[0] = g.astype(BF)
        c1 = tx.send(gnv.at[0], rgc.at[1], w.pc)
        f2[...] = part(w.xm)
        c1.wait_recv()
        gnv[1] = (f2[...] + rgc[1].astype(F32)).astype(BF)
        gxx = tx.send(gnv.at[1], rgx, w.px)
        rest(0, w.dm, g, l5)
        l7 = fetch(2, w.cm)
        rest(1, w.xm, f2[...], l6)
        l8 = fetch(3, mp)
        g = part(w.cm)
        tx.sent(c1)
        gnv[0] = g.astype(BF)
        c2 = tx.send(gnv.at[0], rgc.at[0], w.pc)
        rest(2, w.cm, g, l7)
        f2[...] = part(mp)
        rest(3, mp, f2[...], l8)
        dwqv[...] = acc[...].T.astype(BF).reshape(dwqv.shape)
        qy = tx.send(dwqv.at[:, 1 - y], ryq, w.py)
        lane = lax.broadcasted_iota(jnp.int32, (cols, d), 1)
        pick = lane == lax.broadcasted_iota(jnp.int32, (cols, d), 0) + mp * cols
        for i in range(2):
            v = jnp.where(pick, ggv[i * cols : (i + 1) * cols, :], 0.0)
            sumv[2 + i : 3 + i, :] = jnp.sum(v, axis=0, keepdims=True)
        pack_vectors(sumv[...], gbias[0, 0:1, :], gbias[1, 0:1, :], w, small, vt)
        v1 = [tx.send(vt.at[w.cm], rv1.at[0], w.pc), tx.send(vt.at[w.dm], rv1.at[1], w.pc)]
        uy.wait_recv()
        ru[...] = (rxu[:, y].astype(F32) + ryu[...].astype(F32)).astype(BF)
        uz = [tx.send(ru.at[zto[k]], rzu.at[k - 1], w.pz[k]) for k in range(1, nz)]
        for cp in v1:
            cp.wait_recv()
        vt[w.xm] = vt[w.xm] + rv1[1]
        v2 = tx.send(vt.at[w.xm], rv2, w.px)
        oy.wait_recv()
        ro[...] = (gov[:, y].astype(F32) + ryo[...].astype(F32)).astype(BF)
        oz = [tx.send(ro.at[zto[k]], rzo.at[k - 1], w.pz[k]) for k in range(1, nz)]
        for cp in dz:
            cp.wait_recv()
        tot = ryd[:, z].astype(F32)
        for k in range(nz - 1):
            tot = tot + rzd[k].astype(F32)
        rd[...] = tot[1].astype(BF)
        dx = tx.send(rd, rxd, w.px)
        gd_o[...] = tot[0]
        qy.wait_recv()
        rq[...] = (dwqv[:, y].astype(F32) + ryq[...].astype(F32)).astype(BF)
        qz = [tx.send(rq.at[zto[k]], rzq.at[k - 1], w.pz[k]) for k in range(1, nz)]
        v2.wait_recv()
        vt[mp] = vt[mp] + rv1[0] + rv2[...]
        v3 = tx.send(vt.at[mp, :, 1 - y], rv3, w.py)
        c2.wait_recv()
        f2[...] += rgc[0].astype(F32)
        v3.wait_recv()
        va4[...] = vt[mp, :, y] + rv3[...]
        v4 = [tx.send(va4.at[zto[k]], rv4.at[k - 1], w.pz[k]) for k in range(1, nz)]

        def last(copies, own, got, out):
            for cp in copies:
                cp.wait_recv()
            tot = own.astype(F32)
            for k in range(nz - 1):
                tot = tot + got[k].astype(F32)
            out[...] = tot

        last(uz, ru[z], rzu, gu_o)
        last(oz, ro[z], rzo, go_o)
        last(v4, va4[z], rv4, vec_o)
        dx.wait_recv()
        gd_o[...] += rxd[...].astype(F32)
        last(qz, rq[z], rzq, gq_o)
        gxx.wait_recv()
        g = f2[...] + rgx[...].astype(F32)
        hat, r = norm_rows(tokv[1].astype(F32))
        e = g * rowv[0:1, :]
        m1 = jnp.mean(e, axis=-1, keepdims=True)
        m2 = jnp.mean(e * hat, axis=-1, keepdims=True)
        gtok_o[...] = (f1[...] + (e - m1 - hat * m2) * r).astype(BF)

    projections(tokv, normv, acc)
    tx.finish()


def back(hbm, small_in, nz, heads, small):
    g_own, dwu = hbm[0], hbm[14]
    rows, d = g_own.shape
    drow, unit = dwu.shape[3], dwu.shape[4]
    cols = heads * HEAD
    nmp = d // cols
    t = nmp * rows
    v = pltpu.VMEM
    dma = pltpu.SemaphoreType.DMA
    scratch = [
        v((rows, d), F32), v((rows, d), F32), v((rows, d), F32),
        v((rows, d), BF), v((rows, d), BF), v((rows, d), BF), v((d, rows), BF), v((d, d), BF),
        v((3 * cols, d), BF), v((3 * cols, t), BF), v((cols, t), BF), v((2 * cols, t), F32),
        v((2, nz, drow, unit), BF),
        v((nz, 2, drow, unit), BF), v((nz, drow, unit), BF), v((nz, drow, unit), BF), v((nz - 1, drow, unit), BF),
        v((2, nz, drow, unit), BF), v((nz - 1, 2, drow, unit), BF), v((drow, unit), BF), v((drow, unit), BF),
        v((nmp, cols, rows), BF), v((cols, t), BF),
        v((nmp, nz, 2, drow, cols), BF), v((2, nz, 2, drow, cols), BF), v((nz, 2, drow, cols), BF),
        v((nz, 2, drow, cols), BF), v((nz, 2, drow, cols), BF),
        v((nz, drow, cols), BF), v((nz, drow, cols), BF), v((nz - 1, drow, cols), BF),
        v((3 * cols, t), BF),
        v((heads, 2 * HEAD, rows), BF), v((heads, t, 2 * HEAD), BF), v((heads, t, 2 * HEAD), BF),
        v((heads, 2 * HEAD, rows), BF), v((cols, t), F32), v((cols, t), F32), v((cols, rows), F32),
        v((2, rows, d), BF), v((2, rows, d), BF), v((3 * cols, d), F32),
        v((2, rows, d), BF), v((2, rows, d), BF), v((rows, d), BF),
        v((nz, 2, drow, 3 * cols), BF), v((nz, drow, 3 * cols), BF), v((nz, drow, 3 * cols), BF),
        v((nz - 1, drow, 3 * cols), BF),
        v((8, d), F32), v((2 * cols, 1), F32),
        v((nmp, nz, 2, 16, 128), F32), v((2, nz, 2, 16, 128), F32), v((nz, 2, 16, 128), F32),
        v((nz, 16, 128), F32), v((nz, 16, 128), F32), v((nz - 1, 16, 128), F32),
        dma((64,)), dma((64,)), dma((32,)),
    ]
    return pl.pallas_call(
        functools.partial(back_kernel, nz, heads, small),
        out_shape=(
            sds((rows, d), BF),
            sds((rows, d), BF),
            sds((drow, 3 * cols), F32),
            sds((drow, cols), F32),
            sds((drow, unit), F32),
            sds((drow, unit), F32),
            sds((16, 128), F32),
        ),
        in_specs=[ANY] * len(hbm) + [VM] * len(small_in),
        out_specs=(VM,) * 7,
        scratch_shapes=scratch,
        compiler_params=params(collective_id=5, has_side_effects=True),
        cost_estimate=cost(40e9, 60 * 2**20),
        name="back",
    )(*hbm, *small_in)


def spans(ids):
    b = ids.reshape(-1, TB)
    low = jnp.min(jnp.where(b < 0, 1000, b), axis=1)
    high = jnp.max(b, axis=1)
    n = b.shape[0]
    k = jnp.arange(n)
    lo = jnp.sum((high[None, :] < low[:, None]) & (k[None, :] <= k[:, None]), axis=1)
    hi = jnp.sum(low[None, :] <= high[:, None], axis=1)
    return jnp.concatenate([lo, hi]).astype(jnp.int32)


def solution(mesh):
    ndp, nmp = mesh.shape["dp"], mesh.shape["mp"]
    ndev, nz = ndp * nmp, ndp // 2

    def permute(v, kind, k=0):
        pairs = []
        for d in range(ndp):
            for m in range(nmp):
                z, y, x, c = d // 2, d % 2, m // 2, m % 2
                if kind == "core":
                    c = 1 - c
                if kind == "x":
                    x = 1 - x
                if kind == "y":
                    y = 1 - y
                if kind == "z":
                    z = (z + k) % nz
                pairs.append((d * nmp + m, (z * 2 + y) * nmp + x * 2 + c))
        return lax.ppermute(v, ("dp", "mp"), pairs)

    def columns(w, first, second):
        if w.shape[0] % 16:
            own = lax.all_gather(w, "dp", axis=0, tiled=True)[None]
            return [own, permute(own, "x")]
        s = jnp.stack([w] + [permute(w, "z", k) for k in range(1, nz)])
        got = {(0, 0): s}
        one = permute(s, first)
        two = permute(s, second)
        both = permute(one, second)
        got[(0, 1)] = one if first == "y" else two
        got[(1, 0)] = two if first == "y" else one
        got[(1, 1)] = both
        return [got[(0, 0)], got[(0, 1)], got[(1, 0)], got[(1, 1)]]

    def body(
        tokens,
        picture_ids,
        w_qkv,
        w_out,
        w_up,
        w_down,
        ln1_gain,
        ln1_bias,
        q_gain,
        k_gain,
        out_bias,
        ln2_gain,
        ln2_bias,
        up_bias,
        down_bias,
        cotangent,
    ):
        rows, d = tokens.shape[1], tokens.shape[2]
        drow = w_qkv.shape[0]
        cols = w_qkv.shape[2]
        heads = cols // HEAD
        unit = w_up.shape[1]
        dp, mp = lax.axis_index("dp"), lax.axis_index("mp")
        z, y, x, c = dp // 2, dp % 2, mp // 2, mp % 2
        tok, cot = tokens[0], cotangent[0]
        ids = picture_ids
        span = spans(ids[0])
        whole = drow % 16 == 0 and ndev == 32

        vs = [ln1_gain, ln1_bias, q_gain, k_gain, out_bias, ln2_gain, ln2_bias, down_bias, up_bias]
        small = vs[0].shape[0]
        used = 8 * small + up_bias.shape[0]
        if whole:
            (
                normed,
                raw,
                tok_all,
                low,
                wt,
                wot,
                att,
                att_own,
                mid,
                dwu,
                dwd,
                o_own,
                g_own,
                o_got,
                g_got,
                lse,
                rowv,
                gains,
                gbias,
            ) = front(
                tok,
                w_qkv.transpose(1, 0, 2),
                w_out,
                w_up,
                w_down,
                [v.reshape(1, -1) for v in vs],
                cot,
                ids,
                ndp,
                nmp,
            )
            att_own = att_own.reshape(d, rows)
            shape = (2, nz, 2, drow, unit)
            res, gtok, gqw, gow, gup, gdn, vt = back(
                (g_own, g_got, o_own, o_got, mid, cot, att_own, wot.reshape(d, d), wt, low)
                + (att, raw, normed, tok_all, dwu.reshape(shape), dwd.reshape(shape)),
                (lse, rowv, gains, ids, gbias),
                nz,
                heads,
                small,
            )
            vg = [vt[i, :small] for i in range(8)] + [vt[8, : nmp * small]]
            return (
                res[None],
                gtok[None],
                gqw.reshape(drow, 3, cols),
                gow,
                gup,
                gdn,
                *vg[:7],
                vg[8],
                vg[7],
            )
        else:
            flat = jnp.concatenate(vs)
            vec = jnp.pad(flat, (0, 1024 - used)).reshape(8, 128)
            wcat = jnp.concatenate([w_qkv.reshape(drow, 3 * cols), w_out], axis=1)
            tok_all, w_all, vec_all = gather_all(tok, wcat, vec, ndp, nmp)
            vec_all = vec_all.reshape(nmp, ndp, 1024).transpose(1, 0, 2).reshape(ndev, 1024)
            gain1, shift1, qg, kg, obias, gain2, shift2, dbias = [
                vec_all[:, i * small : (i + 1) * small].reshape(1, d) for i in range(8)
            ]
            ubias = vec_all[:, 8 * small : used].reshape(nmp, unit)
            gains = jnp.concatenate(
                [
                    lax.dynamic_slice_in_dim(qg[0], mp * cols, cols),
                    lax.dynamic_slice_in_dim(kg[0], mp * cols, cols),
                ]
            ).reshape(2 * cols, 1)

            ups = columns(w_up, "y", "x")
            downs = columns(w_down, "x", "y")
            cot_other = permute(cot, "core")

            normed, raw, low, wt = project(
                tok_all, w_all.reshape(d, 3 * cols + w_out.shape[1]), gain1, shift1, gains, heads
            )
            wo0 = wt[3 * cols :]
            wo1 = permute(wo0, "x")
            wo2, wo3 = permute(wo0, "core"), permute(wo1, "core")
            wos = (wo0, wo1, wo2, wo3)
            att, lse = attend(span, low, ids, heads)
            att_own = swap(att, True, nmp, 1).reshape(d, rows)
            mid, n2 = middle_part(att_own, wos, tok, obias, gain2, shift2)
            n2_other = permute(n2, "core")
        o_own, o_send, g_own, g_send, dwu, dwd, gbias = feed(
            n2, n2_other, cot, cot_other, ubias, ups, downs, nz
        )
        g_got = permute(g_send, "core")
        gmid, gatt, gwo, sums2 = middle_back(g_own, g_got, mid, cot, att_own, wos, gain2, nmp)
        o_got = permute(o_send, "core")
        result = (mid + o_own + o_got.astype(F32) + dbias).astype(BF)
        dout = swap(gatt, False, nmp, 2)
        gproj, ggain = attend_back(span, low, raw, att, lse, dout, ids, gains, heads)
        order = jnp.stack([mp, x * 2 + 1 - c, (1 - x) * 2 + c, (1 - x) * 2 + 1 - c]).astype(jnp.int32)
        gn, gwq, sums1 = project_back(order, gproj, normed, tok_all, wt[: 3 * cols])
        got = permute(gn[1::2], "core")
        mine = gn[0::2].astype(F32) + got.astype(F32)
        far = permute(mine[1].astype(BF), "x")
        gnormed = mine[0] + far.astype(F32)
        grad_tokens = tokens_back(gnormed, tok, gain1, gmid)

        def pick(v, i):
            return lax.dynamic_index_in_dim(v, i, 0, keepdims=False)

        def along(v, kind):
            i = {"x": None, "y": y}[kind]
            if i is None:
                keep, send = v[0], v[1]
            else:
                keep, send = pick(v, i), pick(v, 1 - i)
            return (keep.astype(F32) + permute(send, kind).astype(F32)).astype(BF)

        def along_z(v):
            total = pick(v, z).astype(F32)
            for k in range(1, nz):
                total = total + permute(pick(v, (z + k) % nz), "z", k).astype(F32)
            return total

        def over_dp(v):
            if drow % 16:
                return lax.psum_scatter(v.astype(F32), "dp", scatter_dimension=0, tiled=True)
            v = v.reshape(nz, 2, drow, v.shape[-1]).transpose(1, 0, 2, 3)
            return along_z(along(v, "y"))

        def reduce_columns(v, y_first):
            if drow % 16 or not y_first:
                return over_dp(along(v, "x"))
            v = v.reshape(2, nz, 2, drow, unit).transpose(2, 0, 1, 3, 4)
            return along_z(along(along(v, "y"), "x"))

        grad_up = reduce_columns(dwu, False)
        grad_down = reduce_columns(dwd, True)
        mine_o = jnp.stack([pick(gwo, mp), pick(gwo, (1 - x) * 2 + c)])
        send_o = jnp.stack([pick(gwo, x * 2 + 1 - c), pick(gwo, (1 - x) * 2 + 1 - c)])
        go = (mine_o.astype(F32) + permute(send_o, "core").astype(F32)).astype(BF)
        go = along(go, "x")
        grad_att = over_dp(jnp.concatenate([gwq, go], axis=1))

        def spread(v, at, size):
            return lax.dynamic_update_slice_in_dim(jnp.zeros((size,), F32), v, at, 0)

        gq = spread(ggain[:cols, 0], mp * cols, d)
        gk = spread(ggain[cols:, 0], mp * cols, d)
        gb = spread(gbias[0, 0], mp * unit, nmp * unit)
        gb = gb + spread(gbias[1, 0], ((1 - x) * 2 + c) * unit, nmp * unit)
        eight = jnp.stack([sums1[0], sums1[1], gq, gk, sums2[0], sums2[1], sums2[2], sums2[3]])
        parts = jnp.concatenate(
            [
                eight.reshape(8, ndev, small).transpose(1, 0, 2).reshape(ndev, 8 * small),
                gb.reshape(ndev, used - 8 * small),
            ],
            axis=1,
        )
        parts = jnp.pad(parts, ((0, 0), (0, 1024 - used))).reshape(ndev, 8, 128)
        tot = vector_sums(parts, ndp, nmp).reshape(1024)
        vgrads = [tot[i * small : (i + 1) * small] for i in range(8)] + [tot[8 * small : used]]

        return (
            result[None],
            grad_tokens[None],
            grad_att[:, : 3 * cols].reshape(drow, 3, cols),
            grad_att[:, 3 * cols :],
            grad_up,
            grad_down,
            vgrads[0],
            vgrads[1],
            vgrads[2],
            vgrads[3],
            vgrads[4],
            vgrads[5],
            vgrads[6],
            vgrads[8],
            vgrads[7],
        )

    vec_spec = P(("dp", "mp"))
    return jax.shard_map(
        body,
        mesh=mesh,
        in_specs=(
            P("dp", "mp", None),
            P("dp", None),
            P("dp", None, "mp"),
            P("dp", "mp"),
            P("dp", "mp"),
            P("dp", "mp"),
        )
        + (vec_spec,) * 9
        + (P("dp", "mp", None),),
        out_specs=(
            P("dp", "mp", None),
            P("dp", "mp", None),
            P("dp", None, "mp"),
            P("dp", "mp"),
            P("dp", "mp"),
            P("dp", "mp"),
        )
        + (vec_spec,) * 9,
        check_vma=False,
    )
```

```python
import functools

import jax
import jax.numpy as jnp
from jax import lax
from jax.experimental import pallas as pl
from jax.experimental.pallas import tpu as pltpu
from jax.sharding import PartitionSpec as P

F32 = jnp.float32
BF = jnp.bfloat16
HEAD = 64
EPS = 1e-06
TB = 512
BIG = 32768.0
LOG2E = 1.4426950408889634
MESH = pl.DeviceIdType.MESH
ANY = pl.BlockSpec(memory_space=pl.ANY)
VM = pl.BlockSpec(memory_space=pltpu.VMEM)
SM = pl.BlockSpec(memory_space=pltpu.SMEM)
VLIM = 60 * 1024 * 1024


def nn(a, b):
    return lax.dot_general(a, b, (((1,), (0,)), ((), ())), preferred_element_type=F32)


def nt(a, b):
    return lax.dot_general(a, b, (((1,), (1,)), ((), ())), preferred_element_type=F32)


def tn(a, b):
    return lax.dot_general(a, b, (((0,), (0,)), ((), ())), preferred_element_type=F32)


def sds(shape, dtype):
    return jax.ShapeDtypeStruct(shape, dtype)


def params(**kw):
    return pltpu.CompilerParams(vmem_limit_bytes=VLIM, **kw)


def cost(flops, nbytes, trans=0):
    return pl.CostEstimate(flops=int(flops), bytes_accessed=int(nbytes), transcendentals=int(trans))


def rcopy(src, dst, ssem, rsem, peer):
    return pltpu.make_async_remote_copy(
        src_ref=src,
        dst_ref=dst,
        send_sem=ssem,
        recv_sem=rsem,
        device_id=peer,
        device_id_type=MESH,
    )


def greet(peers):
    bar = pltpu.get_barrier_semaphore()
    for p in peers:
        pl.semaphore_signal(bar, inc=1, device_id=p, device_id_type=MESH)
    pl.semaphore_wait(bar, len(peers))


def gather_kernel(
    nz, nc, tok, w, vec, tok_all, w_all, vec_all, loc, zs, zr, ys, yr, xs, xr, cs, cr, tx, rx, tc, rc
):
    dp, mp = lax.axis_index("dp"), lax.axis_index("mp")
    z, y, x, c = dp // 2, dp % 2, mp // 2, mp % 2
    xm, cm, dm = (1 - x) * 2 + c, x * 2 + 1 - c, (1 - x) * 2 + 1 - c
    ypeer, xpeer, cpeer = (z * 2 + 1 - y, mp), (dp, xm), (dp, cm)
    zpeers = [(((z + k) % nz) * 2 + y, mp) for k in range(1, nz)]
    greet(zpeers + [ypeer, xpeer, cpeer])
    rows = tok.shape[0] // nc
    xt = []
    for i in range(nc):
        part = pl.ds(i * rows, rows)
        cp = rcopy(tok.at[part], tok_all.at[mp, part], tx.at[i], rx.at[i], xpeer)
        cp.start()
        xt.append(cp)
    zc = []
    for k in range(1, nz):
        for kind, (src, dst) in enumerate(((vec, vec_all.at[mp, dp]), (w, w_all.at[dp]))):
            cp = rcopy(src, dst, zs.at[kind, k], zr.at[kind, k], zpeers[k - 1])
            cp.start()
            zc.append(cp)
    yc = []
    for kind, (src, dst) in enumerate(((vec, vec_all.at[mp, dp]), (w, w_all.at[dp]))):
        cp = rcopy(src, dst, ys.at[kind, 0], yr.at[kind, 0], ypeer)
        cp.start()
        yc.append(cp)
    own_tok = rcopy(tok, tok_all.at[mp], tc.at[nc], rc.at[nc], cpeer)
    own_tok.start()
    locs = [
        pltpu.make_async_copy(tok, tok_all.at[mp], loc.at[0]),
        pltpu.make_async_copy(w, w_all.at[dp], loc.at[1]),
        pltpu.make_async_copy(vec, vec_all.at[mp, dp], loc.at[2]),
    ]
    for cp in locs:
        cp.start()
    for k in range(1, nz):
        src_dp = ((z + nz - k) % nz) * 2 + y
        for kind in range(2):
            zc[(k - 1) * 2 + kind].wait_recv()
            ref = (vec_all.at[mp, src_dp], w_all.at[src_dp])[kind]
            cp = rcopy(ref, ref, ys.at[kind, k], yr.at[kind, k], ypeer)
            cp.start()
            yc.append(cp)
    ct = []

    def forward(i):
        part = pl.ds(i * rows, rows)
        xt[i].wait_recv()
        cp = rcopy(tok_all.at[xm, part], tok_all.at[xm, part], tc.at[i], rc.at[i], cpeer)
        cp.start()
        ct.append(cp)

    forward(0)
    for cp in locs:
        cp.wait()
    for k in range(nz):
        yc[k * 2].wait_recv()
    vx = rcopy(vec_all.at[mp], vec_all.at[mp], xs, xr, xpeer)
    vx.start()
    vc0 = rcopy(vec_all.at[mp], vec_all.at[mp], cs.at[0], cr.at[0], cpeer)
    vc0.start()
    if nc > 1:
        forward(1)
    vx.wait_recv()
    vc1 = rcopy(vec_all.at[xm], vec_all.at[xm], cs.at[1], cr.at[1], cpeer)
    vc1.start()
    for i in range(2, nc):
        forward(i)
    for k in range(nz):
        yc[k * 2 + 1].wait_recv()
    for cp in ct:
        cp.wait_recv()
    own_tok.wait()
    vc0.wait()
    vc1.wait()
    vx.wait_send()
    for cp in zc + yc + xt + ct:
        cp.wait_send()


def gather_all(tok, w, vec, ndp, nmp):
    nz, nc = ndp // 2, 4
    dma = pltpu.SemaphoreType.DMA
    return pl.pallas_call(
        functools.partial(gather_kernel, nz, nc),
        out_shape=(
            sds((nmp,) + tok.shape, BF),
            sds((ndp,) + w.shape, BF),
            sds((nmp, ndp) + vec.shape, F32),
        ),
        in_specs=[ANY] * 3,
        out_specs=(ANY,) * 3,
        scratch_shapes=[
            dma((3,)),
            dma((2, nz)),
            dma((2, nz)),
            dma((2, nz)),
            dma((2, nz)),
            dma,
            dma,
            dma((2,)),
            dma((2,)),
            dma((nc,)),
            dma((nc,)),
            dma((nc + 1,)),
            dma((nc + 1,)),
        ],
        compiler_params=pltpu.CompilerParams(collective_id=0, has_side_effects=True),
        name="gather_start",
    )(tok, w, vec)


def swap_kernel(forward, nmp, src, dst, loc, ss, rs):
    dp, mp = lax.axis_index("dp"), lax.axis_index("mp")
    own = dst.shape[2] if forward else src.shape[2]
    peers = [(mp + k) % nmp for k in range(1, nmp)]
    greet([(dp, m) for m in peers])

    def ends(m):
        if forward:
            return src.at[:, pl.ds(pl.multiple_of(m * own, own), own)], dst.at[mp]
        return src.at[m], dst.at[:, pl.ds(pl.multiple_of(mp * own, own), own)]

    cps = []
    for k, m in enumerate(peers):
        s, d = ends(m)
        cp = rcopy(s, d, ss.at[k], rs.at[k], (dp, m))
        cp.start()
        cps.append(cp)
    s, d = ends(mp)
    lc = pltpu.make_async_copy(s, d, loc)
    lc.start()
    lc.wait()
    for cp in cps:
        cp.wait()


def swap(src, forward, nmp, cid):
    dma = pltpu.SemaphoreType.DMA
    if forward:
        shape = (nmp, src.shape[0], src.shape[1] // nmp)
    else:
        shape = (src.shape[1], src.shape[2] * nmp)
    return pl.pallas_call(
        functools.partial(swap_kernel, forward, nmp),
        out_shape=sds(shape, BF),
        in_specs=[ANY],
        out_specs=ANY,
        scratch_shapes=[dma, dma((nmp - 1,)), dma((nmp - 1,))],
        compiler_params=pltpu.CompilerParams(collective_id=cid, has_side_effects=True),
        name="swap_fwd" if forward else "swap_bwd",
    )(src)


def vector_kernel(ndp, nmp, src, out, got, ss, rs):
    dp, mp = lax.axis_index("dp"), lax.axis_index("mp")
    me, n = dp * nmp + mp, ndp * nmp
    peers = [(me + k) % n for k in range(1, n)]
    greet([(p // nmp, p % nmp) for p in peers])
    cps = []
    for k, p in enumerate(peers):
        cp = rcopy(src.at[p], got.at[k], ss.at[k], rs.at[k], (p // nmp, p % nmp))
        cp.start()
        cps.append(cp)
    total = src[me]
    for k, cp in enumerate(cps):
        cp.wait_recv()
        total = total + got[k]
    out[...] = total
    for cp in cps:
        cp.wait_send()


def vector_sums(parts, ndp, nmp):
    n = ndp * nmp
    dma = pltpu.SemaphoreType.DMA
    return pl.pallas_call(
        functools.partial(vector_kernel, ndp, nmp),
        out_shape=sds(parts.shape[1:], F32),
        in_specs=[VM],
        out_specs=VM,
        scratch_shapes=[pltpu.VMEM((n - 1,) + parts.shape[1:], F32), dma((n - 1,)), dma((n - 1,))],
        compiler_params=pltpu.CompilerParams(collective_id=3, has_side_effects=True),
        name="vector_sums",
    )(parts)


def norm_rows(v):
    centre = jnp.mean(v, axis=-1, keepdims=True)
    v = v - centre
    r = lax.rsqrt(jnp.mean(v * v, axis=-1, keepdims=True) + EPS)
    return v * r, r


def norm_cols(v):
    centre = jnp.mean(v, axis=0, keepdims=True)
    v = v - centre
    r = lax.rsqrt(jnp.mean(v * v, axis=0, keepdims=True) + EPS)
    return v * r, r


def qkv_kernel(heads, tok, w, gain, shift, gains, normed, raw, low, wt):
    @pl.when(pl.program_id(0) == 0)
    def _():
        wt[...] = w[...].T

    cols = heads * HEAD
    hat, _ = norm_rows(tok[0].astype(F32))
    n = (hat * gain[...] + shift[...]).astype(BF)
    normed[...] = n
    proj = nt(wt[0 : 3 * cols, :], n)
    raw[...] = proj[0 : 2 * cols]
    for h in range(2 * heads):
        part = slice(h * HEAD, (h + 1) * HEAD)
        hat, _ = norm_cols(proj[part])
        low[part, :] = (hat * gains[part, :]).astype(BF)
    low[2 * cols :, :] = proj[2 * cols :].astype(BF)


def project(tok_all, w, gain, shift, gains, heads):
    nb, rows, d = tok_all.shape
    cols = heads * HEAD
    t = nb * rows
    full = lambda shape: pl.BlockSpec(shape, lambda i: (0,) * len(shape))
    return pl.pallas_call(
        functools.partial(qkv_kernel, heads),
        grid=(nb,),
        out_shape=(
            sds((t, d), BF),
            sds((2 * cols, t), F32),
            sds((3 * cols, t), BF),
            sds((w.shape[1], w.shape[0]), BF),
        ),
        in_specs=[
            pl.BlockSpec((1, rows, d), lambda i: (i, 0, 0)),
            full(w.shape),
            full((1, d)),
            full((1, d)),
            full((2 * cols, 1)),
        ],
        out_specs=(
            pl.BlockSpec((rows, d), lambda i: (i, 0)),
            pl.BlockSpec((2 * cols, rows), lambda i: (0, i)),
            pl.BlockSpec((3 * cols, rows), lambda i: (0, i)),
            full((w.shape[1], w.shape[0])),
        ),
        compiler_params=params(),
        cost_estimate=cost(2 * t * d * 3 * cols, 12 * 2**20),
        name="project_qkv",
    )(tok_all, w, gain, shift, gains)


def masks(ids):
    t = ids.shape[1]
    r = lax.broadcasted_iota(jnp.int32, (HEAD, t), 0)
    pad = ids < 0
    mq = jnp.where((r == ids) | ((r == 31) & pad), 1.0, 0.0)
    mk = jnp.where((r <= 31) & (r != ids), -BIG, 0.0)
    mk = jnp.where((r >= 32) & (r < 35), 1.0, mk)
    return r, mq, mk


def three(v):
    a = v.astype(BF).astype(F32)
    b = (v - a).astype(BF).astype(F32)
    return a, b, v - a - b


SCALE = HEAD**-0.5


def attend_kernel(heads, nblk, span, low, ids, out, lse, qa, ka, va, acc):
    cols = heads * HEAD
    t = ids.shape[1]
    _, mq, mk = masks(ids[...])
    mq, mk = mq.astype(BF), mk.astype(BF)
    one = jnp.where(lax.broadcasted_iota(jnp.int32, (16, t), 0) == 0, 1.0, 0.0).astype(BF)
    for h in range(heads):
        qa[h, 0:HEAD, :] = low[h * HEAD : (h + 1) * HEAD, :]
        qa[h, HEAD:, :] = mq
        k = low[cols + h * HEAD : cols + (h + 1) * HEAD, :]
        ka[h, :, :] = jnp.concatenate([k, mk], axis=0).T
        va[h, 0:HEAD, :] = low[2 * cols + h * HEAD : 2 * cols + (h + 1) * HEAD, :]
        va[h, HEAD:, :] = one
    acc[...] = jnp.zeros_like(acc)

    def row(i, _):
        qi = pl.ds(pl.multiple_of(i * TB, TB), TB)

        def col(j, _):
            kj = pl.ds(pl.multiple_of(j * TB, TB), TB)
            s = [nn(ka[h, kj, :], qa[h, :, qi]) for h in range(heads)]
            p = [jnp.exp2(v * (SCALE * LOG2E)).astype(BF) for v in s]
            for h in range(heads):
                acc[h, :, qi] += nn(va[h, :, kj], p[h])
            return 0

        return lax.fori_loop(span[i], span[nblk + i], col, 0)

    lax.fori_loop(0, nblk, row, 0)
    pad = ids[...] < 0
    lse[...] = jnp.zeros_like(lse)
    for h in range(heads):
        total = jnp.where(pad, 1.0, acc[h, HEAD : HEAD + 1, :])
        value = low[2 * cols + h * HEAD : 2 * cols + (h + 1) * HEAD, :].astype(F32)
        o = jnp.where(pad, value, acc[h, 0:HEAD, :] * (1.0 / total))
        out[h * HEAD : (h + 1) * HEAD, :] = o.astype(BF)
        lse[h : h + 1, :] = jnp.log(total)


def attend(span, low, ids, heads):
    cols, t = heads * HEAD, low.shape[1]
    return pl.pallas_call(
        functools.partial(attend_kernel, heads, t // TB),
        out_shape=(sds((cols, t), BF), sds((8, t), F32)),
        in_specs=[SM, VM, VM],
        out_specs=(VM, VM),
        scratch_shapes=[
            pltpu.VMEM((heads, 2 * HEAD, t), BF),
            pltpu.VMEM((heads, t, 2 * HEAD), BF),
            pltpu.VMEM((heads, HEAD + 16, t), BF),
            pltpu.VMEM((heads, HEAD + 16, t), F32),
        ],
        compiler_params=params(),
        cost_estimate=cost(12e9, 4 * 2**20),
        name="attend",
    )(span, low, ids)


def head_back(raw, gain, grad):
    hat, r = norm_cols(raw)
    e = grad * gain
    m1 = jnp.mean(e, axis=0, keepdims=True)
    m2 = jnp.mean(e * hat, axis=0, keepdims=True)
    return (e - m1 - hat * m2) * r, jnp.sum(grad * hat, axis=1, keepdims=True)


def attend_back_kernel(
    heads, nblk, span, low, raw, att, lse, dout, ids, gains, gproj, ggain, qa, ka, va, da, dq, dk, dv
):
    cols = heads * HEAD
    t = ids.shape[1]
    r, mq, mk = masks(ids[...])
    mk = mk.astype(BF)
    one = jnp.where(r < 3, 1.0, 0.0).astype(BF)
    for h in range(heads):
        hs = slice(h * HEAD, (h + 1) * HEAD)
        qa[h, 0:HEAD, :] = low[hs, :]
        a, b, c = three(lse[h : h + 1, :] * (-1.0 / SCALE))
        m = jnp.where(r == 32, a, jnp.where(r == 33, b, jnp.where(r == 34, c, mq)))
        qa[h, HEAD:, :] = m.astype(BF)
        k = low[cols + h * HEAD : cols + (h + 1) * HEAD, :]
        ka[h, :, :] = jnp.concatenate([k, mk], axis=0).T
        v = low[2 * cols + h * HEAD : 2 * cols + (h + 1) * HEAD, :]
        va[h, :, :] = jnp.concatenate([v, one], axis=0).T
        do = dout[hs, :]
        delta = jnp.sum(do.astype(F32) * att[hs, :].astype(F32), axis=0, keepdims=True)
        a, b, c = three(-delta)
        da[h, 0:HEAD, :] = do
        da[h, HEAD:, :] = jnp.where(
            r == 0, a, jnp.where(r == 1, b, jnp.where(r == 2, c, 0.0))
        ).astype(BF)
    dq[...] = jnp.zeros_like(dq)
    dk[...] = jnp.zeros_like(dk)
    dv[...] = jnp.zeros_like(dv)

    def row(i, _):
        qi = pl.ds(pl.multiple_of(i * TB, TB), TB)

        def col(j, _):
            kj = pl.ds(pl.multiple_of(j * TB, TB), TB)
            s = [nn(ka[h, kj, :], qa[h, :, qi]) for h in range(heads)]
            d = [nn(va[h, kj, :], da[h, :, qi]) for h in range(heads)]
            p = [jnp.exp2(v * (SCALE * LOG2E)) for v in s]
            ds = [(p[h] * d[h]).astype(BF) for h in range(heads)]
            for h in range(heads):
                hs = pl.ds(h * HEAD, HEAD)
                dv[hs, kj] += nt(dout[hs, qi], p[h].astype(BF))
                dk[hs, kj] += nt(low[hs, qi], ds[h])
                dq[hs, qi] += nn(low[pl.ds(cols + h * HEAD, HEAD), kj], ds[h])
            return 0

        return lax.fori_loop(span[i], span[nblk + i], col, 0)

    lax.fori_loop(0, nblk, row, 0)
    pad = ids[...] < 0
    for h in range(heads):
        hs = slice(h * HEAD, (h + 1) * HEAD)
        for part, grad in ((0, dq), (1, dk)):
            ps = slice(part * cols + h * HEAD, part * cols + (h + 1) * HEAD)
            g, gg = head_back(raw[ps, :], gains[ps, :], grad[hs, :] * SCALE)
            gproj[ps, :] = g.astype(BF)
            ggain[ps, :] = gg
        g = dv[hs, :] + jnp.where(pad, dout[hs, :].astype(F32), 0.0)
        gproj[2 * cols + h * HEAD : 2 * cols + (h + 1) * HEAD, :] = g.astype(BF)


def attend_back(span, low, raw, att, lse, dout, ids, gains, heads):
    cols, t = heads * HEAD, low.shape[1]
    return pl.pallas_call(
        functools.partial(attend_back_kernel, heads, t // TB),
        out_shape=(sds((3 * cols, t), BF), sds((2 * cols, 1), F32)),
        in_specs=[SM] + [VM] * 7,
        out_specs=(VM, VM),
        scratch_shapes=[
            pltpu.VMEM((heads, 2 * HEAD, t), BF),
            pltpu.VMEM((heads, t, 2 * HEAD), BF),
            pltpu.VMEM((heads, t, 2 * HEAD), BF),
            pltpu.VMEM((heads, 2 * HEAD, t), BF),
            pltpu.VMEM((cols, t), F32),
            pltpu.VMEM((cols, t), F32),
            pltpu.VMEM((cols, t), F32),
        ],
        compiler_params=params(),
        cost_estimate=cost(30e9, 12 * 2**20),
        name="attend_back",
    )(span, low, raw, att, lse, dout, ids, gains)


def place_out(pieces, dest):
    mp = lax.axis_index("mp")
    x, c = mp // 2, mp % 2
    order = (mp, (1 - x) * 2 + c, x * 2 + 1 - c, (1 - x) * 2 + 1 - c)
    rows = pieces[0].shape[0]
    for piece, m in zip(pieces, order):
        dest[pl.ds(pl.multiple_of(m * rows, rows), rows), :] = piece[...]


def middle_kernel(att, w0, w1, w2, w3, tok, bias, gain, shift, mid, low, wo):
    place_out((w0, w1, w2, w3), wo)
    m = tok[...].astype(F32) + tn(att[...], wo[...]) + bias[...]
    mid[...] = m
    hat, _ = norm_rows(m)
    low[...] = (hat * gain[...] + shift[...]).astype(BF)


def middle_part(att, wos, tok, bias, gain, shift):
    rows, d = tok.shape
    return pl.pallas_call(
        middle_kernel,
        out_shape=(sds((rows, d), F32), sds((rows, d), BF)),
        in_specs=[VM] * 9,
        out_specs=(VM, VM),
        scratch_shapes=[pltpu.VMEM((d, d), BF)],
        compiler_params=params(),
        cost_estimate=cost(2 * rows * d * d, 6 * 2**20),
        name="middle",
    )(att, *wos, tok, bias, gain, shift)


def middle_back_kernel(nmp, g0, g1, mid, cot, att, *refs):
    pieces, (gain, gmid, gatt, gwo, sums, wo) = refs[:-6], refs[-6:]
    if len(pieces) > 1:
        place_out(pieces, wo)
    else:
        wo = pieces[0]
    gy = cot[...].astype(F32)
    g = g0[...] + g1[...].astype(F32)
    hat, r = norm_rows(mid[...])
    e = g * gain[...]
    m1 = jnp.mean(e, axis=-1, keepdims=True)
    m2 = jnp.mean(e * hat, axis=-1, keepdims=True)
    gm = gy + (e - m1 - hat * m2) * r
    gmid[...] = gm
    low = gm.astype(BF)
    rows = att.shape[0] // nmp
    ga = nt(wo[...], low).astype(BF)
    for m in range(nmp):
        gatt[m] = ga[m * rows : (m + 1) * rows]
    gw = nt(gm.T.astype(BF), att[...]).astype(BF)
    mp = lax.axis_index("mp")
    for m in range(nmp):
        gwo[m] = gw[:, m * rows : (m + 1) * rows]
    sums[...] = jnp.zeros_like(sums)
    for k, v in enumerate((gm, g * hat, g, gy)):
        sums[k : k + 1, :] = jnp.sum(v, axis=0, keepdims=True)


def middle_back(g0, g1, mid, cot, att, wos, gain, nmp):
    rows, d = mid.shape
    return pl.pallas_call(
        functools.partial(middle_back_kernel, nmp),
        out_shape=(
            sds((rows, d), F32),
            sds((nmp, d // nmp, rows), BF),
            sds((nmp, d, d // nmp), BF),
            sds((8, d), F32),
        ),
        in_specs=[VM] * (6 + len(wos)),
        out_specs=(VM,) * 4,
        scratch_shapes=[pltpu.VMEM((d, d), BF)],
        compiler_params=params(),
        cost_estimate=cost(4 * rows * d * d, 10 * 2**20),
        name="middle_back",
    )(g0, g1, mid, cot, att, *wos, gain)


def feed_kernel(npiece, nz, first, *refs):
    n0, n1, c0, c1, bias = refs[:5]
    pieces = refs[5 : 5 + npiece]
    out_own, out_send, g_own, g_send, dwu, dwd, gbias = refs[5 + npiece : 12 + npiece]
    wu, wd, n2, gy, n2t, gyt, acts, gps, oacc, gacc, sem = refs[12 + npiece :]
    dp, mp = lax.axis_index("dp"), lax.axis_index("mp")
    z, y, x, c = dp // 2, dp % 2, mp // 2, mp % 2
    copies = []
    half = npiece // 2
    for a, piece in enumerate(pieces):
        dest = (wu, wd)[a // half]
        rel = a % half
        count, rows = piece.shape[0], piece.shape[1]
        for k in range(count):
            if half <= 2:
                at, colidx = 0, (k if half == 1 else rel)
            else:
                zz = (z + nz - k) % nz
                at = (zz * 2 + (y if rel % 2 == 0 else 1 - y)) * rows
                at, colidx = pl.multiple_of(at, rows), rel // 2
            cp = pltpu.make_async_copy(piece.at[k], dest.at[colidx, pl.ds(at, rows), :], sem.at[a, k])
            cp.start()
            copies.append(cp)
    hr = n0.shape[0]
    for i, (n, g) in enumerate(((n0, c0), (n1, c1))):
        part = slice(i * hr, (i + 1) * hr)
        n2[part, :] = n[...]
        gy[part, :] = g[...]
        n2t[:, part] = n[...].T
        gyt[:, part] = g[...].T
    oacc[...] = jnp.zeros_like(oacc)
    gacc[...] = jnp.zeros_like(gacc)
    for cp in copies:
        cp.wait()
    rows, d = n2.shape
    cw = acts.shape[1]
    per = wu.shape[2] // cw
    ones = jnp.ones((16, rows), BF)

    def chunk(i, _):
        col, off = i // per, pl.multiple_of((i % per) * cw, cw)
        cs = pl.ds(off, cw)
        m = jnp.where(col == 0, mp, (1 - x) * 2 + c)
        b = bias[pl.ds(first + m, 1), cs]
        for rb in range(rows // 256):
            rs = slice(rb * 256, (rb + 1) * 256)
            u = nn(n2[rs, :], wu[col, :, cs]) + b
            ga = nn(gy[rs, :], wd[col, :, cs])
            cdf = 0.5 + 0.5 * lax.erf(u * 0.7071067811865476)
            act = (u * cdf).astype(BF)
            gp = (ga * (cdf + u * (jnp.exp(-0.5 * u * u) * 0.3989422804014327))).astype(BF)
            acts[rs, :] = act
            gps[rs, :] = gp
            oacc[rs, :] += nt(act, wd[col, :, cs])
            gacc[rs, :] += nt(gp, wu[col, :, cs])
        dwd[col, :, cs] = nn(gyt[...], acts[...]).astype(BF)
        dwu[col, :, cs] = nn(n2t[...], gps[...]).astype(BF)
        gbias[col, :, cs] = nn(ones, gps[...])[0:8]
        return 0

    lax.fori_loop(0, 2 * per, chunk, 0)
    out_own[...] = oacc[0:hr]
    out_send[...] = oacc[hr:].astype(BF)
    g_own[...] = gacc[0:hr]
    g_send[...] = gacc[hr:].astype(BF)


def feed(n0, n1, c0, c1, bias, ups, downs, nz):
    hr, d = n0.shape
    rows, cw = 2 * hr, 256
    unit = ups[0].shape[2]
    pieces = list(ups) + list(downs)
    kmax = max(p.shape[0] for p in pieces)
    vm = pltpu.VMEM
    return pl.pallas_call(
        functools.partial(feed_kernel, len(pieces), nz, bias.shape[0] // 16 * 8),
        out_shape=(
            sds((hr, d), F32),
            sds((hr, d), BF),
            sds((hr, d), F32),
            sds((hr, d), BF),
            sds((2, d, unit), BF),
            sds((2, d, unit), BF),
            sds((2, 8, unit), F32),
        ),
        in_specs=[VM] * 5 + [ANY] * len(pieces),
        out_specs=(VM,) * 7,
        scratch_shapes=[
            vm((2, d, unit), BF),
            vm((2, d, unit), BF),
            vm((rows, d), BF),
            vm((rows, d), BF),
            vm((d, rows), BF),
            vm((d, rows), BF),
            vm((rows, cw), BF),
            vm((rows, cw), BF),
            vm((rows, d), F32),
            vm((rows, d), F32),
            pltpu.SemaphoreType.DMA((len(pieces), kmax)),
        ],
        compiler_params=params(),
        cost_estimate=cost(12 * rows * d * 2 * unit, 22 * 2**20),
        name="feed_forward",
    )(n0, n1, c0, c1, bias, *pieces)


def project_back_kernel(order, gproj, normed, tok, wt, gn, gw, sums, acc):
    @pl.when(pl.program_id(0) == 0)
    def _():
        acc[...] = jnp.zeros_like(acc)
        sums[...] = jnp.zeros_like(sums)

    acc[...] += nn(gproj[...], normed[...])
    g = tn(gproj[...], wt[...])
    gn[0] = g.astype(BF)
    hat, _ = norm_rows(tok[0].astype(F32))
    sums[0:1, :] += jnp.sum(g * hat, axis=0, keepdims=True)
    sums[1:2, :] += jnp.sum(g, axis=0, keepdims=True)

    @pl.when(pl.program_id(0) == pl.num_programs(0) - 1)
    def _():
        gw[...] = acc[...].T.astype(BF)


def project_back(order, gproj, normed, tok_all, wt):
    nb, rows, d = tok_all.shape
    n = gproj.shape[0]
    t = nb * rows
    return pl.pallas_call(
        project_back_kernel,
        grid_spec=pltpu.PrefetchScalarGridSpec(
            num_scalar_prefetch=1,
            grid=(nb,),
            in_specs=[
                pl.BlockSpec((n, rows), lambda i, o: (0, o[i])),
                pl.BlockSpec((rows, d), lambda i, o: (o[i], 0)),
                pl.BlockSpec((1, rows, d), lambda i, o: (o[i], 0, 0)),
                pl.BlockSpec((n, d), lambda i, o: (0, 0)),
            ],
            out_specs=(
                pl.BlockSpec((1, rows, d), lambda i, o: (i, 0, 0)),
                pl.BlockSpec((d, n), lambda i, o: (0, 0)),
                pl.BlockSpec((8, d), lambda i, o: (0, 0)),
            ),
            scratch_shapes=[pltpu.VMEM((n, d), F32)],
        ),
        out_shape=(sds((nb, rows, d), BF), sds((d, n), BF), sds((8, d), F32)),
        compiler_params=params(),
        cost_estimate=cost(4 * t * d * n, 14 * 2**20),
        name="project_back",
    )(order, gproj, normed, tok_all, wt)


def tokens_back(gn, tok, gain, gmid):
    hat, r = norm_rows(tok.astype(F32))
    e = gn * gain
    m1 = jnp.mean(e, axis=-1, keepdims=True)
    m2 = jnp.mean(e * hat, axis=-1, keepdims=True)
    return (gmid + (e - m1 - hat * m2) * r).astype(BF)


class Where:
    def __init__(self, nz):
        dp, mp = lax.axis_index("dp"), lax.axis_index("mp")
        z, y, x, c = dp // 2, dp % 2, mp // 2, mp % 2
        self.dp, self.mp, self.z, self.y, self.x, self.c = dp, mp, z, y, x, c
        self.xm, self.cm, self.dm = (1 - x) * 2 + c, x * 2 + 1 - c, (1 - x) * 2 + 1 - c
        self.ydp = z * 2 + 1 - y
        self.zfrom = [((z + nz - k) % nz) * 2 + y for k in range(nz)]
        self.yfrom = [((z + nz - k) % nz) * 2 + 1 - y for k in range(nz)]
        self.py, self.px, self.pc, self.pd = (self.ydp, mp), (dp, self.xm), (dp, self.cm), (dp, self.dm)
        self.pz = [None] + [(((z + k) % nz) * 2 + y, mp) for k in range(1, nz)]
        self.all = self.pz[1:] + [self.py, self.px, self.pc, self.pd]


class Sender:
    def __init__(self, ss, rs):
        self.ss, self.rs, self.n, self.open = ss, rs, 0, []

    def send(self, src, dst, peer):
        cp = rcopy(src, dst, self.ss.at[self.n], self.rs.at[self.n], peer)
        cp.start()
        self.n += 1
        self.open.append(cp)
        return cp

    def sent(self, cp):
        cp.wait_send()
        self.open = [o for o in self.open if o is not cp]

    def finish(self):
        for cp in self.open:
            cp.wait_send()


def vector_rows(vecv, small, d):
    nmp, ndp, vr, lanes = vecv.shape
    v = vecv[...].reshape(nmp * ndp * vr, lanes)
    parts = [p.astype(BF) for p in three(v)]
    lane = lax.broadcasted_iota(jnp.int32, (lanes, d), 1)
    sub = lax.broadcasted_iota(jnp.int32, (lanes, d), 0)
    s = lax.broadcasted_iota(jnp.int32, (nmp * ndp, vr, d), 0)
    col = lax.broadcasted_iota(jnp.int32, (nmp * ndp, vr, d), 2)
    dev = (s % ndp) * nmp + s // ndp

    def spread(width):
        sel = jnp.where(lane % width == sub, 1.0, 0.0).astype(BF)
        return sum(nn(p, sel) for p in parts).reshape(nmp * ndp, vr, d)

    a = jnp.sum(jnp.where(col // small == dev, spread(small), 0.0), axis=0)
    wide = nmp * small
    b = spread(wide)
    per = nmp * ndp // nmp
    ups = []
    for m in range(nmp):
        keep = (dev // per == m) & (col // wide == dev % per)
        ups.append(jnp.sum(jnp.where(keep, b, 0.0), axis=0)[8:9])
    return a[0:8], jnp.concatenate(ups, axis=0)


def front_kernel(nz, heads, small, *refs):
    tok, wup, wdn, cot = refs[:4]
    wq, wo, ids = refs[4:7]
    vecs = refs[7:16]
    normed_o, raw_o, tok_o, low_h, wt_h, wot_h, att_h, own_h, mid_h = refs[16:25]
    dwu_h, dwd_h, oown_h, gown_h, ogot_h, ggot_h = refs[25:31]
    lse, rows_o, gains, gbias = refs[31:35]
    tokv, wqv, vecv, normv, rawv, low_o, wt_o, wotv, att_o, own_o, mid_o, n2_o = refs[35:47]
    qa, ka, va, acc, wu_o, wd_o, cotv, cotx_o, n2x_o = refs[47:56]
    n2t, gyt, acts, gps, oacc, gacc, dwu, dwd, osend, gsend, ss, rs, ls = refs[56:]
    w = Where(nz)
    dp, mp = w.dp, w.mp
    cols = heads * HEAD
    t, d = normv.shape
    nmp, rows = tokv.shape[0], tokv.shape[1]
    greet(w.all)
    tx = Sender(ss, rs)
    count, late = [0], []

    def keep(src, dst, wait_late=True):
        cp = pltpu.make_async_copy(src, dst, ls.at[count[0]])
        cp.start()
        count[0] += 1
        if wait_late:
            late.append(cp)
        return cp

    nc = 4
    part = [pl.ds(i * (rows // nc), rows // nc) for i in range(nc)]
    xt = [tx.send(tok.at[part[i]], tokv.at[mp, part[i]], w.px) for i in range(nc)]
    vecv[mp, dp] = jnp.zeros(vecv.shape[2:], F32)
    for i, v in enumerate(vecs):
        vecv[mp, dp, i : i + 1, 0 : v.shape[1]] = v[...]
    ref = vecv.at[mp, dp]
    vz = [None] + [tx.send(ref, ref, w.pz[k]) for k in range(1, nz)]
    vy = [tx.send(ref, ref, w.py)]
    for i in range(3):
        wqv[dp, :, i * cols : (i + 1) * cols] = wq[i]
    wqv[dp, :, 3 * cols :] = wo[...]
    ref = wqv.at[dp]
    qz = [None] + [tx.send(ref, ref, w.pz[k]) for k in range(1, nz)]
    qy = [tx.send(ref, ref, w.py)]
    dx = tx.send(wdn, wd_o.at[1, dp], w.px)
    ux = [tx.send(wup, wu_o.at[1, dp], w.px)]
    ctok = tx.send(tok, tokv.at[mp], w.pc)
    cx = tx.send(cot, cotx_o, w.pc)
    own_tok = keep(tok, tokv.at[mp], False)
    own_w = [keep(wup, wu_o.at[0, dp], False), keep(wdn, wd_o.at[0, dp], False)]
    own_cot = keep(cot, cotv, False)
    for k in range(1, nz):
        vz[k].wait_recv()
        ref = vecv.at[mp, w.zfrom[k]]
        vy.append(tx.send(ref, ref, w.py))
    for k in range(nz):
        vy[k].wait_recv()
    vx = tx.send(vecv.at[mp], vecv.at[mp], w.px)
    vc = tx.send(vecv.at[mp], vecv.at[mp], w.pc)
    for k in range(1, nz):
        qz[k].wait_recv()
        ref = wqv.at[w.zfrom[k]]
        qy.append(tx.send(ref, ref, w.py))
    uz = [None] + [tx.send(wup, wu_o.at[0, dp], w.pz[k]) for k in range(1, nz)]
    uy = [tx.send(wup, wu_o.at[0, dp], w.py)]
    dy = [tx.send(wdn, wd_o.at[0, dp], w.py)]
    vx.wait_recv()
    vd = tx.send(vecv.at[w.xm], vecv.at[w.xm], w.pc)
    ct = []

    def forward(i):
        xt[i].wait_recv()
        ref = tokv.at[w.xm, part[i]]
        ct.append(tx.send(ref, ref, w.pc))

    forward(0)
    forward(1)
    vc.wait_recv()
    vd.wait_recv()
    main, ups = vector_rows(vecv, small, d)
    rows_o[0:8, :] = main
    rows_o[8:12, :] = ups
    rows_o[12:16, :] = jnp.zeros((4, d), F32)
    lane = lax.broadcasted_iota(jnp.int32, (cols, d), 1)
    pick = lane == lax.broadcasted_iota(jnp.int32, (cols, d), 0) + mp * cols
    for i in range(2):
        gains[i * cols : (i + 1) * cols, :] = jnp.sum(
            jnp.where(pick, main[2 + i : 3 + i], 0.0), axis=1, keepdims=True
        )
    for k in range(nz):
        qy[k].wait_recv()
    wall = wqv[...].reshape(d, 4 * cols).T
    wt_o[...] = wall[0 : 3 * cols]
    wotv[mp] = wall[3 * cols :]
    keep(wt_o, wt_h)
    one = jnp.where(lax.broadcasted_iota(jnp.int32, (16, rows), 0) == 0, 1.0, 0.0).astype(BF)

    def project(m):
        ts = pl.ds(pl.multiple_of(m * rows, rows), rows)
        hat, _ = norm_rows(tokv[m].astype(F32))
        n = (hat * rows_o[0:1, :] + rows_o[1:2, :]).astype(BF)
        normv[ts, :] = n
        proj = nt(wt_o[...], n)
        rawv[:, ts] = proj[0 : 2 * cols]
        _, mq, mk = masks(ids[:, ts])
        mq, mk = mq.astype(BF), mk.astype(BF)
        for h in range(heads):
            qs, ks = h * HEAD, cols + h * HEAD
            hat, _ = norm_cols(proj[qs : qs + HEAD])
            q = (hat * gains[qs : qs + HEAD, :]).astype(BF)
            low_o[qs : qs + HEAD, ts] = q
            qa[h, 0:HEAD, ts] = q
            qa[h, HEAD:, ts] = mq
            hat, _ = norm_cols(proj[ks : ks + HEAD])
            k = (hat * gains[ks : ks + HEAD, :]).astype(BF)
            low_o[ks : ks + HEAD, ts] = k
            ka[h, ts, :] = jnp.concatenate([k, mk], axis=0).T
            v = proj[2 * cols + h * HEAD : 2 * cols + (h + 1) * HEAD].astype(BF)
            low_o[2 * cols + h * HEAD : 2 * cols + (h + 1) * HEAD, ts] = v
            va[h, 0:HEAD, ts] = v
            va[h, HEAD:, ts] = one

    own_tok.wait()
    project(mp)
    forward(2)
    ctok.wait_recv()
    forward(3)
    project(w.cm)
    ox = tx.send(wotv.at[mp], wotv.at[mp], w.px)
    oc = tx.send(wotv.at[mp], wotv.at[mp], w.pc)
    uy[0].wait_recv()
    uw = [tx.send(wu_o.at[0, w.ydp], wu_o.at[1, w.ydp], w.px)]
    dz = [None] + [tx.send(wdn, wd_o.at[0, dp], w.pz[k]) for k in range(1, nz)]
    for cp in ct:
        cp.wait_recv()

    def both(i, _):
        project(jnp.where(i == 0, w.xm, w.dm))
        return 0

    lax.fori_loop(0, 2, both, 0)
    keep(normv, normed_o)
    keep(rawv, raw_o)
    keep(tokv, tok_o)
    keep(low_o, low_h)
    for k in range(1, nz):
        uz[k].wait_recv()
        ref = wu_o.at[0, w.zfrom[k]]
        uy.append(tx.send(ref, ref, w.py))
        ux.append(tx.send(ref, wu_o.at[1, w.zfrom[k]], w.px))
    dx.wait_recv()
    ref = wd_o.at[1, dp]
    ez = [None] + [tx.send(ref, ref, w.pz[k]) for k in range(1, nz)]
    ey = [tx.send(ref, ref, w.py)]

    def attend_row(i):
        qi = pl.ds(pl.multiple_of(i * rows, rows), rows)
        acc[...] = jnp.zeros_like(acc)

        def tile(j, _):
            kj = pl.ds(pl.multiple_of(j * rows, rows), rows)
            s = [nn(ka[h, kj, :], qa[h, :, qi]) for h in range(heads)]
            p = [jnp.exp2(v * (SCALE * LOG2E)).astype(BF) for v in s]
            for h in range(heads):
                acc[h] += nn(va[h, :, kj], p[h])
            return 0

        lax.fori_loop(jnp.maximum(i - 2, 0), jnp.minimum(i + 3, nmp), tile, 0)
        pad = ids[:, qi] < 0
        lse[:, qi] = jnp.zeros((8, rows), F32)
        for h in range(heads):
            total = jnp.where(pad, 1.0, acc[h, HEAD : HEAD + 1, :])
            value = va[h, 0:HEAD, qi].astype(F32)
            o = jnp.where(pad, value, acc[h, 0:HEAD, :] * (1.0 / total))
            att_o[h * HEAD : (h + 1) * HEAD, qi] = o.astype(BF)
            lse[h : h + 1, qi] = jnp.log(total)
        return att_o.at[:, qi]

    at = [tx.send(attend_row(w.xm), own_o.at[mp], w.px)]
    at.append(tx.send(attend_row(w.dm), own_o.at[mp], w.pd))
    for k in range(1, nz):
        uy[k].wait_recv()
        ref = wu_o.at[0, w.yfrom[k]]
        uw.append(tx.send(ref, wu_o.at[1, w.yfrom[k]], w.px))
    ox.wait_recv()
    od = tx.send(wotv.at[w.xm], wotv.at[w.xm], w.pc)
    at.append(tx.send(attend_row(w.cm), own_o.at[mp], w.pc))
    for k in range(1, nz):
        dz[k].wait_recv()
        ref = wd_o.at[0, w.zfrom[k]]
        dy.append(tx.send(ref, ref, w.py))
    own = keep(attend_row(mp), own_o.at[mp], False)
    keep(att_o, att_h)
    oc.wait_recv()
    od.wait_recv()
    keep(wotv, wot_h)
    own.wait()
    for cp in at:
        cp.wait_recv()
    keep(own_o, own_h)
    m = tokv[mp].astype(F32) + rows_o[4:5, :]
    m = m + tn(own_o[...].reshape(d, rows), wotv[...].reshape(d, d))
    mid_o[...] = m
    keep(mid_o, mid_h)
    hat, _ = norm_rows(m)
    n2_o[...] = (hat * rows_o[5:6, :] + rows_o[6:7, :]).astype(BF)
    nx = tx.send(n2_o, n2x_o, w.pc)
    own_cot.wait()
    cx.wait_recv()
    gyt[:, 0:rows] = cotv[...].T
    gyt[:, rows:] = cotx_o[...].T
    n2t[:, 0:rows] = n2_o[...].T
    for k in range(1, nz):
        ez[k].wait_recv()
        ref = wd_o.at[1, w.zfrom[k]]
        ey.append(tx.send(ref, ref, w.py))
    nx.wait_recv()
    n2t[:, rows:] = n2x_o[...].T
    unit = wu_o.shape[3]
    ones = jnp.ones((16, 2 * rows), BF)
    step = rows // 2

    def column(i, m):
        wu, wd = wu_o[i].reshape(d, unit), wd_o[i].reshape(d, unit)
        b = rows_o[pl.ds(8 + m, 1), :]
        for rb in range(4):
            rs = slice(rb * step, (rb + 1) * step)
            src = slice((rb % 2) * step, (rb % 2 + 1) * step)
            u = nn((n2_o, n2x_o)[rb // 2][src, :], wu) + b
            ga = nn((cotv, cotx_o)[rb // 2][src, :], wd)
            cdf = 0.5 + 0.5 * lax.erf(u * 0.7071067811865476)
            acts[rs, :] = (u * cdf).astype(BF)
            gps[rs, :] = (ga * (cdf + u * (jnp.exp(-0.5 * u * u) * 0.3989422804014327))).astype(BF)
        if i == 0:
            oacc[...] = nt(acts[...], wd)
            gacc[...] = nt(gps[...], wu)
        else:
            gacc[...] += nt(gps[...], wu)
            gsend[...] = gacc[rows:].astype(BF)
            gx = tx.send(gsend, ggot_h, w.pc)
            oacc[...] += nt(acts[...], wd)
            osend[...] = oacc[rows:].astype(BF)
            sent.extend([gx, tx.send(osend, ogot_h, w.pc)])
            keep(gacc.at[0:rows], gown_h)
            keep(oacc.at[0:rows], oown_h)
        dwd[i] = nn(gyt[...], acts[...]).astype(BF)
        keep(dwd.at[i], dwd_h.at[i])
        dwu[i] = nn(n2t[...], gps[...]).astype(BF)
        keep(dwu.at[i], dwu_h.at[i])
        gbias[i] = nn(ones, gps[...])[0:8]

    sent = []
    for cp in own_w:
        cp.wait()
    for cp in dy:
        cp.wait_recv()
    column(0, mp)
    for cp in ux + ey + uw:
        cp.wait_recv()
    column(1, w.xm)
    for cp in sent:
        cp.wait_recv()
    tx.finish()
    for cp in late:
        cp.wait()


def front(tok, wq, wo, wup, wdn, vecs, cot, ids, ndp, nmp):
    rows, d = tok.shape
    drow, unit, cols = wup.shape[0], wup.shape[1], wo.shape[1]
    small = vecs[0].shape[1]
    heads, t, nsend, nlocal = cols // HEAD, rows * nmp, 80, 32
    dma, vm = pltpu.SemaphoreType.DMA, pltpu.VMEM
    return pl.pallas_call(
        functools.partial(front_kernel, ndp // 2, heads, small),
        out_shape=(
            sds((t, d), BF),
            sds((2 * cols, t), F32),
            sds((nmp, rows, d), BF),
            sds((3 * cols, t), BF),
            sds((3 * cols, d), BF),
            sds((nmp, cols, d), BF),
            sds((cols, t), BF),
            sds((nmp, cols, rows), BF),
            sds((rows, d), F32),
            sds((2, d, unit), BF),
            sds((2, d, unit), BF),
            sds((rows, d), F32),
            sds((rows, d), F32),
            sds((rows, d), BF),
            sds((rows, d), BF),
            sds((8, t), F32),
            sds((16, d), F32),
            sds((2 * cols, 1), F32),
            sds((2, 8, unit), F32),
        ),
        in_specs=[ANY] * 4 + [VM] * 12,
        out_specs=(ANY,) * 15 + (VM,) * 4,
        scratch_shapes=[
            vm((nmp, rows, d), BF),
            vm((ndp, drow, 4 * cols), BF),
            vm((nmp, ndp, 16, 128), F32),
            vm((t, d), BF),
            vm((2 * cols, t), F32),
            vm((3 * cols, t), BF),
            vm((3 * cols, d), BF),
            vm((nmp, cols, d), BF),
            vm((cols, t), BF),
            vm((nmp, cols, rows), BF),
            vm((rows, d), F32),
            vm((rows, d), BF),
            vm((heads, 2 * HEAD, t), BF),
            vm((heads, t, 2 * HEAD), BF),
            vm((heads, HEAD + 16, t), BF),
            vm((heads, HEAD + 16, rows), F32),
            vm((2, ndp, drow, unit), BF),
            vm((2, ndp, drow, unit), BF),
            vm((rows, d), BF),
            vm((rows, d), BF),
            vm((rows, d), BF),
            vm((d, 2 * rows), BF),
            vm((d, 2 * rows), BF),
            vm((2 * rows, unit), BF),
            vm((2 * rows, unit), BF),
            vm((2 * rows, d), F32),
            vm((2 * rows, d), F32),
            vm((2, d, unit), BF),
            vm((2, d, unit), BF),
            vm((rows, d), BF),
            vm((rows, d), BF),
            dma((nsend,)),
            dma((nsend,)),
            dma((nlocal,)),
        ],
        compiler_params=params(collective_id=4, has_side_effects=True),
        cost_estimate=cost(40e9, 60 * 2**20),
        name="front",
    )(tok, wup, wdn, cot, wq, wo, ids, *vecs)


def three_sum(m, sel):
    return sum(nn(p.astype(BF), sel) for p in three(m))


def pack_vectors(main, gb0, gb1, w, small, vt):
    nmp, nz = vt.shape[0], vt.shape[1]
    n, d = nmp * nz * 2, main.shape[1]
    s = lax.broadcasted_iota(jnp.int32, (n, 8, d), 0)
    v = lax.broadcasted_iota(jnp.int32, (n, 8, d), 1)
    l = lax.broadcasted_iota(jnp.int32, (n, 8, d), 2)
    per = n // nmp
    dev = (s % per) * nmp + s // per
    sub = lax.broadcasted_iota(jnp.int32, (d, 128), 0)
    lane = lax.broadcasted_iota(jnp.int32, (d, 128), 1)
    m = jnp.where(l // small == dev, main[None], 0.0).reshape(n * 8, d)
    sel = jnp.where(sub % small == lane, 1.0, 0.0).astype(BF)
    a = three_sum(m, sel).reshape(n, 8, 128)
    wide = nmp * small
    here = (l // wide == dev % per) & (v == 0)
    m = jnp.where(here & (dev // per == w.mp), gb0[None], 0.0)
    m = m + jnp.where(here & (dev // per == w.xm), gb1[None], 0.0)
    sel = jnp.where(sub % wide == lane, 1.0, 0.0).astype(BF)
    b = three_sum(m.reshape(n * 8, d), sel).reshape(n, 8, 128)
    vt[...] = jnp.concatenate([a, b], axis=1).reshape(vt.shape)


def back_kernel(nz, heads, small, *refs):
    g_own, g_send, o_own, o_send, mid, cot, att_own, wot, wt, low = refs[:10]
    att, raw, normed, tok_all, dwu, dwd, lse, rowv, gains, ids, gbias = refs[10:21]
    res_o, gtok_o, gq_o, go_o, gu_o, gd_o, vec_o = refs[21:28]
    (
        f1, f2, f3, ggot, ogot, cotv, attov, wotv, wtv, lowv, attv, rawv, dwdc, dwuc,
        rxu, ryu, ru, rzu, ryd, rzd, rd, rxd, gattv, doutv, gwov, rco, go2, rxo, gov, ryo, ro, rzo,
        gprojv, qa, ka, va, da, dk, dv, dqa, tokv, normv, acc, gnv, rgc, rgx, dwqv, ryq, rq, rzq, sumv, ggv, vt, rv1, rv2, rv3, va4, rv4,
        ss, rs, ls,
    ) = refs[28:]
    w = Where(nz)
    dp, mp, z, y = w.dp, w.mp, w.z, w.y
    cols = heads * HEAD
    t = lowv.shape[1]
    rows, d = f1.shape
    nmp = t // rows
    greet(w.all)
    tx = Sender(ss, rs)
    count = [0]
    zto = [(z + k) % nz for k in range(nz)]

    def load(src, dst):
        cp = pltpu.make_async_copy(src, dst, ls.at[count[0]])
        cp.start()
        count[0] += 1
        return cp

    l1 = [load(g_send, ggot), load(g_own, f1), load(mid, f2), load(cot, cotv), load(wot, wotv)]
    l2 = [load(o_send, ogot), load(o_own, f3), load(att_own, attov), load(low, lowv), load(att, attv)]
    far = [2 % nz, 1 % nz] + list(range(3, nz)) + [0]
    dy, ux, uy, dz, uz, own_d, own_u = {}, {}, {}, [], [], {}, {}

    def fetch_own(n):
        if n < nz:
            k = far[n]
            own_d[k] = load(dwd.at[:, zto[k], y], dwdc.at[n % 2])
            own_u[k] = load(dwu.at[0, zto[k]], dwuc.at[n % 2])

    def down_y(n):
        k = far[n]
        own_d[k].wait()
        dy[k].wait_recv()
        for c in range(2):
            ryd[c, zto[k]] = (ryd[c, zto[k]].astype(F32) + dwdc[n % 2, c].astype(F32)).astype(BF)
        if k:
            dz.append(tx.send(ryd.at[:, zto[k]], rzd.at[k - 1], w.pz[k]))

    def up_x(n):
        k = far[n]
        own_u[k].wait()
        ux[k].wait_recv()
        rxu[zto[k]] = (rxu[zto[k]].astype(F32) + dwuc[n % 2].astype(F32)).astype(BF)
        uy[k] = tx.send(rxu.at[zto[k], 1 - y], ryu.at[zto[k]], w.py)

    def up_y(n):
        k = far[n]
        uy[k].wait_recv()
        ru[zto[k]] = (rxu[zto[k], y].astype(F32) + ryu[zto[k]].astype(F32)).astype(BF)
        if k:
            uz.append(tx.send(ru.at[zto[k]], rzu.at[k - 1], w.pz[k]))

    for k in far:
        dy[k] = tx.send(dwd.at[:, zto[k], 1 - y], ryd.at[:, zto[k]], w.py)
    ux[far[0]] = tx.send(dwu.at[1, zto[far[0]]], rxu.at[zto[far[0]]], w.px)
    l3 = [load(wt, wtv), load(raw, rawv)]
    fetch_own(0)
    fetch_own(1)

    for cp in l1:
        cp.wait()
    gy = cotv[...].astype(F32)
    g = f1[...] + ggot[...].astype(F32)
    hat, r = norm_rows(f2[...])
    e = g * rowv[5:6, :]
    m1 = jnp.mean(e, axis=-1, keepdims=True)
    m2 = jnp.mean(e * hat, axis=-1, keepdims=True)
    gm = gy + (e - m1 - hat * m2) * r
    sumv[...] = jnp.zeros_like(sumv)
    for k, v in enumerate((gm, g * hat, g, gy)):
        sumv[4 + k : 5 + k, :] = jnp.sum(v, axis=0, keepdims=True)
    f1[...] = gm
    gmb = gm.astype(BF)
    gattv[...] = nt(wotv[...], gmb).astype(BF).reshape(nmp, cols, rows)

    def block(m):
        return pl.ds(pl.multiple_of(m * rows, rows), rows)

    ax = tx.send(gattv.at[w.xm], doutv.at[:, block(mp)], w.px)
    ad = tx.send(gattv.at[w.dm], doutv.at[:, block(mp)], w.pd)
    ac = tx.send(gattv.at[w.cm], doutv.at[:, block(mp)], w.pc)
    for k in far[1:]:
        ux[k] = tx.send(dwu.at[1, zto[k]], rxu.at[zto[k]], w.px)
    own = load(gattv.at[mp], doutv.at[:, block(mp)])
    for cp in l2:
        cp.wait()
    res_o[...] = (f2[...] + f3[...] + ogot[...].astype(F32) + rowv[7:8, :]).astype(BF)
    gw = nt(gm.T.astype(BF), attov[...]).astype(BF)
    for m in range(nmp):
        gwov[m] = gw[:, m * cols : (m + 1) * cols].reshape(gwov.shape[1:])
    oc = [tx.send(gwov.at[w.cm], rco.at[0], w.pc), tx.send(gwov.at[w.dm], rco.at[1], w.pc)]
    for cp in l3:
        cp.wait()
    down_y(0)
    ggv[...] = jnp.zeros_like(ggv)

    def attention(qa, ka, va, da, dk, dv):
        def build(m, _):
            ts = block(m)
            r, _, mk = masks(ids[:, ts])
            mk = mk.astype(BF)
            one = jnp.where(r < 3, 1.0, 0.0).astype(BF)
            for h in range(heads):
                k = lowv[cols + h * HEAD : cols + (h + 1) * HEAD, ts]
                ka[h, ts, :] = jnp.concatenate([k, mk], axis=0).T
                v = lowv[2 * cols + h * HEAD : 2 * cols + (h + 1) * HEAD, ts]
                va[h, ts, :] = jnp.concatenate([v, one], axis=0).T
            return 0

        lax.fori_loop(0, nmp, build, 0)
        dk[...] = jnp.zeros_like(dk)
        dv[...] = jnp.zeros_like(dv)

        def row(i):
            qi = block(i)
            r, mq, _ = masks(ids[:, qi])
            for h in range(heads):
                hs = slice(h * HEAD, (h + 1) * HEAD)
                qa[h, 0:HEAD, :] = lowv[hs, qi]
                a, b, c = three(lse[h : h + 1, qi] * (-1.0 / SCALE))
                aug = jnp.where(r == 32, a, jnp.where(r == 33, b, jnp.where(r == 34, c, mq)))
                qa[h, HEAD:, :] = aug.astype(BF)
                do = doutv[hs, qi]
                delta = jnp.sum(do.astype(F32) * attv[hs, qi].astype(F32), axis=0, keepdims=True)
                a, b, c = three(-delta)
                da[h, 0:HEAD, :] = do
                da[h, HEAD:, :] = jnp.where(
                    r == 0, a, jnp.where(r == 1, b, jnp.where(r == 2, c, 0.0))
                ).astype(BF)
            dqa[...] = jnp.zeros_like(dqa)

            def tile(j, _):
                kj = block(j)
                s = [nn(ka[h, kj, :], qa[h]) for h in range(heads)]
                e = [nn(va[h, kj, :], da[h]) for h in range(heads)]
                p = [jnp.exp2(v * (SCALE * LOG2E)) for v in s]
                ds = [(p[h] * e[h]).astype(BF) for h in range(heads)]
                for h in range(heads):
                    hs = slice(h * HEAD, (h + 1) * HEAD)
                    dv[hs, kj] += nt(da[h, 0:HEAD, :], p[h].astype(BF))
                    dk[hs, kj] += nt(lowv[hs, qi], ds[h])
                    dqa[hs, :] += nn(lowv[cols + h * HEAD : cols + (h + 1) * HEAD, kj], ds[h])
                return 0

            lax.fori_loop(jnp.maximum(i - 2, 0), jnp.minimum(i + 3, nmp), tile, 0)
            for h in range(heads):
                hs = slice(h * HEAD, (h + 1) * HEAD)
                v, gg = head_back(rawv[hs, qi], gains[hs, :], dqa[hs, :] * SCALE)
                gprojv[hs, qi] = v.astype(BF)
                ggv[hs, :] += gg

        up_x(0)
        fetch_own(2)
        own.wait()
        row(mp)
        down_y(1)
        for cp in oc:
            cp.wait_recv()
        go2[...] = (gwov[w.xm].astype(F32) + rco[1].astype(F32)).astype(BF)
        oxx = tx.send(go2, rxo, w.px)
        ac.wait_recv()
        row(w.cm)
        down_y(2)
        up_x(1)
        up_y(0)
        fetch_own(3)
        ax.wait_recv()
        row(w.xm)
        down_y(3)
        up_x(2)
        up_y(1)
        ad.wait_recv()
        row(w.dm)
        up_x(3)
        up_y(2)
        oxx.wait_recv()
        gov[...] = (gwov[mp].astype(F32) + rco[0].astype(F32) + rxo[...].astype(F32)).astype(BF)
        oy = tx.send(gov.at[:, 1 - y], ryo, w.py)

        def keys(m, _):
            ts = block(m)
            pad = ids[:, ts] < 0
            for h in range(heads):
                hs = slice(h * HEAD, (h + 1) * HEAD)
                ps = slice(cols + h * HEAD, cols + (h + 1) * HEAD)
                v, gg = head_back(rawv[ps, ts], gains[ps, :], dk[hs, ts] * SCALE)
                gprojv[ps, ts] = v.astype(BF)
                ggv[ps, :] += gg
                v = dv[hs, ts] + jnp.where(pad, doutv[hs, ts].astype(F32), 0.0)
                gprojv[2 * cols + h * HEAD : 2 * cols + (h + 1) * HEAD, ts] = v.astype(BF)
            return 0

        lax.fori_loop(0, nmp, keys, 0)
        return oy

    oy = attention(qa, ka, va, da, dk, dv)

    def projections(tokv, normv, acc):
        acc[...] = jnp.zeros_like(acc)

        def part(m):
            return tn(gprojv[:, block(m)], wtv[...])

        order = (w.dm, w.xm, w.cm, mp)

        def fetch_norm(n):
            return load(normed.at[block(order[n]), :], normv.at[n % 2])

        def fetch_tok(n):
            return load(tok_all.at[order[n]], tokv.at[n % 2])

        def weights(n, cp):
            cp.wait()
            acc[...] += nn(gprojv[:, block(order[n])], normv[n % 2])

        def gain_sums(n, g, cp):
            cp.wait()
            hat, _ = norm_rows(tokv[n % 2].astype(F32))
            sumv[0:1, :] += jnp.sum(g * hat, axis=0, keepdims=True)
            sumv[1:2, :] += jnp.sum(g, axis=0, keepdims=True)

        n0, n1, t0, t1 = fetch_norm(0), fetch_norm(1), fetch_tok(0), fetch_tok(1)
        g = part(w.dm)
        gnv[0] = g.astype(BF)
        c1 = tx.send(gnv.at[0], rgc.at[1], w.pc)
        f2[...] = part(w.xm)
        c1.wait_recv()
        gnv[1] = (f2[...] + rgc[1].astype(F32)).astype(BF)
        gxx = tx.send(gnv.at[1], rgx, w.px)
        weights(0, n0)
        n2 = fetch_norm(2)
        weights(1, n1)
        n3 = fetch_norm(3)
        weights(2, n2)
        weights(3, n3)
        dwqv[...] = acc[...].T.astype(BF).reshape(dwqv.shape)
        qy = {}
        for k in far:
            qy[k] = tx.send(dwqv.at[zto[k], 1 - y], ryq.at[zto[k]], w.py)
        up_y(3)
        gain_sums(0, g, t0)
        t2 = fetch_tok(2)
        qz = []

        def qkv_y(n):
            k = far[n]
            qy[k].wait_recv()
            rq[zto[k]] = (dwqv[zto[k], y].astype(F32) + ryq[zto[k]].astype(F32)).astype(BF)
            if k:
                qz.append(tx.send(rq.at[zto[k]], rzq.at[k - 1], w.pz[k]))

        oy.wait_recv()
        ro[...] = (gov[:, y].astype(F32) + ryo[...].astype(F32)).astype(BF)
        oz = [tx.send(ro.at[zto[k]], rzo.at[k - 1], w.pz[k]) for k in range(1, nz)]
        gain_sums(1, f2[...], t1)
        t3 = fetch_tok(3)
        qkv_y(0)
        for cp in dz:
            cp.wait_recv()
        tot = ryd[:, z].astype(F32)
        for k in range(nz - 1):
            tot = tot + rzd[k].astype(F32)
        rd[...] = tot[1].astype(BF)
        dx = tx.send(rd, rxd, w.px)
        gd_o[...] = tot[0]
        g = part(w.cm)
        tx.sent(c1)
        gnv[0] = g.astype(BF)
        c2 = tx.send(gnv.at[0], rgc.at[0], w.pc)
        gain_sums(2, g, t2)
        qkv_y(1)
        f2[...] = part(mp)
        gain_sums(3, f2[...], t3)
        qkv_y(2)
        qkv_y(3)
        lane = lax.broadcasted_iota(jnp.int32, (cols, d), 1)
        pick = lane == lax.broadcasted_iota(jnp.int32, (cols, d), 0) + mp * cols
        for i in range(2):
            v = jnp.where(pick, ggv[i * cols : (i + 1) * cols, :], 0.0)
            sumv[2 + i : 3 + i, :] = jnp.sum(v, axis=0, keepdims=True)
        pack_vectors(sumv[...], gbias[0, 0:1, :], gbias[1, 0:1, :], w, small, vt)
        v1 = [tx.send(vt.at[w.cm], rv1.at[0], w.pc), tx.send(vt.at[w.dm], rv1.at[1], w.pc)]
        for cp in v1:
            cp.wait_recv()
        vt[w.xm] = vt[w.xm] + rv1[1]
        v2 = tx.send(vt.at[w.xm], rv2, w.px)
        v2.wait_recv()
        vt[mp] = vt[mp] + rv1[0] + rv2[...]
        v3 = tx.send(vt.at[mp, :, 1 - y], rv3, w.py)
        c2.wait_recv()
        f2[...] += rgc[0].astype(F32)
        v3.wait_recv()
        va4[...] = vt[mp, :, y] + rv3[...]
        v4 = [tx.send(va4.at[zto[k]], rv4.at[k - 1], w.pz[k]) for k in range(1, nz)]

        def last(copies, own, got, out):
            for cp in copies:
                cp.wait_recv()
            tot = own.astype(F32)
            for k in range(nz - 1):
                tot = tot + got[k].astype(F32)
            out[...] = tot

        last(uz, ru[z], rzu, gu_o)
        last(oz, ro[z], rzo, go_o)
        last(v4, va4[z], rv4, vec_o)
        dx.wait_recv()
        gd_o[...] += rxd[...].astype(F32)
        last(qz, rq[z], rzq, gq_o)
        gxx.wait_recv()
        g = f2[...] + rgx[...].astype(F32)
        hat, r = norm_rows(tokv[1].astype(F32))
        e = g * rowv[0:1, :]
        m1 = jnp.mean(e, axis=-1, keepdims=True)
        m2 = jnp.mean(e * hat, axis=-1, keepdims=True)
        gtok_o[...] = (f1[...] + (e - m1 - hat * m2) * r).astype(BF)

    projections(tokv, normv, acc)
    tx.finish()


def back(hbm, small_in, nz, heads, small):
    g_own, dwu = hbm[0], hbm[14]
    rows, d = g_own.shape
    drow, unit = dwu.shape[3], dwu.shape[4]
    cols = heads * HEAD
    nmp = d // cols
    t = nmp * rows
    v = pltpu.VMEM
    dma = pltpu.SemaphoreType.DMA
    scratch = [
        v((rows, d), F32), v((rows, d), F32), v((rows, d), F32),
        v((rows, d), BF), v((rows, d), BF), v((rows, d), BF), v((d, rows), BF), v((d, d), BF),
        v((3 * cols, d), BF), v((3 * cols, t), BF), v((cols, t), BF), v((2 * cols, t), F32),
        v((2, 2, drow, unit), BF), v((2, 2, drow, unit), BF),
        v((nz, 2, drow, unit), BF), v((nz, drow, unit), BF), v((nz, drow, unit), BF), v((nz - 1, drow, unit), BF),
        v((2, nz, drow, unit), BF), v((nz - 1, 2, drow, unit), BF), v((drow, unit), BF), v((drow, unit), BF),
        v((nmp, cols, rows), BF), v((cols, t), BF),
        v((nmp, nz, 2, drow, cols), BF), v((2, nz, 2, drow, cols), BF), v((nz, 2, drow, cols), BF),
        v((nz, 2, drow, cols), BF), v((nz, 2, drow, cols), BF),
        v((nz, drow, cols), BF), v((nz, drow, cols), BF), v((nz - 1, drow, cols), BF),
        v((3 * cols, t), BF),
        v((heads, 2 * HEAD, rows), BF), v((heads, t, 2 * HEAD), BF), v((heads, t, 2 * HEAD), BF),
        v((heads, 2 * HEAD, rows), BF), v((cols, t), F32), v((cols, t), F32), v((cols, rows), F32),
        v((2, rows, d), BF), v((2, rows, d), BF), v((3 * cols, d), F32),
        v((2, rows, d), BF), v((2, rows, d), BF), v((rows, d), BF),
        v((nz, 2, drow, 3 * cols), BF), v((nz, drow, 3 * cols), BF), v((nz, drow, 3 * cols), BF),
        v((nz - 1, drow, 3 * cols), BF),
        v((8, d), F32), v((2 * cols, 1), F32),
        v((nmp, nz, 2, 16, 128), F32), v((2, nz, 2, 16, 128), F32), v((nz, 2, 16, 128), F32),
        v((nz, 16, 128), F32), v((nz, 16, 128), F32), v((nz - 1, 16, 128), F32),
        dma((64,)), dma((64,)), dma((40,)),
    ]
    return pl.pallas_call(
        functools.partial(back_kernel, nz, heads, small),
        out_shape=(
            sds((rows, d), BF),
            sds((rows, d), BF),
            sds((drow, 3 * cols), F32),
            sds((drow, cols), F32),
            sds((drow, unit), F32),
            sds((drow, unit), F32),
            sds((16, 128), F32),
        ),
        in_specs=[ANY] * len(hbm) + [VM] * len(small_in),
        out_specs=(VM,) * 7,
        scratch_shapes=scratch,
        compiler_params=params(collective_id=5, has_side_effects=True),
        cost_estimate=cost(40e9, 60 * 2**20),
        name="back",
    )(*hbm, *small_in)


def finish_kernel(small, wide, res, gtok, gq, go, gu, gd, vec, *outs):
    outs[0][...] = res[...]
    outs[1][...] = gtok[...]
    cols = go.shape[1]
    for i in range(3):
        outs[2][i] = gq[:, i * cols : (i + 1) * cols]
    outs[3][...] = go[...]
    outs[4][...] = gu[...]
    outs[5][...] = gd[...]
    for i in range(8):
        outs[6 + i][...] = vec[i : i + 1, 0:small]
    outs[14][...] = vec[8:9, 0:wide]


def finish(res, gtok, gq, go, gu, gd, vec, small, wide):
    n = 4

    def rows(a):
        return pl.BlockSpec((a.shape[0] // n, a.shape[1]), lambda i: (i, 0))

    def whole(shape):
        return pl.BlockSpec(shape, lambda i: (0,) * len(shape))

    drow, cols = go.shape
    like = [sds(a.shape, a.dtype) for a in (res, gtok)]
    like += [sds((3, drow, cols), F32)] + [sds(a.shape, F32) for a in (go, gu, gd)]
    like += [sds((1, small), F32)] * 8 + [sds((1, wide), F32)]
    specs = [rows(res), rows(gtok), pl.BlockSpec((3, drow // n, cols), lambda i: (0, i, 0))]
    specs += [rows(go), rows(gu), rows(gd)] + [whole((1, small))] * 8 + [whole((1, wide))]
    return pl.pallas_call(
        functools.partial(finish_kernel, small, wide),
        grid=(n,),
        out_shape=tuple(like),
        in_specs=[rows(a) for a in (res, gtok, gq, go, gu, gd)] + [whole(vec.shape)],
        out_specs=tuple(specs),
        compiler_params=params(),
        name="finish",
    )(res, gtok, gq, go, gu, gd, vec)


def spans(ids):
    b = ids.reshape(-1, TB)
    low = jnp.min(jnp.where(b < 0, 1000, b), axis=1)
    high = jnp.max(b, axis=1)
    n = b.shape[0]
    k = jnp.arange(n)
    lo = jnp.sum((high[None, :] < low[:, None]) & (k[None, :] <= k[:, None]), axis=1)
    hi = jnp.sum(low[None, :] <= high[:, None], axis=1)
    return jnp.concatenate([lo, hi]).astype(jnp.int32)


def solution(mesh):
    ndp, nmp = mesh.shape["dp"], mesh.shape["mp"]
    ndev, nz = ndp * nmp, ndp // 2

    def permute(v, kind, k=0):
        pairs = []
        for d in range(ndp):
            for m in range(nmp):
                z, y, x, c = d // 2, d % 2, m // 2, m % 2
                if kind == "core":
                    c = 1 - c
                if kind == "x":
                    x = 1 - x
                if kind == "y":
                    y = 1 - y
                if kind == "z":
                    z = (z + k) % nz
                pairs.append((d * nmp + m, (z * 2 + y) * nmp + x * 2 + c))
        return lax.ppermute(v, ("dp", "mp"), pairs)

    def columns(w, first, second):
        if w.shape[0] % 16:
            own = lax.all_gather(w, "dp", axis=0, tiled=True)[None]
            return [own, permute(own, "x")]
        s = jnp.stack([w] + [permute(w, "z", k) for k in range(1, nz)])
        got = {(0, 0): s}
        one = permute(s, first)
        two = permute(s, second)
        both = permute(one, second)
        got[(0, 1)] = one if first == "y" else two
        got[(1, 0)] = two if first == "y" else one
        got[(1, 1)] = both
        return [got[(0, 0)], got[(0, 1)], got[(1, 0)], got[(1, 1)]]

    def body(
        tokens,
        picture_ids,
        w_qkv,
        w_out,
        w_up,
        w_down,
        ln1_gain,
        ln1_bias,
        q_gain,
        k_gain,
        out_bias,
        ln2_gain,
        ln2_bias,
        up_bias,
        down_bias,
        cotangent,
    ):
        rows, d = tokens.shape[1], tokens.shape[2]
        drow = w_qkv.shape[0]
        cols = w_qkv.shape[2]
        heads = cols // HEAD
        unit = w_up.shape[1]
        dp, mp = lax.axis_index("dp"), lax.axis_index("mp")
        z, y, x, c = dp // 2, dp % 2, mp // 2, mp % 2
        tok, cot = tokens[0], cotangent[0]
        ids = picture_ids
        span = spans(ids[0])
        whole = drow % 16 == 0 and ndev == 32

        vs = [ln1_gain, ln1_bias, q_gain, k_gain, out_bias, ln2_gain, ln2_bias, down_bias, up_bias]
        small = vs[0].shape[0]
        used = 8 * small + up_bias.shape[0]
        if whole:
            (
                normed,
                raw,
                tok_all,
                low,
                wt,
                wot,
                att,
                att_own,
                mid,
                dwu,
                dwd,
                o_own,
                g_own,
                o_got,
                g_got,
                lse,
                rowv,
                gains,
                gbias,
            ) = front(
                tok,
                w_qkv.transpose(1, 0, 2),
                w_out,
                w_up,
                w_down,
                [v.reshape(1, -1) for v in vs],
                cot,
                ids,
                ndp,
                nmp,
            )
            att_own = att_own.reshape(d, rows)
            shape = (2, nz, 2, drow, unit)
            res, gtok, gqw, gow, gup, gdn, vt = back(
                (g_own, g_got, o_own, o_got, mid, cot, att_own, wot.reshape(d, d), wt, low)
                + (att, raw, normed, tok_all, dwu.reshape(shape), dwd.reshape(shape)),
                (lse, rowv, gains, ids, gbias),
                nz,
                heads,
                small,
            )
            out = finish(res, gtok, gqw, gow, gup, gdn, vt, small, nmp * small)
            vg = [v.reshape(-1) for v in out[6:]]
            return (
                out[0][None],
                out[1][None],
                out[2].transpose(1, 0, 2),
                out[3],
                out[4],
                out[5],
                *vg[:7],
                vg[8],
                vg[7],
            )
        else:
            flat = jnp.concatenate(vs)
            vec = jnp.pad(flat, (0, 1024 - used)).reshape(8, 128)
            wcat = jnp.concatenate([w_qkv.reshape(drow, 3 * cols), w_out], axis=1)
            tok_all, w_all, vec_all = gather_all(tok, wcat, vec, ndp, nmp)
            vec_all = vec_all.reshape(nmp, ndp, 1024).transpose(1, 0, 2).reshape(ndev, 1024)
            gain1, shift1, qg, kg, obias, gain2, shift2, dbias = [
                vec_all[:, i * small : (i + 1) * small].reshape(1, d) for i in range(8)
            ]
            ubias = vec_all[:, 8 * small : used].reshape(nmp, unit)
            gains = jnp.concatenate(
                [
                    lax.dynamic_slice_in_dim(qg[0], mp * cols, cols),
                    lax.dynamic_slice_in_dim(kg[0], mp * cols, cols),
                ]
            ).reshape(2 * cols, 1)

            ups = columns(w_up, "y", "x")
            downs = columns(w_down, "x", "y")
            cot_other = permute(cot, "core")

            normed, raw, low, wt = project(
                tok_all, w_all.reshape(d, 3 * cols + w_out.shape[1]), gain1, shift1, gains, heads
            )
            wo0 = wt[3 * cols :]
            wo1 = permute(wo0, "x")
            wo2, wo3 = permute(wo0, "core"), permute(wo1, "core")
            wos = (wo0, wo1, wo2, wo3)
            att, lse = attend(span, low, ids, heads)
            att_own = swap(att, True, nmp, 1).reshape(d, rows)
            mid, n2 = middle_part(att_own, wos, tok, obias, gain2, shift2)
            n2_other = permute(n2, "core")
        o_own, o_send, g_own, g_send, dwu, dwd, gbias = feed(
            n2, n2_other, cot, cot_other, ubias, ups, downs, nz
        )
        g_got = permute(g_send, "core")
        gmid, gatt, gwo, sums2 = middle_back(g_own, g_got, mid, cot, att_own, wos, gain2, nmp)
        o_got = permute(o_send, "core")
        result = (mid + o_own + o_got.astype(F32) + dbias).astype(BF)
        dout = swap(gatt, False, nmp, 2)
        gproj, ggain = attend_back(span, low, raw, att, lse, dout, ids, gains, heads)
        order = jnp.stack([mp, x * 2 + 1 - c, (1 - x) * 2 + c, (1 - x) * 2 + 1 - c]).astype(jnp.int32)
        gn, gwq, sums1 = project_back(order, gproj, normed, tok_all, wt[: 3 * cols])
        got = permute(gn[1::2], "core")
        mine = gn[0::2].astype(F32) + got.astype(F32)
        far = permute(mine[1].astype(BF), "x")
        gnormed = mine[0] + far.astype(F32)
        grad_tokens = tokens_back(gnormed, tok, gain1, gmid)

        def pick(v, i):
            return lax.dynamic_index_in_dim(v, i, 0, keepdims=False)

        def along(v, kind):
            i = {"x": None, "y": y}[kind]
            if i is None:
                keep, send = v[0], v[1]
            else:
                keep, send = pick(v, i), pick(v, 1 - i)
            return (keep.astype(F32) + permute(send, kind).astype(F32)).astype(BF)

        def along_z(v):
            total = pick(v, z).astype(F32)
            for k in range(1, nz):
                total = total + permute(pick(v, (z + k) % nz), "z", k).astype(F32)
            return total

        def over_dp(v):
            if drow % 16:
                return lax.psum_scatter(v.astype(F32), "dp", scatter_dimension=0, tiled=True)
            v = v.reshape(nz, 2, drow, v.shape[-1]).transpose(1, 0, 2, 3)
            return along_z(along(v, "y"))

        def reduce_columns(v, y_first):
            if drow % 16 or not y_first:
                return over_dp(along(v, "x"))
            v = v.reshape(2, nz, 2, drow, unit).transpose(2, 0, 1, 3, 4)
            return along_z(along(along(v, "y"), "x"))

        grad_up = reduce_columns(dwu, False)
        grad_down = reduce_columns(dwd, True)
        mine_o = jnp.stack([pick(gwo, mp), pick(gwo, (1 - x) * 2 + c)])
        send_o = jnp.stack([pick(gwo, x * 2 + 1 - c), pick(gwo, (1 - x) * 2 + 1 - c)])
        go = (mine_o.astype(F32) + permute(send_o, "core").astype(F32)).astype(BF)
        go = along(go, "x")
        grad_att = over_dp(jnp.concatenate([gwq, go], axis=1))

        def spread(v, at, size):
            return lax.dynamic_update_slice_in_dim(jnp.zeros((size,), F32), v, at, 0)

        gq = spread(ggain[:cols, 0], mp * cols, d)
        gk = spread(ggain[cols:, 0], mp * cols, d)
        gb = spread(gbias[0, 0], mp * unit, nmp * unit)
        gb = gb + spread(gbias[1, 0], ((1 - x) * 2 + c) * unit, nmp * unit)
        eight = jnp.stack([sums1[0], sums1[1], gq, gk, sums2[0], sums2[1], sums2[2], sums2[3]])
        parts = jnp.concatenate(
            [
                eight.reshape(8, ndev, small).transpose(1, 0, 2).reshape(ndev, 8 * small),
                gb.reshape(ndev, used - 8 * small),
            ],
            axis=1,
        )
        parts = jnp.pad(parts, ((0, 0), (0, 1024 - used))).reshape(ndev, 8, 128)
        tot = vector_sums(parts, ndp, nmp).reshape(1024)
        vgrads = [tot[i * small : (i + 1) * small] for i in range(8)] + [tot[8 * small : used]]

        return (
            result[None],
            grad_tokens[None],
            grad_att[:, : 3 * cols].reshape(drow, 3, cols),
            grad_att[:, 3 * cols :],
            grad_up,
            grad_down,
            vgrads[0],
            vgrads[1],
            vgrads[2],
            vgrads[3],
            vgrads[4],
            vgrads[5],
            vgrads[6],
            vgrads[8],
            vgrads[7],
        )

    vec_spec = P(("dp", "mp"))
    return jax.shard_map(
        body,
        mesh=mesh,
        in_specs=(
            P("dp", "mp", None),
            P("dp", None),
            P("dp", None, "mp"),
            P("dp", "mp"),
            P("dp", "mp"),
            P("dp", "mp"),
        )
        + (vec_spec,) * 9
        + (P("dp", "mp", None),),
        out_specs=(
            P("dp", "mp", None),
            P("dp", "mp", None),
            P("dp", None, "mp"),
            P("dp", "mp"),
            P("dp", "mp"),
            P("dp", "mp"),
        )
        + (vec_spec,) * 9,
        check_vma=False,
    )
```

```python
import functools

import jax
import jax.numpy as jnp
from jax import lax
from jax.experimental import pallas as pl
from jax.experimental.pallas import tpu as pltpu
from jax.sharding import PartitionSpec as P

F32 = jnp.float32
BF = jnp.bfloat16
HEAD = 64
EPS = 1e-06
TB = 512
BIG = 32768.0
LOG2E = 1.4426950408889634
MESH = pl.DeviceIdType.MESH
ANY = pl.BlockSpec(memory_space=pl.ANY)
VM = pl.BlockSpec(memory_space=pltpu.VMEM)
SM = pl.BlockSpec(memory_space=pltpu.SMEM)
VLIM = 60 * 1024 * 1024


def nn(a, b):
    return lax.dot_general(a, b, (((1,), (0,)), ((), ())), preferred_element_type=F32)


def nt(a, b):
    return lax.dot_general(a, b, (((1,), (1,)), ((), ())), preferred_element_type=F32)


def tn(a, b):
    return lax.dot_general(a, b, (((0,), (0,)), ((), ())), preferred_element_type=F32)


def sds(shape, dtype):
    return jax.ShapeDtypeStruct(shape, dtype)


def params(**kw):
    return pltpu.CompilerParams(vmem_limit_bytes=VLIM, **kw)


def cost(flops, nbytes, trans=0):
    return pl.CostEstimate(flops=int(flops), bytes_accessed=int(nbytes), transcendentals=int(trans))


def rcopy(src, dst, ssem, rsem, peer):
    return pltpu.make_async_remote_copy(
        src_ref=src,
        dst_ref=dst,
        send_sem=ssem,
        recv_sem=rsem,
        device_id=peer,
        device_id_type=MESH,
    )


def greet(peers):
    bar = pltpu.get_barrier_semaphore()
    for p in peers:
        pl.semaphore_signal(bar, inc=1, device_id=p, device_id_type=MESH)
    pl.semaphore_wait(bar, len(peers))


def gather_kernel(
    nz, nc, tok, w, vec, tok_all, w_all, vec_all, loc, zs, zr, ys, yr, xs, xr, cs, cr, tx, rx, tc, rc
):
    dp, mp = lax.axis_index("dp"), lax.axis_index("mp")
    z, y, x, c = dp // 2, dp % 2, mp // 2, mp % 2
    xm, cm, dm = (1 - x) * 2 + c, x * 2 + 1 - c, (1 - x) * 2 + 1 - c
    ypeer, xpeer, cpeer = (z * 2 + 1 - y, mp), (dp, xm), (dp, cm)
    zpeers = [(((z + k) % nz) * 2 + y, mp) for k in range(1, nz)]
    greet(zpeers + [ypeer, xpeer, cpeer])
    rows = tok.shape[0] // nc
    xt = []
    for i in range(nc):
        part = pl.ds(i * rows, rows)
        cp = rcopy(tok.at[part], tok_all.at[mp, part], tx.at[i], rx.at[i], xpeer)
        cp.start()
        xt.append(cp)
    zc = []
    for k in range(1, nz):
        for kind, (src, dst) in enumerate(((vec, vec_all.at[mp, dp]), (w, w_all.at[dp]))):
            cp = rcopy(src, dst, zs.at[kind, k], zr.at[kind, k], zpeers[k - 1])
            cp.start()
            zc.append(cp)
    yc = []
    for kind, (src, dst) in enumerate(((vec, vec_all.at[mp, dp]), (w, w_all.at[dp]))):
        cp = rcopy(src, dst, ys.at[kind, 0], yr.at[kind, 0], ypeer)
        cp.start()
        yc.append(cp)
    own_tok = rcopy(tok, tok_all.at[mp], tc.at[nc], rc.at[nc], cpeer)
    own_tok.start()
    locs = [
        pltpu.make_async_copy(tok, tok_all.at[mp], loc.at[0]),
        pltpu.make_async_copy(w, w_all.at[dp], loc.at[1]),
        pltpu.make_async_copy(vec, vec_all.at[mp, dp], loc.at[2]),
    ]
    for cp in locs:
        cp.start()
    for k in range(1, nz):
        src_dp = ((z + nz - k) % nz) * 2 + y
        for kind in range(2):
            zc[(k - 1) * 2 + kind].wait_recv()
            ref = (vec_all.at[mp, src_dp], w_all.at[src_dp])[kind]
            cp = rcopy(ref, ref, ys.at[kind, k], yr.at[kind, k], ypeer)
            cp.start()
            yc.append(cp)
    ct = []

    def forward(i):
        part = pl.ds(i * rows, rows)
        xt[i].wait_recv()
        cp = rcopy(tok_all.at[xm, part], tok_all.at[xm, part], tc.at[i], rc.at[i], cpeer)
        cp.start()
        ct.append(cp)

    forward(0)
    for cp in locs:
        cp.wait()
    for k in range(nz):
        yc[k * 2].wait_recv()
    vx = rcopy(vec_all.at[mp], vec_all.at[mp], xs, xr, xpeer)
    vx.start()
    vc0 = rcopy(vec_all.at[mp], vec_all.at[mp], cs.at[0], cr.at[0], cpeer)
    vc0.start()
    if nc > 1:
        forward(1)
    vx.wait_recv()
    vc1 = rcopy(vec_all.at[xm], vec_all.at[xm], cs.at[1], cr.at[1], cpeer)
    vc1.start()
    for i in range(2, nc):
        forward(i)
    for k in range(nz):
        yc[k * 2 + 1].wait_recv()
    for cp in ct:
        cp.wait_recv()
    own_tok.wait()
    vc0.wait()
    vc1.wait()
    vx.wait_send()
    for cp in zc + yc + xt + ct:
        cp.wait_send()


def gather_all(tok, w, vec, ndp, nmp):
    nz, nc = ndp // 2, 4
    dma = pltpu.SemaphoreType.DMA
    return pl.pallas_call(
        functools.partial(gather_kernel, nz, nc),
        out_shape=(
            sds((nmp,) + tok.shape, BF),
            sds((ndp,) + w.shape, BF),
            sds((nmp, ndp) + vec.shape, F32),
        ),
        in_specs=[ANY] * 3,
        out_specs=(ANY,) * 3,
        scratch_shapes=[
            dma((3,)),
            dma((2, nz)),
            dma((2, nz)),
            dma((2, nz)),
            dma((2, nz)),
            dma,
            dma,
            dma((2,)),
            dma((2,)),
            dma((nc,)),
            dma((nc,)),
            dma((nc + 1,)),
            dma((nc + 1,)),
        ],
        compiler_params=pltpu.CompilerParams(collective_id=0, has_side_effects=True),
        name="gather_start",
    )(tok, w, vec)


def swap_kernel(forward, nmp, src, dst, loc, ss, rs):
    dp, mp = lax.axis_index("dp"), lax.axis_index("mp")
    own = dst.shape[2] if forward else src.shape[2]
    peers = [(mp + k) % nmp for k in range(1, nmp)]
    greet([(dp, m) for m in peers])

    def ends(m):
        if forward:
            return src.at[:, pl.ds(pl.multiple_of(m * own, own), own)], dst.at[mp]
        return src.at[m], dst.at[:, pl.ds(pl.multiple_of(mp * own, own), own)]

    cps = []
    for k, m in enumerate(peers):
        s, d = ends(m)
        cp = rcopy(s, d, ss.at[k], rs.at[k], (dp, m))
        cp.start()
        cps.append(cp)
    s, d = ends(mp)
    lc = pltpu.make_async_copy(s, d, loc)
    lc.start()
    lc.wait()
    for cp in cps:
        cp.wait()


def swap(src, forward, nmp, cid):
    dma = pltpu.SemaphoreType.DMA
    if forward:
        shape = (nmp, src.shape[0], src.shape[1] // nmp)
    else:
        shape = (src.shape[1], src.shape[2] * nmp)
    return pl.pallas_call(
        functools.partial(swap_kernel, forward, nmp),
        out_shape=sds(shape, BF),
        in_specs=[ANY],
        out_specs=ANY,
        scratch_shapes=[dma, dma((nmp - 1,)), dma((nmp - 1,))],
        compiler_params=pltpu.CompilerParams(collective_id=cid, has_side_effects=True),
        name="swap_fwd" if forward else "swap_bwd",
    )(src)


def vector_kernel(ndp, nmp, src, out, got, ss, rs):
    dp, mp = lax.axis_index("dp"), lax.axis_index("mp")
    me, n = dp * nmp + mp, ndp * nmp
    peers = [(me + k) % n for k in range(1, n)]
    greet([(p // nmp, p % nmp) for p in peers])
    cps = []
    for k, p in enumerate(peers):
        cp = rcopy(src.at[p], got.at[k], ss.at[k], rs.at[k], (p // nmp, p % nmp))
        cp.start()
        cps.append(cp)
    total = src[me]
    for k, cp in enumerate(cps):
        cp.wait_recv()
        total = total + got[k]
    out[...] = total
    for cp in cps:
        cp.wait_send()


def vector_sums(parts, ndp, nmp):
    n = ndp * nmp
    dma = pltpu.SemaphoreType.DMA
    return pl.pallas_call(
        functools.partial(vector_kernel, ndp, nmp),
        out_shape=sds(parts.shape[1:], F32),
        in_specs=[VM],
        out_specs=VM,
        scratch_shapes=[pltpu.VMEM((n - 1,) + parts.shape[1:], F32), dma((n - 1,)), dma((n - 1,))],
        compiler_params=pltpu.CompilerParams(collective_id=3, has_side_effects=True),
        name="vector_sums",
    )(parts)


def norm_rows(v):
    centre = jnp.mean(v, axis=-1, keepdims=True)
    v = v - centre
    r = lax.rsqrt(jnp.mean(v * v, axis=-1, keepdims=True) + EPS)
    return v * r, r


def norm_cols(v):
    centre = jnp.mean(v, axis=0, keepdims=True)
    v = v - centre
    r = lax.rsqrt(jnp.mean(v * v, axis=0, keepdims=True) + EPS)
    return v * r, r


def qkv_kernel(heads, tok, w, gain, shift, gains, normed, raw, low, wt):
    @pl.when(pl.program_id(0) == 0)
    def _():
        wt[...] = w[...].T

    cols = heads * HEAD
    hat, _ = norm_rows(tok[0].astype(F32))
    n = (hat * gain[...] + shift[...]).astype(BF)
    normed[...] = n
    proj = nt(wt[0 : 3 * cols, :], n)
    raw[...] = proj[0 : 2 * cols]
    for h in range(2 * heads):
        part = slice(h * HEAD, (h + 1) * HEAD)
        hat, _ = norm_cols(proj[part])
        low[part, :] = (hat * gains[part, :]).astype(BF)
    low[2 * cols :, :] = proj[2 * cols :].astype(BF)


def project(tok_all, w, gain, shift, gains, heads):
    nb, rows, d = tok_all.shape
    cols = heads * HEAD
    t = nb * rows
    full = lambda shape: pl.BlockSpec(shape, lambda i: (0,) * len(shape))
    return pl.pallas_call(
        functools.partial(qkv_kernel, heads),
        grid=(nb,),
        out_shape=(
            sds((t, d), BF),
            sds((2 * cols, t), F32),
            sds((3 * cols, t), BF),
            sds((w.shape[1], w.shape[0]), BF),
        ),
        in_specs=[
            pl.BlockSpec((1, rows, d), lambda i: (i, 0, 0)),
            full(w.shape),
            full((1, d)),
            full((1, d)),
            full((2 * cols, 1)),
        ],
        out_specs=(
            pl.BlockSpec((rows, d), lambda i: (i, 0)),
            pl.BlockSpec((2 * cols, rows), lambda i: (0, i)),
            pl.BlockSpec((3 * cols, rows), lambda i: (0, i)),
            full((w.shape[1], w.shape[0])),
        ),
        compiler_params=params(),
        cost_estimate=cost(2 * t * d * 3 * cols, 12 * 2**20),
        name="project_qkv",
    )(tok_all, w, gain, shift, gains)


def masks(ids):
    t = ids.shape[1]
    r = lax.broadcasted_iota(jnp.int32, (HEAD, t), 0)
    pad = ids < 0
    mq = jnp.where((r == ids) | ((r == 31) & pad), 1.0, 0.0)
    mk = jnp.where((r <= 31) & (r != ids), -BIG, 0.0)
    mk = jnp.where((r >= 32) & (r < 35), 1.0, mk)
    return r, mq, mk


def three(v):
    a = v.astype(BF).astype(F32)
    b = (v - a).astype(BF).astype(F32)
    return a, b, v - a - b


SCALE = HEAD**-0.5


def attend_kernel(heads, nblk, span, low, ids, out, lse, qa, ka, va, acc):
    cols = heads * HEAD
    t = ids.shape[1]
    _, mq, mk = masks(ids[...])
    mq, mk = mq.astype(BF), mk.astype(BF)
    one = jnp.where(lax.broadcasted_iota(jnp.int32, (16, t), 0) == 0, 1.0, 0.0).astype(BF)
    for h in range(heads):
        qa[h, 0:HEAD, :] = low[h * HEAD : (h + 1) * HEAD, :]
        qa[h, HEAD:, :] = mq
        k = low[cols + h * HEAD : cols + (h + 1) * HEAD, :]
        ka[h, :, :] = jnp.concatenate([k, mk], axis=0).T
        va[h, 0:HEAD, :] = low[2 * cols + h * HEAD : 2 * cols + (h + 1) * HEAD, :]
        va[h, HEAD:, :] = one
    acc[...] = jnp.zeros_like(acc)

    def row(i, _):
        qi = pl.ds(pl.multiple_of(i * TB, TB), TB)

        def col(j, _):
            kj = pl.ds(pl.multiple_of(j * TB, TB), TB)
            s = [nn(ka[h, kj, :], qa[h, :, qi]) for h in range(heads)]
            p = [jnp.exp2(v * (SCALE * LOG2E)).astype(BF) for v in s]
            for h in range(heads):
                acc[h, :, qi] += nn(va[h, :, kj], p[h])
            return 0

        return lax.fori_loop(span[i], span[nblk + i], col, 0)

    lax.fori_loop(0, nblk, row, 0)
    pad = ids[...] < 0
    lse[...] = jnp.zeros_like(lse)
    for h in range(heads):
        total = jnp.where(pad, 1.0, acc[h, HEAD : HEAD + 1, :])
        value = low[2 * cols + h * HEAD : 2 * cols + (h + 1) * HEAD, :].astype(F32)
        o = jnp.where(pad, value, acc[h, 0:HEAD, :] * (1.0 / total))
        out[h * HEAD : (h + 1) * HEAD, :] = o.astype(BF)
        lse[h : h + 1, :] = jnp.log(total)


def attend(span, low, ids, heads):
    cols, t = heads * HEAD, low.shape[1]
    return pl.pallas_call(
        functools.partial(attend_kernel, heads, t // TB),
        out_shape=(sds((cols, t), BF), sds((8, t), F32)),
        in_specs=[SM, VM, VM],
        out_specs=(VM, VM),
        scratch_shapes=[
            pltpu.VMEM((heads, 2 * HEAD, t), BF),
            pltpu.VMEM((heads, t, 2 * HEAD), BF),
            pltpu.VMEM((heads, HEAD + 16, t), BF),
            pltpu.VMEM((heads, HEAD + 16, t), F32),
        ],
        compiler_params=params(),
        cost_estimate=cost(12e9, 4 * 2**20),
        name="attend",
    )(span, low, ids)


def head_back(raw, gain, grad):
    hat, r = norm_cols(raw)
    e = grad * gain
    m1 = jnp.mean(e, axis=0, keepdims=True)
    m2 = jnp.mean(e * hat, axis=0, keepdims=True)
    return (e - m1 - hat * m2) * r, jnp.sum(grad * hat, axis=1, keepdims=True)


def attend_back_kernel(
    heads, nblk, span, low, raw, att, lse, dout, ids, gains, gproj, ggain, qa, ka, va, da, dq, dk, dv
):
    cols = heads * HEAD
    t = ids.shape[1]
    r, mq, mk = masks(ids[...])
    mk = mk.astype(BF)
    one = jnp.where(r < 3, 1.0, 0.0).astype(BF)
    for h in range(heads):
        hs = slice(h * HEAD, (h + 1) * HEAD)
        qa[h, 0:HEAD, :] = low[hs, :]
        a, b, c = three(lse[h : h + 1, :] * (-1.0 / SCALE))
        m = jnp.where(r == 32, a, jnp.where(r == 33, b, jnp.where(r == 34, c, mq)))
        qa[h, HEAD:, :] = m.astype(BF)
        k = low[cols + h * HEAD : cols + (h + 1) * HEAD, :]
        ka[h, :, :] = jnp.concatenate([k, mk], axis=0).T
        v = low[2 * cols + h * HEAD : 2 * cols + (h + 1) * HEAD, :]
        va[h, :, :] = jnp.concatenate([v, one], axis=0).T
        do = dout[hs, :]
        delta = jnp.sum(do.astype(F32) * att[hs, :].astype(F32), axis=0, keepdims=True)
        a, b, c = three(-delta)
        da[h, 0:HEAD, :] = do
        da[h, HEAD:, :] = jnp.where(
            r == 0, a, jnp.where(r == 1, b, jnp.where(r == 2, c, 0.0))
        ).astype(BF)
    dq[...] = jnp.zeros_like(dq)
    dk[...] = jnp.zeros_like(dk)
    dv[...] = jnp.zeros_like(dv)

    def row(i, _):
        qi = pl.ds(pl.multiple_of(i * TB, TB), TB)

        def col(j, _):
            kj = pl.ds(pl.multiple_of(j * TB, TB), TB)
            s = [nn(ka[h, kj, :], qa[h, :, qi]) for h in range(heads)]
            d = [nn(va[h, kj, :], da[h, :, qi]) for h in range(heads)]
            p = [jnp.exp2(v * (SCALE * LOG2E)) for v in s]
            ds = [(p[h] * d[h]).astype(BF) for h in range(heads)]
            for h in range(heads):
                hs = pl.ds(h * HEAD, HEAD)
                dv[hs, kj] += nt(dout[hs, qi], p[h].astype(BF))
                dk[hs, kj] += nt(low[hs, qi], ds[h])
                dq[hs, qi] += nn(low[pl.ds(cols + h * HEAD, HEAD), kj], ds[h])
            return 0

        return lax.fori_loop(span[i], span[nblk + i], col, 0)

    lax.fori_loop(0, nblk, row, 0)
    pad = ids[...] < 0
    for h in range(heads):
        hs = slice(h * HEAD, (h + 1) * HEAD)
        for part, grad in ((0, dq), (1, dk)):
            ps = slice(part * cols + h * HEAD, part * cols + (h + 1) * HEAD)
            g, gg = head_back(raw[ps, :], gains[ps, :], grad[hs, :] * SCALE)
            gproj[ps, :] = g.astype(BF)
            ggain[ps, :] = gg
        g = dv[hs, :] + jnp.where(pad, dout[hs, :].astype(F32), 0.0)
        gproj[2 * cols + h * HEAD : 2 * cols + (h + 1) * HEAD, :] = g.astype(BF)


def attend_back(span, low, raw, att, lse, dout, ids, gains, heads):
    cols, t = heads * HEAD, low.shape[1]
    return pl.pallas_call(
        functools.partial(attend_back_kernel, heads, t // TB),
        out_shape=(sds((3 * cols, t), BF), sds((2 * cols, 1), F32)),
        in_specs=[SM] + [VM] * 7,
        out_specs=(VM, VM),
        scratch_shapes=[
            pltpu.VMEM((heads, 2 * HEAD, t), BF),
            pltpu.VMEM((heads, t, 2 * HEAD), BF),
            pltpu.VMEM((heads, t, 2 * HEAD), BF),
            pltpu.VMEM((heads, 2 * HEAD, t), BF),
            pltpu.VMEM((cols, t), F32),
            pltpu.VMEM((cols, t), F32),
            pltpu.VMEM((cols, t), F32),
        ],
        compiler_params=params(),
        cost_estimate=cost(30e9, 12 * 2**20),
        name="attend_back",
    )(span, low, raw, att, lse, dout, ids, gains)


def place_out(pieces, dest):
    mp = lax.axis_index("mp")
    x, c = mp // 2, mp % 2
    order = (mp, (1 - x) * 2 + c, x * 2 + 1 - c, (1 - x) * 2 + 1 - c)
    rows = pieces[0].shape[0]
    for piece, m in zip(pieces, order):
        dest[pl.ds(pl.multiple_of(m * rows, rows), rows), :] = piece[...]


def middle_kernel(att, w0, w1, w2, w3, tok, bias, gain, shift, mid, low, wo):
    place_out((w0, w1, w2, w3), wo)
    m = tok[...].astype(F32) + tn(att[...], wo[...]) + bias[...]
    mid[...] = m
    hat, _ = norm_rows(m)
    low[...] = (hat * gain[...] + shift[...]).astype(BF)


def middle_part(att, wos, tok, bias, gain, shift):
    rows, d = tok.shape
    return pl.pallas_call(
        middle_kernel,
        out_shape=(sds((rows, d), F32), sds((rows, d), BF)),
        in_specs=[VM] * 9,
        out_specs=(VM, VM),
        scratch_shapes=[pltpu.VMEM((d, d), BF)],
        compiler_params=params(),
        cost_estimate=cost(2 * rows * d * d, 6 * 2**20),
        name="middle",
    )(att, *wos, tok, bias, gain, shift)


def middle_back_kernel(nmp, g0, g1, mid, cot, att, *refs):
    pieces, (gain, gmid, gatt, gwo, sums, wo) = refs[:-6], refs[-6:]
    if len(pieces) > 1:
        place_out(pieces, wo)
    else:
        wo = pieces[0]
    gy = cot[...].astype(F32)
    g = g0[...] + g1[...].astype(F32)
    hat, r = norm_rows(mid[...])
    e = g * gain[...]
    m1 = jnp.mean(e, axis=-1, keepdims=True)
    m2 = jnp.mean(e * hat, axis=-1, keepdims=True)
    gm = gy + (e - m1 - hat * m2) * r
    gmid[...] = gm
    low = gm.astype(BF)
    rows = att.shape[0] // nmp
    ga = nt(wo[...], low).astype(BF)
    for m in range(nmp):
        gatt[m] = ga[m * rows : (m + 1) * rows]
    gw = nt(gm.T.astype(BF), att[...]).astype(BF)
    mp = lax.axis_index("mp")
    for m in range(nmp):
        gwo[m] = gw[:, m * rows : (m + 1) * rows]
    sums[...] = jnp.zeros_like(sums)
    for k, v in enumerate((gm, g * hat, g, gy)):
        sums[k : k + 1, :] = jnp.sum(v, axis=0, keepdims=True)


def middle_back(g0, g1, mid, cot, att, wos, gain, nmp):
    rows, d = mid.shape
    return pl.pallas_call(
        functools.partial(middle_back_kernel, nmp),
        out_shape=(
            sds((rows, d), F32),
            sds((nmp, d // nmp, rows), BF),
            sds((nmp, d, d // nmp), BF),
            sds((8, d), F32),
        ),
        in_specs=[VM] * (6 + len(wos)),
        out_specs=(VM,) * 4,
        scratch_shapes=[pltpu.VMEM((d, d), BF)],
        compiler_params=params(),
        cost_estimate=cost(4 * rows * d * d, 10 * 2**20),
        name="middle_back",
    )(g0, g1, mid, cot, att, *wos, gain)


def feed_kernel(npiece, nz, first, *refs):
    n0, n1, c0, c1, bias = refs[:5]
    pieces = refs[5 : 5 + npiece]
    out_own, out_send, g_own, g_send, dwu, dwd, gbias = refs[5 + npiece : 12 + npiece]
    wu, wd, n2, gy, n2t, gyt, acts, gps, oacc, gacc, sem = refs[12 + npiece :]
    dp, mp = lax.axis_index("dp"), lax.axis_index("mp")
    z, y, x, c = dp // 2, dp % 2, mp // 2, mp % 2
    copies = []
    half = npiece // 2
    for a, piece in enumerate(pieces):
        dest = (wu, wd)[a // half]
        rel = a % half
        count, rows = piece.shape[0], piece.shape[1]
        for k in range(count):
            if half <= 2:
                at, colidx = 0, (k if half == 1 else rel)
            else:
                zz = (z + nz - k) % nz
                at = (zz * 2 + (y if rel % 2 == 0 else 1 - y)) * rows
                at, colidx = pl.multiple_of(at, rows), rel // 2
            cp = pltpu.make_async_copy(piece.at[k], dest.at[colidx, pl.ds(at, rows), :], sem.at[a, k])
            cp.start()
            copies.append(cp)
    hr = n0.shape[0]
    for i, (n, g) in enumerate(((n0, c0), (n1, c1))):
        part = slice(i * hr, (i + 1) * hr)
        n2[part, :] = n[...]
        gy[part, :] = g[...]
        n2t[:, part] = n[...].T
        gyt[:, part] = g[...].T
    oacc[...] = jnp.zeros_like(oacc)
    gacc[...] = jnp.zeros_like(gacc)
    for cp in copies:
        cp.wait()
    rows, d = n2.shape
    cw = acts.shape[1]
    per = wu.shape[2] // cw
    ones = jnp.ones((16, rows), BF)

    def chunk(i, _):
        col, off = i // per, pl.multiple_of((i % per) * cw, cw)
        cs = pl.ds(off, cw)
        m = jnp.where(col == 0, mp, (1 - x) * 2 + c)
        b = bias[pl.ds(first + m, 1), cs]
        for rb in range(rows // 256):
            rs = slice(rb * 256, (rb + 1) * 256)
            u = nn(n2[rs, :], wu[col, :, cs]) + b
            ga = nn(gy[rs, :], wd[col, :, cs])
            cdf = 0.5 + 0.5 * lax.erf(u * 0.7071067811865476)
            act = (u * cdf).astype(BF)
            gp = (ga * (cdf + u * (jnp.exp(-0.5 * u * u) * 0.3989422804014327))).astype(BF)
            acts[rs, :] = act
            gps[rs, :] = gp
            oacc[rs, :] += nt(act, wd[col, :, cs])
            gacc[rs, :] += nt(gp, wu[col, :, cs])
        dwd[col, :, cs] = nn(gyt[...], acts[...]).astype(BF)
        dwu[col, :, cs] = nn(n2t[...], gps[...]).astype(BF)
        gbias[col, :, cs] = nn(ones, gps[...])[0:8]
        return 0

    lax.fori_loop(0, 2 * per, chunk, 0)
    out_own[...] = oacc[0:hr]
    out_send[...] = oacc[hr:].astype(BF)
    g_own[...] = gacc[0:hr]
    g_send[...] = gacc[hr:].astype(BF)


def feed(n0, n1, c0, c1, bias, ups, downs, nz):
    hr, d = n0.shape
    rows, cw = 2 * hr, 256
    unit = ups[0].shape[2]
    pieces = list(ups) + list(downs)
    kmax = max(p.shape[0] for p in pieces)
    vm = pltpu.VMEM
    return pl.pallas_call(
        functools.partial(feed_kernel, len(pieces), nz, bias.shape[0] // 16 * 8),
        out_shape=(
            sds((hr, d), F32),
            sds((hr, d), BF),
            sds((hr, d), F32),
            sds((hr, d), BF),
            sds((2, d, unit), BF),
            sds((2, d, unit), BF),
            sds((2, 8, unit), F32),
        ),
        in_specs=[VM] * 5 + [ANY] * len(pieces),
        out_specs=(VM,) * 7,
        scratch_shapes=[
            vm((2, d, unit), BF),
            vm((2, d, unit), BF),
            vm((rows, d), BF),
            vm((rows, d), BF),
            vm((d, rows), BF),
            vm((d, rows), BF),
            vm((rows, cw), BF),
            vm((rows, cw), BF),
            vm((rows, d), F32),
            vm((rows, d), F32),
            pltpu.SemaphoreType.DMA((len(pieces), kmax)),
        ],
        compiler_params=params(),
        cost_estimate=cost(12 * rows * d * 2 * unit, 22 * 2**20),
        name="feed_forward",
    )(n0, n1, c0, c1, bias, *pieces)


def project_back_kernel(order, gproj, normed, tok, wt, gn, gw, sums, acc):
    @pl.when(pl.program_id(0) == 0)
    def _():
        acc[...] = jnp.zeros_like(acc)
        sums[...] = jnp.zeros_like(sums)

    acc[...] += nn(gproj[...], normed[...])
    g = tn(gproj[...], wt[...])
    gn[0] = g.astype(BF)
    hat, _ = norm_rows(tok[0].astype(F32))
    sums[0:1, :] += jnp.sum(g * hat, axis=0, keepdims=True)
    sums[1:2, :] += jnp.sum(g, axis=0, keepdims=True)

    @pl.when(pl.program_id(0) == pl.num_programs(0) - 1)
    def _():
        gw[...] = acc[...].T.astype(BF)


def project_back(order, gproj, normed, tok_all, wt):
    nb, rows, d = tok_all.shape
    n = gproj.shape[0]
    t = nb * rows
    return pl.pallas_call(
        project_back_kernel,
        grid_spec=pltpu.PrefetchScalarGridSpec(
            num_scalar_prefetch=1,
            grid=(nb,),
            in_specs=[
                pl.BlockSpec((n, rows), lambda i, o: (0, o[i])),
                pl.BlockSpec((rows, d), lambda i, o: (o[i], 0)),
                pl.BlockSpec((1, rows, d), lambda i, o: (o[i], 0, 0)),
                pl.BlockSpec((n, d), lambda i, o: (0, 0)),
            ],
            out_specs=(
                pl.BlockSpec((1, rows, d), lambda i, o: (i, 0, 0)),
                pl.BlockSpec((d, n), lambda i, o: (0, 0)),
                pl.BlockSpec((8, d), lambda i, o: (0, 0)),
            ),
            scratch_shapes=[pltpu.VMEM((n, d), F32)],
        ),
        out_shape=(sds((nb, rows, d), BF), sds((d, n), BF), sds((8, d), F32)),
        compiler_params=params(),
        cost_estimate=cost(4 * t * d * n, 14 * 2**20),
        name="project_back",
    )(order, gproj, normed, tok_all, wt)


def tokens_back(gn, tok, gain, gmid):
    hat, r = norm_rows(tok.astype(F32))
    e = gn * gain
    m1 = jnp.mean(e, axis=-1, keepdims=True)
    m2 = jnp.mean(e * hat, axis=-1, keepdims=True)
    return (gmid + (e - m1 - hat * m2) * r).astype(BF)


class Where:
    def __init__(self, nz):
        dp, mp = lax.axis_index("dp"), lax.axis_index("mp")
        z, y, x, c = dp // 2, dp % 2, mp // 2, mp % 2
        self.dp, self.mp, self.z, self.y, self.x, self.c = dp, mp, z, y, x, c
        self.xm, self.cm, self.dm = (1 - x) * 2 + c, x * 2 + 1 - c, (1 - x) * 2 + 1 - c
        self.ydp = z * 2 + 1 - y
        self.zfrom = [((z + nz - k) % nz) * 2 + y for k in range(nz)]
        self.yfrom = [((z + nz - k) % nz) * 2 + 1 - y for k in range(nz)]
        self.py, self.px, self.pc, self.pd = (self.ydp, mp), (dp, self.xm), (dp, self.cm), (dp, self.dm)
        self.pz = [None] + [(((z + k) % nz) * 2 + y, mp) for k in range(1, nz)]
        self.all = self.pz[1:] + [self.py, self.px, self.pc, self.pd]


class Sender:
    def __init__(self, ss, rs):
        self.ss, self.rs, self.n, self.open = ss, rs, 0, []

    def send(self, src, dst, peer):
        cp = rcopy(src, dst, self.ss.at[self.n], self.rs.at[self.n], peer)
        cp.start()
        self.n += 1
        self.open.append(cp)
        return cp

    def sent(self, cp):
        cp.wait_send()
        self.open = [o for o in self.open if o is not cp]

    def finish(self):
        for cp in self.open:
            cp.wait_send()


def vector_rows(vecv, small, d):
    nmp, ndp, vr, lanes = vecv.shape
    v = vecv[...].reshape(nmp * ndp * vr, lanes)
    parts = [p.astype(BF) for p in three(v)]
    lane = lax.broadcasted_iota(jnp.int32, (lanes, d), 1)
    sub = lax.broadcasted_iota(jnp.int32, (lanes, d), 0)
    s = lax.broadcasted_iota(jnp.int32, (nmp * ndp, vr, d), 0)
    col = lax.broadcasted_iota(jnp.int32, (nmp * ndp, vr, d), 2)
    dev = (s % ndp) * nmp + s // ndp

    def spread(width):
        sel = jnp.where(lane % width == sub, 1.0, 0.0).astype(BF)
        return sum(nn(p, sel) for p in parts).reshape(nmp * ndp, vr, d)

    a = jnp.sum(jnp.where(col // small == dev, spread(small), 0.0), axis=0)
    wide = nmp * small
    b = spread(wide)
    per = nmp * ndp // nmp
    ups = []
    for m in range(nmp):
        keep = (dev // per == m) & (col // wide == dev % per)
        ups.append(jnp.sum(jnp.where(keep, b, 0.0), axis=0)[8:9])
    return a[0:8], jnp.concatenate(ups, axis=0)


def front_kernel(nz, heads, small, *refs):
    tok, wup, wdn, cot = refs[:4]
    wq, wo, ids = refs[4:7]
    vecs = refs[7:16]
    normed_o, raw_o, tok_o, low_h, wt_h, wot_h, att_h, own_h, mid_h = refs[16:25]
    dwu_h, dwd_h, oown_h, gown_h, ogot_h, ggot_h = refs[25:31]
    lse, rows_o, gains, gbias = refs[31:35]
    tokv, wqv, vecv, normv, rawv, low_o, wt_o, wotv, att_o, own_o, mid_o, n2_o = refs[35:47]
    qa, ka, va, acc, wu_o, wd_o, cotv, cotx_o, n2x_o = refs[47:56]
    n2t, gyt, acts, gps, oacc, gacc, dwu, dwd, osend, gsend, ss, rs, ls = refs[56:]
    w = Where(nz)
    dp, mp = w.dp, w.mp
    cols = heads * HEAD
    t, d = normv.shape
    nmp, rows = tokv.shape[0], tokv.shape[1]
    greet(w.all)
    tx = Sender(ss, rs)
    count, late = [0], []

    def keep(src, dst, wait_late=True):
        cp = pltpu.make_async_copy(src, dst, ls.at[count[0]])
        cp.start()
        count[0] += 1
        if wait_late:
            late.append(cp)
        return cp

    nc = 4
    part = [pl.ds(i * (rows // nc), rows // nc) for i in range(nc)]
    xt = [tx.send(tok.at[part[i]], tokv.at[mp, part[i]], w.px) for i in range(nc)]
    vecv[mp, dp] = jnp.zeros(vecv.shape[2:], F32)
    for i, v in enumerate(vecs):
        vecv[mp, dp, i : i + 1, 0 : v.shape[1]] = v[...]
    ref = vecv.at[mp, dp]
    vz = [None] + [tx.send(ref, ref, w.pz[k]) for k in range(1, nz)]
    vy = [tx.send(ref, ref, w.py)]
    for i in range(3):
        wqv[dp, :, i * cols : (i + 1) * cols] = wq[i]
    wqv[dp, :, 3 * cols :] = wo[...]
    ref = wqv.at[dp]
    qz = [None] + [tx.send(ref, ref, w.pz[k]) for k in range(1, nz)]
    qy = [tx.send(ref, ref, w.py)]
    dx = tx.send(wdn, wd_o.at[1, dp], w.px)
    ux = [tx.send(wup, wu_o.at[1, dp], w.px)]
    ctok = tx.send(tok, tokv.at[mp], w.pc)
    cx = tx.send(cot, cotx_o, w.pc)
    own_tok = keep(tok, tokv.at[mp], False)
    own_w = [keep(wup, wu_o.at[0, dp], False), keep(wdn, wd_o.at[0, dp], False)]
    own_cot = keep(cot, cotv, False)
    for k in range(1, nz):
        vz[k].wait_recv()
        ref = vecv.at[mp, w.zfrom[k]]
        vy.append(tx.send(ref, ref, w.py))
    for k in range(nz):
        vy[k].wait_recv()
    vx = tx.send(vecv.at[mp], vecv.at[mp], w.px)
    vc = tx.send(vecv.at[mp], vecv.at[mp], w.pc)
    for k in range(1, nz):
        qz[k].wait_recv()
        ref = wqv.at[w.zfrom[k]]
        qy.append(tx.send(ref, ref, w.py))
    uz = [None] + [tx.send(wup, wu_o.at[0, dp], w.pz[k]) for k in range(1, nz)]
    uy = [tx.send(wup, wu_o.at[0, dp], w.py)]
    dy = [tx.send(wdn, wd_o.at[0, dp], w.py)]
    vx.wait_recv()
    vd = tx.send(vecv.at[w.xm], vecv.at[w.xm], w.pc)
    ct = []

    def forward(i):
        xt[i].wait_recv()
        ref = tokv.at[w.xm, part[i]]
        ct.append(tx.send(ref, ref, w.pc))

    forward(0)
    forward(1)
    vc.wait_recv()
    vd.wait_recv()
    main, ups = vector_rows(vecv, small, d)
    rows_o[0:8, :] = main
    rows_o[8:12, :] = ups
    rows_o[12:16, :] = jnp.zeros((4, d), F32)
    lane = lax.broadcasted_iota(jnp.int32, (cols, d), 1)
    pick = lane == lax.broadcasted_iota(jnp.int32, (cols, d), 0) + mp * cols
    for i in range(2):
        gains[i * cols : (i + 1) * cols, :] = jnp.sum(
            jnp.where(pick, main[2 + i : 3 + i], 0.0), axis=1, keepdims=True
        )
    for k in range(nz):
        qy[k].wait_recv()
    wall = wqv[...].reshape(d, 4 * cols).T
    wt_o[...] = wall[0 : 3 * cols]
    wotv[mp] = wall[3 * cols :]
    keep(wt_o, wt_h)
    one = jnp.where(lax.broadcasted_iota(jnp.int32, (16, rows), 0) == 0, 1.0, 0.0).astype(BF)

    def project(m):
        ts = pl.ds(pl.multiple_of(m * rows, rows), rows)
        hat, _ = norm_rows(tokv[m].astype(F32))
        n = (hat * rows_o[0:1, :] + rows_o[1:2, :]).astype(BF)
        normv[ts, :] = n
        proj = nt(wt_o[...], n)
        rawv[:, ts] = proj[0 : 2 * cols]
        _, mq, mk = masks(ids[:, ts])
        mq, mk = mq.astype(BF), mk.astype(BF)
        for h in range(heads):
            qs, ks = h * HEAD, cols + h * HEAD
            hat, _ = norm_cols(proj[qs : qs + HEAD])
            q = (hat * gains[qs : qs + HEAD, :]).astype(BF)
            low_o[qs : qs + HEAD, ts] = q
            qa[h, 0:HEAD, ts] = q
            qa[h, HEAD:, ts] = mq
            hat, _ = norm_cols(proj[ks : ks + HEAD])
            k = (hat * gains[ks : ks + HEAD, :]).astype(BF)
            low_o[ks : ks + HEAD, ts] = k
            ka[h, ts, :] = jnp.concatenate([k, mk], axis=0).T
            v = proj[2 * cols + h * HEAD : 2 * cols + (h + 1) * HEAD].astype(BF)
            low_o[2 * cols + h * HEAD : 2 * cols + (h + 1) * HEAD, ts] = v
            va[h, 0:HEAD, ts] = v
            va[h, HEAD:, ts] = one

    own_tok.wait()
    forward(2)
    ctok.wait_recv()
    forward(3)

    def near(i, _):
        project(jnp.where(i == 0, mp, w.cm))
        return 0

    lax.fori_loop(0, 2, near, 0)
    ox = tx.send(wotv.at[mp], wotv.at[mp], w.px)
    oc = tx.send(wotv.at[mp], wotv.at[mp], w.pc)
    uy[0].wait_recv()
    uw = [tx.send(wu_o.at[0, w.ydp], wu_o.at[1, w.ydp], w.px)]
    dz = [None] + [tx.send(wdn, wd_o.at[0, dp], w.pz[k]) for k in range(1, nz)]
    for cp in ct:
        cp.wait_recv()

    def both(i, _):
        project(jnp.where(i == 0, w.xm, w.dm))
        return 0

    lax.fori_loop(0, 2, both, 0)
    keep(normv, normed_o)
    keep(rawv, raw_o)
    keep(tokv, tok_o)
    keep(low_o, low_h)
    for k in range(1, nz):
        uz[k].wait_recv()
        ref = wu_o.at[0, w.zfrom[k]]
        uy.append(tx.send(ref, ref, w.py))
        ux.append(tx.send(ref, wu_o.at[1, w.zfrom[k]], w.px))
    dx.wait_recv()
    ref = wd_o.at[1, dp]
    ez = [None] + [tx.send(ref, ref, w.pz[k]) for k in range(1, nz)]
    ey = [tx.send(ref, ref, w.py)]

    def attend_row(i):
        qi = pl.ds(pl.multiple_of(i * rows, rows), rows)
        acc[...] = jnp.zeros_like(acc)

        def tile(j, _):
            kj = pl.ds(pl.multiple_of(j * rows, rows), rows)
            s = [nn(ka[h, kj, :], qa[h, :, qi]) for h in range(heads)]
            p = [jnp.exp2(v * (SCALE * LOG2E)).astype(BF) for v in s]
            for h in range(heads):
                acc[h] += nn(va[h, :, kj], p[h])
            return 0

        lax.fori_loop(jnp.maximum(i - 2, 0), jnp.minimum(i + 3, nmp), tile, 0)
        pad = ids[:, qi] < 0
        lse[:, qi] = jnp.zeros((8, rows), F32)
        for h in range(heads):
            total = jnp.where(pad, 1.0, acc[h, HEAD : HEAD + 1, :])
            value = va[h, 0:HEAD, qi].astype(F32)
            o = jnp.where(pad, value, acc[h, 0:HEAD, :] * (1.0 / total))
            att_o[h * HEAD : (h + 1) * HEAD, qi] = o.astype(BF)
            lse[h : h + 1, qi] = jnp.log(total)
        return att_o.at[:, qi]

    at = [tx.send(attend_row(w.xm), own_o.at[mp], w.px)]
    at.append(tx.send(attend_row(w.dm), own_o.at[mp], w.pd))
    for k in range(1, nz):
        uy[k].wait_recv()
        ref = wu_o.at[0, w.yfrom[k]]
        uw.append(tx.send(ref, wu_o.at[1, w.yfrom[k]], w.px))
    ox.wait_recv()
    od = tx.send(wotv.at[w.xm], wotv.at[w.xm], w.pc)
    at.append(tx.send(attend_row(w.cm), own_o.at[mp], w.pc))
    for k in range(1, nz):
        dz[k].wait_recv()
        ref = wd_o.at[0, w.zfrom[k]]
        dy.append(tx.send(ref, ref, w.py))
    own = keep(attend_row(mp), own_o.at[mp], False)
    keep(att_o, att_h)
    oc.wait_recv()
    od.wait_recv()
    keep(wotv, wot_h)
    own.wait()
    for cp in at:
        cp.wait_recv()
    keep(own_o, own_h)
    m = tokv[mp].astype(F32) + rows_o[4:5, :]
    m = m + tn(own_o[...].reshape(d, rows), wotv[...].reshape(d, d))
    mid_o[...] = m
    keep(mid_o, mid_h)
    hat, _ = norm_rows(m)
    n2_o[...] = (hat * rows_o[5:6, :] + rows_o[6:7, :]).astype(BF)
    nx = tx.send(n2_o, n2x_o, w.pc)
    own_cot.wait()
    cx.wait_recv()
    gyt[:, 0:rows] = cotv[...].T
    gyt[:, rows:] = cotx_o[...].T
    n2t[:, 0:rows] = n2_o[...].T
    for k in range(1, nz):
        ez[k].wait_recv()
        ref = wd_o.at[1, w.zfrom[k]]
        ey.append(tx.send(ref, ref, w.py))
    nx.wait_recv()
    n2t[:, rows:] = n2x_o[...].T
    unit = wu_o.shape[3]
    ones = jnp.ones((16, 2 * rows), BF)
    step = rows // 2

    def column(i, m):
        wu, wd = wu_o[i].reshape(d, unit), wd_o[i].reshape(d, unit)
        b = rows_o[pl.ds(8 + m, 1), :]
        for rb in range(4):
            rs = slice(rb * step, (rb + 1) * step)
            src = slice((rb % 2) * step, (rb % 2 + 1) * step)
            u = nn((n2_o, n2x_o)[rb // 2][src, :], wu) + b
            ga = nn((cotv, cotx_o)[rb // 2][src, :], wd)
            cdf = 0.5 + 0.5 * lax.erf(u * 0.7071067811865476)
            acts[rs, :] = (u * cdf).astype(BF)
            gps[rs, :] = (ga * (cdf + u * (jnp.exp(-0.5 * u * u) * 0.3989422804014327))).astype(BF)
        if i == 0:
            oacc[...] = nt(acts[...], wd)
            gacc[...] = nt(gps[...], wu)
        else:
            gacc[...] += nt(gps[...], wu)
            gsend[...] = gacc[rows:].astype(BF)
            gx = tx.send(gsend, ggot_h, w.pc)
            oacc[...] += nt(acts[...], wd)
            osend[...] = oacc[rows:].astype(BF)
            sent.extend([gx, tx.send(osend, ogot_h, w.pc)])
            keep(gacc.at[0:rows], gown_h)
            keep(oacc.at[0:rows], oown_h)
        dwd[i] = nn(gyt[...], acts[...]).astype(BF)
        keep(dwd.at[i], dwd_h.at[i])
        dwu[i] = nn(n2t[...], gps[...]).astype(BF)
        keep(dwu.at[i], dwu_h.at[i])
        gbias[i] = nn(ones, gps[...])[0:8]

    sent = []
    for cp in own_w:
        cp.wait()
    for cp in dy:
        cp.wait_recv()
    column(0, mp)
    for cp in ux + ey + uw:
        cp.wait_recv()
    column(1, w.xm)
    for cp in sent:
        cp.wait_recv()
    tx.finish()
    for cp in late:
        cp.wait()


def front(tok, wq, wo, wup, wdn, vecs, cot, ids, ndp, nmp):
    rows, d = tok.shape
    drow, unit, cols = wup.shape[0], wup.shape[1], wo.shape[1]
    small = vecs[0].shape[1]
    heads, t, nsend, nlocal = cols // HEAD, rows * nmp, 80, 32
    dma, vm = pltpu.SemaphoreType.DMA, pltpu.VMEM
    return pl.pallas_call(
        functools.partial(front_kernel, ndp // 2, heads, small),
        out_shape=(
            sds((t, d), BF),
            sds((2 * cols, t), F32),
            sds((nmp, rows, d), BF),
            sds((3 * cols, t), BF),
            sds((3 * cols, d), BF),
            sds((nmp, cols, d), BF),
            sds((cols, t), BF),
            sds((nmp, cols, rows), BF),
            sds((rows, d), F32),
            sds((2, d, unit), BF),
            sds((2, d, unit), BF),
            sds((rows, d), F32),
            sds((rows, d), F32),
            sds((rows, d), BF),
            sds((rows, d), BF),
            sds((8, t), F32),
            sds((16, d), F32),
            sds((2 * cols, 1), F32),
            sds((2, 8, unit), F32),
        ),
        in_specs=[ANY] * 4 + [VM] * 12,
        out_specs=(ANY,) * 15 + (VM,) * 4,
        scratch_shapes=[
            vm((nmp, rows, d), BF),
            vm((ndp, drow, 4 * cols), BF),
            vm((nmp, ndp, 16, 128), F32),
            vm((t, d), BF),
            vm((2 * cols, t), F32),
            vm((3 * cols, t), BF),
            vm((3 * cols, d), BF),
            vm((nmp, cols, d), BF),
            vm((cols, t), BF),
            vm((nmp, cols, rows), BF),
            vm((rows, d), F32),
            vm((rows, d), BF),
            vm((heads, 2 * HEAD, t), BF),
            vm((heads, t, 2 * HEAD), BF),
            vm((heads, HEAD + 16, t), BF),
            vm((heads, HEAD + 16, rows), F32),
            vm((2, ndp, drow, unit), BF),
            vm((2, ndp, drow, unit), BF),
            vm((rows, d), BF),
            vm((rows, d), BF),
            vm((rows, d), BF),
            vm((d, 2 * rows), BF),
            vm((d, 2 * rows), BF),
            vm((2 * rows, unit), BF),
            vm((2 * rows, unit), BF),
            vm((2 * rows, d), F32),
            vm((2 * rows, d), F32),
            vm((2, d, unit), BF),
            vm((2, d, unit), BF),
            vm((rows, d), BF),
            vm((rows, d), BF),
            dma((nsend,)),
            dma((nsend,)),
            dma((nlocal,)),
        ],
        compiler_params=params(collective_id=4, has_side_effects=True),
        cost_estimate=cost(40e9, 60 * 2**20),
        name="front",
    )(tok, wup, wdn, cot, wq, wo, ids, *vecs)


def three_sum(m, sel):
    return sum(nn(p.astype(BF), sel) for p in three(m))


def pack_vectors(main, gb0, gb1, w, small, vt):
    nmp, nz = vt.shape[0], vt.shape[1]
    n, d = nmp * nz * 2, main.shape[1]
    s = lax.broadcasted_iota(jnp.int32, (n, 8, d), 0)
    v = lax.broadcasted_iota(jnp.int32, (n, 8, d), 1)
    l = lax.broadcasted_iota(jnp.int32, (n, 8, d), 2)
    per = n // nmp
    dev = (s % per) * nmp + s // per
    sub = lax.broadcasted_iota(jnp.int32, (d, 128), 0)
    lane = lax.broadcasted_iota(jnp.int32, (d, 128), 1)
    m = jnp.where(l // small == dev, main[None], 0.0).reshape(n * 8, d)
    sel = jnp.where(sub % small == lane, 1.0, 0.0).astype(BF)
    a = three_sum(m, sel).reshape(n, 8, 128)
    wide = nmp * small
    here = (l // wide == dev % per) & (v == 0)
    m = jnp.where(here & (dev // per == w.mp), gb0[None], 0.0)
    m = m + jnp.where(here & (dev // per == w.xm), gb1[None], 0.0)
    sel = jnp.where(sub % wide == lane, 1.0, 0.0).astype(BF)
    b = three_sum(m.reshape(n * 8, d), sel).reshape(n, 8, 128)
    vt[...] = jnp.concatenate([a, b], axis=1).reshape(vt.shape)


def back_kernel(nz, heads, small, *refs):
    g_own, g_send, o_own, o_send, mid, cot, att_own, wot, wt, low = refs[:10]
    att, raw, normed, tok_all, dwu, dwd, lse, rowv, gains, ids, gbias = refs[10:21]
    res_o, gtok_o, gq_o, go_o, gu_o, gd_o, vec_o = refs[21:28]
    (
        f1, f2, f3, ggot, ogot, cotv, attov, wotv, wtv, lowv, attv, rawv, dwdc, dwuc,
        rxu, ryu, ru, rzu, ryd, rzd, rd, rxd, gattv, doutv, gwov, rco, go2, rxo, gov, ryo, ro, rzo,
        gprojv, qa, ka, va, da, dk, dv, dqa, tokv, normv, acc, gnv, rgc, rgx, dwqv, ryq, rq, rzq, sumv, ggv, vt, rv1, rv2, rv3, va4, rv4,
        ss, rs, ls,
    ) = refs[28:]
    w = Where(nz)
    dp, mp, z, y = w.dp, w.mp, w.z, w.y
    cols = heads * HEAD
    t = lowv.shape[1]
    rows, d = f1.shape
    nmp = t // rows
    greet(w.all)
    tx = Sender(ss, rs)
    count = [0]
    zto = [(z + k) % nz for k in range(nz)]

    def load(src, dst):
        cp = pltpu.make_async_copy(src, dst, ls.at[count[0]])
        cp.start()
        count[0] += 1
        return cp

    l1 = [load(g_send, ggot), load(g_own, f1), load(mid, f2), load(cot, cotv), load(wot, wotv)]
    l2 = [load(o_send, ogot), load(o_own, f3), load(att_own, attov), load(low, lowv), load(att, attv)]
    far = [2 % nz, 1 % nz] + list(range(3, nz)) + [0]
    dy, ux, uy, dz, uz, own_d, own_u = {}, {}, {}, [], [], {}, {}

    def fetch_own(n):
        if n < nz:
            k = far[n]
            own_d[k] = load(dwd.at[:, zto[k], y], dwdc.at[n % 2])
            own_u[k] = load(dwu.at[0, zto[k]], dwuc.at[n % 2])

    def down_y(n):
        k = far[n]
        own_d[k].wait()
        dy[k].wait_recv()
        for c in range(2):
            ryd[c, zto[k]] = (ryd[c, zto[k]].astype(F32) + dwdc[n % 2, c].astype(F32)).astype(BF)
        if k:
            dz.append(tx.send(ryd.at[:, zto[k]], rzd.at[k - 1], w.pz[k]))

    def up_x(n):
        k = far[n]
        own_u[k].wait()
        ux[k].wait_recv()
        rxu[zto[k]] = (rxu[zto[k]].astype(F32) + dwuc[n % 2].astype(F32)).astype(BF)
        uy[k] = tx.send(rxu.at[zto[k], 1 - y], ryu.at[zto[k]], w.py)

    def up_y(n):
        k = far[n]
        uy[k].wait_recv()
        ru[zto[k]] = (rxu[zto[k], y].astype(F32) + ryu[zto[k]].astype(F32)).astype(BF)
        if k:
            uz.append(tx.send(ru.at[zto[k]], rzu.at[k - 1], w.pz[k]))

    for k in far:
        dy[k] = tx.send(dwd.at[:, zto[k], 1 - y], ryd.at[:, zto[k]], w.py)
    ux[far[0]] = tx.send(dwu.at[1, zto[far[0]]], rxu.at[zto[far[0]]], w.px)
    l3 = [load(wt, wtv), load(raw, rawv)]
    fetch_own(0)
    fetch_own(1)

    for cp in l1:
        cp.wait()
    gy = cotv[...].astype(F32)
    g = f1[...] + ggot[...].astype(F32)
    hat, r = norm_rows(f2[...])
    e = g * rowv[5:6, :]
    m1 = jnp.mean(e, axis=-1, keepdims=True)
    m2 = jnp.mean(e * hat, axis=-1, keepdims=True)
    gm = gy + (e - m1 - hat * m2) * r
    sumv[...] = jnp.zeros_like(sumv)
    for k, v in enumerate((gm, g * hat, g, gy)):
        sumv[4 + k : 5 + k, :] = jnp.sum(v, axis=0, keepdims=True)
    f1[...] = gm
    gmb = gm.astype(BF)
    gattv[...] = nt(wotv[...], gmb).astype(BF).reshape(nmp, cols, rows)

    def block(m):
        return pl.ds(pl.multiple_of(m * rows, rows), rows)

    ax = tx.send(gattv.at[w.xm], doutv.at[:, block(mp)], w.px)
    ad = tx.send(gattv.at[w.dm], doutv.at[:, block(mp)], w.pd)
    ac = tx.send(gattv.at[w.cm], doutv.at[:, block(mp)], w.pc)
    for k in far[1:]:
        ux[k] = tx.send(dwu.at[1, zto[k]], rxu.at[zto[k]], w.px)
    own = load(gattv.at[mp], doutv.at[:, block(mp)])
    for cp in l2:
        cp.wait()
    res_o[...] = (f2[...] + f3[...] + ogot[...].astype(F32) + rowv[7:8, :]).astype(BF)
    gw = nt(gm.T.astype(BF), attov[...]).astype(BF)
    for m in range(nmp):
        gwov[m] = gw[:, m * cols : (m + 1) * cols].reshape(gwov.shape[1:])
    oc = [tx.send(gwov.at[w.cm], rco.at[0], w.pc), tx.send(gwov.at[w.dm], rco.at[1], w.pc)]
    for cp in l3:
        cp.wait()
    down_y(0)
    ggv[...] = jnp.zeros_like(ggv)

    def attention(qa, ka, va, da, dk, dv):
        def build(m, _):
            ts = block(m)
            r, _, mk = masks(ids[:, ts])
            mk = mk.astype(BF)
            one = jnp.where(r < 3, 1.0, 0.0).astype(BF)
            for h in range(heads):
                k = lowv[cols + h * HEAD : cols + (h + 1) * HEAD, ts]
                ka[h, ts, :] = jnp.concatenate([k, mk], axis=0).T
                v = lowv[2 * cols + h * HEAD : 2 * cols + (h + 1) * HEAD, ts]
                va[h, ts, :] = jnp.concatenate([v, one], axis=0).T
            return 0

        lax.fori_loop(0, nmp, build, 0)
        dk[...] = jnp.zeros_like(dk)
        dv[...] = jnp.zeros_like(dv)

        def row(i):
            qi = block(i)
            r, mq, _ = masks(ids[:, qi])
            for h in range(heads):
                hs = slice(h * HEAD, (h + 1) * HEAD)
                qa[h, 0:HEAD, :] = lowv[hs, qi]
                a, b, c = three(lse[h : h + 1, qi] * (-1.0 / SCALE))
                aug = jnp.where(r == 32, a, jnp.where(r == 33, b, jnp.where(r == 34, c, mq)))
                qa[h, HEAD:, :] = aug.astype(BF)
                do = doutv[hs, qi]
                delta = jnp.sum(do.astype(F32) * attv[hs, qi].astype(F32), axis=0, keepdims=True)
                a, b, c = three(-delta)
                da[h, 0:HEAD, :] = do
                da[h, HEAD:, :] = jnp.where(
                    r == 0, a, jnp.where(r == 1, b, jnp.where(r == 2, c, 0.0))
                ).astype(BF)
            dqa[...] = jnp.zeros_like(dqa)

            def tile(j, _):
                kj = block(j)
                s = [nn(ka[h, kj, :], qa[h]) for h in range(heads)]
                e = [nn(va[h, kj, :], da[h]) for h in range(heads)]
                p = [jnp.exp2(v * (SCALE * LOG2E)) for v in s]
                ds = [(p[h] * e[h]).astype(BF) for h in range(heads)]
                for h in range(heads):
                    hs = slice(h * HEAD, (h + 1) * HEAD)
                    dv[hs, kj] += nt(da[h, 0:HEAD, :], p[h].astype(BF))
                    dk[hs, kj] += nt(lowv[hs, qi], ds[h])
                    dqa[hs, :] += nn(lowv[cols + h * HEAD : cols + (h + 1) * HEAD, kj], ds[h])
                return 0

            lax.fori_loop(jnp.maximum(i - 2, 0), jnp.minimum(i + 3, nmp), tile, 0)
            for h in range(heads):
                hs = slice(h * HEAD, (h + 1) * HEAD)
                v, gg = head_back(rawv[hs, qi], gains[hs, :], dqa[hs, :] * SCALE)
                gprojv[hs, qi] = v.astype(BF)
                ggv[hs, :] += gg

        up_x(0)
        fetch_own(2)
        own.wait()
        row(mp)
        down_y(1)
        for cp in oc:
            cp.wait_recv()
        go2[...] = (gwov[w.xm].astype(F32) + rco[1].astype(F32)).astype(BF)
        oxx = tx.send(go2, rxo, w.px)
        ac.wait_recv()
        row(w.cm)
        down_y(2)
        up_x(1)
        up_y(0)
        fetch_own(3)
        ax.wait_recv()
        row(w.xm)
        down_y(3)
        up_x(2)
        up_y(1)
        ad.wait_recv()
        row(w.dm)
        up_x(3)
        up_y(2)
        oxx.wait_recv()
        gov[...] = (gwov[mp].astype(F32) + rco[0].astype(F32) + rxo[...].astype(F32)).astype(BF)
        oy = tx.send(gov.at[:, 1 - y], ryo, w.py)

        def keys(m, _):
            ts = block(m)
            pad = ids[:, ts] < 0
            for h in range(heads):
                hs = slice(h * HEAD, (h + 1) * HEAD)
                ps = slice(cols + h * HEAD, cols + (h + 1) * HEAD)
                v, gg = head_back(rawv[ps, ts], gains[ps, :], dk[hs, ts] * SCALE)
                gprojv[ps, ts] = v.astype(BF)
                ggv[ps, :] += gg
                v = dv[hs, ts] + jnp.where(pad, doutv[hs, ts].astype(F32), 0.0)
                gprojv[2 * cols + h * HEAD : 2 * cols + (h + 1) * HEAD, ts] = v.astype(BF)
            return 0

        lax.fori_loop(0, nmp, keys, 0)
        return oy

    oy = attention(qa, ka, va, da, dk, dv)

    def projections(tokv, normv, acc):
        acc[...] = jnp.zeros_like(acc)

        def part(m):
            return tn(gprojv[:, block(m)], wtv[...])

        order = (w.dm, w.xm, w.cm, mp)

        def fetch_norm(n):
            return load(normed.at[block(order[n]), :], normv.at[n % 2])

        def fetch_tok(n):
            return load(tok_all.at[order[n]], tokv.at[n % 2])

        def weights(n, cp):
            cp.wait()
            acc[...] += nn(gprojv[:, block(order[n])], normv[n % 2])

        def gain_sums(n, g, cp):
            cp.wait()
            hat, _ = norm_rows(tokv[n % 2].astype(F32))
            sumv[0:1, :] += jnp.sum(g * hat, axis=0, keepdims=True)
            sumv[1:2, :] += jnp.sum(g, axis=0, keepdims=True)

        n0, n1, t0, t1 = fetch_norm(0), fetch_norm(1), fetch_tok(0), fetch_tok(1)
        g = part(w.dm)
        gnv[0] = g.astype(BF)
        c1 = tx.send(gnv.at[0], rgc.at[1], w.pc)
        f2[...] = part(w.xm)
        c1.wait_recv()
        gnv[1] = (f2[...] + rgc[1].astype(F32)).astype(BF)
        gxx = tx.send(gnv.at[1], rgx, w.px)
        weights(0, n0)
        n2 = fetch_norm(2)
        weights(1, n1)
        n3 = fetch_norm(3)
        weights(2, n2)
        weights(3, n3)
        dwqv[...] = acc[...].T.astype(BF).reshape(dwqv.shape)
        qy = {}
        for k in far:
            qy[k] = tx.send(dwqv.at[zto[k], 1 - y], ryq.at[zto[k]], w.py)
        up_y(3)
        gain_sums(0, g, t0)
        t2 = fetch_tok(2)
        qz = []

        def qkv_y(n):
            k = far[n]
            qy[k].wait_recv()
            rq[zto[k]] = (dwqv[zto[k], y].astype(F32) + ryq[zto[k]].astype(F32)).astype(BF)
            if k:
                qz.append(tx.send(rq.at[zto[k]], rzq.at[k - 1], w.pz[k]))

        oy.wait_recv()
        ro[...] = (gov[:, y].astype(F32) + ryo[...].astype(F32)).astype(BF)
        oz = [tx.send(ro.at[zto[k]], rzo.at[k - 1], w.pz[k]) for k in range(1, nz)]
        gain_sums(1, f2[...], t1)
        t3 = fetch_tok(3)
        qkv_y(0)
        for cp in dz:
            cp.wait_recv()
        tot = ryd[:, z].astype(F32)
        for k in range(nz - 1):
            tot = tot + rzd[k].astype(F32)
        rd[...] = tot[1].astype(BF)
        dx = tx.send(rd, rxd, w.px)
        gd_o[...] = tot[0]
        g = part(w.cm)
        tx.sent(c1)
        gnv[0] = g.astype(BF)
        c2 = tx.send(gnv.at[0], rgc.at[0], w.pc)
        gain_sums(2, g, t2)
        qkv_y(1)
        f2[...] = part(mp)
        gain_sums(3, f2[...], t3)
        qkv_y(2)
        qkv_y(3)
        lane = lax.broadcasted_iota(jnp.int32, (cols, d), 1)
        pick = lane == lax.broadcasted_iota(jnp.int32, (cols, d), 0) + mp * cols
        for i in range(2):
            v = jnp.where(pick, ggv[i * cols : (i + 1) * cols, :], 0.0)
            sumv[2 + i : 3 + i, :] = jnp.sum(v, axis=0, keepdims=True)
        pack_vectors(sumv[...], gbias[0, 0:1, :], gbias[1, 0:1, :], w, small, vt)
        v1 = [tx.send(vt.at[w.cm], rv1.at[0], w.pc), tx.send(vt.at[w.dm], rv1.at[1], w.pc)]
        for cp in v1:
            cp.wait_recv()
        vt[w.xm] = vt[w.xm] + rv1[1]
        v2 = tx.send(vt.at[w.xm], rv2, w.px)
        v2.wait_recv()
        vt[mp] = vt[mp] + rv1[0] + rv2[...]
        v3 = tx.send(vt.at[mp, :, 1 - y], rv3, w.py)
        c2.wait_recv()
        f2[...] += rgc[0].astype(F32)
        v3.wait_recv()
        va4[...] = vt[mp, :, y] + rv3[...]
        v4 = [tx.send(va4.at[zto[k]], rv4.at[k - 1], w.pz[k]) for k in range(1, nz)]

        def last(copies, own, got, out):
            for cp in copies:
                cp.wait_recv()
            tot = own.astype(F32)
            for k in range(nz - 1):
                tot = tot + got[k].astype(F32)
            out[...] = tot

        last(uz, ru[z], rzu, gu_o)
        last(oz, ro[z], rzo, go_o)
        last(v4, va4[z], rv4, vec_o)
        dx.wait_recv()
        gd_o[...] += rxd[...].astype(F32)
        last(qz, rq[z], rzq, gq_o)
        gxx.wait_recv()
        g = f2[...] + rgx[...].astype(F32)
        hat, r = norm_rows(tokv[1].astype(F32))
        e = g * rowv[0:1, :]
        m1 = jnp.mean(e, axis=-1, keepdims=True)
        m2 = jnp.mean(e * hat, axis=-1, keepdims=True)
        gtok_o[...] = (f1[...] + (e - m1 - hat * m2) * r).astype(BF)

    projections(tokv, normv, acc)
    tx.finish()


def back(hbm, small_in, nz, heads, small):
    g_own, dwu = hbm[0], hbm[14]
    rows, d = g_own.shape
    drow, unit = dwu.shape[3], dwu.shape[4]
    cols = heads * HEAD
    nmp = d // cols
    t = nmp * rows
    v = pltpu.VMEM
    dma = pltpu.SemaphoreType.DMA
    scratch = [
        v((rows, d), F32), v((rows, d), F32), v((rows, d), F32),
        v((rows, d), BF), v((rows, d), BF), v((rows, d), BF), v((d, rows), BF), v((d, d), BF),
        v((3 * cols, d), BF), v((3 * cols, t), BF), v((cols, t), BF), v((2 * cols, t), F32),
        v((2, 2, drow, unit), BF), v((2, 2, drow, unit), BF),
        v((nz, 2, drow, unit), BF), v((nz, drow, unit), BF), v((nz, drow, unit), BF), v((nz - 1, drow, unit), BF),
        v((2, nz, drow, unit), BF), v((nz - 1, 2, drow, unit), BF), v((drow, unit), BF), v((drow, unit), BF),
        v((nmp, cols, rows), BF), v((cols, t), BF),
        v((nmp, nz, 2, drow, cols), BF), v((2, nz, 2, drow, cols), BF), v((nz, 2, drow, cols), BF),
        v((nz, 2, drow, cols), BF), v((nz, 2, drow, cols), BF),
        v((nz, drow, cols), BF), v((nz, drow, cols), BF), v((nz - 1, drow, cols), BF),
        v((3 * cols, t), BF),
        v((heads, 2 * HEAD, rows), BF), v((heads, t, 2 * HEAD), BF), v((heads, t, 2 * HEAD), BF),
        v((heads, 2 * HEAD, rows), BF), v((cols, t), F32), v((cols, t), F32), v((cols, rows), F32),
        v((2, rows, d), BF), v((2, rows, d), BF), v((3 * cols, d), F32),
        v((2, rows, d), BF), v((2, rows, d), BF), v((rows, d), BF),
        v((nz, 2, drow, 3 * cols), BF), v((nz, drow, 3 * cols), BF), v((nz, drow, 3 * cols), BF),
        v((nz - 1, drow, 3 * cols), BF),
        v((8, d), F32), v((2 * cols, 1), F32),
        v((nmp, nz, 2, 16, 128), F32), v((2, nz, 2, 16, 128), F32), v((nz, 2, 16, 128), F32),
        v((nz, 16, 128), F32), v((nz, 16, 128), F32), v((nz - 1, 16, 128), F32),
        dma((64,)), dma((64,)), dma((40,)),
    ]
    return pl.pallas_call(
        functools.partial(back_kernel, nz, heads, small),
        out_shape=(
            sds((rows, d), BF),
            sds((rows, d), BF),
            sds((drow, 3 * cols), F32),
            sds((drow, cols), F32),
            sds((drow, unit), F32),
            sds((drow, unit), F32),
            sds((16, 128), F32),
        ),
        in_specs=[ANY] * len(hbm) + [VM] * len(small_in),
        out_specs=(VM,) * 7,
        scratch_shapes=scratch,
        compiler_params=params(collective_id=5, has_side_effects=True),
        cost_estimate=cost(40e9, 60 * 2**20),
        name="back",
    )(*hbm, *small_in)


def finish_kernel(small, wide, res, gtok, gq, go, gu, gd, vec, *outs):
    outs[0][...] = res[...]
    outs[1][...] = gtok[...]
    cols = go.shape[1]
    for i in range(3):
        outs[2][i] = gq[:, i * cols : (i + 1) * cols]
    outs[3][...] = go[...]
    outs[4][...] = gu[...]
    outs[5][...] = gd[...]
    for i in range(8):
        outs[6 + i][...] = vec[i : i + 1, 0:small]
    outs[14][...] = vec[8:9, 0:wide]


def finish(res, gtok, gq, go, gu, gd, vec, small, wide):
    n = 2

    def rows(a):
        return pl.BlockSpec((a.shape[0] // n, a.shape[1]), lambda i: (i, 0))

    def whole(shape):
        return pl.BlockSpec(shape, lambda i: (0,) * len(shape))

    drow, cols = go.shape
    like = [sds(a.shape, a.dtype) for a in (res, gtok)]
    like += [sds((3, drow, cols), F32)] + [sds(a.shape, F32) for a in (go, gu, gd)]
    like += [sds((1, small), F32)] * 8 + [sds((1, wide), F32)]
    specs = [rows(res), rows(gtok), pl.BlockSpec((3, drow // n, cols), lambda i: (0, i, 0))]
    specs += [rows(go), rows(gu), rows(gd)] + [whole((1, small))] * 8 + [whole((1, wide))]
    return pl.pallas_call(
        functools.partial(finish_kernel, small, wide),
        grid=(n,),
        out_shape=tuple(like),
        in_specs=[rows(a) for a in (res, gtok, gq, go, gu, gd)] + [whole(vec.shape)],
        out_specs=tuple(specs),
        compiler_params=params(),
        name="finish",
    )(res, gtok, gq, go, gu, gd, vec)


def spans(ids):
    b = ids.reshape(-1, TB)
    low = jnp.min(jnp.where(b < 0, 1000, b), axis=1)
    high = jnp.max(b, axis=1)
    n = b.shape[0]
    k = jnp.arange(n)
    lo = jnp.sum((high[None, :] < low[:, None]) & (k[None, :] <= k[:, None]), axis=1)
    hi = jnp.sum(low[None, :] <= high[:, None], axis=1)
    return jnp.concatenate([lo, hi]).astype(jnp.int32)


def solution(mesh):
    ndp, nmp = mesh.shape["dp"], mesh.shape["mp"]
    ndev, nz = ndp * nmp, ndp // 2

    def permute(v, kind, k=0):
        pairs = []
        for d in range(ndp):
            for m in range(nmp):
                z, y, x, c = d // 2, d % 2, m // 2, m % 2
                if kind == "core":
                    c = 1 - c
                if kind == "x":
                    x = 1 - x
                if kind == "y":
                    y = 1 - y
                if kind == "z":
                    z = (z + k) % nz
                pairs.append((d * nmp + m, (z * 2 + y) * nmp + x * 2 + c))
        return lax.ppermute(v, ("dp", "mp"), pairs)

    def columns(w, first, second):
        if w.shape[0] % 16:
            own = lax.all_gather(w, "dp", axis=0, tiled=True)[None]
            return [own, permute(own, "x")]
        s = jnp.stack([w] + [permute(w, "z", k) for k in range(1, nz)])
        got = {(0, 0): s}
        one = permute(s, first)
        two = permute(s, second)
        both = permute(one, second)
        got[(0, 1)] = one if first == "y" else two
        got[(1, 0)] = two if first == "y" else one
        got[(1, 1)] = both
        return [got[(0, 0)], got[(0, 1)], got[(1, 0)], got[(1, 1)]]

    def body(
        tokens,
        picture_ids,
        w_qkv,
        w_out,
        w_up,
        w_down,
        ln1_gain,
        ln1_bias,
        q_gain,
        k_gain,
        out_bias,
        ln2_gain,
        ln2_bias,
        up_bias,
        down_bias,
        cotangent,
    ):
        rows, d = tokens.shape[1], tokens.shape[2]
        drow = w_qkv.shape[0]
        cols = w_qkv.shape[2]
        heads = cols // HEAD
        unit = w_up.shape[1]
        dp, mp = lax.axis_index("dp"), lax.axis_index("mp")
        z, y, x, c = dp // 2, dp % 2, mp // 2, mp % 2
        tok, cot = tokens[0], cotangent[0]
        ids = picture_ids
        span = spans(ids[0])
        whole = drow % 16 == 0 and ndev == 32

        vs = [ln1_gain, ln1_bias, q_gain, k_gain, out_bias, ln2_gain, ln2_bias, down_bias, up_bias]
        small = vs[0].shape[0]
        used = 8 * small + up_bias.shape[0]
        if whole:
            (
                normed,
                raw,
                tok_all,
                low,
                wt,
                wot,
                att,
                att_own,
                mid,
                dwu,
                dwd,
                o_own,
                g_own,
                o_got,
                g_got,
                lse,
                rowv,
                gains,
                gbias,
            ) = front(
                tok,
                w_qkv.transpose(1, 0, 2),
                w_out,
                w_up,
                w_down,
                [v.reshape(1, -1) for v in vs],
                cot,
                ids,
                ndp,
                nmp,
            )
            att_own = att_own.reshape(d, rows)
            shape = (2, nz, 2, drow, unit)
            res, gtok, gqw, gow, gup, gdn, vt = back(
                (g_own, g_got, o_own, o_got, mid, cot, att_own, wot.reshape(d, d), wt, low)
                + (att, raw, normed, tok_all, dwu.reshape(shape), dwd.reshape(shape)),
                (lse, rowv, gains, ids, gbias),
                nz,
                heads,
                small,
            )
            out = finish(res, gtok, gqw, gow, gup, gdn, vt, small, nmp * small)
            vg = [v.reshape(-1) for v in out[6:]]
            return (
                out[0][None],
                out[1][None],
                out[2].transpose(1, 0, 2),
                out[3],
                out[4],
                out[5],
                *vg[:7],
                vg[8],
                vg[7],
            )
        else:
            flat = jnp.concatenate(vs)
            vec = jnp.pad(flat, (0, 1024 - used)).reshape(8, 128)
            wcat = jnp.concatenate([w_qkv.reshape(drow, 3 * cols), w_out], axis=1)
            tok_all, w_all, vec_all = gather_all(tok, wcat, vec, ndp, nmp)
            vec_all = vec_all.reshape(nmp, ndp, 1024).transpose(1, 0, 2).reshape(ndev, 1024)
            gain1, shift1, qg, kg, obias, gain2, shift2, dbias = [
                vec_all[:, i * small : (i + 1) * small].reshape(1, d) for i in range(8)
            ]
            ubias = vec_all[:, 8 * small : used].reshape(nmp, unit)
            gains = jnp.concatenate(
                [
                    lax.dynamic_slice_in_dim(qg[0], mp * cols, cols),
                    lax.dynamic_slice_in_dim(kg[0], mp * cols, cols),
                ]
            ).reshape(2 * cols, 1)

            ups = columns(w_up, "y", "x")
            downs = columns(w_down, "x", "y")
            cot_other = permute(cot, "core")

            normed, raw, low, wt = project(
                tok_all, w_all.reshape(d, 3 * cols + w_out.shape[1]), gain1, shift1, gains, heads
            )
            wo0 = wt[3 * cols :]
            wo1 = permute(wo0, "x")
            wo2, wo3 = permute(wo0, "core"), permute(wo1, "core")
            wos = (wo0, wo1, wo2, wo3)
            att, lse = attend(span, low, ids, heads)
            att_own = swap(att, True, nmp, 1).reshape(d, rows)
            mid, n2 = middle_part(att_own, wos, tok, obias, gain2, shift2)
            n2_other = permute(n2, "core")
        o_own, o_send, g_own, g_send, dwu, dwd, gbias = feed(
            n2, n2_other, cot, cot_other, ubias, ups, downs, nz
        )
        g_got = permute(g_send, "core")
        gmid, gatt, gwo, sums2 = middle_back(g_own, g_got, mid, cot, att_own, wos, gain2, nmp)
        o_got = permute(o_send, "core")
        result = (mid + o_own + o_got.astype(F32) + dbias).astype(BF)
        dout = swap(gatt, False, nmp, 2)
        gproj, ggain = attend_back(span, low, raw, att, lse, dout, ids, gains, heads)
        order = jnp.stack([mp, x * 2 + 1 - c, (1 - x) * 2 + c, (1 - x) * 2 + 1 - c]).astype(jnp.int32)
        gn, gwq, sums1 = project_back(order, gproj, normed, tok_all, wt[: 3 * cols])
        got = permute(gn[1::2], "core")
        mine = gn[0::2].astype(F32) + got.astype(F32)
        far = permute(mine[1].astype(BF), "x")
        gnormed = mine[0] + far.astype(F32)
        grad_tokens = tokens_back(gnormed, tok, gain1, gmid)

        def pick(v, i):
            return lax.dynamic_index_in_dim(v, i, 0, keepdims=False)

        def along(v, kind):
            i = {"x": None, "y": y}[kind]
            if i is None:
                keep, send = v[0], v[1]
            else:
                keep, send = pick(v, i), pick(v, 1 - i)
            return (keep.astype(F32) + permute(send, kind).astype(F32)).astype(BF)

        def along_z(v):
            total = pick(v, z).astype(F32)
            for k in range(1, nz):
                total = total + permute(pick(v, (z + k) % nz), "z", k).astype(F32)
            return total

        def over_dp(v):
            if drow % 16:
                return lax.psum_scatter(v.astype(F32), "dp", scatter_dimension=0, tiled=True)
            v = v.reshape(nz, 2, drow, v.shape[-1]).transpose(1, 0, 2, 3)
            return along_z(along(v, "y"))

        def reduce_columns(v, y_first):
            if drow % 16 or not y_first:
                return over_dp(along(v, "x"))
            v = v.reshape(2, nz, 2, drow, unit).transpose(2, 0, 1, 3, 4)
            return along_z(along(along(v, "y"), "x"))

        grad_up = reduce_columns(dwu, False)
        grad_down = reduce_columns(dwd, True)
        mine_o = jnp.stack([pick(gwo, mp), pick(gwo, (1 - x) * 2 + c)])
        send_o = jnp.stack([pick(gwo, x * 2 + 1 - c), pick(gwo, (1 - x) * 2 + 1 - c)])
        go = (mine_o.astype(F32) + permute(send_o, "core").astype(F32)).astype(BF)
        go = along(go, "x")
        grad_att = over_dp(jnp.concatenate([gwq, go], axis=1))

        def spread(v, at, size):
            return lax.dynamic_update_slice_in_dim(jnp.zeros((size,), F32), v, at, 0)

        gq = spread(ggain[:cols, 0], mp * cols, d)
        gk = spread(ggain[cols:, 0], mp * cols, d)
        gb = spread(gbias[0, 0], mp * unit, nmp * unit)
        gb = gb + spread(gbias[1, 0], ((1 - x) * 2 + c) * unit, nmp * unit)
        eight = jnp.stack([sums1[0], sums1[1], gq, gk, sums2[0], sums2[1], sums2[2], sums2[3]])
        parts = jnp.concatenate(
            [
                eight.reshape(8, ndev, small).transpose(1, 0, 2).reshape(ndev, 8 * small),
                gb.reshape(ndev, used - 8 * small),
            ],
            axis=1,
        )
        parts = jnp.pad(parts, ((0, 0), (0, 1024 - used))).reshape(ndev, 8, 128)
        tot = vector_sums(parts, ndp, nmp).reshape(1024)
        vgrads = [tot[i * small : (i + 1) * small] for i in range(8)] + [tot[8 * small : used]]

        return (
            result[None],
            grad_tokens[None],
            grad_att[:, : 3 * cols].reshape(drow, 3, cols),
            grad_att[:, 3 * cols :],
            grad_up,
            grad_down,
            vgrads[0],
            vgrads[1],
            vgrads[2],
            vgrads[3],
            vgrads[4],
            vgrads[5],
            vgrads[6],
            vgrads[8],
            vgrads[7],
        )

    vec_spec = P(("dp", "mp"))
    return jax.shard_map(
        body,
        mesh=mesh,
        in_specs=(
            P("dp", "mp", None),
            P("dp", None),
            P("dp", None, "mp"),
            P("dp", "mp"),
            P("dp", "mp"),
            P("dp", "mp"),
        )
        + (vec_spec,) * 9
        + (P("dp", "mp", None),),
        out_specs=(
            P("dp", "mp", None),
            P("dp", "mp", None),
            P("dp", None, "mp"),
            P("dp", "mp"),
            P("dp", "mp"),
            P("dp", "mp"),
        )
        + (vec_spec,) * 9,
        check_vma=False,
    )
```
